32 devices in a mesh: bucket: 4 (over z), fsdp: 8 (over y, x, core).
Axes of the slice: x: 2, y: 2, z: 4, core: 2. Of those that a mesh axis runs over, the one named last changes fastest.
Arguments:
- tokens: bfloat16 [32, 128, 1536], P(('bucket', 'fsdp')), may hold values from -6 to 6
- cond: bfloat16 [32, 4, 1024], P(('bucket', 'fsdp')), may hold values from -6 to 6
- text: bfloat16 [32, 256, 4096], P(('bucket', 'fsdp')), may hold values from -6 to 6
- segments: int32 [32, 128], P(('bucket', 'fsdp')), may hold values from 0 to 3, never falling along the last dimension, each value on 1 to 64 neighbouring positions
- positions: int32 [32, 2, 128], P(('bucket', 'fsdp')), may hold values from 0 to 63
- counts: int32 [4], replicated, may hold values from 256 to 1024
- ada_weight: bfloat16 [1024, 6144], P('fsdp'), may hold values from -0.1875 to 0.1875
- ada_bias: bfloat16 [6144], P('fsdp'), may hold values from -1.5 to 1.5
- gains: bfloat16 [6, 1536], P(None, 'fsdp'), may hold values from 0.099609375 to 1.8984375
- attn_weight: bfloat16 [3, 1536, 1536], P(None, 'fsdp'), may hold values from -0.15625 to 0.15625
- out_weight: bfloat16 [1536, 1536], P('fsdp'), may hold values from -0.625 to 0.625
- text_weight: bfloat16 [2, 4096, 1536], P(None, 'fsdp'), may hold values from -0.09375 to 0.09375
- ffn_weight: bfloat16 [2, 1536, 4096], P(None, 'fsdp'), may hold values from -0.15625 to 0.15625
- down_weight: bfloat16 [4096, 1536], P('fsdp'), may hold values from -0.09375 to 0.09375
- cotangent: bfloat16 [32, 128, 1536], P(('bucket', 'fsdp')), may hold values from -6 to 6
Outputs:
- block_out: bfloat16 [32, 128, 1536], P(('bucket', 'fsdp'))
- token_grad: float32 [32, 128, 1536], P(('bucket', 'fsdp'))
- ada_weight_grad: float32 [1024, 6144], P(('bucket', 'fsdp'))
- ada_bias_grad: float32 [6144], P(('bucket', 'fsdp'))
- gains_grad: float32 [6, 1536], P(None, ('bucket', 'fsdp'))
- attn_weight_grad: float32 [3, 1536, 1536], P(None, ('bucket', 'fsdp'))
- out_weight_grad: float32 [1536, 1536], P(('bucket', 'fsdp'))
- text_weight_grad: float32 [2, 4096, 1536], P(None, ('bucket', 'fsdp'))
- ffn_weight_grad: float32 [2, 1536, 4096], P(None, ('bucket', 'fsdp'))
- down_weight_grad: float32 [4096, 1536], P(('bucket', 'fsdp'))
The draws below stay inside these ranges and needn't reach their ends.
Inputs may be any that keep to these rules, and one draw needn't show every extreme that they name: `segments`: in each row image numbers never fall, every image holds one token or more, and one image holds exactly half of the row's 128 tokens.
All inputs are finite; a program needn't handle non-finite values.
Results may differ from the reference program's by a relative error of at most 0.014.
The reference program's roundings to bfloat16 on the way count: a program that leaves them out, or rounds other values in their place, can miss the bound.
Values may be sent and summed in bfloat16 or wider, within the bound.
A program may use at most 512 MiB of HBM per device.

```python
import math
import jax
import jax.numpy as jnp
import numpy as np
from jax import lax

D = 1536
HEADS = 24
HDIM = 64
FF = 4096
TXTD = 4096
CDIM = 1024
ROW = 128
IMGS = 4
TXT = 64
ROWS = 32
N_BUCKET = 4
N_FSDP = 8


def set_ends(values, rng, least, largest):
    longest = values.shape.index(max(values.shape))
    spots = []
    for shift in (0, 1):
        where = [jax.random.randint(jax.random.fold_in(rng, axis), (), 0, length) for axis, length in enumerate(values.shape)]
        where[longest] = (where[longest] + shift) % values.shape[longest]
        spots.append(tuple(where))
    return values.at[spots[0]].set(least).at[spots[1]].set(largest)


def with_spikes(entries, stream_key, source, target, blocks, factor):
    def block_of(dim):
        return (jnp.arange(entries.shape[dim]) // (entries.shape[dim] // blocks)).reshape((-1,) + (1,) * (entries.ndim - 1 - dim))

    one_side = jax.random.permutation(stream_key, blocks)[block_of(target)]
    second = (block_of(target) + blocks // 2) % blocks
    return jnp.where((block_of(source) == one_side) | (block_of(source) == second), factor * entries, entries)


def levels(stream_key, extent, shards, smallest, largest):
    level, own = 1.0, jax.random.fold_in(stream_key, 6)
    for dim, blocks in shards:
        draws = jnp.exp(jax.random.uniform(jax.random.fold_in(own, dim), (blocks,), jnp.float32, smallest / len(shards), largest / len(shards)))
        level = level * jnp.repeat(draws, extent[dim] // blocks).reshape([-1 if axis == dim else 1 for axis in range(len(extent))])
    return level


def length_profile(amount, total, reach, slope):
    portions = [(1 << 20) // math.isqrt(standing ** slope) + 1 for standing in range(2, amount + 1)]
    surplus, holding = total - reach - (amount - 1), [1] * (amount - 1)
    while surplus > 0:
        movable = [i for i in range(amount - 1) if holding[i] < reach]
        whole, left = sum([portions[i] for i in movable]), surplus
        for i in movable:
            extra = min(reach - holding[i], max(1, left * portions[i] // whole), surplus)
            holding[i] = holding[i] + extra
            surplus = surplus - extra
    return np.array([reach] + holding)


def uneven_parts(own_key, count, total, bound, slope):
    if count == 2:
        one = jax.random.randint(own_key, (), max(1, total - bound), min(bound, total - 1) + 1)
        return jnp.stack([one, total - one])
    lengths = jnp.asarray(length_profile(count, total, bound, slope), jnp.int32)
    pairs = (count - 1) // 2
    giver, taker = lengths[1:1 + 2 * pairs:2], lengths[2:2 + 2 * pairs:2]
    margin = jnp.minimum(giver - 1, bound - taker)
    shifted = jax.random.randint(jax.random.fold_in(own_key, 1), (pairs,), 0, 1 << 20) % (margin + 1)
    lengths = lengths.at[1:1 + 2 * pairs:2].set(giver - shifted).at[2:2 + 2 * pairs:2].set(taker + shifted)
    return lengths[jax.random.permutation(jax.random.fold_in(own_key, 2), count)]


def gaussian(own_key, shape, spread, bound, split=(), kind=jnp.bfloat16):
    loudness = levels(own_key, shape, split, -0.22, 0.18) if split else 1.0
    values = jax.random.normal(own_key, shape, jnp.float32) * spread * loudness
    return jnp.minimum(jnp.maximum(values, -bound), bound).astype(kind)


def noise_with(key, extent, width, bound, pieces, heavy, held_as=jnp.bfloat16):
    values = width * jax.random.normal(key, extent, jnp.float32)
    if pieces:
        values = values * levels(key, extent, pieces, -0.22, 0.18)
    return jnp.clip(with_spikes(values, jax.random.fold_in(key, 3), *heavy), -bound, bound).astype(held_as)


def setup_inputs(seed: int = 0) -> dict:
    key_of = jax.random.split(jax.random.key(seed), 16)
    tokens = noise_with(key_of[0], (ROWS, ROW, D), 1.0, 6.0, ((0, 32),), (0, 2, 32, 2.75))
    cond = gaussian(key_of[1], (ROWS, IMGS, CDIM), 1.0, 6.0, ((0, 32),))
    text = gaussian(key_of[2], (ROWS, IMGS * TXT, TXTD), 1.0, 6.0, ((0, 32),))
    segments = jax.vmap(lambda own: jnp.searchsorted(jnp.cumsum(uneven_parts(own, IMGS, ROW, ROW // 2, 1)), jnp.arange(ROW), side="right"))(jax.random.split(key_of[3], ROWS)).reshape((ROWS, ROW)).astype(jnp.int32)
    positions = set_ends(jax.random.randint(key_of[4], (ROWS, 2, ROW), 0, 64), jax.random.fold_in(key_of[4], 1), 0, 63).astype(jnp.int32)
    counts = set_ends(jax.random.randint(key_of[5], (N_BUCKET,), ROW * N_FSDP // 4, ROW * N_FSDP + 1), jax.random.fold_in(key_of[5], 1), ROW * N_FSDP // 4, ROW * N_FSDP).astype(jnp.int32)
    ada_weight = gaussian(key_of[6], (CDIM, 4 * D), CDIM ** -0.5, 0.1875, ((0, 8),))
    ada_bias = gaussian(key_of[7], (4 * D,), 0.3, 1.5, ((0, 8),))
    gains = jnp.clip(1.0 + 0.18 * jax.random.normal(key_of[8], (6, D), jnp.float32), 0.099609375, 1.8984375).astype(jnp.bfloat16)
    attn_weight = gaussian(key_of[9], (3, D, D), D ** -0.5, 0.15625, ((1, 8),))
    out_weight = gaussian(key_of[10], (D, D), (D // 16) ** -0.5, 0.625, ((0, 8),))
    text_weight = gaussian(key_of[11], (2, TXTD, D), TXTD ** -0.5, 0.09375, ((1, 8),))
    ffn_weight = gaussian(key_of[12], (2, D, FF), D ** -0.5, 0.15625, ((1, 8),))
    down_weight = gaussian(key_of[13], (FF, D), FF ** -0.5, 0.09375, ((0, 8),))
    cotangent = gaussian(key_of[14], (ROWS, ROW, D), 1.0, 6.0, ((0, 32),))
    return dict(tokens=tokens, cond=cond, text=text, segments=segments, positions=positions, counts=counts, ada_weight=ada_weight, ada_bias=ada_bias, gains=gains, attn_weight=attn_weight, out_weight=out_weight, text_weight=text_weight, ffn_weight=ffn_weight, down_weight=down_weight, cotangent=cotangent)


@jax.custom_vjp
def low(v):
    return lax.optimization_barrier(v.astype(jnp.bfloat16)).astype(jnp.float32)

@jax.custom_vjp
def low_back(v):
    return v

def low_keep(v):
    return (low(v), None)

def low_pass(kept, grad):
    return (grad,)

def back_keep(v):
    return (v, None)

def back_low(kept, grad):
    return (low(grad),)
low.defvjp(low_keep, low_pass)
low_back.defvjp(back_keep, back_low)
HIGH = lax.Precision.HIGHEST
EPS = 1e-06
NEGATIVE = -1e+30

def matmul(left, right):
    return jnp.dot(left, right, precision=HIGH)

def silu(v):
    return v * jax.nn.sigmoid(v)

def norm_rows(v):
    return v * lax.rsqrt(lax.optimization_barrier(jnp.mean(v * v, axis=-1, keepdims=True)) + EPS)

def rotary_tables(pos):
    quarter = HDIM // 4
    freq = 10000.0 ** (-jnp.arange(quarter, dtype=jnp.float32) / quarter)
    angle = jnp.transpose(pos.astype(jnp.float32), (1, 0))[:, :, None] * freq[None, None, :]
    return (jnp.cos(angle), jnp.sin(angle))

def rotate(v, cosine, sine):
    rows = v.shape[0]
    parts = v.reshape(rows, HEADS, 2, 2, HDIM // 4)
    first = parts[:, :, :, 0]
    second = parts[:, :, :, 1]
    cosine = cosine[:, None]
    sine = sine[:, None]
    turned = jnp.stack([first * cosine - second * sine, first * sine + second * cosine], axis=3)
    return turned.reshape(rows, HEADS * HDIM)

def attend(query, keys, values, allowed):
    rows = query.shape[0]
    count = keys.shape[0]
    q_heads = query.reshape(rows, HEADS, HDIM)
    k_heads = keys.reshape(count, HEADS, HDIM)
    v_heads = values.reshape(count, HEADS, HDIM)
    scores = low_back(jnp.einsum('rhd,khd->hrk', q_heads, k_heads, precision=HIGH) * HDIM ** (-0.5))
    scores = jnp.where(allowed[None], scores, NEGATIVE)
    top = lax.optimization_barrier(jnp.max(scores, axis=-1, keepdims=True))
    expo = jnp.exp(scores - top)
    probs = low(expo / lax.optimization_barrier(jnp.sum(expo, axis=-1, keepdims=True)))
    return jnp.einsum('hrk,khd->rhd', probs, v_heads, precision=HIGH).reshape(rows, HEADS * HDIM)

def layer(params, x, cond, text, seg, pos):
    ada_w, ada_b, gains, attn_w, out_w, text_w, ffn_w, down_w = params
    cond_act = low(silu(cond))
    mod = low_back(matmul(cond_act, ada_w)) + ada_b[None, :]
    pick = (seg[:, None] == jnp.arange(IMGS, dtype=jnp.int32)[None, :]).astype(jnp.float32)
    per_token = matmul(pick, mod)
    scale1 = per_token[:, :D]
    gate1 = per_token[:, D:2 * D]
    scale2 = per_token[:, 2 * D:3 * D]
    gate2 = per_token[:, 3 * D:]
    h_one = low(norm_rows(x) * gains[0] * (1.0 + scale1))
    query = low_back(matmul(h_one, attn_w[0]))
    keyed = low_back(matmul(h_one, attn_w[1]))
    valued = low(low_back(matmul(h_one, attn_w[2])))
    cosine, sine = rotary_tables(pos)
    q_rot = low(rotate(norm_rows(query) * gains[2], cosine, sine))
    k_rot = low(rotate(norm_rows(keyed) * gains[3], cosine, sine))
    text_keys = low_back(matmul(text, text_w[0]))
    text_vals = low(low_back(matmul(text, text_w[1])))
    text_norm = low(norm_rows(text_keys) * gains[4])
    same = seg[:, None] == seg[None, :]
    owner = jnp.arange(IMGS * TXT, dtype=jnp.int32) // TXT
    mine = seg[:, None] == owner[None, :]
    self_out = low_back(attend(q_rot, k_rot, valued, same))
    cross_out = low_back(attend(q_rot, text_norm, text_vals, mine))
    comb = low(self_out + jnp.tanh(gains[5]) * cross_out)
    branch = low_back(matmul(comb, out_w))
    x_one = x + jnp.tanh(gate1) * branch
    h_two = low(norm_rows(x_one) * gains[1] * (1.0 + scale2))
    gate_pre = low_back(matmul(h_two, ffn_w[0]))
    upper = low_back(matmul(h_two, ffn_w[1]))
    hidden = low(silu(gate_pre) * upper)
    ffn_out = low_back(matmul(hidden, down_w))
    return x_one + jnp.tanh(gate2) * ffn_out

def reference(tokens, cond, text, segments, positions, counts, ada_weight, ada_bias, gains, attn_weight, out_weight, text_weight, ffn_weight, down_weight, cotangent):
    params = tuple((p.astype(jnp.float32) for p in (ada_weight, ada_bias, gains, attn_weight, out_weight, text_weight, ffn_weight, down_weight)))
    totals = counts.astype(jnp.float32)
    bucket_weight = N_BUCKET * totals / jnp.sum(totals)
    row_weight = jnp.repeat(bucket_weight, N_FSDP)
    zeros = tuple((jnp.zeros(p.shape, jnp.float32) for p in params))

    def one_row(acc, item):
        row_x, row_c, row_t, row_s, row_p, row_g, weight = item

        def forward(prm, xv):
            return layer(prm, xv, row_c.astype(jnp.float32), row_t.astype(jnp.float32), row_s, row_p)
        result, pull = jax.vjp(forward, params, row_x.astype(jnp.float32))
        grads, grad_x = pull(row_g.astype(jnp.float32) * weight)
        acc = tuple((a + b for a, b in zip(acc, grads)))
        return (acc, (result.astype(jnp.bfloat16), grad_x))
    acc, outs = lax.scan(one_row, zeros, (tokens, cond, text, segments, positions, cotangent, row_weight))
    return (outs[0], outs[1], acc[0], acc[1], acc[2], acc[3], acc[4], acc[5], acc[6], acc[7])
```

```python
import jax
import jax.numpy as jnp
from jax import lax
from jax.experimental import pallas as pl
from jax.experimental.pallas import tpu as pltpu
from jax.sharding import PartitionSpec as P

D = 1536
HEADS = 24
HDIM = 64
IMGS = 4
TXT = 64


EPS = 1e-06
NEGATIVE = -1e30
HIGH = lax.Precision.HIGHEST


def silu(v):
    return v * jax.nn.sigmoid(v)


def norm_rows(v):
    inverse = lax.rsqrt(jnp.mean(v * v, axis=-1, keepdims=True) + EPS)
    return (v * inverse, inverse)


def norm_back(grad, normed, inverse):
    return inverse * (grad - normed * jnp.mean(grad * normed, axis=-1, keepdims=True))


def rotary_tables(pos):
    quarter = HDIM // 4
    freq = 10000.0 ** (-jnp.arange(quarter, dtype=jnp.float32) / quarter)
    angle = jnp.transpose(pos.astype(jnp.float32), (1, 0))[:, :, None] * freq[None, None, :]
    return (jnp.cos(angle), jnp.sin(angle))


def rotate(v, cosine, sine):
    rows = v.shape[0]
    parts = v.reshape(rows, HEADS, 2, 2, HDIM // 4)
    first = parts[:, :, :, 0]
    second = parts[:, :, :, 1]
    cosine = cosine[:, None]
    sine = sine[:, None]
    turned = jnp.stack([first * cosine - second * sine, first * sine + second * cosine], axis=3)
    return turned.reshape(rows, HEADS * HDIM)


def to_pairs(v):
    return jnp.transpose(v.reshape(v.shape[0], HEADS // 2, 2 * HDIM), (1, 0, 2))


def from_pairs(v):
    return jnp.transpose(v, (1, 0, 2)).reshape(v.shape[1], HEADS * HDIM)


def pair_scores(query, keys):
    q_heads = query.reshape(query.shape[0], 2, HDIM)
    k_heads = keys.reshape(keys.shape[0], 2, HDIM)
    return jnp.einsum(
        "rhd,khd->hrk", q_heads, k_heads, preferred_element_type=jnp.float32
    ) * HDIM ** (-0.5)


def attend_forward(q_b, k_b, v_b, allowed):

    def one_pair(item):
        query, keys, values = item
        scores = jnp.where(allowed[None], pair_scores(query, keys), NEGATIVE)
        top = jnp.max(scores, axis=-1, keepdims=True)
        expo = jnp.exp(scores - top)
        total = jnp.sum(expo, axis=-1, keepdims=True)
        probs = (expo / total).astype(jnp.bfloat16)
        result = jnp.einsum(
            "hrk,khd->rhd",
            probs,
            values.reshape(values.shape[0], 2, HDIM),
            preferred_element_type=jnp.float32,
        )
        return (result.reshape(query.shape[0], 2 * HDIM), (top + jnp.log(total))[..., 0])

    outputs, saved = lax.map(one_pair, (to_pairs(q_b), to_pairs(k_b), to_pairs(v_b)))
    return (from_pairs(outputs), saved)


def attend_back(q_b, k_b, v_b, saved, grad_b, allowed):

    def one_pair(item):
        query, keys, values, lse_pair, grad = item
        rows = query.shape[0]
        count = keys.shape[0]
        scores = jnp.where(allowed[None], pair_scores(query, keys), NEGATIVE)
        probs = jnp.exp(scores - lse_pair[..., None])
        probs_b = probs.astype(jnp.bfloat16)
        grad_heads = grad.reshape(rows, 2, HDIM)
        dprob = jnp.einsum(
            "rhd,khd->hrk",
            grad_heads,
            values.reshape(count, 2, HDIM),
            preferred_element_type=jnp.float32,
        )
        dscore = (probs * (dprob - jnp.sum(probs * dprob, axis=-1, keepdims=True))).astype(
            jnp.bfloat16
        )
        factor = HDIM ** (-0.5)
        dquery = (
            jnp.einsum(
                "hrk,khd->rhd",
                dscore,
                keys.reshape(count, 2, HDIM),
                preferred_element_type=jnp.float32,
            )
            * factor
        )
        dkeys = (
            jnp.einsum(
                "hrk,rhd->khd",
                dscore,
                query.reshape(rows, 2, HDIM),
                preferred_element_type=jnp.float32,
            )
            * factor
        )
        dvalues = jnp.einsum(
            "hrk,rhd->khd", probs_b, grad_heads, preferred_element_type=jnp.float32
        )
        return (
            dquery.reshape(rows, 2 * HDIM),
            dkeys.reshape(count, 2 * HDIM),
            dvalues.reshape(count, 2 * HDIM),
        )

    d_query, d_keys, d_values = lax.map(
        one_pair, (to_pairs(q_b), to_pairs(k_b), to_pairs(v_b), saved, to_pairs(grad_b))
    )
    return (from_pairs(d_query), from_pairs(d_keys), from_pairs(d_values))


def mult(left, right):
    return jnp.dot(left, right, preferred_element_type=jnp.float32)


def per_device_general(
    tokens,
    cond,
    text,
    segments,
    positions,
    counts,
    ada_weight,
    ada_bias,
    gains,
    attn_weight,
    out_weight,
    text_weight,
    ffn_weight,
    down_weight,
    cotangent,
):
    ada_w, ada_b, gain_rows, attn_w, out_w, text_w = (
        lax.all_gather(ada_weight, "fsdp", axis=0, tiled=True),
        lax.all_gather(ada_bias, "fsdp", axis=0, tiled=True),
        lax.all_gather(gains, "fsdp", axis=1, tiled=True),
        lax.all_gather(attn_weight, "fsdp", axis=1, tiled=True),
        lax.all_gather(out_weight, "fsdp", axis=0, tiled=True),
        lax.all_gather(text_weight, "fsdp", axis=1, tiled=True),
    )
    gain_f = gain_rows.astype(jnp.float32)
    x = tokens[0].astype(jnp.float32)
    seg = segments[0]
    cosine, sine = rotary_tables(positions[0])
    text_b = text[0]
    cond_act = silu(cond[0].astype(jnp.float32)).astype(jnp.bfloat16)
    mod = mult(cond_act, ada_w) + ada_b.astype(jnp.float32)[None, :]
    pick = (seg[:, None] == jnp.arange(IMGS, dtype=jnp.int32)[None, :]).astype(jnp.float32)
    per_token = jnp.dot(pick, mod, precision=HIGH)
    scale1 = per_token[:, :D]
    gate1 = per_token[:, D : 2 * D]
    scale2 = per_token[:, 2 * D : 3 * D]
    gate2 = per_token[:, 3 * D :]
    normed1, inverse1 = norm_rows(x)
    h_one = (normed1 * gain_f[0] * (1.0 + scale1)).astype(jnp.bfloat16)
    query = mult(h_one, attn_w[0])
    keyed = mult(h_one, attn_w[1])
    valued = mult(h_one, attn_w[2]).astype(jnp.bfloat16)
    q_norm, q_inv = norm_rows(query)
    k_norm, k_inv = norm_rows(keyed)
    q_rot = rotate(q_norm * gain_f[2], cosine, sine).astype(jnp.bfloat16)
    k_rot = rotate(k_norm * gain_f[3], cosine, sine).astype(jnp.bfloat16)
    text_keys = mult(text_b, text_w[0])
    text_vals = mult(text_b, text_w[1]).astype(jnp.bfloat16)
    t_norm, t_inv = norm_rows(text_keys)
    text_rot = (t_norm * gain_f[4]).astype(jnp.bfloat16)
    same = seg[:, None] == seg[None, :]
    owner = jnp.arange(IMGS * TXT, dtype=jnp.int32) // TXT
    mine = seg[:, None] == owner[None, :]
    self_out, self_lse = attend_forward(q_rot, k_rot, valued, same)
    cross_out, cross_lse = attend_forward(q_rot, text_rot, text_vals, mine)
    cross_gate = jnp.tanh(gain_f[5])
    comb = (self_out + cross_gate * cross_out).astype(jnp.bfloat16)
    branch = mult(comb, out_w)
    tanh_one = jnp.tanh(gate1)
    x_one = x + tanh_one * branch
    normed2, inverse2 = norm_rows(x_one)
    h_two = (normed2 * gain_f[1] * (1.0 + scale2)).astype(jnp.bfloat16)
    ffn_w, down_w = (
        lax.all_gather(ffn_weight, "fsdp", axis=1, tiled=True),
        lax.all_gather(down_weight, "fsdp", axis=0, tiled=True),
    )
    gate_pre = mult(h_two, ffn_w[0])
    upper = mult(h_two, ffn_w[1])
    sigm = jax.nn.sigmoid(gate_pre)
    silu_pre = gate_pre * sigm
    hidden = (silu_pre * upper).astype(jnp.bfloat16)
    ffn_out = mult(hidden, down_w)
    tanh_two = jnp.tanh(gate2)
    block_out = (x_one + tanh_two * ffn_out).astype(jnp.bfloat16)
    totals = counts.astype(jnp.float32)
    here = jnp.sum(
        jnp.where(
            jnp.arange(totals.shape[0], dtype=jnp.int32) == lax.axis_index("bucket"), totals, 0.0
        )
    )
    weight = lax.axis_size("bucket") * here / jnp.sum(totals)
    grad = cotangent[0].astype(jnp.float32) * weight
    back_ffn, back_down = (
        lax.all_gather(ffn_weight, "fsdp", axis=1, tiled=True),
        lax.all_gather(down_weight, "fsdp", axis=0, tiled=True),
    )
    d_gate2 = grad * ffn_out * (1.0 - tanh_two * tanh_two)
    d_ffn = (grad * tanh_two).astype(jnp.bfloat16)
    d_hidden = mult(d_ffn, back_down.T)
    g_down = mult(hidden.T, d_ffn)
    d_pre = (d_hidden * upper * sigm * (1.0 + gate_pre * (1.0 - sigm))).astype(jnp.bfloat16)
    d_up = (d_hidden * silu_pre).astype(jnp.bfloat16)
    d_h_two = mult(d_pre, back_ffn[0].T) + mult(d_up, back_ffn[1].T)
    g_ffn = jnp.stack([mult(h_two.T, d_pre), mult(h_two.T, d_up)])
    s_ffn, s_down = (
        lax.psum_scatter(g_ffn, ("bucket", "fsdp"), scatter_dimension=1, tiled=True),
        lax.psum_scatter(g_down, ("bucket", "fsdp"), scatter_dimension=0, tiled=True),
    )
    back_attn, back_out = (
        lax.all_gather(attn_weight, "fsdp", axis=1, tiled=True),
        lax.all_gather(out_weight, "fsdp", axis=0, tiled=True),
    )
    g_gain_one = jnp.sum(d_h_two * normed2 * (1.0 + scale2), axis=0)
    d_scale2 = d_h_two * normed2 * gain_f[1]
    d_x_one = grad + norm_back(d_h_two * gain_f[1] * (1.0 + scale2), normed2, inverse2)
    d_gate1 = d_x_one * branch * (1.0 - tanh_one * tanh_one)
    d_branch = (d_x_one * tanh_one).astype(jnp.bfloat16)
    d_comb = mult(d_branch, back_out.T)
    g_out = mult(comb.T, d_branch)
    g_gain_five = jnp.sum(d_comb * cross_out, axis=0) * (1.0 - cross_gate * cross_gate)
    d_self = d_comb.astype(jnp.bfloat16)
    d_cross = (d_comb * cross_gate).astype(jnp.bfloat16)
    dq_self, dk_self, dv_self = attend_back(q_rot, k_rot, valued, self_lse, d_self, same)
    dq_cross, dk_text, dv_text = attend_back(q_rot, text_rot, text_vals, cross_lse, d_cross, mine)
    d_q_norm = rotate(dq_self + dq_cross, cosine, -sine)
    g_gain_two = jnp.sum(d_q_norm * q_norm, axis=0)
    d_query = norm_back(d_q_norm * gain_f[2], q_norm, q_inv).astype(jnp.bfloat16)
    d_k_norm = rotate(dk_self, cosine, -sine)
    g_gain_three = jnp.sum(d_k_norm * k_norm, axis=0)
    d_keyed = norm_back(d_k_norm * gain_f[3], k_norm, k_inv).astype(jnp.bfloat16)
    d_valued = dv_self.astype(jnp.bfloat16)
    g_gain_four = jnp.sum(dk_text * t_norm, axis=0)
    d_text_keys = norm_back(dk_text * gain_f[4], t_norm, t_inv).astype(jnp.bfloat16)
    d_text_vals = dv_text.astype(jnp.bfloat16)
    g_text = jnp.stack([mult(text_b.T, d_text_keys), mult(text_b.T, d_text_vals)])
    d_h_one = (
        mult(d_query, back_attn[0].T)
        + mult(d_keyed, back_attn[1].T)
        + mult(d_valued, back_attn[2].T)
    )
    g_attn = jnp.stack([mult(h_one.T, d_query), mult(h_one.T, d_keyed), mult(h_one.T, d_valued)])
    g_gain_zero = jnp.sum(d_h_one * normed1 * (1.0 + scale1), axis=0)
    d_scale1 = d_h_one * normed1 * gain_f[0]
    token_grad = d_x_one + norm_back(d_h_one * gain_f[0] * (1.0 + scale1), normed1, inverse1)
    d_token_mod = jnp.concatenate([d_scale1, d_gate1, d_scale2, d_gate2], axis=1)
    d_mod = jnp.dot(pick.T, d_token_mod, precision=HIGH)
    g_ada_b = jnp.sum(d_mod, axis=0)
    g_ada_w = mult(cond_act.T, d_mod.astype(jnp.bfloat16))
    g_gains = jnp.stack(
        [g_gain_zero, g_gain_one, g_gain_two, g_gain_three, g_gain_four, g_gain_five]
    )
    s_ada_w, s_ada_b, s_gains, s_attn, s_out, s_text = (
        lax.psum_scatter(g_ada_w, ("bucket", "fsdp"), scatter_dimension=0, tiled=True),
        lax.psum_scatter(g_ada_b, ("bucket", "fsdp"), scatter_dimension=0, tiled=True),
        lax.psum_scatter(g_gains, ("bucket", "fsdp"), scatter_dimension=1, tiled=True),
        lax.psum_scatter(g_attn, ("bucket", "fsdp"), scatter_dimension=1, tiled=True),
        lax.psum_scatter(g_out, ("bucket", "fsdp"), scatter_dimension=0, tiled=True),
        lax.psum_scatter(g_text, ("bucket", "fsdp"), scatter_dimension=1, tiled=True),
    )
    return (
        block_out[None],
        token_grad[None],
        s_ada_w,
        s_ada_b,
        s_gains,
        s_attn,
        s_out,
        s_text,
        s_ffn,
        s_down,
    )


ROW = 128
CHIPS = 4
HW = D // CHIPS
PAIRS = HW // 128


def swap(v, mask):
    return lax.ppermute(v, "fsdp", [(i, i ^ mask) for i in range(8)])


def at_x(v):
    return swap(v, 2)


def at_y(v):
    return swap(v, 4)


def at_core(v):
    return swap(v, 1)


def reorder(parts, index):
    bit = 1
    while bit < len(parts):
        odd = (index // bit) % 2 == 1
        parts = [jnp.where(odd, parts[j ^ bit], parts[j]) for j in range(len(parts))]
        bit *= 2
    return parts


def gather4(v):
    half = v.shape[0] // 2
    by_x = at_x(v)
    by_y = at_y(v)
    far = jnp.concatenate([at_y(by_x[:half]), at_x(by_y[half:])], axis=0)
    return [v, by_x, by_y, far]


def reduce4(parts):
    half = parts[0].shape[0] // 2
    low = jnp.bfloat16
    far_x = at_x(parts[3][:half].astype(low))
    far_y = at_y(parts[3][half:].astype(low))
    from_xa = at_x(parts[1][:half].astype(low))
    from_yb = at_y(parts[2][half:].astype(low))
    from_ya = at_y((parts[2][:half] + far_x.astype(jnp.float32)).astype(low))
    from_xb = at_x((parts[1][half:] + far_y.astype(jnp.float32)).astype(low))
    top = parts[0][:half] + from_xa.astype(jnp.float32) + from_ya.astype(jnp.float32)
    bottom = parts[0][half:] + from_yb.astype(jnp.float32) + from_xb.astype(jnp.float32)
    return jnp.concatenate([top, bottom], axis=0)


def exchange4(pick):
    return [pick(0), at_x(pick(1)), at_y(pick(2)), swap(pick(3), 6)]


def sum4(v):
    v = v + at_x(v)
    return v + at_y(v)


def sum4_rows(v):
    rows = v.reshape(CHIPS, -1)
    rows = rows + jnp.stack([at_x(rows)[j ^ 1] for j in range(CHIPS)])
    rows = rows + jnp.stack([at_y(rows)[j ^ 2] for j in range(CHIPS)])
    return rows.reshape(-1)


def both_cores(mine, core, axis):
    other = at_core(mine)
    first = jnp.where(core == 0, mine, other)
    second = jnp.where(core == 0, other, mine)
    return first, second


def column_weights(shard, chip, core, width):
    count, rows, _ = shard.shape
    got = exchange4(
        lambda j: lax.dynamic_slice_in_dim(shard, jnp.bitwise_xor(chip, j) * width, width, axis=2)
    )
    mine = jnp.stack(reorder(got, chip), axis=1)
    first, second = both_cores(mine, core, 0)
    return jnp.stack([first, second], axis=2).reshape(count, 8 * rows, width)


def row_weights(shard, core):
    first, second = both_cores(shard, core, 0)
    return jnp.concatenate([first, second], axis=0)


def core_half(view, core, axis):
    low = jnp.bfloat16
    keep = lax.dynamic_index_in_dim(view, core, axis, keepdims=False)
    give = lax.dynamic_index_in_dim(view, 1 - core, axis, keepdims=False)
    return keep + at_core(give.astype(low)).astype(jnp.float32)


def reduce_buckets(view, plane):
    low = jnp.bfloat16
    size = view.shape[0]
    up = down = None
    for step in range(1, size):
        piece = lax.dynamic_index_in_dim(
            view, jnp.minimum(plane + size - step, size - 1), 0, keepdims=False
        )
        if up is not None:
            piece = piece + up.astype(jnp.float32)
        up = lax.ppermute(piece.astype(low), "bucket", [(i, i + 1) for i in range(step)])
        piece = lax.dynamic_index_in_dim(
            view, jnp.maximum(plane - size + step, 0), 0, keepdims=False
        )
        if down is not None:
            piece = piece + down.astype(jnp.float32)
        down = lax.ppermute(
            piece.astype(low), "bucket", [(size - 1 - i, size - 2 - i) for i in range(step)]
        )
    own = lax.dynamic_index_in_dim(view, plane, 0, keepdims=False)
    return own + up.astype(jnp.float32) + down.astype(jnp.float32)


def to_column_owner(block, chip):
    got = exchange4(
        lambda j: lax.dynamic_index_in_dim(
            block, jnp.bitwise_xor(chip, j), 0, keepdims=False
        ).astype(jnp.bfloat16)
    )
    return jnp.concatenate(reorder(got, chip), axis=-1).astype(jnp.float32)


def to_row_owner(block):
    pairs = [
        (a * 8 + b * 2 + k, b * 8 + a * 2 + k) for a in range(4) for b in range(4) for k in range(2)
    ]
    return lax.ppermute(block.astype(jnp.bfloat16), ("bucket", "fsdp"), pairs).astype(jnp.float32)


def column_grad(partial, chip, core, plane):
    count, rows, width = partial.shape
    view = partial.reshape(count, 4, 4, 2, rows // 32, width)
    half = core_half(view, core, 3)
    mine = reduce_buckets(jnp.transpose(half, (1, 0, 2, 3, 4)), plane)
    return to_column_owner(jnp.transpose(mine, (1, 0, 2, 3)), chip)


def row_grad(partial, core, plane):
    rows, width = partial.shape
    half = core_half(partial.reshape(4, 2, rows // 8, width), core, 1)
    return to_row_owner(reduce_buckets(half, plane))


def partner(u):
    lane = lax.broadcasted_iota(jnp.int32, u.shape, 1)
    ahead = pltpu.roll(u, u.shape[1] - 16, 1)
    behind = pltpu.roll(u, 16, 1)
    return jnp.where((lane // 16) % 2 == 0, ahead, behind)


def dot_t(a, b):
    return lax.dot_general(a, b, (((1,), (1,)), ((), ())), preferred_element_type=jnp.float32)


def dot_n(a, b):
    return lax.dot_general(a, b, (((1,), (0,)), ((), ())), preferred_element_type=jnp.float32)


def t_dot(a, b):
    return lax.dot_general(a, b, (((0,), (0,)), ((), ())), preferred_element_type=jnp.float32)


def softmax_of(scores, allowed):
    scores = jnp.where(allowed, scores * HDIM ** (-0.5), NEGATIVE)
    top = jnp.max(scores, axis=-1, keepdims=True)
    expo = jnp.exp(scores - top)
    return expo / jnp.sum(expo, axis=-1, keepdims=True)


def head_mask(v, head):
    lane = lax.broadcasted_iota(jnp.int32, v.shape, 1)
    return jnp.where((lane // HDIM) == head, v, jnp.zeros_like(v))


def masks_of(seg_col, seg_row, captions):
    same = seg_col == seg_row
    owner = lax.broadcasted_iota(jnp.int32, (seg_col.shape[0], captions), 1) // TXT
    return same, seg_col == owner


def attend_kernel(
    q_ref, k_ref, v_ref, iq_ref, ik_ref, cos_ref, sin_ref, tk_ref, it_ref, tv_ref, sc_ref, sr_ref,
    g_ref, comb_ref, cross_ref, qr_ref, kr_ref, tr_ref,
):
    same, mine = masks_of(sc_ref[...], sr_ref[0], tk_ref.shape[0])
    cosine = cos_ref[...]
    sine = sin_ref[...]
    low = jnp.bfloat16
    for pair in range(PAIRS):
        at = pl.ds(pair * 128, 128)
        qn = q_ref[:, at] * iq_ref[...] * g_ref[2:3, at]
        kn = k_ref[:, at] * ik_ref[...] * g_ref[3:4, at]
        qr = (qn * cosine + partner(qn) * sine).astype(low)
        kr = (kn * cosine + partner(kn) * sine).astype(low)
        tr = (tk_ref[:, at] * it_ref[...] * g_ref[4:5, at]).astype(low)
        qr_ref[:, at] = qr
        kr_ref[:, at] = kr
        tr_ref[:, at] = tr
        vv = v_ref[:, at]
        tv = tv_ref[:, at]
        self_out = jnp.zeros(qn.shape, jnp.float32)
        cross_out = jnp.zeros(qn.shape, jnp.float32)
        for head in range(2):
            qh = head_mask(qr, head)
            probs = softmax_of(dot_t(qh, kr), same).astype(low)
            self_out = self_out + head_mask(dot_n(probs, vv), head)
            probs = softmax_of(dot_t(qh, tr), mine).astype(low)
            cross_out = cross_out + head_mask(dot_n(probs, tv), head)
        cross_ref[:, at] = cross_out
        comb_ref[:, at] = (self_out + jnp.tanh(g_ref[5:6, at]) * cross_out).astype(low)


def attend_back_kernel(
    qr_ref, kr_ref, v_ref, tr_ref, tv_ref, dc_ref, cross_ref, q_ref, k_ref, tk_ref, iq_ref, ik_ref,
    it_ref, cos_ref, sin_ref, sc_ref, sr_ref, g_ref,
    dq_ref, dk_ref, dv_ref, dt_ref, dtv_ref, sq_ref, sk_ref, st_ref, gg_ref,
):
    same, mine = masks_of(sc_ref[...], sr_ref[0], tk_ref.shape[0])
    cosine = cos_ref[...]
    sine = sin_ref[...]
    low = jnp.bfloat16
    factor = HDIM ** (-0.5)
    gg_ref[...] = jnp.zeros(gg_ref.shape, jnp.float32)
    sum_q = sum_k = sum_t = 0.0
    for pair in range(PAIRS):
        at = pl.ds(pair * 128, 128)
        qr = qr_ref[:, at]
        kr = kr_ref[:, at]
        vv = v_ref[:, at]
        tr = tr_ref[:, at]
        tv = tv_ref[:, at]
        dcomb = dc_ref[:, at]
        d_self = dcomb.astype(low)
        d_cross = (dcomb * jnp.tanh(g_ref[5:6, at])).astype(low)
        dq = jnp.zeros(dcomb.shape, jnp.float32)
        dk = jnp.zeros(dcomb.shape, jnp.float32)
        dv = jnp.zeros(dcomb.shape, jnp.float32)
        dt = jnp.zeros((tr.shape[0], 128), jnp.float32)
        dtv = jnp.zeros((tr.shape[0], 128), jnp.float32)
        for head in range(2):
            qh = head_mask(qr, head)
            probs = softmax_of(dot_t(qh, kr), same)
            grad = head_mask(d_self, head)
            dprob = dot_t(grad, vv)
            dscore = probs * (dprob - jnp.sum(probs * dprob, axis=-1, keepdims=True))
            dscore = dscore.astype(low)
            dq = dq + dot_n(dscore, head_mask(kr, head))
            dk = dk + t_dot(dscore, qh)
            dv = dv + t_dot(probs.astype(low), grad)
            probs = softmax_of(dot_t(qh, tr), mine)
            grad = head_mask(d_cross, head)
            dprob = dot_t(grad, tv)
            dscore = probs * (dprob - jnp.sum(probs * dprob, axis=-1, keepdims=True))
            dscore = dscore.astype(low)
            dq = dq + dot_n(dscore, head_mask(tr, head))
            dt = dt + t_dot(dscore, qh)
            dtv = dtv + t_dot(probs.astype(low), grad)
        dq = dq * factor
        dk = dk * factor
        dt = dt * factor
        dq = dq * cosine - partner(dq) * sine
        dk = dk * cosine - partner(dk) * sine
        q_norm = q_ref[:, at] * iq_ref[...]
        k_norm = k_ref[:, at] * ik_ref[...]
        t_norm = tk_ref[:, at] * it_ref[...]
        gg_ref[0, 0:1, at] = jnp.sum(dq * q_norm, axis=0, keepdims=True)
        gg_ref[0, 1:2, at] = jnp.sum(dk * k_norm, axis=0, keepdims=True)
        gg_ref[0, 2:3, at] = jnp.sum(dt * t_norm, axis=0, keepdims=True)
        gg_ref[0, 3:4, at] = jnp.sum(dcomb * cross_ref[:, at], axis=0, keepdims=True)
        dq = dq * g_ref[2:3, at]
        dk = dk * g_ref[3:4, at]
        dt = dt * g_ref[4:5, at]
        sum_q = sum_q + jnp.sum(dq * q_norm, axis=-1, keepdims=True)
        sum_k = sum_k + jnp.sum(dk * k_norm, axis=-1, keepdims=True)
        sum_t = sum_t + jnp.sum(dt * t_norm, axis=-1, keepdims=True)
        dq_ref[:, at] = dq
        dk_ref[:, at] = dk
        dv_ref[:, at] = dv.astype(low)
        dt_ref[:, at] = dt
        dtv_ref[:, at] = dtv.astype(low)
    sq_ref[...] = sum_q
    sk_ref[...] = sum_k
    st_ref[...] = sum_t


def row_spec(rows, width):
    return pl.BlockSpec((rows, width), lambda i: (i, 0))


def attend_all(q, k, v, iq, ik, cosine, sine, tk, it, tv, seg_col, seg_row, gains):
    cap = IMGS * TXT
    low = jnp.bfloat16
    big = row_spec(ROW, HW)
    text = row_spec(cap, HW)
    one = row_spec(ROW, 1)
    table = row_spec(ROW, 128)
    shape = jax.ShapeDtypeStruct
    return pl.pallas_call(
        attend_kernel,
        grid=(CHIPS,),
        in_specs=[
            big, big, big, one, one, table, table, text, row_spec(cap, 1), text, one,
            pl.BlockSpec((1, 1, ROW), lambda i: (i, 0, 0)),
            pl.BlockSpec((6, HW), lambda i: (0, 0)),
        ],
        out_specs=[big, big, big, big, text],
        out_shape=[
            shape((CHIPS * ROW, HW), low),
            shape((CHIPS * ROW, HW), jnp.float32),
            shape((CHIPS * ROW, HW), low),
            shape((CHIPS * ROW, HW), low),
            shape((CHIPS * cap, HW), low),
        ],
        cost_estimate=pl.CostEstimate(
            flops=4 * 24 * 128 * 384 * 128, bytes_accessed=10_000_000, transcendentals=1_200_000
        ),
    )(q, k, v, iq, ik, cosine, sine, tk, it, tv, seg_col, seg_row, gains)


def attend_all_back(
    qr, kr, v, tr, tv, dcomb, cross, q, k, tk, iq, ik, it, cosine, sine, seg_col, seg_row, gains
):
    cap = IMGS * TXT
    low = jnp.bfloat16
    big = row_spec(ROW, HW)
    text = row_spec(cap, HW)
    one = row_spec(ROW, 1)
    table = row_spec(ROW, 128)
    shape = jax.ShapeDtypeStruct
    return pl.pallas_call(
        attend_back_kernel,
        grid=(CHIPS,),
        in_specs=[
            big, big, big, text, text, big, big, big, big, text, one, one, row_spec(cap, 1), table,
            table, one,
            pl.BlockSpec((1, 1, ROW), lambda i: (i, 0, 0)),
            pl.BlockSpec((6, HW), lambda i: (0, 0)),
        ],
        out_specs=[
            big, big, big, text, text, one, one, row_spec(cap, 1),
            pl.BlockSpec((1, 8, HW), lambda i: (i, 0, 0)),
        ],
        out_shape=[
            shape((CHIPS * ROW, HW), jnp.float32),
            shape((CHIPS * ROW, HW), jnp.float32),
            shape((CHIPS * ROW, HW), low),
            shape((CHIPS * cap, HW), jnp.float32),
            shape((CHIPS * cap, HW), low),
            shape((CHIPS * ROW, 1), jnp.float32),
            shape((CHIPS * ROW, 1), jnp.float32),
            shape((CHIPS * cap, 1), jnp.float32),
            shape((CHIPS, 8, HW), jnp.float32),
        ],
        cost_estimate=pl.CostEstimate(
            flops=10 * 24 * 128 * 384 * 128, bytes_accessed=20_000_000, transcendentals=1_200_000
        ),
    )(qr, kr, v, tr, tv, dcomb, cross, q, k, tk, iq, ik, it, cosine, sine, seg_col, seg_row, gains)


def per_device(
    tokens,
    cond,
    text,
    segments,
    positions,
    counts,
    ada_weight,
    ada_bias,
    gains,
    attn_weight,
    out_weight,
    text_weight,
    ffn_weight,
    down_weight,
    cotangent,
):
    low = jnp.bfloat16
    full = jnp.float32
    plane = lax.axis_index("bucket")
    slot = lax.axis_index("fsdp")
    core = slot % 2
    chip = slot // 2
    ff = ffn_weight.shape[2] // CHIPS

    cond_act = silu(cond[0].astype(full)).astype(low)
    packed = []
    for j in range(8):
        piece = lax.dynamic_slice_in_dim(cond_act, jnp.bitwise_xor(slot, j) * 128, 128, axis=1)
        piece = jnp.concatenate([piece.reshape(4, 128), gains.reshape(9, 128)], axis=0)
        packed.append(piece if j == 0 else swap(piece, j))
    conds = jnp.concatenate([p[:4] for p in packed], axis=0)
    gain_f = jnp.stack(reorder([p[4:].reshape(6, 192) for p in packed], slot), axis=1)
    gain_f = gain_f.reshape(6, D).astype(full)
    bias = lax.dynamic_update_slice_in_dim(
        jnp.zeros((ada_weight.shape[1],), full), ada_bias.astype(full), slot * ada_bias.shape[0], 0
    )
    mod_parts = (mult(conds, ada_weight) + bias[None, :]).reshape(8, IMGS, -1)
    mod = mod_parts[0]
    for j in range(1, 8):
        mod = mod + swap(mod_parts[j], j)

    seg = segments[0]
    index = jnp.concatenate([seg[None, :], positions[0]], axis=0)
    indices = [index, at_x(index), at_y(index), swap(index, 6)]
    seg_all = jnp.stack([i[0] for i in indices])
    pos_all = jnp.stack([i[1:] for i in indices])
    seg_col = seg_all.reshape(CHIPS * ROW, 1)
    seg_row = seg_all.reshape(CHIPS, 1, ROW)
    lane = jnp.arange(128, dtype=jnp.int32)
    quarter = HDIM // 4
    freq = (10000.0 ** (-jnp.arange(quarter, dtype=full) / quarter))[lane % quarter]
    where_row = ((lane // 32) % 2 == 0)[None, None, :]
    pos_lane = jnp.where(where_row, pos_all[:, 0, :, None], pos_all[:, 1, :, None]).astype(full)
    angle = (pos_lane * freq[None, None, :]).reshape(CHIPS * ROW, 128)
    cosine = jnp.cos(angle)
    sine = jnp.where(((lane // quarter) % 2 == 0)[None, :], -1.0, 1.0) * jnp.sin(angle)

    attn_w = column_weights(attn_weight, chip, core, HW)
    text_w = column_weights(text_weight, chip, core, HW)
    ffn_w = column_weights(ffn_weight, chip, core, ff)
    out_w = row_weights(out_weight, core)
    down_w = row_weights(down_weight, core)
    gain_s = lax.dynamic_slice_in_dim(gain_f, chip * HW, HW, axis=1)

    def per_token(part):
        rows = mod[:, part * D : (part + 1) * D]
        out = rows[IMGS - 1][None, :]
        for i in range(IMGS - 2, -1, -1):
            out = jnp.where(seg[:, None] == i, rows[i][None, :], out)
        return out

    scale1 = per_token(0)
    gate1 = per_token(1)
    scale2 = per_token(2)
    gate2 = per_token(3)
    tanh_one = jnp.tanh(gate1)
    tanh_two = jnp.tanh(gate2)

    x = tokens[0].astype(full)
    normed1, inverse1 = norm_rows(x)
    h_one = (normed1 * gain_f[0] * (1.0 + scale1)).astype(low)
    h_all = jnp.concatenate(gather4(h_one), axis=0)
    query = mult(h_all, attn_w[0])
    keyed = mult(h_all, attn_w[1])
    valued = mult(h_all, attn_w[2]).astype(low)
    squares = jnp.stack(
        [jnp.sum(query * query, axis=-1), jnp.sum(keyed * keyed, axis=-1)]
    ).reshape(2, CHIPS, ROW)
    squares = sum4_rows(jnp.transpose(squares, (1, 0, 2)))
    squares = jnp.transpose(squares.reshape(CHIPS, 2, ROW), (1, 0, 2)).reshape(2, CHIPS * ROW)
    inv_qk = lax.rsqrt(squares / D + EPS)[:, :, None]

    text_parts = gather4(text[0])
    text_all = jnp.concatenate(text_parts, axis=0)
    text_keys = mult(text_all, text_w[0])
    text_vals = mult(text_all, text_w[1]).astype(low)
    inv_t = lax.rsqrt(sum4_rows(jnp.sum(text_keys * text_keys, axis=-1)) / D + EPS)[:, None]

    comb, cross_out, q_rot, k_rot, text_rot = attend_all(
        query, keyed, valued, inv_qk[0], inv_qk[1], cosine, sine, text_keys, inv_t, text_vals,
        seg_col, seg_row, gain_s,
    )
    branch = reduce4(list(mult(comb, out_w).reshape(CHIPS, ROW, D)))
    x_one = x + tanh_one * branch
    normed2, inverse2 = norm_rows(x_one)
    h_two = (normed2 * gain_f[1] * (1.0 + scale2)).astype(low)
    h_two_all = jnp.concatenate(gather4(h_two), axis=0)

    totals = counts.astype(full)
    here = jnp.sum(jnp.where(jnp.arange(totals.shape[0], dtype=jnp.int32) == plane, totals, 0.0))
    weight = lax.axis_size("bucket") * here / jnp.sum(totals)
    grad = cotangent[0].astype(full) * weight
    d_ffn = (grad * tanh_two).astype(low)
    d_ffn_all = jnp.concatenate(gather4(d_ffn), axis=0)

    gate_pre = mult(h_two_all, ffn_w[0])
    upper = mult(h_two_all, ffn_w[1])
    d_hidden = dot_t(d_ffn_all, down_w)
    sigm = jax.nn.sigmoid(gate_pre)
    silu_pre = gate_pre * sigm
    hidden = (silu_pre * upper).astype(low)
    d_pre = (d_hidden * upper * sigm * (1.0 + gate_pre * (1.0 - sigm))).astype(low)
    d_up = (d_hidden * silu_pre).astype(low)
    d_h_two = reduce4(
        list((dot_t(d_pre, ffn_w[0]) + dot_t(d_up, ffn_w[1])).reshape(CHIPS, ROW, D))
    )
    ffn_out = reduce4(list(mult(hidden, down_w).reshape(CHIPS, ROW, D)))
    block_out = (x_one + tanh_two * ffn_out).astype(low)
    d_gate2 = grad * ffn_out * (1.0 - tanh_two * tanh_two)

    g_gain_one = jnp.sum(d_h_two * normed2 * (1.0 + scale2), axis=0)
    d_scale2 = d_h_two * normed2 * gain_f[1]
    d_x_one = grad + norm_back(d_h_two * gain_f[1] * (1.0 + scale2), normed2, inverse2)
    d_gate1 = d_x_one * branch * (1.0 - tanh_one * tanh_one)
    d_branch = (d_x_one * tanh_one).astype(low)
    d_branch_all = jnp.concatenate(gather4(d_branch), axis=0)

    s_down = row_grad(t_dot(hidden, d_ffn_all), core, plane)
    s_ffn = column_grad(
        jnp.stack([t_dot(h_two_all, d_pre), t_dot(h_two_all, d_up)]), chip, core, plane
    )

    d_comb = dot_t(d_branch_all, out_w)
    (
        dq, dk, d_valued, dt, d_text_vals, sum_q, sum_k, sum_t, gg,
    ) = attend_all_back(
        q_rot, k_rot, valued, text_rot, text_vals, d_comb, cross_out, query, keyed, text_keys,
        inv_qk[0], inv_qk[1], inv_t, cosine, sine, seg_col, seg_row, gain_s,
    )
    sums = jnp.concatenate([s.reshape(CHIPS, -1) for s in (sum_q, sum_k, sum_t)], axis=1)
    sums = sum4_rows(sums).reshape(CHIPS, -1) / D
    mean_q = sums[:, :ROW].reshape(-1, 1)
    mean_k = sums[:, ROW : 2 * ROW].reshape(-1, 1)
    mean_t = sums[:, 2 * ROW :].reshape(-1, 1)
    d_query = (inv_qk[0] * (dq - query * inv_qk[0] * mean_q)).astype(low)
    d_keyed = (inv_qk[1] * (dk - keyed * inv_qk[1] * mean_k)).astype(low)
    d_text_keys = (inv_t * (dt - text_keys * inv_t * mean_t)).astype(low)
    d_h_one = reduce4(
        list(
            (
                dot_t(d_query, attn_w[0]) + dot_t(d_keyed, attn_w[1]) + dot_t(d_valued, attn_w[2])
            ).reshape(CHIPS, ROW, D)
        )
    )
    s_text = column_grad(
        jnp.stack([t_dot(text_all, d_text_keys), t_dot(text_all, d_text_vals)]), chip, core, plane
    )
    s_attn = column_grad(
        jnp.stack([t_dot(h_all, d_query), t_dot(h_all, d_keyed), t_dot(h_all, d_valued)]),
        chip, core, plane,
    )
    s_out = row_grad(t_dot(comb, d_branch_all), core, plane)

    g_gain_zero = jnp.sum(d_h_one * normed1 * (1.0 + scale1), axis=0)
    d_scale1 = d_h_one * normed1 * gain_f[0]
    token_grad = d_x_one + norm_back(d_h_one * gain_f[0] * (1.0 + scale1), normed1, inverse1)
    d_token_mod = jnp.concatenate([d_scale1, d_gate1, d_scale2, d_gate2], axis=1)
    pick = (seg[:, None] == jnp.arange(IMGS, dtype=jnp.int32)[None, :]).astype(full)
    d_mod = jnp.dot(pick.T, d_token_mod, precision=HIGH)

    gg = jnp.sum(gg, axis=0)[:4]
    cross_gate = jnp.tanh(gain_s[5])
    gg = gg.at[3].multiply(1.0 - cross_gate * cross_gate)
    spread = lax.dynamic_update_slice_in_dim(jnp.zeros((4, D), full), gg, chip * HW, axis=1)
    small = jnp.concatenate(
        [g_gain_zero[None], g_gain_one[None], spread, jnp.sum(d_mod, axis=0).reshape(4, D)], axis=0
    )
    small = small + at_core(small)
    small = sum4(small)
    small = small + lax.ppermute(small, "bucket", [(i, i ^ 1) for i in range(4)])
    small = small + lax.ppermute(small, "bucket", [(i, i ^ 2) for i in range(4)])
    rank = plane * 8 + slot
    s_gains = lax.dynamic_slice_in_dim(small[:6], rank * 48, 48, axis=1)
    s_ada_b = lax.dynamic_slice_in_dim(small[6:].reshape(-1), rank * 192, 192, axis=0)

    mod_low = d_mod.astype(low)
    mods = jnp.concatenate(gather4(mod_low), axis=0)
    planes_m = [mods]
    for shift in (1, 2, 3):
        planes_m.append(
            lax.ppermute(mods, "bucket", [(i, i ^ shift) for i in range(4)])
        )
    mods = jnp.concatenate(planes_m, axis=0)
    mods = jnp.concatenate([mods, at_core(mods)], axis=0)
    conds_all = jnp.concatenate(gather4(cond_act), axis=0)
    planes_c = [conds_all]
    for shift in (1, 2, 3):
        planes_c.append(
            lax.ppermute(conds_all, "bucket", [(i, i ^ shift) for i in range(4)])
        )
    conds_all = jnp.concatenate(planes_c, axis=0)
    conds_all = jnp.concatenate([conds_all, at_core(conds_all)], axis=0)
    s_ada_w = t_dot(lax.dynamic_slice_in_dim(conds_all, rank * 32, 32, axis=1), mods)

    return (
        block_out[None],
        token_grad[None],
        s_ada_w,
        s_ada_b,
        s_gains,
        s_attn,
        s_out,
        s_text,
        s_ffn,
        s_down,
    )


def solution(mesh):
    in_specs = (
        P(("bucket", "fsdp"), None, None),
        P(("bucket", "fsdp"), None, None),
        P(("bucket", "fsdp"), None, None),
        P(("bucket", "fsdp"), None),
        P(("bucket", "fsdp"), None, None),
        P(),
        P("fsdp", None),
        P("fsdp"),
        P(None, "fsdp"),
        P(None, "fsdp", None),
        P("fsdp", None),
        P(None, "fsdp", None),
        P(None, "fsdp", None),
        P("fsdp", None),
        P(("bucket", "fsdp"), None, None),
    )
    out_specs = (
        P(("bucket", "fsdp"), None, None),
        P(("bucket", "fsdp"), None, None),
        P(("bucket", "fsdp"), None),
        P(("bucket", "fsdp")),
        P(None, ("bucket", "fsdp")),
        P(None, ("bucket", "fsdp"), None),
        P(("bucket", "fsdp"), None),
        P(None, ("bucket", "fsdp"), None),
        P(None, ("bucket", "fsdp"), None),
        P(("bucket", "fsdp"), None),
    )
    fast = mesh.shape["fsdp"] == 8 and mesh.shape["bucket"] == 4
    return jax.shard_map(
        per_device if fast else per_device_general, mesh=mesh, in_specs=in_specs, out_specs=out_specs, check_vma=False
    )
```

```python
import jax
import jax.numpy as jnp
from jax import lax
from jax.experimental import pallas as pl
from jax.experimental.pallas import tpu as pltpu
from jax.sharding import PartitionSpec as P

D = 1536
HEADS = 24
HDIM = 64
IMGS = 4
TXT = 64


EPS = 1e-06
NEGATIVE = -1e30
HIGH = lax.Precision.HIGHEST


def silu(v):
    return v * jax.nn.sigmoid(v)


def norm_rows(v):
    inverse = lax.rsqrt(jnp.mean(v * v, axis=-1, keepdims=True) + EPS)
    return (v * inverse, inverse)


def norm_back(grad, normed, inverse):
    return inverse * (grad - normed * jnp.mean(grad * normed, axis=-1, keepdims=True))


def rotary_tables(pos):
    quarter = HDIM // 4
    freq = 10000.0 ** (-jnp.arange(quarter, dtype=jnp.float32) / quarter)
    angle = jnp.transpose(pos.astype(jnp.float32), (1, 0))[:, :, None] * freq[None, None, :]
    return (jnp.cos(angle), jnp.sin(angle))


def rotate(v, cosine, sine):
    rows = v.shape[0]
    parts = v.reshape(rows, HEADS, 2, 2, HDIM // 4)
    first = parts[:, :, :, 0]
    second = parts[:, :, :, 1]
    cosine = cosine[:, None]
    sine = sine[:, None]
    turned = jnp.stack([first * cosine - second * sine, first * sine + second * cosine], axis=3)
    return turned.reshape(rows, HEADS * HDIM)


def to_pairs(v):
    return jnp.transpose(v.reshape(v.shape[0], HEADS // 2, 2 * HDIM), (1, 0, 2))


def from_pairs(v):
    return jnp.transpose(v, (1, 0, 2)).reshape(v.shape[1], HEADS * HDIM)


def pair_scores(query, keys):
    q_heads = query.reshape(query.shape[0], 2, HDIM)
    k_heads = keys.reshape(keys.shape[0], 2, HDIM)
    return jnp.einsum(
        "rhd,khd->hrk", q_heads, k_heads, preferred_element_type=jnp.float32
    ) * HDIM ** (-0.5)


def attend_forward(q_b, k_b, v_b, allowed):

    def one_pair(item):
        query, keys, values = item
        scores = jnp.where(allowed[None], pair_scores(query, keys), NEGATIVE)
        top = jnp.max(scores, axis=-1, keepdims=True)
        expo = jnp.exp(scores - top)
        total = jnp.sum(expo, axis=-1, keepdims=True)
        probs = (expo / total).astype(jnp.bfloat16)
        result = jnp.einsum(
            "hrk,khd->rhd",
            probs,
            values.reshape(values.shape[0], 2, HDIM),
            preferred_element_type=jnp.float32,
        )
        return (result.reshape(query.shape[0], 2 * HDIM), (top + jnp.log(total))[..., 0])

    outputs, saved = lax.map(one_pair, (to_pairs(q_b), to_pairs(k_b), to_pairs(v_b)))
    return (from_pairs(outputs), saved)


def attend_back(q_b, k_b, v_b, saved, grad_b, allowed):

    def one_pair(item):
        query, keys, values, lse_pair, grad = item
        rows = query.shape[0]
        count = keys.shape[0]
        scores = jnp.where(allowed[None], pair_scores(query, keys), NEGATIVE)
        probs = jnp.exp(scores - lse_pair[..., None])
        probs_b = probs.astype(jnp.bfloat16)
        grad_heads = grad.reshape(rows, 2, HDIM)
        dprob = jnp.einsum(
            "rhd,khd->hrk",
            grad_heads,
            values.reshape(count, 2, HDIM),
            preferred_element_type=jnp.float32,
        )
        dscore = (probs * (dprob - jnp.sum(probs * dprob, axis=-1, keepdims=True))).astype(
            jnp.bfloat16
        )
        factor = HDIM ** (-0.5)
        dquery = (
            jnp.einsum(
                "hrk,khd->rhd",
                dscore,
                keys.reshape(count, 2, HDIM),
                preferred_element_type=jnp.float32,
            )
            * factor
        )
        dkeys = (
            jnp.einsum(
                "hrk,rhd->khd",
                dscore,
                query.reshape(rows, 2, HDIM),
                preferred_element_type=jnp.float32,
            )
            * factor
        )
        dvalues = jnp.einsum(
            "hrk,rhd->khd", probs_b, grad_heads, preferred_element_type=jnp.float32
        )
        return (
            dquery.reshape(rows, 2 * HDIM),
            dkeys.reshape(count, 2 * HDIM),
            dvalues.reshape(count, 2 * HDIM),
        )

    d_query, d_keys, d_values = lax.map(
        one_pair, (to_pairs(q_b), to_pairs(k_b), to_pairs(v_b), saved, to_pairs(grad_b))
    )
    return (from_pairs(d_query), from_pairs(d_keys), from_pairs(d_values))


def mult(left, right):
    return jnp.dot(left, right, preferred_element_type=jnp.float32)


def per_device_general(
    tokens,
    cond,
    text,
    segments,
    positions,
    counts,
    ada_weight,
    ada_bias,
    gains,
    attn_weight,
    out_weight,
    text_weight,
    ffn_weight,
    down_weight,
    cotangent,
):
    ada_w, ada_b, gain_rows, attn_w, out_w, text_w = (
        lax.all_gather(ada_weight, "fsdp", axis=0, tiled=True),
        lax.all_gather(ada_bias, "fsdp", axis=0, tiled=True),
        lax.all_gather(gains, "fsdp", axis=1, tiled=True),
        lax.all_gather(attn_weight, "fsdp", axis=1, tiled=True),
        lax.all_gather(out_weight, "fsdp", axis=0, tiled=True),
        lax.all_gather(text_weight, "fsdp", axis=1, tiled=True),
    )
    gain_f = gain_rows.astype(jnp.float32)
    x = tokens[0].astype(jnp.float32)
    seg = segments[0]
    cosine, sine = rotary_tables(positions[0])
    text_b = text[0]
    cond_act = silu(cond[0].astype(jnp.float32)).astype(jnp.bfloat16)
    mod = mult(cond_act, ada_w) + ada_b.astype(jnp.float32)[None, :]
    pick = (seg[:, None] == jnp.arange(IMGS, dtype=jnp.int32)[None, :]).astype(jnp.float32)
    per_token = jnp.dot(pick, mod, precision=HIGH)
    scale1 = per_token[:, :D]
    gate1 = per_token[:, D : 2 * D]
    scale2 = per_token[:, 2 * D : 3 * D]
    gate2 = per_token[:, 3 * D :]
    normed1, inverse1 = norm_rows(x)
    h_one = (normed1 * gain_f[0] * (1.0 + scale1)).astype(jnp.bfloat16)
    query = mult(h_one, attn_w[0])
    keyed = mult(h_one, attn_w[1])
    valued = mult(h_one, attn_w[2]).astype(jnp.bfloat16)
    q_norm, q_inv = norm_rows(query)
    k_norm, k_inv = norm_rows(keyed)
    q_rot = rotate(q_norm * gain_f[2], cosine, sine).astype(jnp.bfloat16)
    k_rot = rotate(k_norm * gain_f[3], cosine, sine).astype(jnp.bfloat16)
    text_keys = mult(text_b, text_w[0])
    text_vals = mult(text_b, text_w[1]).astype(jnp.bfloat16)
    t_norm, t_inv = norm_rows(text_keys)
    text_rot = (t_norm * gain_f[4]).astype(jnp.bfloat16)
    same = seg[:, None] == seg[None, :]
    owner = jnp.arange(IMGS * TXT, dtype=jnp.int32) // TXT
    mine = seg[:, None] == owner[None, :]
    self_out, self_lse = attend_forward(q_rot, k_rot, valued, same)
    cross_out, cross_lse = attend_forward(q_rot, text_rot, text_vals, mine)
    cross_gate = jnp.tanh(gain_f[5])
    comb = (self_out + cross_gate * cross_out).astype(jnp.bfloat16)
    branch = mult(comb, out_w)
    tanh_one = jnp.tanh(gate1)
    x_one = x + tanh_one * branch
    normed2, inverse2 = norm_rows(x_one)
    h_two = (normed2 * gain_f[1] * (1.0 + scale2)).astype(jnp.bfloat16)
    ffn_w, down_w = (
        lax.all_gather(ffn_weight, "fsdp", axis=1, tiled=True),
        lax.all_gather(down_weight, "fsdp", axis=0, tiled=True),
    )
    gate_pre = mult(h_two, ffn_w[0])
    upper = mult(h_two, ffn_w[1])
    sigm = jax.nn.sigmoid(gate_pre)
    silu_pre = gate_pre * sigm
    hidden = (silu_pre * upper).astype(jnp.bfloat16)
    ffn_out = mult(hidden, down_w)
    tanh_two = jnp.tanh(gate2)
    block_out = (x_one + tanh_two * ffn_out).astype(jnp.bfloat16)
    totals = counts.astype(jnp.float32)
    here = jnp.sum(
        jnp.where(
            jnp.arange(totals.shape[0], dtype=jnp.int32) == lax.axis_index("bucket"), totals, 0.0
        )
    )
    weight = lax.axis_size("bucket") * here / jnp.sum(totals)
    grad = cotangent[0].astype(jnp.float32) * weight
    back_ffn, back_down = (
        lax.all_gather(ffn_weight, "fsdp", axis=1, tiled=True),
        lax.all_gather(down_weight, "fsdp", axis=0, tiled=True),
    )
    d_gate2 = grad * ffn_out * (1.0 - tanh_two * tanh_two)
    d_ffn = (grad * tanh_two).astype(jnp.bfloat16)
    d_hidden = mult(d_ffn, back_down.T)
    g_down = mult(hidden.T, d_ffn)
    d_pre = (d_hidden * upper * sigm * (1.0 + gate_pre * (1.0 - sigm))).astype(jnp.bfloat16)
    d_up = (d_hidden * silu_pre).astype(jnp.bfloat16)
    d_h_two = mult(d_pre, back_ffn[0].T) + mult(d_up, back_ffn[1].T)
    g_ffn = jnp.stack([mult(h_two.T, d_pre), mult(h_two.T, d_up)])
    s_ffn, s_down = (
        lax.psum_scatter(g_ffn, ("bucket", "fsdp"), scatter_dimension=1, tiled=True),
        lax.psum_scatter(g_down, ("bucket", "fsdp"), scatter_dimension=0, tiled=True),
    )
    back_attn, back_out = (
        lax.all_gather(attn_weight, "fsdp", axis=1, tiled=True),
        lax.all_gather(out_weight, "fsdp", axis=0, tiled=True),
    )
    g_gain_one = jnp.sum(d_h_two * normed2 * (1.0 + scale2), axis=0)
    d_scale2 = d_h_two * normed2 * gain_f[1]
    d_x_one = grad + norm_back(d_h_two * gain_f[1] * (1.0 + scale2), normed2, inverse2)
    d_gate1 = d_x_one * branch * (1.0 - tanh_one * tanh_one)
    d_branch = (d_x_one * tanh_one).astype(jnp.bfloat16)
    d_comb = mult(d_branch, back_out.T)
    g_out = mult(comb.T, d_branch)
    g_gain_five = jnp.sum(d_comb * cross_out, axis=0) * (1.0 - cross_gate * cross_gate)
    d_self = d_comb.astype(jnp.bfloat16)
    d_cross = (d_comb * cross_gate).astype(jnp.bfloat16)
    dq_self, dk_self, dv_self = attend_back(q_rot, k_rot, valued, self_lse, d_self, same)
    dq_cross, dk_text, dv_text = attend_back(q_rot, text_rot, text_vals, cross_lse, d_cross, mine)
    d_q_norm = rotate(dq_self + dq_cross, cosine, -sine)
    g_gain_two = jnp.sum(d_q_norm * q_norm, axis=0)
    d_query = norm_back(d_q_norm * gain_f[2], q_norm, q_inv).astype(jnp.bfloat16)
    d_k_norm = rotate(dk_self, cosine, -sine)
    g_gain_three = jnp.sum(d_k_norm * k_norm, axis=0)
    d_keyed = norm_back(d_k_norm * gain_f[3], k_norm, k_inv).astype(jnp.bfloat16)
    d_valued = dv_self.astype(jnp.bfloat16)
    g_gain_four = jnp.sum(dk_text * t_norm, axis=0)
    d_text_keys = norm_back(dk_text * gain_f[4], t_norm, t_inv).astype(jnp.bfloat16)
    d_text_vals = dv_text.astype(jnp.bfloat16)
    g_text = jnp.stack([mult(text_b.T, d_text_keys), mult(text_b.T, d_text_vals)])
    d_h_one = (
        mult(d_query, back_attn[0].T)
        + mult(d_keyed, back_attn[1].T)
        + mult(d_valued, back_attn[2].T)
    )
    g_attn = jnp.stack([mult(h_one.T, d_query), mult(h_one.T, d_keyed), mult(h_one.T, d_valued)])
    g_gain_zero = jnp.sum(d_h_one * normed1 * (1.0 + scale1), axis=0)
    d_scale1 = d_h_one * normed1 * gain_f[0]
    token_grad = d_x_one + norm_back(d_h_one * gain_f[0] * (1.0 + scale1), normed1, inverse1)
    d_token_mod = jnp.concatenate([d_scale1, d_gate1, d_scale2, d_gate2], axis=1)
    d_mod = jnp.dot(pick.T, d_token_mod, precision=HIGH)
    g_ada_b = jnp.sum(d_mod, axis=0)
    g_ada_w = mult(cond_act.T, d_mod.astype(jnp.bfloat16))
    g_gains = jnp.stack(
        [g_gain_zero, g_gain_one, g_gain_two, g_gain_three, g_gain_four, g_gain_five]
    )
    s_ada_w, s_ada_b, s_gains, s_attn, s_out, s_text = (
        lax.psum_scatter(g_ada_w, ("bucket", "fsdp"), scatter_dimension=0, tiled=True),
        lax.psum_scatter(g_ada_b, ("bucket", "fsdp"), scatter_dimension=0, tiled=True),
        lax.psum_scatter(g_gains, ("bucket", "fsdp"), scatter_dimension=1, tiled=True),
        lax.psum_scatter(g_attn, ("bucket", "fsdp"), scatter_dimension=1, tiled=True),
        lax.psum_scatter(g_out, ("bucket", "fsdp"), scatter_dimension=0, tiled=True),
        lax.psum_scatter(g_text, ("bucket", "fsdp"), scatter_dimension=1, tiled=True),
    )
    return (
        block_out[None],
        token_grad[None],
        s_ada_w,
        s_ada_b,
        s_gains,
        s_attn,
        s_out,
        s_text,
        s_ffn,
        s_down,
    )


ROW = 128
CHIPS = 4
HW = D // CHIPS
PAIRS = HW // 128


def swap(v, mask):
    return lax.ppermute(v, "fsdp", [(i, i ^ mask) for i in range(8)])


def at_x(v):
    return swap(v, 2)


def at_y(v):
    return swap(v, 4)


def at_core(v):
    return swap(v, 1)


def reorder(parts, index):
    bit = 1
    while bit < len(parts):
        odd = (index // bit) % 2 == 1
        parts = [jnp.where(odd, parts[j ^ bit], parts[j]) for j in range(len(parts))]
        bit *= 2
    return parts


def gather4(v):
    half = v.shape[0] // 2
    by_x = at_x(v)
    by_y = at_y(v)
    far = jnp.concatenate([at_y(by_x[:half]), at_x(by_y[half:])], axis=0)
    return [v, by_x, by_y, far]


def reduce4(parts):
    half = parts[0].shape[0] // 2
    low = jnp.bfloat16
    far_x = at_x(parts[3][:half].astype(low))
    far_y = at_y(parts[3][half:].astype(low))
    from_xa = at_x(parts[1][:half].astype(low))
    from_yb = at_y(parts[2][half:].astype(low))
    from_ya = at_y((parts[2][:half] + far_x.astype(jnp.float32)).astype(low))
    from_xb = at_x((parts[1][half:] + far_y.astype(jnp.float32)).astype(low))
    top = parts[0][:half] + from_xa.astype(jnp.float32) + from_ya.astype(jnp.float32)
    bottom = parts[0][half:] + from_yb.astype(jnp.float32) + from_xb.astype(jnp.float32)
    return jnp.concatenate([top, bottom], axis=0)


def exchange4(pick):
    return [pick(0), at_x(pick(1)), at_y(pick(2)), swap(pick(3), 6)]


def sum4(v):
    v = v + at_x(v)
    return v + at_y(v)


def sum4_rows(v):
    rows = v.reshape(CHIPS, -1)
    rows = rows + jnp.stack([at_x(rows)[j ^ 1] for j in range(CHIPS)])
    rows = rows + jnp.stack([at_y(rows)[j ^ 2] for j in range(CHIPS)])
    return rows.reshape(-1)


def both_cores(mine, core, axis):
    other = at_core(mine)
    first = jnp.where(core == 0, mine, other)
    second = jnp.where(core == 0, other, mine)
    return first, second


def column_weights(shard, chip, core, width):
    count, rows, _ = shard.shape
    got = exchange4(
        lambda j: lax.dynamic_slice_in_dim(shard, jnp.bitwise_xor(chip, j) * width, width, axis=2)
    )
    mine = jnp.stack(reorder(got, chip), axis=1)
    first, second = both_cores(mine, core, 0)
    return jnp.stack([first, second], axis=2).reshape(count, 8 * rows, width)


def row_weights(shard, core):
    first, second = both_cores(shard, core, 0)
    return jnp.concatenate([first, second], axis=0)


def core_half(view, core, axis):
    low = jnp.bfloat16
    keep = lax.dynamic_index_in_dim(view, core, axis, keepdims=False)
    give = lax.dynamic_index_in_dim(view, 1 - core, axis, keepdims=False)
    return keep + at_core(give.astype(low)).astype(jnp.float32)


def reduce_buckets(view, plane):
    low = jnp.bfloat16
    size = view.shape[0]
    up = down = None
    for step in range(1, size):
        piece = lax.dynamic_index_in_dim(
            view, jnp.minimum(plane + size - step, size - 1), 0, keepdims=False
        )
        if up is not None:
            piece = piece + up.astype(jnp.float32)
        up = lax.ppermute(piece.astype(low), "bucket", [(i, i + 1) for i in range(step)])
        piece = lax.dynamic_index_in_dim(
            view, jnp.maximum(plane - size + step, 0), 0, keepdims=False
        )
        if down is not None:
            piece = piece + down.astype(jnp.float32)
        down = lax.ppermute(
            piece.astype(low), "bucket", [(size - 1 - i, size - 2 - i) for i in range(step)]
        )
    own = lax.dynamic_index_in_dim(view, plane, 0, keepdims=False)
    return own + up.astype(jnp.float32) + down.astype(jnp.float32)


def to_column_owner(block, chip):
    got = exchange4(
        lambda j: lax.dynamic_index_in_dim(
            block, jnp.bitwise_xor(chip, j), 0, keepdims=False
        ).astype(jnp.bfloat16)
    )
    return jnp.concatenate(reorder(got, chip), axis=-1).astype(jnp.float32)


def to_row_owner(block):
    pairs = [
        (a * 8 + b * 2 + k, b * 8 + a * 2 + k) for a in range(4) for b in range(4) for k in range(2)
    ]
    return lax.ppermute(block.astype(jnp.bfloat16), ("bucket", "fsdp"), pairs).astype(jnp.float32)


def column_grad(partial, chip, core, plane):
    count, rows, width = partial.shape
    view = partial.reshape(count, 4, 4, 2, rows // 32, width)
    half = core_half(view, core, 3)
    mine = reduce_buckets(jnp.transpose(half, (1, 0, 2, 3, 4)), plane)
    return to_column_owner(jnp.transpose(mine, (1, 0, 2, 3)), chip)


def row_grad(partial, core, plane):
    rows, width = partial.shape
    half = core_half(partial.reshape(4, 2, rows // 8, width), core, 1)
    return to_row_owner(reduce_buckets(half, plane))


def partner(u):
    lane = lax.broadcasted_iota(jnp.int32, u.shape, 1)
    ahead = pltpu.roll(u, u.shape[1] - 16, 1)
    behind = pltpu.roll(u, 16, 1)
    return jnp.where((lane // 16) % 2 == 0, ahead, behind)


def dot_t(a, b):
    return lax.dot_general(a, b, (((1,), (1,)), ((), ())), preferred_element_type=jnp.float32)


def dot_n(a, b):
    return lax.dot_general(a, b, (((1,), (0,)), ((), ())), preferred_element_type=jnp.float32)


def t_dot(a, b):
    return lax.dot_general(a, b, (((0,), (0,)), ((), ())), preferred_element_type=jnp.float32)


def softmax_of(scores, allowed):
    scores = jnp.where(allowed, scores * HDIM ** (-0.5), NEGATIVE)
    top = jnp.max(scores, axis=-1, keepdims=True)
    expo = jnp.exp(scores - top)
    return expo / jnp.sum(expo, axis=-1, keepdims=True)


def head_mask(v, head):
    lane = lax.broadcasted_iota(jnp.int32, v.shape, 1)
    return jnp.where((lane // HDIM) == head, v, jnp.zeros_like(v))


def masks_of(seg_col, seg_row, captions):
    same = seg_col == seg_row
    owner = lax.broadcasted_iota(jnp.int32, (seg_col.shape[0], captions), 1) // TXT
    return same, seg_col == owner


def attend_kernel(
    q_ref, k_ref, v_ref, iq_ref, ik_ref, cos_ref, sin_ref, tk_ref, it_ref, tv_ref, sc_ref, sr_ref,
    g_ref, comb_ref, cross_ref, qr_ref, kr_ref, tr_ref,
):
    same, mine = masks_of(sc_ref[...], sr_ref[0], tk_ref.shape[0])
    cosine = cos_ref[...]
    sine = sin_ref[...]
    low = jnp.bfloat16
    for pair in range(PAIRS):
        at = pl.ds(pair * 128, 128)
        qn = q_ref[:, at] * iq_ref[...] * g_ref[2:3, at]
        kn = k_ref[:, at] * ik_ref[...] * g_ref[3:4, at]
        qr = (qn * cosine + partner(qn) * sine).astype(low)
        kr = (kn * cosine + partner(kn) * sine).astype(low)
        tr = (tk_ref[:, at] * it_ref[...] * g_ref[4:5, at]).astype(low)
        qr_ref[:, at] = qr
        kr_ref[:, at] = kr
        tr_ref[:, at] = tr
        vv = v_ref[:, at]
        tv = tv_ref[:, at]
        self_out = jnp.zeros(qn.shape, jnp.float32)
        cross_out = jnp.zeros(qn.shape, jnp.float32)
        for head in range(2):
            qh = head_mask(qr, head)
            probs = softmax_of(dot_t(qh, kr), same).astype(low)
            self_out = self_out + head_mask(dot_n(probs, vv), head)
            probs = softmax_of(dot_t(qh, tr), mine).astype(low)
            cross_out = cross_out + head_mask(dot_n(probs, tv), head)
        cross_ref[:, at] = cross_out
        comb_ref[:, at] = (self_out + jnp.tanh(g_ref[5:6, at]) * cross_out).astype(low)


def attend_back_kernel(
    qr_ref, kr_ref, v_ref, tr_ref, tv_ref, dc_ref, cross_ref, q_ref, k_ref, tk_ref, iq_ref, ik_ref,
    it_ref, cos_ref, sin_ref, sc_ref, sr_ref, g_ref,
    dq_ref, dk_ref, dv_ref, dt_ref, dtv_ref, gg_ref,
):
    same, mine = masks_of(sc_ref[...], sr_ref[...], tk_ref.shape[0])
    cosine = cos_ref[...]
    sine = sin_ref[...]
    low = jnp.bfloat16
    factor = HDIM ** (-0.5)
    for pair in range(PAIRS):
        at = pl.ds(pair * 128, 128)
        qr = qr_ref[:, at]
        kr = kr_ref[:, at]
        vv = v_ref[:, at]
        tr = tr_ref[:, at]
        tv = tv_ref[:, at]
        dcomb = dc_ref[:, at]
        d_self = dcomb.astype(low)
        d_cross = (dcomb * jnp.tanh(g_ref[5:6, at])).astype(low)
        dq = jnp.zeros(dcomb.shape, jnp.float32)
        dk = jnp.zeros(dcomb.shape, jnp.float32)
        dv = jnp.zeros(dcomb.shape, jnp.float32)
        dt = jnp.zeros((tr.shape[0], 128), jnp.float32)
        dtv = jnp.zeros((tr.shape[0], 128), jnp.float32)
        for head in range(2):
            qh = head_mask(qr, head)
            probs = softmax_of(dot_t(qh, kr), same)
            grad = head_mask(d_self, head)
            dprob = dot_t(grad, vv)
            dscore = probs * (dprob - jnp.sum(probs * dprob, axis=-1, keepdims=True))
            dscore = dscore.astype(low)
            dq = dq + dot_n(dscore, head_mask(kr, head))
            dk = dk + t_dot(dscore, qh)
            dv = dv + t_dot(probs.astype(low), grad)
            probs = softmax_of(dot_t(qh, tr), mine)
            grad = head_mask(d_cross, head)
            dprob = dot_t(grad, tv)
            dscore = probs * (dprob - jnp.sum(probs * dprob, axis=-1, keepdims=True))
            dscore = dscore.astype(low)
            dq = dq + dot_n(dscore, head_mask(tr, head))
            dt = dt + t_dot(dscore, qh)
            dtv = dtv + t_dot(probs.astype(low), grad)
        dq = dq * factor
        dk = dk * factor
        dt = dt * factor
        dq = dq * cosine - partner(dq) * sine
        dk = dk * cosine - partner(dk) * sine
        q_norm = q_ref[:, at] * iq_ref[...]
        k_norm = k_ref[:, at] * ik_ref[...]
        t_norm = tk_ref[:, at] * it_ref[...]
        gg_ref[0:1, at] += jnp.sum(dq * q_norm, axis=0, keepdims=True)
        gg_ref[1:2, at] += jnp.sum(dk * k_norm, axis=0, keepdims=True)
        gg_ref[2:3, at] += jnp.sum(dt * t_norm, axis=0, keepdims=True)
        gg_ref[3:4, at] += jnp.sum(dcomb * cross_ref[:, at], axis=0, keepdims=True)
        dq = dq * g_ref[2:3, at]
        dk = dk * g_ref[3:4, at]
        dt = dt * g_ref[4:5, at]
        dq_ref[:, at] = dq
        dk_ref[:, at] = dk
        dv_ref[:, at] = dv.astype(low)
        dt_ref[:, at] = dt
        dtv_ref[:, at] = dtv.astype(low)


MESH_IDS = pl.DeviceIdType.MESH
VMEM_SPEC = pl.BlockSpec(memory_space=pltpu.VMEM)
ANY_SPEC = pl.BlockSpec(memory_space=pl.ANY)


class Net:
    def __init__(self, send_sems, recv_sems):
        self.me = lax.axis_index("fsdp")
        self.send_sems = send_sems
        self.recv_sems = recv_sems
        self.count = 0
        self.all = []

    def peer(self, mask):
        out = self.me
        for bit in (1, 2, 4):
            if mask & bit:
                out = out + bit * (1 - 2 * ((self.me // bit) % 2))
        return out

    def meet(self, masks):
        sem = pltpu.get_barrier_semaphore()
        for mask in masks:
            pl.semaphore_signal(
                sem, inc=1, device_id={"fsdp": self.peer(mask)}, device_id_type=MESH_IDS
            )
        pl.semaphore_wait(sem, len(masks))

    def send(self, src, dst, mask):
        copy = pltpu.make_async_remote_copy(
            src_ref=src,
            dst_ref=dst,
            send_sem=self.send_sems.at[self.count],
            recv_sem=self.recv_sems.at[self.count],
            device_id={"fsdp": self.peer(mask)},
            device_id_type=MESH_IDS,
        )
        self.count += 1
        copy.start()
        self.all.append(copy)
        return copy

    def close(self):
        for copy in self.all:
            copy.wait_send()


def net_scratch(count):
    return [pltpu.SemaphoreType.DMA((count,)), pltpu.SemaphoreType.DMA((count,))]


def share4_start(net, out):
    return net.send(out.at[0], out.at[1], 2), net.send(out.at[0], out.at[2], 4)


def share4_relay(net, out, by_x, by_y):
    half = out.shape[1] // 2
    top, bottom = pl.ds(0, half), pl.ds(half, half)
    by_x.wait_recv()
    first = net.send(out.at[1, top], out.at[3, top], 4)
    by_y.wait_recv()
    second = net.send(out.at[2, bottom], out.at[3, bottom], 2)
    return first, second


def collect4(net, part, buf, far):
    half = far.shape[1]
    rows = (pl.ds(0, half), pl.ds(half, half))
    low = jnp.bfloat16
    full = jnp.float32
    for i in (0, 1):
        buf[2, rows[i]] = part(3, i).astype(low)
    far_x = net.send(buf.at[2, rows[0]], far.at[0], 2)
    far_y = net.send(buf.at[2, rows[1]], far.at[1], 4)
    buf[0, rows[0]] = part(1, 0).astype(low)
    one_a = net.send(buf.at[0, rows[0]], buf.at[3, rows[0]], 2)
    buf[1, rows[1]] = part(2, 1).astype(low)
    two_b = net.send(buf.at[1, rows[1]], buf.at[4, rows[1]], 4)
    later = []

    def middle():
        far_x.wait_recv()
        buf[1, rows[0]] = (part(2, 0) + far[0].astype(full)).astype(low)
        later.append(net.send(buf.at[1, rows[0]], buf.at[4, rows[0]], 4))
        far_y.wait_recv()
        buf[0, rows[1]] = (part(1, 1) + far[1].astype(full)).astype(low)
        later.append(net.send(buf.at[0, rows[1]], buf.at[3, rows[1]], 2))

    def finish(i):
        (one_a, two_b)[i].wait_recv()
        later[i].wait_recv()
        return part(0, i) + buf[3, rows[i]].astype(full) + buf[4, rows[i]].astype(full)

    return middle, finish


def pick_rows(table, seg, first):
    out = table[first + IMGS - 1 : first + IMGS]
    for i in range(IMGS - 2, -1, -1):
        out = jnp.where(seg == i, table[first + i : first + i + 1], out)
    return out


def row_sums(a, b):
    ones = jnp.ones((8, a.shape[1]), jnp.float32)

    def one(v):
        return lax.dot_general(
            ones, v, (((1,), (1,)), ((), ())), precision=HIGH, preferred_element_type=jnp.float32
        )

    if b is None:
        return one(a)
    got = one(a)
    return jnp.where(lax.broadcasted_iota(jnp.int32, got.shape, 0) < 4, got, one(b))


ALL_PEERS = (1, 2, 3, 4, 5, 6, 7)


def open_kernel(
    cond_ref, gain_ref, bias_ref, ada_ref, tok_ref, seg_ref, idx_ref, attn_ref, textw_ref, text_ref,
    mod_ref, gains_ref, h_ref, idxs_ref, aw_ref, ta_ref, q_ref, k_ref, v_ref, tk_ref, tv_ref,
    iqk_ref, it_ref,
    conds, parts, mods, gbuf, tw_ref, sums, tsums, local_sems, send_sems, recv_sems,
):
    low = jnp.bfloat16
    full = jnp.float32
    net = Net(send_sems, recv_sems)
    me = net.me
    chip = me // 2
    net.meet(ALL_PEERS)

    act = cond_ref[...].astype(full)
    act = (act * jax.nn.sigmoid(act)).astype(low).astype(full)
    for j in range(8):
        gbuf[8, :, 128 * j : 128 * j + 128] = act[:, 128 * j : 128 * j + 128]
    waits = []
    for m in ALL_PEERS:
        at = pl.ds(pl.multiple_of(net.peer(m) * 128, 128), 128)
        waits.append(net.send(gbuf.at[8, :, at], conds.at[m], m))
    conds[0] = gbuf[8, :, pl.ds(pl.multiple_of(me * 128, 128), 128)]
    gwaits = [net.send(gain_ref, gbuf.at[m], m) for m in ALL_PEERS]
    iwaits = [net.send(idx_ref, idxs_ref.at[i], m) for i, m in ((1, 2), (2, 4), (3, 6))]
    idxs_ref[0] = idx_ref[...]

    def spread(src, dst, rows, width, sem):
        def cut(c):
            return src.at[:, :, pl.ds(pl.multiple_of(c * width, 128), width)]

        def put(f):
            return dst.at[:, pl.ds(pl.multiple_of(f * rows, rows), rows), :]

        here = pltpu.make_async_copy(cut(chip), put(me), sem)
        here.start()
        core = net.send(cut(chip), put(me), 1)
        away = [net.send(cut(net.peer(m) // 2), put(me), m) for m in (2, 4, 6)]
        return here, core, away, put

    for w in waits:
        w.wait_recv()
    lhs = jnp.concatenate([conds[m] for m in range(8)], axis=0).astype(low)
    half_cols = 3072
    step = 512

    def mod_cols(i, _):
        lo = pl.ds(pl.multiple_of(i * step, step), step)
        hi = pl.ds(pl.multiple_of(half_cols + i * step, step), step)
        a = jnp.dot(lhs, ada_ref[:, lo], preferred_element_type=full)
        b = jnp.dot(lhs, ada_ref[:, hi], preferred_element_type=full)
        row = lax.broadcasted_iota(jnp.int32, (8, step), 0)
        for m in range(8):
            parts[m, :, lo] = (
                jnp.where(row < 4, a[8 * m : 8 * m + 8], b[8 * m : 8 * m + 8]) + bias_ref[:, lo]
            )
        return 0

    lax.fori_loop(0, half_cols // step, mod_cols, 0)
    waits = [net.send(parts.at[m], mods.at[m], m) for m in ALL_PEERS]
    attn_io = spread(attn_ref, aw_ref, attn_ref.shape[1], HW, local_sems.at[0])
    text_io = spread(textw_ref, tw_ref, textw_ref.shape[1], HW, local_sems.at[1])
    own_text = pltpu.make_async_copy(text_ref, ta_ref.at[0], local_sems.at[2])
    own_text.start()
    for w in gwaits:
        w.wait_recv()
    gains = gain_ref[...]
    for m in ALL_PEERS:
        gains = gains + gbuf[m]
    gains_ref[...] = gains
    for w in waits:
        w.wait_recv()

    def mod_sum(i, _):
        at = pl.ds(pl.multiple_of(i * step, step), step)
        total = parts[0, :, at]
        for m in ALL_PEERS:
            total = total + mods[m, :, at]
        mod_ref[:, at] = total
        return 0

    lax.fori_loop(0, half_cols // step, mod_sum, 0)

    block = 32

    def first_norm(i, _):
        at = pl.ds(pl.multiple_of(i * block, block), block)
        x = tok_ref[at, :].astype(full)
        normed = x * lax.rsqrt(jnp.mean(x * x, axis=-1, keepdims=True) + EPS)
        scale = pick_rows(mod_ref[:, :D], seg_ref[at, :], 0)
        h_ref[0, at, :] = (normed * gains_ref[0:1, :] * (1.0 + scale)).astype(low)
        return 0

    lax.fori_loop(0, ROW // block, first_norm, 0)
    hx, hy = share4_start(net, h_ref)

    def pass_on(io):
        here, core, away, put = io
        here.wait()
        return [core] + [
            (c.wait_recv(), net.send(put(net.peer(m)), put(net.peer(m)), 1))[1]
            for c, m in zip(away, (2, 4, 6))
        ]

    attn_core = pass_on(attn_io)
    text_core = pass_on(text_io)
    h_far = share4_relay(net, h_ref, hx, hy)
    own_text.wait()
    chunks = 4
    size = ta_ref.shape[1] // chunks
    tx, ty = [None] * chunks, [None] * chunks
    for s in range(chunks):
        i, j = s, (s + chunks // 2) % chunks
        at = pl.ds(i * size, size)
        tx[i] = net.send(ta_ref.at[0, at], ta_ref.at[1, at], 2)
        at = pl.ds(j * size, size)
        ty[j] = net.send(ta_ref.at[0, at], ta_ref.at[2, at], 4)

    for c in attn_core:
        c.wait_recv()
    for c in h_far:
        c.wait_recv()

    for j in range(CHIPS):
        h = h_ref[j]
        at = pl.ds(j * ROW, ROW)
        qv = jnp.dot(h, aw_ref[0], preferred_element_type=full)
        q_ref[at, :] = qv
        kv = jnp.dot(h, aw_ref[1], preferred_element_type=full)
        k_ref[at, :] = kv
        v_ref[at, :] = jnp.dot(h, aw_ref[2], preferred_element_type=full).astype(low)
        sums[0, :, at] = row_sums(qv * qv, kv * kv)
    sum_io = [net.send(sums.at[0], sums.at[i], m) for i, m in ((1, 2), (2, 4), (3, 6))]

    for c in text_core:
        c.wait_recv()

    def text_rows(j, lo, count):
        kt = 1024

        def body(i, acc):
            at = pl.ds(pl.multiple_of(i * kt, kt), kt)
            rows = ta_ref[j, pl.ds(lo, count), at]
            return (
                acc[0] + jnp.dot(rows, tw_ref[0, at, :], preferred_element_type=full),
                acc[1] + jnp.dot(rows, tw_ref[1, at, :], preferred_element_type=full),
            )

        zero = jnp.zeros((count, HW), full)
        keys, vals = lax.fori_loop(0, TXTD_OF(ta_ref) // kt, body, (zero, zero))
        at = pl.ds(j * ta_ref.shape[1] + lo, count)
        tk_ref[at, :] = keys
        tv_ref[at, :] = vals.astype(low)
        tsums[0, :, at] = row_sums(keys * keys, None)

    cap = ta_ref.shape[1]
    half = cap // 2
    for lo in (0, half):
        text_rows(0, lo, half)
    relays = []
    for s in range(chunks // 2):
        i, j = s, s + chunks // 2
        tx[i].wait_recv()
        at = pl.ds(i * size, size)
        relays.append(net.send(ta_ref.at[1, at], ta_ref.at[3, at], 4))
        ty[j].wait_recv()
        at = pl.ds(j * size, size)
        relays.append(net.send(ta_ref.at[2, at], ta_ref.at[3, at], 2))
    for i, c in enumerate(sum_io):
        c.wait_recv()
    for j in range(CHIPS):
        total = sums[0, :, pl.ds(j * ROW, ROW)]
        for i in (1, 2, 3):
            total = total + sums[i, :, pl.ds((j ^ i) * ROW, ROW)]
        iqk_ref[:, pl.ds(j * ROW, ROW)] = lax.rsqrt(total / D + EPS)
    text_rows(1, 0, half)
    text_rows(2, half, half)
    for s in range(chunks // 2):
        tx[s + chunks // 2].wait_recv()
        ty[s].wait_recv()
    text_rows(1, half, half)
    text_rows(2, 0, half)
    for c in relays:
        c.wait_recv()
    for lo in (0, half):
        text_rows(3, lo, half)
    sum_io = [net.send(tsums.at[0], tsums.at[i], m) for i, m in ((1, 2), (2, 4), (3, 6))]
    for c in sum_io:
        c.wait_recv()
    for j in range(CHIPS):
        total = tsums[0, :, pl.ds(j * cap, cap)]
        for i in (1, 2, 3):
            total = total + tsums[i, :, pl.ds((j ^ i) * cap, cap)]
        it_ref[:, pl.ds(j * cap, cap)] = lax.rsqrt(total / D + EPS)
    for c in iwaits:
        c.wait_recv()
    net.close()


def TXTD_OF(ref):
    return ref.shape[2]


def open_layer(cond8, gain_pad, bias_pad, ada, tok, seg_col, idx, attn, textw, text):
    low = jnp.bfloat16
    full = jnp.float32
    shape = jax.ShapeDtypeStruct
    cap, txtd = text.shape
    V = VMEM_SPEC
    return pl.pallas_call(
        open_kernel,
        in_specs=[V, V, V, V, V, V, V, ANY_SPEC, ANY_SPEC, ANY_SPEC],
        out_specs=[V] * 13,
        out_shape=[
            shape((8, 3072), full),
            shape((8, D), full),
            shape((CHIPS, ROW, D), low),
            shape((CHIPS, 8, ROW), jnp.int32),
            shape((3, D, HW), low),
            shape((CHIPS, cap, txtd), low),
            shape((CHIPS * ROW, HW), full),
            shape((CHIPS * ROW, HW), full),
            shape((CHIPS * ROW, HW), low),
            shape((CHIPS * cap, HW), full),
            shape((CHIPS * cap, HW), low),
            shape((8, CHIPS * ROW), full),
            shape((8, CHIPS * cap), full),
        ],
        scratch_shapes=[
            pltpu.VMEM((8, 8, 128), full),
            pltpu.VMEM((8, 8, 3072), full),
            pltpu.VMEM((8, 8, 3072), full),
            pltpu.VMEM((9, 8, D), full),
            pltpu.VMEM((2, txtd, HW), low),
            pltpu.VMEM((CHIPS, 8, CHIPS * ROW), full),
            pltpu.VMEM((CHIPS, 8, CHIPS * cap), full),
            pltpu.SemaphoreType.DMA((3,)),
            *net_scratch(64),
        ],
        compiler_params=pltpu.CompilerParams(
            collective_id=1, has_side_effects=True, vmem_limit_bytes=56 * 1024 * 1024
        ),
        cost_estimate=pl.CostEstimate(
            flops=10_000_000_000, bytes_accessed=400_000_000, transcendentals=0
        ),
    )(cond8, gain_pad, bias_pad, ada, tok, seg_col, idx, attn, textw, text)


class Chain:
    def __init__(self, net, grad, mine, arrive, total, sems, columns):
        self.net = net
        self.grad = grad
        self.mine = mine
        self.arrive = arrive
        self.total = total
        self.sems = sems
        self.columns = columns
        self.plane = lax.axis_index("bucket")
        self.core = net.me % 2

    def piece(self, ref, p):
        return ref.at[:, p] if self.columns else ref.at[p]

    def half(self, core):
        return self.grad.at[:, :, :, core] if self.columns else self.grad.at[:, core]

    def each(self, ref, body):
        lead = ref.shape[:-2]
        if not lead:
            body(())
            return
        total = 1
        for n in lead:
            total *= n

        def step(i, _):
            index = []
            for n in reversed(lead):
                index.insert(0, i % n)
                i = i // n
            body(tuple(index))
            return 0

        lax.fori_loop(0, total, step, 0)

    def core_start(self, keep=None, sem=None):
        self.exchange = self.net.send(self.half(1 - self.core), self.mine, 1)
        self.keep = self.half(self.core)
        self.load = None
        if keep is not None:
            self.load = pltpu.make_async_copy(self.keep, keep, sem)
            self.load.start()
            self.keep = keep

    def add(self, into, other):
        def body(index):
            value = into[index].astype(jnp.float32) + other[index].astype(jnp.float32)
            into[index] = value.astype(into.dtype)

        self.each(into, body)

    def core_finish(self):
        self.exchange.wait_recv()
        if self.load is not None:
            self.load.wait()
        self.add(self.mine, self.keep)

    def copy(self, up, p, slot):
        first = 0 if up else 8
        return pltpu.make_async_remote_copy(
            src_ref=self.piece(self.mine, p),
            dst_ref=self.arrive.at[slot],
            send_sem=self.sems.at[first + p],
            recv_sem=self.sems.at[first + 4 + p],
            device_id={"bucket": self.plane + (1 if up else -1)},
            device_id_type=MESH_IDS,
        )

    def moves(self, t):
        up = self.plane + 3 - t
        down = self.plane - 3 + t
        return (
            (True, up, up, self.plane <= t, self.plane >= 1),
            (False, down, 4 if t == 2 else down, self.plane >= 3 - t, self.plane <= 2),
        )

    def step(self, t):
        for up, p, slot, sends, inner in self.moves(t):

            @pl.when(sends)
            def _(up=up, p=p, slot=slot, inner=inner):
                @pl.when(inner)
                def _():
                    self.copy(up, p, p).wait_recv()
                    self.add(self.piece(self.mine, p), self.arrive.at[p])

                self.copy(up, p, slot).start()

    def finish(self):
        own = self.piece(self.mine, self.plane)

        def first(index):
            self.total[index] = own[index].astype(jnp.float32)

        self.each(self.total, first)
        for up, slot, inner in ((True, self.plane, self.plane >= 1), (False, 4, self.plane <= 2)):

            @pl.when(inner)
            def _(up=up, slot=slot):
                self.copy(up, self.plane, slot).wait_recv()
                self.add(self.total, self.arrive.at[slot])

    def close(self):
        for t in range(3):
            for up, p, slot, sends, inner in self.moves(t):

                @pl.when(sends)
                def _(up=up, p=p, slot=slot):
                    self.copy(up, p, slot).wait_send()


def chain_scratch(columns, shape, width):
    low = jnp.bfloat16
    if columns:
        n, rows = shape
        return [
            pltpu.VMEM((n, 4, 4, rows, width), low),
            pltpu.VMEM((5, n, 4, rows, width), low),
            pltpu.VMEM((n, 4, rows, width), jnp.float32),
            pltpu.SemaphoreType.DMA((16,)),
        ]
    return [
        pltpu.VMEM((4, shape, width), low),
        pltpu.VMEM((5, shape, width), low),
        pltpu.VMEM((shape, width), jnp.float32),
        pltpu.SemaphoreType.DMA((16,)),
    ]


class Columns:
    def __init__(self, net, total, stage, wide, out):
        self.net, self.total, self.stage, self.wide, self.out = net, total, stage, wide, out

    def start(self):
        net = self.net
        chip = net.me // 2
        n, _, rows, width = self.total.shape
        at = pl.ds(pl.multiple_of(chip * width, width), width)

        def cast(i, _):
            self.stage[i // 4, i % 4] = self.total[i // 4, i % 4].astype(jnp.bfloat16)
            return 0

        lax.fori_loop(0, n * 4, cast, 0)
        self.copies = [
            net.send(self.stage.at[:, net.peer(m) // 2], self.wide.at[:, :, at], m)
            for m in (2, 4, 6)
        ]
        for i in range(n):
            self.wide[i, :, at] = self.stage[i, chip]

    def finish(self):
        for c in self.copies:
            c.wait_recv()
        for i in range(self.out.shape[0]):
            self.out[i] = self.wide[i].astype(jnp.float32)


def meet_all(net):
    plane = lax.axis_index("bucket")
    chip = net.me // 2
    sem = pltpu.get_barrier_semaphore()
    for mask in ALL_PEERS:
        pl.semaphore_signal(
            sem, inc=1, device_id={"fsdp": net.peer(mask)}, device_id_type=MESH_IDS
        )
    for inner, step in ((plane >= 1, -1), (plane <= 2, 1)):

        @pl.when(inner)
        def _(step=step):
            pl.semaphore_signal(
                sem, inc=1, device_id={"bucket": plane + step}, device_id_type=MESH_IDS
            )

    @pl.when(chip != plane)
    def _():
        pl.semaphore_signal(
            sem,
            inc=1,
            device_id={"bucket": chip, "fsdp": plane * 2 + net.me % 2},
            device_id_type=MESH_IDS,
        )

    one = jnp.int32(1)
    zero = jnp.int32(0)
    count = (
        7
        + jnp.where(plane >= 1, one, zero)
        + jnp.where(plane <= 2, one, zero)
        + jnp.where(chip != plane, one, zero)
    )
    pl.semaphore_wait(sem, count)


def transposed(net, src, dst, sems):
    plane = lax.axis_index("bucket")
    return pltpu.make_async_remote_copy(
        src_ref=src,
        dst_ref=dst,
        send_sem=sems.at[0],
        recv_sem=sems.at[1],
        device_id={"bucket": net.me // 2, "fsdp": plane * 2 + net.me % 2},
        device_id_type=MESH_IDS,
    )


def close_kernel(
    text_g, attn_g, out_g,
    text_o, attn_o, out_o,
    tm, ta, tt, ts, am, aa, at_, as_, om, oa, ot, os_,
    t_wide, a_wide, t_stage, a_stage, o_stage, o_got, o_sem, send_sems, recv_sems,
):
    net = Net(send_sems, recv_sems)
    meet_all(net)
    plane = lax.axis_index("bucket")
    chip = net.me // 2
    out = Chain(net, out_g, om, oa, ot, os_, False)
    attn = Chain(net, attn_g, am, aa, at_, as_, True)
    text = Chain(net, text_g, tm, ta, tt, ts, True)
    chains = [out, attn, text]
    for c in chains:
        c.core_start()
    for c in chains:
        c.core_finish()
        c.step(0)
    for t in (1, 2):
        for c in chains:
            c.step(t)
    out.finish()
    o_stage[...] = ot[...].astype(jnp.bfloat16)

    @pl.when(chip != plane)
    def _():
        transposed(net, o_stage, o_got, o_sem).start()

    attn.finish()
    attn_cols = Columns(net, at_, a_stage, a_wide, attn_o)
    attn_cols.start()

    @pl.when(chip != plane)
    def _():
        transposed(net, o_stage, o_got, o_sem).wait()
        out_o[...] = o_got[...].astype(jnp.float32)

    @pl.when(chip == plane)
    def _():
        out_o[...] = ot[...]

    attn_cols.finish()
    text.finish()
    text_cols = Columns(net, tt, t_stage, t_wide, text_o)
    text_cols.start()
    text_cols.finish()
    for c in chains:
        c.close()
    net.close()


def close_layer(text_g, attn_g, out_g):
    low = jnp.bfloat16
    full = jnp.float32
    shape = jax.ShapeDtypeStruct
    V = VMEM_SPEC
    tr, tw = text_g.shape[-2:]
    ar, aw = attn_g.shape[-2:]
    orow, ow = out_g.shape[-2:]
    return pl.pallas_call(
        close_kernel,
        in_specs=[V] * 3,
        out_specs=[V] * 3,
        out_shape=[
            shape((2, tr, 4 * tw), full),
            shape((3, ar, 4 * aw), full),
            shape((orow, ow), full),
        ],
        scratch_shapes=[
            *chain_scratch(True, (2, tr), tw),
            *chain_scratch(True, (3, ar), aw),
            *chain_scratch(False, orow, ow),
            pltpu.VMEM((2, tr, 4 * tw), low),
            pltpu.VMEM((3, ar, 4 * aw), low),
            pltpu.VMEM((2, 4, tr, tw), low),
            pltpu.VMEM((3, 4, ar, aw), low),
            pltpu.VMEM((orow, ow), low),
            pltpu.VMEM((orow, ow), low),
            pltpu.SemaphoreType.DMA((2,)),
            *net_scratch(16),
        ],
        compiler_params=pltpu.CompilerParams(
            collective_id=2, has_side_effects=True, vmem_limit_bytes=63 * 1024 * 1024
        ),
        cost_estimate=pl.CostEstimate(
            flops=1_000_000, bytes_accessed=400_000_000, transcendentals=0
        ),
    )(text_g, attn_g, out_g)


def column_of(v):
    return jnp.transpose(v)[:, 0:1]


def back_kernel(
    dh2_ref, fo_ref, x1_ref, branch_ref, cot_ref, w_ref, mod_ref, seg_ref, gain_ref, tok_ref,
    sr_ref, gs_ref, *rest,
):
    late, rest = rest[:LATE], rest[LATE:]
    places, rest = rest[-LATE - 1 : -1], rest[: -LATE - 1] + rest[-1:]
    loads = [
        pltpu.make_async_copy(src, dst, rest[-1].at[i])
        for i, (src, dst) in enumerate(zip(late, places))
    ]
    back_body(
        dh2_ref, fo_ref, x1_ref, branch_ref, cot_ref, w_ref, mod_ref, seg_ref, gain_ref, tok_ref,
        *places, sr_ref, gs_ref, *rest[:-1], loads,
    )


LATE = 17


def back_body(
    dh2_ref, fo_ref, x1_ref, branch_ref, cot_ref, w_ref, mod_ref, seg_ref, gain_ref, tok_ref,
    ow_ref, aw_ref, qr_ref, kr_ref, v_ref, tr_ref, tv_ref, cross_ref, q_ref, k_ref, tk_ref,
    iq_ref, ik_ref, it_ref, cos_ref, sin_ref, sc_ref, sr_ref, gs_ref, ffn_g, down_g,
    block_o, token_o, db_ref, dq_o, dk_o, dv_o, dt_o, dtv_o, dmod_o, gg_o, gs_o, ffn_o, down_o,
    dx_s, dc_s, dqf, dkf, dtf, part_s, sums, tsums, buf_a, far_a, buf_b, far_b, buf_c, far_c,
    fm, fa, ft, fs, dm, da, dt_c, ds_, f_wide, f_stage, d_stage, d_got, d_sem,
    f_keep, d_keep, keep_sem, send_sems, recv_sems, loads,
):
    low = jnp.bfloat16
    full = jnp.float32
    net = Net(send_sems, recv_sems)
    meet_all(net)
    plane = lax.axis_index("bucket")
    chip = net.me // 2
    ffn = Chain(net, ffn_g, fm, fa, ft, fs, True)
    down = Chain(net, down_g, dm, da, dt_c, ds_, False)
    ffn.core_start(f_keep, keep_sem.at[0])
    down.core_start(d_keep, keep_sem.at[1])
    for c in loads:
        c.start()

    def rows_of(ref):
        half = ROW // 2
        return lambda j, i: ref[pl.ds(j * ROW + i * half, half), :].astype(full)

    middle, finish = collect4(net, rows_of(dh2_ref), buf_a, far_a)
    middle()
    ffn.core_finish()
    ffn.step(0)
    down.core_finish()
    down.step(0)
    half = ROW // 2
    for i in (0, 1):
        dx_s[pl.ds(i * half, half), :] = finish(i)
    part_s[pl.ds(0, ROW), :] = dx_s[...]
    block = 32
    weight = w_ref[0:1, 0:1]

    def second_norm(at):
        x1 = x1_ref[at, :]
        inverse = lax.rsqrt(jnp.mean(x1 * x1, axis=-1, keepdims=True) + EPS)
        scale = pick_rows(mod_ref[:, :D], seg_ref[at, :], 4)
        return x1 * inverse, inverse, scale

    def to_branch(b, _):
        at = pl.ds(pl.multiple_of(b * block, block), block)
        normed, inverse, scale = second_norm(at)
        dn = dx_s[at, :] * gain_ref[1:2, :] * (1.0 + scale)
        back = inverse * (dn - normed * jnp.mean(dn * normed, axis=-1, keepdims=True))
        dx = cot_ref[at, :].astype(full) * weight + back
        dx_s[at, :] = dx
        gate = jnp.tanh(pick_rows(mod_ref[:, D:], seg_ref[at, :], 0))
        db_ref[0, at, :] = (dx * gate).astype(low)
        return 0

    lax.fori_loop(0, ROW // block, to_branch, 0)
    bx, by = share4_start(net, db_ref)

    def by_image(value, seg, row, lo):
        for i in range(IMGS):
            dmod_o[row + i : row + i + 1, lo : lo + D] += jnp.sum(
                jnp.where(seg == i, value, 0.0), axis=0, keepdims=True
            )

    dmod_o[...] = jnp.zeros(dmod_o.shape, full)
    gg_o[...] = jnp.zeros(gg_o.shape, full)

    def second_sums(b, _):
        at = pl.ds(pl.multiple_of(b * block, block), block)
        normed, inverse, scale = second_norm(at)
        seg = seg_ref[at, :]
        dh = part_s[at, :] * normed
        gg_o[1:2, :] += jnp.sum(dh * (1.0 + scale), axis=0, keepdims=True)
        by_image(dh * gain_ref[1:2, :], seg, 4, 0)
        gate = jnp.tanh(pick_rows(mod_ref[:, D:], seg, 0))
        by_image(dx_s[at, :] * branch_ref[at, :] * (1.0 - gate * gate), seg, 0, D)
        return 0

    lax.fori_loop(0, ROW // block, second_sums, 0)
    far = share4_relay(net, db_ref, bx, by)
    middle_b, finish_b = collect4(net, rows_of(fo_ref), buf_b, far_b)
    gs_o[...] = jnp.zeros(gs_o.shape, full)
    for c in loads:
        c.wait()
    cap = IMGS * TXT

    def attention_row(j, _):
        @pl.when(j == 3)
        def _():
            for c in far:
                c.wait_recv()

        @pl.when(j == 1)
        def _():
            ffn.step(1)
            down.step(1)

        @pl.when(j == 3)
        def _():
            ffn.step(2)
            down.step(2)

        rows = pl.ds(pl.multiple_of(j * ROW, ROW), ROW)
        text = pl.ds(pl.multiple_of(j * cap, cap), cap)
        dc_s[...] = dot_t(db_ref[j], ow_ref[...])
        dqv, dkv, dtv = dqf.at[rows], dkf.at[rows], dtf.at[text]
        attend_back_kernel(
            qr_ref.at[rows], kr_ref.at[rows], v_ref.at[rows], tr_ref.at[text], tv_ref.at[text],
            dc_s, cross_ref.at[rows], q_ref.at[rows], k_ref.at[rows], tk_ref.at[text],
            iq_ref.at[rows], ik_ref.at[rows], it_ref.at[text], cos_ref.at[rows], sin_ref.at[rows],
            sc_ref.at[rows], sr_ref.at[j], gs_ref,
            dqv, dkv, dv_o.at[rows], dtv, dtv_o.at[text], gs_o,
        )
        sums[0, :, rows] = row_sums(
            dqv[...] * (q_ref[rows, :] * iq_ref[rows, :]),
            dkv[...] * (k_ref[rows, :] * ik_ref[rows, :]),
        )
        tsums[0, :, text] = row_sums(dtv[...] * (tk_ref[text, :] * it_ref[text, :]), None)
        return 0

    lax.fori_loop(0, CHIPS, attention_row, 0)
    sum_io = []
    for i, m in ((1, 2), (2, 4), (3, 6)):
        sum_io.append(net.send(sums.at[0], sums.at[i], m))
        sum_io.append(net.send(tsums.at[0], tsums.at[i], m))
    middle_b()
    for i in (0, 1):
        part_s[pl.ds(i * half, half), :] = finish_b(i)

    def block_rows(b, _):
        at = pl.ds(pl.multiple_of(b * block, block), block)
        seg = seg_ref[at, :]
        gate = jnp.tanh(pick_rows(mod_ref[:, D:], seg, 4))
        out = part_s[at, :]
        block_o[at, :] = (x1_ref[at, :] + gate * out).astype(low)
        grad = cot_ref[at, :].astype(full) * weight
        by_image(grad * out * (1.0 - gate * gate), seg, 4, D)
        return 0

    for c in sum_io:
        c.wait_recv()
    for j in range(CHIPS):
        rows = pl.ds(j * ROW, ROW)
        text = pl.ds(j * cap, cap)
        total = sums[0, :, rows]
        words = tsums[0, :, text]
        for i in (1, 2, 3):
            total = total + sums[i, :, pl.ds((j ^ i) * ROW, ROW)]
            words = words + tsums[i, :, pl.ds((j ^ i) * cap, cap)]
        mean = jnp.transpose(total / D)
        iq, ik, it = iq_ref[rows, :], ik_ref[rows, :], it_ref[text, :]
        dq_o[rows, :] = (iq * (dqf[rows, :] - q_ref[rows, :] * iq * mean[:, 0:1])).astype(low)
        dk_o[rows, :] = (ik * (dkf[rows, :] - k_ref[rows, :] * ik * mean[:, 4:5])).astype(low)
        mean = jnp.transpose(words / D)
        dt_o[text, :] = (it * (dtf[text, :] - tk_ref[text, :] * it * mean[:, 0:1])).astype(low)

    lax.fori_loop(0, ROW // block, block_rows, 0)
    wide = 256

    def first_grad(n, _):
        at = pl.ds(pl.multiple_of(n * wide, wide), wide)
        part_s[:, at] = (
            dot_t(dq_o[...], aw_ref[0, at, :])
            + dot_t(dk_o[...], aw_ref[1, at, :])
            + dot_t(dv_o[...], aw_ref[2, at, :])
        )
        return 0

    lax.fori_loop(0, D // wide, first_grad, 0)
    middle_c, finish_c = collect4(net, rows_of(part_s), buf_c, far_c)
    ffn.finish()
    f_cols = Columns(net, ft, f_stage, f_wide, ffn_o)
    middle_c()
    f_cols.start()
    down.finish()
    d_stage[...] = dt_c[...].astype(low)

    @pl.when(chip != plane)
    def _():
        transposed(net, d_stage, d_got, d_sem).start()

    for i in (0, 1):
        part_s[pl.ds(i * half, half), :] = finish_c(i)

    def first_rows(b, _):
        at = pl.ds(pl.multiple_of(b * block, block), block)
        x = tok_ref[at, :].astype(full)
        inverse = lax.rsqrt(jnp.mean(x * x, axis=-1, keepdims=True) + EPS)
        normed = x * inverse
        seg = seg_ref[at, :]
        scale = pick_rows(mod_ref[:, :D], seg, 0)
        dh = part_s[at, :]
        gg_o[0:1, :] += jnp.sum(dh * normed * (1.0 + scale), axis=0, keepdims=True)
        by_image(dh * normed * gain_ref[0:1, :], seg, 0, 0)
        dn = dh * gain_ref[0:1, :] * (1.0 + scale)
        token_o[at, :] = dx_s[at, :] + inverse * (
            dn - normed * jnp.mean(dn * normed, axis=-1, keepdims=True)
        )
        return 0

    lax.fori_loop(0, ROW // block, first_rows, 0)
    f_cols.finish()

    @pl.when(chip != plane)
    def _():
        transposed(net, d_stage, d_got, d_sem).wait()
        down_o[...] = d_got[...].astype(full)

    @pl.when(chip == plane)
    def _():
        down_o[...] = dt_c[...]

    ffn.close()
    down.close()
    net.close()


def back_layer(early, late, ffn_g, down_g):
    low = jnp.bfloat16
    full = jnp.float32
    shape = jax.ShapeDtypeStruct
    V = VMEM_SPEC
    cap = IMGS * TXT
    fr, fw = ffn_g.shape[-2:]
    dr, dw = down_g.shape[-2:]
    tok = CHIPS * ROW
    reduce_scratch = [pltpu.VMEM((5, ROW, D), low), pltpu.VMEM((2, ROW // 2, D), low)]
    return pl.pallas_call(
        back_kernel,
        in_specs=[V] * len(early) + [ANY_SPEC] * (LATE + 2),
        out_specs=[V] * 13,
        out_shape=[
            shape((ROW, D), low),
            shape((ROW, D), full),
            shape((CHIPS, ROW, D), low),
            shape((tok, HW), low),
            shape((tok, HW), low),
            shape((tok, HW), low),
            shape((CHIPS * cap, HW), low),
            shape((CHIPS * cap, HW), low),
            shape((8, 2 * D), full),
            shape((8, D), full),
            shape((8, HW), full),
            shape((2, fr, 4 * fw), full),
            shape((dr, dw), full),
        ],
        scratch_shapes=[
            pltpu.VMEM((ROW, D), full),
            pltpu.VMEM((ROW, HW), full),
            pltpu.VMEM((tok, HW), full),
            pltpu.VMEM((tok, HW), full),
            pltpu.VMEM((CHIPS * cap, HW), full),
            pltpu.VMEM((tok, D), full),
            pltpu.VMEM((CHIPS, 8, tok), full),
            pltpu.VMEM((CHIPS, 8, CHIPS * cap), full),
            *reduce_scratch, *reduce_scratch, *reduce_scratch,
            *chain_scratch(True, (2, fr), fw),
            *chain_scratch(False, dr, dw),
            pltpu.VMEM((2, fr, 4 * fw), low),
            pltpu.VMEM((2, 4, fr, fw), low),
            pltpu.VMEM((dr, dw), low),
            pltpu.VMEM((dr, dw), low),
            pltpu.SemaphoreType.DMA((2,)),
            pltpu.VMEM((2, 4, 4, fr, fw), low),
            pltpu.VMEM((4, dr, dw), low),
            pltpu.SemaphoreType.DMA((2,)),
            *net_scratch(48),
            *[pltpu.VMEM(v.shape, v.dtype) for v in late],
            pltpu.SemaphoreType.DMA((LATE,)),
        ],
        compiler_params=pltpu.CompilerParams(
            collective_id=3, has_side_effects=True, vmem_limit_bytes=63 * 1024 * 1024
        ),
        cost_estimate=pl.CostEstimate(
            flops=10_000_000_000, bytes_accessed=400_000_000, transcendentals=0
        ),
    )(*early, *late, ffn_g, down_g)


def row_spec(rows, width):
    return pl.BlockSpec((rows, width), lambda i: (i, 0))


def attend_all(q, k, v, iq, ik, cosine, sine, tk, it, tv, seg_col, seg_row, gains):
    cap = IMGS * TXT
    low = jnp.bfloat16
    big = row_spec(ROW, HW)
    text = row_spec(cap, HW)
    one = row_spec(ROW, 1)
    table = row_spec(ROW, 128)
    shape = jax.ShapeDtypeStruct
    return pl.pallas_call(
        attend_kernel,
        grid=(CHIPS,),
        in_specs=[
            big, big, big, one, one, table, table, text, row_spec(cap, 1), text, one,
            pl.BlockSpec((1, 1, ROW), lambda i: (i, 0, 0)),
            pl.BlockSpec((6, HW), lambda i: (0, 0)),
        ],
        out_specs=[big, big, big, big, text],
        out_shape=[
            shape((CHIPS * ROW, HW), low),
            shape((CHIPS * ROW, HW), jnp.float32),
            shape((CHIPS * ROW, HW), low),
            shape((CHIPS * ROW, HW), low),
            shape((CHIPS * cap, HW), low),
        ],
        cost_estimate=pl.CostEstimate(
            flops=4 * 24 * 128 * 384 * 128, bytes_accessed=10_000_000, transcendentals=1_200_000
        ),
    )(q, k, v, iq, ik, cosine, sine, tk, it, tv, seg_col, seg_row, gains)


def per_device(
    tokens,
    cond,
    text,
    segments,
    positions,
    counts,
    ada_weight,
    ada_bias,
    gains,
    attn_weight,
    out_weight,
    text_weight,
    ffn_weight,
    down_weight,
    cotangent,
):
    low = jnp.bfloat16
    full = jnp.float32
    plane = lax.axis_index("bucket")
    slot = lax.axis_index("fsdp")
    core = slot % 2
    chip = slot // 2
    ff = ffn_weight.shape[2] // CHIPS

    gain_pad = lax.dynamic_update_slice_in_dim(
        jnp.zeros((8, D), full), jnp.pad(gains.astype(full), ((0, 2), (0, 0))), slot * 192, axis=1
    )
    bias = lax.dynamic_update_slice_in_dim(
        jnp.zeros((ada_weight.shape[1],), full), ada_bias.astype(full), slot * ada_bias.shape[0], 0
    )
    bias_pad = jnp.repeat(bias.reshape(2, 3072), 4, axis=0)
    seg = segments[0]
    idx = jnp.concatenate([seg[None, :], positions[0], jnp.zeros((5, ROW), jnp.int32)], axis=0)
    (
        mod, gain_f, h_rows, idx_all, attn_w, text_rows, query, keyed, valued, text_keys, text_vals,
        inv_qk, inv_t,
    ) = open_layer(
        jnp.concatenate([cond[0], cond[0]], axis=0), gain_pad, bias_pad, ada_weight, tokens[0],
        seg[:, None], idx, attn_weight, text_weight, text[0],
    )
    cond_act = silu(cond[0].astype(full)).astype(low)
    h_all = h_rows.reshape(CHIPS * ROW, D)
    text_all = text_rows.reshape(CHIPS * IMGS * TXT, -1)
    inv_qk = jnp.stack([inv_qk[0], inv_qk[4]])[:, :, None]
    inv_t = inv_t[0][:, None]
    seg_all = idx_all[:, 0]
    pos_all = idx_all[:, 1:3]
    seg_col = seg_all.reshape(CHIPS * ROW, 1)
    seg_row = seg_all.reshape(CHIPS, 1, ROW)
    lane = jnp.arange(128, dtype=jnp.int32)
    quarter = HDIM // 4
    freq = (10000.0 ** (-jnp.arange(quarter, dtype=full) / quarter))[lane % quarter]
    where_row = ((lane // 32) % 2 == 0)[None, None, :]
    pos_lane = jnp.where(where_row, pos_all[:, 0, :, None], pos_all[:, 1, :, None]).astype(full)
    angle = (pos_lane * freq[None, None, :]).reshape(CHIPS * ROW, 128)
    cosine = jnp.cos(angle)
    sine = jnp.where(((lane // quarter) % 2 == 0)[None, :], -1.0, 1.0) * jnp.sin(angle)

    ffn_w = column_weights(ffn_weight, chip, core, ff)
    out_w = row_weights(out_weight, core)
    down_w = row_weights(down_weight, core)
    gain_s = lax.dynamic_slice_in_dim(gain_f, chip * HW, HW, axis=1)[:6]

    def per_token(part):
        rows = mod[4 * (part // 2) :, (part % 2) * D : (part % 2 + 1) * D]
        out = rows[IMGS - 1][None, :]
        for i in range(IMGS - 2, -1, -1):
            out = jnp.where(seg[:, None] == i, rows[i][None, :], out)
        return out

    scale1 = per_token(0)
    gate1 = per_token(1)
    scale2 = per_token(2)
    gate2 = per_token(3)
    tanh_one = jnp.tanh(gate1)
    tanh_two = jnp.tanh(gate2)

    x = tokens[0].astype(full)
    normed1, inverse1 = norm_rows(x)
    comb, cross_out, q_rot, k_rot, text_rot = attend_all(
        query, keyed, valued, inv_qk[0], inv_qk[1], cosine, sine, text_keys, inv_t, text_vals,
        seg_col, seg_row, gain_s,
    )
    branch = reduce4(list(mult(comb, out_w).reshape(CHIPS, ROW, D)))
    x_one = x + tanh_one * branch
    normed2, inverse2 = norm_rows(x_one)
    h_two = (normed2 * gain_f[1] * (1.0 + scale2)).astype(low)
    h_two_all = jnp.concatenate(gather4(h_two), axis=0)

    totals = counts.astype(full)
    here = jnp.sum(jnp.where(jnp.arange(totals.shape[0], dtype=jnp.int32) == plane, totals, 0.0))
    weight = lax.axis_size("bucket") * here / jnp.sum(totals)
    grad = cotangent[0].astype(full) * weight
    d_ffn = (grad * tanh_two).astype(low)
    d_ffn_all = jnp.concatenate(gather4(d_ffn), axis=0)

    gate_pre = mult(h_two_all, ffn_w[0])
    upper = mult(h_two_all, ffn_w[1])
    d_hidden = dot_t(d_ffn_all, down_w)
    sigm = jax.nn.sigmoid(gate_pre)
    silu_pre = gate_pre * sigm
    hidden = (silu_pre * upper).astype(low)
    d_pre = (d_hidden * upper * sigm * (1.0 + gate_pre * (1.0 - sigm))).astype(low)
    d_up = (d_hidden * silu_pre).astype(low)
    d_h_two = (dot_t(d_pre, ffn_w[0]) + dot_t(d_up, ffn_w[1])).astype(low)
    ffn_out = mult(hidden, down_w).astype(low)
    g_down = t_dot(hidden, d_ffn_all).astype(low)
    g_ffn = jnp.stack([t_dot(h_two_all, d_pre).astype(low), t_dot(h_two_all, d_up).astype(low)])

    (
        block_out, token_grad, d_branch_rows, d_query, d_keyed, d_valued, d_text_keys, d_text_vals,
        d_mod, gg_full, gg_slice, s_ffn, s_down,
    ) = back_layer(
        [
            d_h_two, ffn_out, x_one, branch, cotangent[0], jnp.full((1, 128), weight, full), mod,
            seg[:, None], gain_f, tokens[0], seg_row, gain_s,
        ],
        [
            out_w, attn_w, q_rot, k_rot, valued, text_rot, text_vals, cross_out, query, keyed,
            text_keys, inv_qk[0], inv_qk[1], inv_t, cosine, sine, seg_col,
        ],
        g_ffn.reshape(2, 4, 4, 2, 48, ff),
        g_down.reshape(4, 2, 128, D),
    )
    d_branch_all = d_branch_rows.reshape(CHIPS * ROW, D)
    g_text = jnp.stack(
        [t_dot(text_all, d_text_keys).astype(low), t_dot(text_all, d_text_vals).astype(low)]
    )
    g_attn = jnp.stack([t_dot(h_all, g).astype(low) for g in (d_query, d_keyed, d_valued)])
    g_out = t_dot(comb, d_branch_all).astype(low)
    s_text, s_attn, s_out = close_layer(
        g_text.reshape(2, 4, 4, 2, 128, HW),
        g_attn.reshape(3, 4, 4, 2, 48, HW),
        g_out.reshape(4, 2, 48, D),
    )

    d_mod = jnp.concatenate([d_mod[:IMGS], d_mod[IMGS:]], axis=1)

    gg = gg_slice[:4]
    cross_gate = jnp.tanh(gain_s[5])
    gg = gg.at[3].multiply(1.0 - cross_gate * cross_gate)
    spread = lax.dynamic_update_slice_in_dim(jnp.zeros((4, D), full), gg, chip * HW, axis=1)
    small = jnp.concatenate(
        [gg_full[:2], spread, jnp.sum(d_mod, axis=0).reshape(4, D)], axis=0
    )
    small = small + at_core(small)
    small = sum4(small)
    small = small + lax.ppermute(small, "bucket", [(i, i ^ 1) for i in range(4)])
    small = small + lax.ppermute(small, "bucket", [(i, i ^ 2) for i in range(4)])
    rank = plane * 8 + slot
    s_gains = lax.dynamic_slice_in_dim(small[:6], rank * 48, 48, axis=1)
    s_ada_b = lax.dynamic_slice_in_dim(small[6:].reshape(-1), rank * 192, 192, axis=0)

    mod_low = d_mod.astype(low)
    mods = jnp.concatenate(gather4(mod_low), axis=0)
    planes_m = [mods]
    for shift in (1, 2, 3):
        planes_m.append(
            lax.ppermute(mods, "bucket", [(i, i ^ shift) for i in range(4)])
        )
    mods = jnp.concatenate(planes_m, axis=0)
    mods = jnp.concatenate([mods, at_core(mods)], axis=0)
    conds_all = jnp.concatenate(gather4(cond_act), axis=0)
    planes_c = [conds_all]
    for shift in (1, 2, 3):
        planes_c.append(
            lax.ppermute(conds_all, "bucket", [(i, i ^ shift) for i in range(4)])
        )
    conds_all = jnp.concatenate(planes_c, axis=0)
    conds_all = jnp.concatenate([conds_all, at_core(conds_all)], axis=0)
    s_ada_w = t_dot(lax.dynamic_slice_in_dim(conds_all, rank * 32, 32, axis=1), mods)

    return (
        block_out[None],
        token_grad[None],
        s_ada_w,
        s_ada_b,
        s_gains,
        s_attn,
        s_out,
        s_text,
        s_ffn,
        s_down,
    )


def solution(mesh):
    in_specs = (
        P(("bucket", "fsdp"), None, None),
        P(("bucket", "fsdp"), None, None),
        P(("bucket", "fsdp"), None, None),
        P(("bucket", "fsdp"), None),
        P(("bucket", "fsdp"), None, None),
        P(),
        P("fsdp", None),
        P("fsdp"),
        P(None, "fsdp"),
        P(None, "fsdp", None),
        P("fsdp", None),
        P(None, "fsdp", None),
        P(None, "fsdp", None),
        P("fsdp", None),
        P(("bucket", "fsdp"), None, None),
    )
    out_specs = (
        P(("bucket", "fsdp"), None, None),
        P(("bucket", "fsdp"), None, None),
        P(("bucket", "fsdp"), None),
        P(("bucket", "fsdp")),
        P(None, ("bucket", "fsdp")),
        P(None, ("bucket", "fsdp"), None),
        P(("bucket", "fsdp"), None),
        P(None, ("bucket", "fsdp"), None),
        P(None, ("bucket", "fsdp"), None),
        P(("bucket", "fsdp"), None),
    )
    fast = mesh.shape["fsdp"] == 8 and mesh.shape["bucket"] == 4
    return jax.shard_map(
        per_device if fast else per_device_general, mesh=mesh, in_specs=in_specs, out_specs=out_specs, check_vma=False
    )
```

```python
import jax
import jax.numpy as jnp
from jax import lax
from jax.experimental import pallas as pl
from jax.experimental.pallas import tpu as pltpu
from jax.sharding import PartitionSpec as P

D = 1536
HEADS = 24
HDIM = 64
IMGS = 4
TXT = 64


EPS = 1e-06
NEGATIVE = -1e30
HIGH = lax.Precision.HIGHEST


def silu(v):
    return v * jax.nn.sigmoid(v)


def norm_rows(v):
    inverse = lax.rsqrt(jnp.mean(v * v, axis=-1, keepdims=True) + EPS)
    return (v * inverse, inverse)


def norm_back(grad, normed, inverse):
    return inverse * (grad - normed * jnp.mean(grad * normed, axis=-1, keepdims=True))


def rotary_tables(pos):
    quarter = HDIM // 4
    freq = 10000.0 ** (-jnp.arange(quarter, dtype=jnp.float32) / quarter)
    angle = jnp.transpose(pos.astype(jnp.float32), (1, 0))[:, :, None] * freq[None, None, :]
    return (jnp.cos(angle), jnp.sin(angle))


def rotate(v, cosine, sine):
    rows = v.shape[0]
    parts = v.reshape(rows, HEADS, 2, 2, HDIM // 4)
    first = parts[:, :, :, 0]
    second = parts[:, :, :, 1]
    cosine = cosine[:, None]
    sine = sine[:, None]
    turned = jnp.stack([first * cosine - second * sine, first * sine + second * cosine], axis=3)
    return turned.reshape(rows, HEADS * HDIM)


def to_pairs(v):
    return jnp.transpose(v.reshape(v.shape[0], HEADS // 2, 2 * HDIM), (1, 0, 2))


def from_pairs(v):
    return jnp.transpose(v, (1, 0, 2)).reshape(v.shape[1], HEADS * HDIM)


def pair_scores(query, keys):
    q_heads = query.reshape(query.shape[0], 2, HDIM)
    k_heads = keys.reshape(keys.shape[0], 2, HDIM)
    return jnp.einsum(
        "rhd,khd->hrk", q_heads, k_heads, preferred_element_type=jnp.float32
    ) * HDIM ** (-0.5)


def attend_forward(q_b, k_b, v_b, allowed):

    def one_pair(item):
        query, keys, values = item
        scores = jnp.where(allowed[None], pair_scores(query, keys), NEGATIVE)
        top = jnp.max(scores, axis=-1, keepdims=True)
        expo = jnp.exp(scores - top)
        total = jnp.sum(expo, axis=-1, keepdims=True)
        probs = (expo / total).astype(jnp.bfloat16)
        result = jnp.einsum(
            "hrk,khd->rhd",
            probs,
            values.reshape(values.shape[0], 2, HDIM),
            preferred_element_type=jnp.float32,
        )
        return (result.reshape(query.shape[0], 2 * HDIM), (top + jnp.log(total))[..., 0])

    outputs, saved = lax.map(one_pair, (to_pairs(q_b), to_pairs(k_b), to_pairs(v_b)))
    return (from_pairs(outputs), saved)


def attend_back(q_b, k_b, v_b, saved, grad_b, allowed):

    def one_pair(item):
        query, keys, values, lse_pair, grad = item
        rows = query.shape[0]
        count = keys.shape[0]
        scores = jnp.where(allowed[None], pair_scores(query, keys), NEGATIVE)
        probs = jnp.exp(scores - lse_pair[..., None])
        probs_b = probs.astype(jnp.bfloat16)
        grad_heads = grad.reshape(rows, 2, HDIM)
        dprob = jnp.einsum(
            "rhd,khd->hrk",
            grad_heads,
            values.reshape(count, 2, HDIM),
            preferred_element_type=jnp.float32,
        )
        dscore = (probs * (dprob - jnp.sum(probs * dprob, axis=-1, keepdims=True))).astype(
            jnp.bfloat16
        )
        factor = HDIM ** (-0.5)
        dquery = (
            jnp.einsum(
                "hrk,khd->rhd",
                dscore,
                keys.reshape(count, 2, HDIM),
                preferred_element_type=jnp.float32,
            )
            * factor
        )
        dkeys = (
            jnp.einsum(
                "hrk,rhd->khd",
                dscore,
                query.reshape(rows, 2, HDIM),
                preferred_element_type=jnp.float32,
            )
            * factor
        )
        dvalues = jnp.einsum(
            "hrk,rhd->khd", probs_b, grad_heads, preferred_element_type=jnp.float32
        )
        return (
            dquery.reshape(rows, 2 * HDIM),
            dkeys.reshape(count, 2 * HDIM),
            dvalues.reshape(count, 2 * HDIM),
        )

    d_query, d_keys, d_values = lax.map(
        one_pair, (to_pairs(q_b), to_pairs(k_b), to_pairs(v_b), saved, to_pairs(grad_b))
    )
    return (from_pairs(d_query), from_pairs(d_keys), from_pairs(d_values))


def mult(left, right):
    return jnp.dot(left, right, preferred_element_type=jnp.float32)


def per_device_general(
    tokens,
    cond,
    text,
    segments,
    positions,
    counts,
    ada_weight,
    ada_bias,
    gains,
    attn_weight,
    out_weight,
    text_weight,
    ffn_weight,
    down_weight,
    cotangent,
):
    ada_w, ada_b, gain_rows, attn_w, out_w, text_w = (
        lax.all_gather(ada_weight, "fsdp", axis=0, tiled=True),
        lax.all_gather(ada_bias, "fsdp", axis=0, tiled=True),
        lax.all_gather(gains, "fsdp", axis=1, tiled=True),
        lax.all_gather(attn_weight, "fsdp", axis=1, tiled=True),
        lax.all_gather(out_weight, "fsdp", axis=0, tiled=True),
        lax.all_gather(text_weight, "fsdp", axis=1, tiled=True),
    )
    gain_f = gain_rows.astype(jnp.float32)
    x = tokens[0].astype(jnp.float32)
    seg = segments[0]
    cosine, sine = rotary_tables(positions[0])
    text_b = text[0]
    cond_act = silu(cond[0].astype(jnp.float32)).astype(jnp.bfloat16)
    mod = mult(cond_act, ada_w) + ada_b.astype(jnp.float32)[None, :]
    pick = (seg[:, None] == jnp.arange(IMGS, dtype=jnp.int32)[None, :]).astype(jnp.float32)
    per_token = jnp.dot(pick, mod, precision=HIGH)
    scale1 = per_token[:, :D]
    gate1 = per_token[:, D : 2 * D]
    scale2 = per_token[:, 2 * D : 3 * D]
    gate2 = per_token[:, 3 * D :]
    normed1, inverse1 = norm_rows(x)
    h_one = (normed1 * gain_f[0] * (1.0 + scale1)).astype(jnp.bfloat16)
    query = mult(h_one, attn_w[0])
    keyed = mult(h_one, attn_w[1])
    valued = mult(h_one, attn_w[2]).astype(jnp.bfloat16)
    q_norm, q_inv = norm_rows(query)
    k_norm, k_inv = norm_rows(keyed)
    q_rot = rotate(q_norm * gain_f[2], cosine, sine).astype(jnp.bfloat16)
    k_rot = rotate(k_norm * gain_f[3], cosine, sine).astype(jnp.bfloat16)
    text_keys = mult(text_b, text_w[0])
    text_vals = mult(text_b, text_w[1]).astype(jnp.bfloat16)
    t_norm, t_inv = norm_rows(text_keys)
    text_rot = (t_norm * gain_f[4]).astype(jnp.bfloat16)
    same = seg[:, None] == seg[None, :]
    owner = jnp.arange(IMGS * TXT, dtype=jnp.int32) // TXT
    mine = seg[:, None] == owner[None, :]
    self_out, self_lse = attend_forward(q_rot, k_rot, valued, same)
    cross_out, cross_lse = attend_forward(q_rot, text_rot, text_vals, mine)
    cross_gate = jnp.tanh(gain_f[5])
    comb = (self_out + cross_gate * cross_out).astype(jnp.bfloat16)
    branch = mult(comb, out_w)
    tanh_one = jnp.tanh(gate1)
    x_one = x + tanh_one * branch
    normed2, inverse2 = norm_rows(x_one)
    h_two = (normed2 * gain_f[1] * (1.0 + scale2)).astype(jnp.bfloat16)
    ffn_w, down_w = (
        lax.all_gather(ffn_weight, "fsdp", axis=1, tiled=True),
        lax.all_gather(down_weight, "fsdp", axis=0, tiled=True),
    )
    gate_pre = mult(h_two, ffn_w[0])
    upper = mult(h_two, ffn_w[1])
    sigm = jax.nn.sigmoid(gate_pre)
    silu_pre = gate_pre * sigm
    hidden = (silu_pre * upper).astype(jnp.bfloat16)
    ffn_out = mult(hidden, down_w)
    tanh_two = jnp.tanh(gate2)
    block_out = (x_one + tanh_two * ffn_out).astype(jnp.bfloat16)
    totals = counts.astype(jnp.float32)
    here = jnp.sum(
        jnp.where(
            jnp.arange(totals.shape[0], dtype=jnp.int32) == lax.axis_index("bucket"), totals, 0.0
        )
    )
    weight = lax.axis_size("bucket") * here / jnp.sum(totals)
    grad = cotangent[0].astype(jnp.float32) * weight
    back_ffn, back_down = (
        lax.all_gather(ffn_weight, "fsdp", axis=1, tiled=True),
        lax.all_gather(down_weight, "fsdp", axis=0, tiled=True),
    )
    d_gate2 = grad * ffn_out * (1.0 - tanh_two * tanh_two)
    d_ffn = (grad * tanh_two).astype(jnp.bfloat16)
    d_hidden = mult(d_ffn, back_down.T)
    g_down = mult(hidden.T, d_ffn)
    d_pre = (d_hidden * upper * sigm * (1.0 + gate_pre * (1.0 - sigm))).astype(jnp.bfloat16)
    d_up = (d_hidden * silu_pre).astype(jnp.bfloat16)
    d_h_two = mult(d_pre, back_ffn[0].T) + mult(d_up, back_ffn[1].T)
    g_ffn = jnp.stack([mult(h_two.T, d_pre), mult(h_two.T, d_up)])
    s_ffn, s_down = (
        lax.psum_scatter(g_ffn, ("bucket", "fsdp"), scatter_dimension=1, tiled=True),
        lax.psum_scatter(g_down, ("bucket", "fsdp"), scatter_dimension=0, tiled=True),
    )
    back_attn, back_out = (
        lax.all_gather(attn_weight, "fsdp", axis=1, tiled=True),
        lax.all_gather(out_weight, "fsdp", axis=0, tiled=True),
    )
    g_gain_one = jnp.sum(d_h_two * normed2 * (1.0 + scale2), axis=0)
    d_scale2 = d_h_two * normed2 * gain_f[1]
    d_x_one = grad + norm_back(d_h_two * gain_f[1] * (1.0 + scale2), normed2, inverse2)
    d_gate1 = d_x_one * branch * (1.0 - tanh_one * tanh_one)
    d_branch = (d_x_one * tanh_one).astype(jnp.bfloat16)
    d_comb = mult(d_branch, back_out.T)
    g_out = mult(comb.T, d_branch)
    g_gain_five = jnp.sum(d_comb * cross_out, axis=0) * (1.0 - cross_gate * cross_gate)
    d_self = d_comb.astype(jnp.bfloat16)
    d_cross = (d_comb * cross_gate).astype(jnp.bfloat16)
    dq_self, dk_self, dv_self = attend_back(q_rot, k_rot, valued, self_lse, d_self, same)
    dq_cross, dk_text, dv_text = attend_back(q_rot, text_rot, text_vals, cross_lse, d_cross, mine)
    d_q_norm = rotate(dq_self + dq_cross, cosine, -sine)
    g_gain_two = jnp.sum(d_q_norm * q_norm, axis=0)
    d_query = norm_back(d_q_norm * gain_f[2], q_norm, q_inv).astype(jnp.bfloat16)
    d_k_norm = rotate(dk_self, cosine, -sine)
    g_gain_three = jnp.sum(d_k_norm * k_norm, axis=0)
    d_keyed = norm_back(d_k_norm * gain_f[3], k_norm, k_inv).astype(jnp.bfloat16)
    d_valued = dv_self.astype(jnp.bfloat16)
    g_gain_four = jnp.sum(dk_text * t_norm, axis=0)
    d_text_keys = norm_back(dk_text * gain_f[4], t_norm, t_inv).astype(jnp.bfloat16)
    d_text_vals = dv_text.astype(jnp.bfloat16)
    g_text = jnp.stack([mult(text_b.T, d_text_keys), mult(text_b.T, d_text_vals)])
    d_h_one = (
        mult(d_query, back_attn[0].T)
        + mult(d_keyed, back_attn[1].T)
        + mult(d_valued, back_attn[2].T)
    )
    g_attn = jnp.stack([mult(h_one.T, d_query), mult(h_one.T, d_keyed), mult(h_one.T, d_valued)])
    g_gain_zero = jnp.sum(d_h_one * normed1 * (1.0 + scale1), axis=0)
    d_scale1 = d_h_one * normed1 * gain_f[0]
    token_grad = d_x_one + norm_back(d_h_one * gain_f[0] * (1.0 + scale1), normed1, inverse1)
    d_token_mod = jnp.concatenate([d_scale1, d_gate1, d_scale2, d_gate2], axis=1)
    d_mod = jnp.dot(pick.T, d_token_mod, precision=HIGH)
    g_ada_b = jnp.sum(d_mod, axis=0)
    g_ada_w = mult(cond_act.T, d_mod.astype(jnp.bfloat16))
    g_gains = jnp.stack(
        [g_gain_zero, g_gain_one, g_gain_two, g_gain_three, g_gain_four, g_gain_five]
    )
    s_ada_w, s_ada_b, s_gains, s_attn, s_out, s_text = (
        lax.psum_scatter(g_ada_w, ("bucket", "fsdp"), scatter_dimension=0, tiled=True),
        lax.psum_scatter(g_ada_b, ("bucket", "fsdp"), scatter_dimension=0, tiled=True),
        lax.psum_scatter(g_gains, ("bucket", "fsdp"), scatter_dimension=1, tiled=True),
        lax.psum_scatter(g_attn, ("bucket", "fsdp"), scatter_dimension=1, tiled=True),
        lax.psum_scatter(g_out, ("bucket", "fsdp"), scatter_dimension=0, tiled=True),
        lax.psum_scatter(g_text, ("bucket", "fsdp"), scatter_dimension=1, tiled=True),
    )
    return (
        block_out[None],
        token_grad[None],
        s_ada_w,
        s_ada_b,
        s_gains,
        s_attn,
        s_out,
        s_text,
        s_ffn,
        s_down,
    )


ROW = 128
CHIPS = 4
HW = D // CHIPS
PAIRS = HW // 128


def swap(v, mask):
    return lax.ppermute(v, "fsdp", [(i, i ^ mask) for i in range(8)])


def at_x(v):
    return swap(v, 2)


def at_y(v):
    return swap(v, 4)


def at_core(v):
    return swap(v, 1)


def gather4(v):
    half = v.shape[0] // 2
    by_x = at_x(v)
    by_y = at_y(v)
    far = jnp.concatenate([at_y(by_x[:half]), at_x(by_y[half:])], axis=0)
    return [v, by_x, by_y, far]


def sum4(v):
    v = v + at_x(v)
    return v + at_y(v)


def partner(u):
    lane = lax.broadcasted_iota(jnp.int32, u.shape, 1)
    ahead = pltpu.roll(u, u.shape[1] - 16, 1)
    behind = pltpu.roll(u, 16, 1)
    return jnp.where((lane // 16) % 2 == 0, ahead, behind)


def dot_t(a, b):
    return lax.dot_general(a, b, (((1,), (1,)), ((), ())), preferred_element_type=jnp.float32)


def dot_n(a, b):
    return lax.dot_general(a, b, (((1,), (0,)), ((), ())), preferred_element_type=jnp.float32)


def t_dot(a, b):
    return lax.dot_general(a, b, (((0,), (0,)), ((), ())), preferred_element_type=jnp.float32)


def softmax_of(scores, allowed):
    scores = jnp.where(allowed, scores * HDIM ** (-0.5), NEGATIVE)
    top = jnp.max(scores, axis=-1, keepdims=True)
    expo = jnp.exp(scores - top)
    return expo / jnp.sum(expo, axis=-1, keepdims=True)


def head_mask(v, head):
    lane = lax.broadcasted_iota(jnp.int32, v.shape, 1)
    return jnp.where((lane // HDIM) == head, v, jnp.zeros_like(v))


def masks_of(seg_col, seg_row, captions):
    same = seg_col == seg_row
    owner = lax.broadcasted_iota(jnp.int32, (seg_col.shape[0], captions), 1) // TXT
    return same, seg_col == owner


def attend_kernel(
    q_ref, k_ref, v_ref, iq_ref, ik_ref, cos_ref, sin_ref, tk_ref, it_ref, tv_ref, sc_ref, sr_ref,
    g_ref, comb_ref, cross_ref, qr_ref, kr_ref, tr_ref,
):
    same, mine = masks_of(sc_ref[...], sr_ref[...], tk_ref.shape[0])
    cosine = cos_ref[...]
    sine = sin_ref[...]
    low = jnp.bfloat16
    for pair in range(PAIRS):
        at = pl.ds(pair * 128, 128)
        qn = q_ref[:, at] * iq_ref[...] * g_ref[2:3, at]
        kn = k_ref[:, at] * ik_ref[...] * g_ref[3:4, at]
        qr = (qn * cosine + partner(qn) * sine).astype(low)
        kr = (kn * cosine + partner(kn) * sine).astype(low)
        tr = (tk_ref[:, at] * it_ref[...] * g_ref[4:5, at]).astype(low)
        qr_ref[:, at] = qr
        kr_ref[:, at] = kr
        tr_ref[:, at] = tr
        vv = v_ref[:, at]
        tv = tv_ref[:, at]
        self_out = jnp.zeros(qn.shape, jnp.float32)
        cross_out = jnp.zeros(qn.shape, jnp.float32)
        for head in range(2):
            qh = head_mask(qr, head)
            probs = softmax_of(dot_t(qh, kr), same).astype(low)
            self_out = self_out + head_mask(dot_n(probs, vv), head)
            probs = softmax_of(dot_t(qh, tr), mine).astype(low)
            cross_out = cross_out + head_mask(dot_n(probs, tv), head)
        cross_ref[:, at] = cross_out
        comb_ref[:, at] = (self_out + jnp.tanh(g_ref[5:6, at]) * cross_out).astype(low)


def attend_back_kernel(
    qr_ref, kr_ref, v_ref, tr_ref, tv_ref, dc_ref, cross_ref, q_ref, k_ref, tk_ref, iq_ref, ik_ref,
    it_ref, cos_ref, sin_ref, sc_ref, sr_ref, g_ref,
    dq_ref, dk_ref, dv_ref, dt_ref, dtv_ref, gg_ref,
):
    same, mine = masks_of(sc_ref[...], sr_ref[...], tk_ref.shape[0])
    cosine = cos_ref[...]
    sine = sin_ref[...]
    low = jnp.bfloat16
    factor = HDIM ** (-0.5)
    for pair in range(PAIRS):
        at = pl.ds(pair * 128, 128)
        qr = qr_ref[:, at]
        kr = kr_ref[:, at]
        vv = v_ref[:, at]
        tr = tr_ref[:, at]
        tv = tv_ref[:, at]
        dcomb = dc_ref[:, at]
        d_self = dcomb.astype(low)
        d_cross = (dcomb * jnp.tanh(g_ref[5:6, at])).astype(low)
        dq = jnp.zeros(dcomb.shape, jnp.float32)
        dk = jnp.zeros(dcomb.shape, jnp.float32)
        dv = jnp.zeros(dcomb.shape, jnp.float32)
        dt = jnp.zeros((tr.shape[0], 128), jnp.float32)
        dtv = jnp.zeros((tr.shape[0], 128), jnp.float32)
        for head in range(2):
            qh = head_mask(qr, head)
            probs = softmax_of(dot_t(qh, kr), same)
            grad = head_mask(d_self, head)
            dprob = dot_t(grad, vv)
            dscore = probs * (dprob - jnp.sum(probs * dprob, axis=-1, keepdims=True))
            dscore = dscore.astype(low)
            dq = dq + dot_n(dscore, head_mask(kr, head))
            dk = dk + t_dot(dscore, qh)
            dv = dv + t_dot(probs.astype(low), grad)
            probs = softmax_of(dot_t(qh, tr), mine)
            grad = head_mask(d_cross, head)
            dprob = dot_t(grad, tv)
            dscore = probs * (dprob - jnp.sum(probs * dprob, axis=-1, keepdims=True))
            dscore = dscore.astype(low)
            dq = dq + dot_n(dscore, head_mask(tr, head))
            dt = dt + t_dot(dscore, qh)
            dtv = dtv + t_dot(probs.astype(low), grad)
        dq = dq * factor
        dk = dk * factor
        dt = dt * factor
        dq = dq * cosine - partner(dq) * sine
        dk = dk * cosine - partner(dk) * sine
        q_norm = q_ref[:, at] * iq_ref[...]
        k_norm = k_ref[:, at] * ik_ref[...]
        t_norm = tk_ref[:, at] * it_ref[...]
        gg_ref[0:1, at] += jnp.sum(dq * q_norm, axis=0, keepdims=True)
        gg_ref[1:2, at] += jnp.sum(dk * k_norm, axis=0, keepdims=True)
        gg_ref[2:3, at] += jnp.sum(dt * t_norm, axis=0, keepdims=True)
        gg_ref[3:4, at] += jnp.sum(dcomb * cross_ref[:, at], axis=0, keepdims=True)
        dq = dq * g_ref[2:3, at]
        dk = dk * g_ref[3:4, at]
        dt = dt * g_ref[4:5, at]
        dq_ref[:, at] = dq
        dk_ref[:, at] = dk
        dv_ref[:, at] = dv.astype(low)
        dt_ref[:, at] = dt
        dtv_ref[:, at] = dtv.astype(low)


MESH_IDS = pl.DeviceIdType.MESH
VMEM_SPEC = pl.BlockSpec(memory_space=pltpu.VMEM)
ANY_SPEC = pl.BlockSpec(memory_space=pl.ANY)


class Net:
    def __init__(self, send_sems, recv_sems):
        self.me = lax.axis_index("fsdp")
        self.send_sems = send_sems
        self.recv_sems = recv_sems
        self.count = 0
        self.all = []

    def peer(self, mask):
        out = self.me
        for bit in (1, 2, 4):
            if mask & bit:
                out = out + bit * (1 - 2 * ((self.me // bit) % 2))
        return out

    def meet(self, masks):
        sem = pltpu.get_barrier_semaphore()
        for mask in masks:
            pl.semaphore_signal(
                sem, inc=1, device_id={"fsdp": self.peer(mask)}, device_id_type=MESH_IDS
            )
        pl.semaphore_wait(sem, len(masks))

    def send(self, src, dst, mask):
        assert self.count < self.send_sems.shape[0]
        copy = pltpu.make_async_remote_copy(
            src_ref=src,
            dst_ref=dst,
            send_sem=self.send_sems.at[self.count],
            recv_sem=self.recv_sems.at[self.count],
            device_id={"fsdp": self.peer(mask)},
            device_id_type=MESH_IDS,
        )
        self.count += 1
        copy.start()
        self.all.append(copy)
        return copy

    def close(self):
        for copy in self.all:
            copy.wait_send()


def net_scratch(count):
    return [pltpu.SemaphoreType.DMA((count,)), pltpu.SemaphoreType.DMA((count,))]


def share4_start(net, out):
    return net.send(out.at[0], out.at[1], 2), net.send(out.at[0], out.at[2], 4)


def share4_relay(net, out, by_x, by_y):
    half = out.shape[1] // 2
    top, bottom = pl.ds(0, half), pl.ds(half, half)
    by_x.wait_recv()
    first = net.send(out.at[1, top], out.at[3, top], 4)
    by_y.wait_recv()
    second = net.send(out.at[2, bottom], out.at[3, bottom], 2)
    return first, second


def collect4(net, part, buf, far):
    half = far.shape[1]
    rows = (pl.ds(0, half), pl.ds(half, half))
    low = jnp.bfloat16
    full = jnp.float32
    for i in (0, 1):
        buf[2, rows[i]] = part(3, i).astype(low)
    far_x = net.send(buf.at[2, rows[0]], far.at[0], 2)
    far_y = net.send(buf.at[2, rows[1]], far.at[1], 4)
    buf[0, rows[0]] = part(1, 0).astype(low)
    one_a = net.send(buf.at[0, rows[0]], buf.at[3, rows[0]], 2)
    buf[1, rows[1]] = part(2, 1).astype(low)
    two_b = net.send(buf.at[1, rows[1]], buf.at[4, rows[1]], 4)
    later = []

    def middle():
        far_x.wait_recv()
        buf[1, rows[0]] = (part(2, 0) + far[0].astype(full)).astype(low)
        later.append(net.send(buf.at[1, rows[0]], buf.at[4, rows[0]], 4))
        far_y.wait_recv()
        buf[0, rows[1]] = (part(1, 1) + far[1].astype(full)).astype(low)
        later.append(net.send(buf.at[0, rows[1]], buf.at[3, rows[1]], 2))

    def finish(i):
        (one_a, two_b)[i].wait_recv()
        later[i].wait_recv()
        return part(0, i) + buf[3, rows[i]].astype(full) + buf[4, rows[i]].astype(full)

    return middle, finish


def pick_rows(table, seg, first):
    out = table[first + IMGS - 1 : first + IMGS]
    for i in range(IMGS - 2, -1, -1):
        out = jnp.where(seg == i, table[first + i : first + i + 1], out)
    return out


def row_sums(a, b):
    ones = jnp.ones((8, a.shape[1]), jnp.float32)

    def one(v):
        return lax.dot_general(
            ones, v, (((1,), (1,)), ((), ())), precision=HIGH, preferred_element_type=jnp.float32
        )

    if b is None:
        return one(a)
    got = one(a)
    return jnp.where(lax.broadcasted_iota(jnp.int32, got.shape, 0) < 4, got, one(b))


def spread(net, src, dst, width, local):
    count, rows, _ = src.shape

    def cut(i, c):
        return src.at[i, :, pl.ds(pl.multiple_of(c * width, 128), width)]

    def put(i, f):
        return dst.at[pl.ds(pl.multiple_of(f * rows, rows), rows), pl.ds(i * width, width)]

    chip = net.me // 2
    ids = range(count)
    here = [local(cut(i, chip), put(i, net.me)) for i in ids]
    core = [net.send(cut(i, chip), put(i, net.me), 1) for i in ids]

    def away(m):
        return [net.send(cut(i, net.peer(m) // 2), put(i, net.me), m) for i in ids]

    def whole(f):
        return dst.at[pl.ds(pl.multiple_of(f * rows, rows), rows), :]

    def pass_on(copies, m):
        for c in copies:
            c.wait_recv()
        return net.send(whole(net.peer(m)), whole(net.peer(m)), 1)

    return here, core, away, pass_on


ALL_PEERS = (1, 2, 3, 4, 5, 6, 7)


def open_kernel(
    cond_ref, gain_ref, bias_ref, ada_ref, tok_ref, seg_ref, idx_ref, attn_ref, textw_ref, text_ref,
    mod_ref, gains_ref, h_ref, idxs_ref, aw_ref, ta_out, q_ref, k_ref, v_ref, tk_ref, tv_ref,
    iqk_ref, it_ref,
    conds, parts, mods, gbuf, tw_ref, ta_ref, sums, tsums, local_sems, out_sems, send_sems,
    recv_sems,
):
    low = jnp.bfloat16
    full = jnp.float32
    net = Net(send_sems, recv_sems)
    me = net.me
    chip = me // 2
    net.meet(ALL_PEERS)

    act = cond_ref[...].astype(full)
    act = (act * jax.nn.sigmoid(act)).astype(low).astype(full)
    for j in range(8):
        gbuf[8, :, 128 * j : 128 * j + 128] = act[:, 128 * j : 128 * j + 128]
    waits = []
    for m in ALL_PEERS:
        at = pl.ds(pl.multiple_of(net.peer(m) * 128, 128), 128)
        waits.append(net.send(gbuf.at[8, :, at], conds.at[m], m))
    conds[0] = gbuf[8, :, pl.ds(pl.multiple_of(me * 128, 128), 128)]
    gwaits = [net.send(gain_ref, gbuf.at[m], m) for m in ALL_PEERS]
    iwaits = [net.send(idx_ref, idxs_ref.at[i], m) for i, m in ((1, 2), (2, 4), (3, 6))]
    idxs_ref[0] = idx_ref[...]

    for w in waits:
        w.wait_recv()
    lhs = jnp.concatenate([conds[m] for m in range(8)], axis=0).astype(low)
    half_cols = 3072
    step = 512

    def mod_cols(i, _):
        lo = pl.ds(pl.multiple_of(i * step, step), step)
        hi = pl.ds(pl.multiple_of(half_cols + i * step, step), step)
        a = jnp.dot(lhs, ada_ref[:, lo], preferred_element_type=full)
        b = jnp.dot(lhs, ada_ref[:, hi], preferred_element_type=full)
        row = lax.broadcasted_iota(jnp.int32, (8, step), 0)
        for m in range(8):
            parts[m, :, lo] = (
                jnp.where(row < 4, a[8 * m : 8 * m + 8], b[8 * m : 8 * m + 8]) + bias_ref[:, lo]
            )
        return 0

    lax.fori_loop(0, half_cols // step, mod_cols, 0)
    waits = [net.send(parts.at[m], mods.at[m], m) for m in ALL_PEERS]

    def local(slot):
        def go(src, dst):
            copy = pltpu.make_async_copy(src, dst, local_sems.at[slot[0]])
            slot[0] += 1
            copy.start()
            return copy

        return go

    slot = [3]
    attn_io = spread(net, attn_ref, aw_ref, HW, local(slot))
    attn_away = [attn_io[2](m) for m in (2, 4, 6)]
    text_io = spread(net, textw_ref, tw_ref, HW, local(slot))
    text_away = [text_io[2](m) for m in (2, 4, 6)]
    own_text = pltpu.make_async_copy(text_ref, ta_ref.at[0], local_sems.at[2])
    own_text.start()
    for w in gwaits:
        w.wait_recv()
    gains = gain_ref[...]
    for m in ALL_PEERS:
        gains = gains + gbuf[m]
    gains_ref[...] = gains
    for w in waits:
        w.wait_recv()

    def mod_sum(i, _):
        at = pl.ds(pl.multiple_of(i * step, step), step)
        total = parts[0, :, at]
        for m in ALL_PEERS:
            total = total + mods[m, :, at]
        mod_ref[:, at] = total
        return 0

    lax.fori_loop(0, half_cols // step, mod_sum, 0)

    block = 32

    def first_norm(i, _):
        at = pl.ds(pl.multiple_of(i * block, block), block)
        x = tok_ref[at, :].astype(full)
        normed = x * lax.rsqrt(jnp.mean(x * x, axis=-1, keepdims=True) + EPS)
        scale = pick_rows(mod_ref[:, :D], seg_ref[at, :], 0)
        h_ref[0, at, :] = (normed * gains_ref[0:1, :] * (1.0 + scale)).astype(low)
        return 0

    lax.fori_loop(0, ROW // block, first_norm, 0)
    hx, hy = share4_start(net, h_ref)

    def all_in(io, away):
        for c in io[0]:
            c.wait()
        return io[1] + [io[3](c, m) for c, m in zip(away, (2, 4, 6))]

    attn_core = all_in(attn_io, attn_away)
    text_core = all_in(text_io, text_away)
    h_far = share4_relay(net, h_ref, hx, hy)
    own_text.wait()

    def keep(j):
        copy = pltpu.make_async_copy(ta_ref.at[j], ta_out.at[j], out_sems.at[j])
        copy.start()
        return copy

    kept = [keep(0)]
    chunks = 4
    size = ta_ref.shape[1] // chunks
    tx, ty = [None] * chunks, [None] * chunks
    for s in range(chunks):
        i, j = s, (s + chunks // 2) % chunks
        at = pl.ds(i * size, size)
        tx[i] = net.send(ta_ref.at[0, at], ta_ref.at[1, at], 2)
        at = pl.ds(j * size, size)
        ty[j] = net.send(ta_ref.at[0, at], ta_ref.at[2, at], 4)

    for c in attn_core:
        c.wait_recv()
    for c in h_far:
        c.wait_recv()

    for j in range(CHIPS):
        h = h_ref[j]
        at = pl.ds(j * ROW, ROW)
        qv = jnp.dot(h, aw_ref[:, :HW], preferred_element_type=full)
        q_ref[at, :] = qv
        kv = jnp.dot(h, aw_ref[:, HW : 2 * HW], preferred_element_type=full)
        k_ref[at, :] = kv
        v_ref[at, :] = jnp.dot(h, aw_ref[:, 2 * HW :], preferred_element_type=full).astype(low)
        sums[0, :, at] = row_sums(qv * qv, kv * kv)
    sum_io = [net.send(sums.at[0], sums.at[i], m) for i, m in ((1, 2), (2, 4), (3, 6))]

    for c in text_core:
        c.wait_recv()

    def text_rows(j, lo, count):
        kt = 1024

        def body(i, acc):
            at = pl.ds(pl.multiple_of(i * kt, kt), kt)
            rows = ta_ref[j, pl.ds(lo, count), at]
            return acc + jnp.dot(rows, tw_ref[at, :], preferred_element_type=full)

        both = lax.fori_loop(0, ta_ref.shape[2] // kt, body, jnp.zeros((count, 2 * HW), full))
        keys, vals = both[:, :HW], both[:, HW:]
        at = pl.ds(j * ta_ref.shape[1] + lo, count)
        tk_ref[at, :] = keys
        tv_ref[at, :] = vals.astype(low)
        tsums[0, :, at] = row_sums(keys * keys, None)

    cap = ta_ref.shape[1]
    half = cap // 2
    for lo in (0, half):
        text_rows(0, lo, half)
    relays = []
    for s in range(chunks // 2):
        i, j = s, s + chunks // 2
        tx[i].wait_recv()
        at = pl.ds(i * size, size)
        relays.append(net.send(ta_ref.at[1, at], ta_ref.at[3, at], 4))
        ty[j].wait_recv()
        at = pl.ds(j * size, size)
        relays.append(net.send(ta_ref.at[2, at], ta_ref.at[3, at], 2))
    for i, c in enumerate(sum_io):
        c.wait_recv()
    for j in range(CHIPS):
        total = sums[0, :, pl.ds(j * ROW, ROW)]
        for i in (1, 2, 3):
            total = total + sums[i, :, pl.ds((j ^ i) * ROW, ROW)]
        iqk_ref[:, pl.ds(j * ROW, ROW)] = lax.rsqrt(total / D + EPS)
    text_rows(1, 0, half)
    text_rows(2, half, half)
    for s in range(chunks // 2):
        tx[s + chunks // 2].wait_recv()
        ty[s].wait_recv()
    kept += [keep(1), keep(2)]
    text_rows(1, half, half)
    text_rows(2, 0, half)
    for c in relays:
        c.wait_recv()
    kept.append(keep(3))
    for lo in (0, half):
        text_rows(3, lo, half)
    sum_io = [net.send(tsums.at[0], tsums.at[i], m) for i, m in ((1, 2), (2, 4), (3, 6))]
    for c in sum_io:
        c.wait_recv()
    for j in range(CHIPS):
        total = tsums[0, :, pl.ds(j * cap, cap)]
        for i in (1, 2, 3):
            total = total + tsums[i, :, pl.ds((j ^ i) * cap, cap)]
        it_ref[:, pl.ds(j * cap, cap)] = lax.rsqrt(total / D + EPS)
    for c in iwaits:
        c.wait_recv()
    for c in kept:
        c.wait()
    net.close()


def open_layer(cond8, gain_pad, bias_pad, ada, tok, seg_col, idx, attn, textw, text):
    low = jnp.bfloat16
    full = jnp.float32
    shape = jax.ShapeDtypeStruct
    cap, txtd = text.shape
    V = VMEM_SPEC
    return pl.pallas_call(
        open_kernel,
        in_specs=[V, V, V, V, V, V, V, ANY_SPEC, ANY_SPEC, ANY_SPEC],
        out_specs=[V] * 5 + [ANY_SPEC] + [V] * 7,
        out_shape=[
            shape((8, 3072), full),
            shape((8, D), full),
            shape((CHIPS, ROW, D), low),
            shape((CHIPS, 8, ROW), jnp.int32),
            shape((D, 3 * HW), low),
            shape((CHIPS, cap, txtd), low),
            shape((CHIPS * ROW, HW), full),
            shape((CHIPS * ROW, HW), full),
            shape((CHIPS * ROW, HW), low),
            shape((CHIPS * cap, HW), full),
            shape((CHIPS * cap, HW), low),
            shape((8, CHIPS * ROW), full),
            shape((8, CHIPS * cap), full),
        ],
        scratch_shapes=[
            pltpu.VMEM((8, 8, 128), full),
            pltpu.VMEM((8, 8, 3072), full),
            pltpu.VMEM((8, 8, 3072), full),
            pltpu.VMEM((9, 8, D), full),
            pltpu.VMEM((txtd, 2 * HW), low),
            pltpu.VMEM((CHIPS, cap, txtd), low),
            pltpu.VMEM((CHIPS, 8, CHIPS * ROW), full),
            pltpu.VMEM((CHIPS, 8, CHIPS * cap), full),
            pltpu.SemaphoreType.DMA((8,)),
            pltpu.SemaphoreType.DMA((CHIPS,)),
            *net_scratch(80),
        ],
        compiler_params=pltpu.CompilerParams(
            collective_id=1, has_side_effects=True, vmem_limit_bytes=56 * 1024 * 1024
        ),
        cost_estimate=pl.CostEstimate(
            flops=10_000_000_000, bytes_accessed=400_000_000, transcendentals=0
        ),
    )(cond8, gain_pad, bias_pad, ada, tok, seg_col, idx, attn, textw, text)


class Chain:
    def __init__(self, net, grad, mine, arrive, total, sems, columns):
        self.net = net
        self.grad = grad
        self.mine = mine
        self.arrive = arrive
        self.total = total
        self.sems = sems
        self.columns = columns
        self.plane = lax.axis_index("bucket")
        self.core = net.me % 2

    def piece(self, ref, p):
        return ref.at[:, p] if self.columns else ref.at[p]

    def half(self, core):
        return self.grad.at[:, :, :, core] if self.columns else self.grad.at[:, core]

    def each(self, ref, body):
        lead = ref.shape[:-2]
        if not lead:
            body(())
            return
        total = 1
        for n in lead:
            total *= n

        def step(i, _):
            index = []
            for n in reversed(lead):
                index.insert(0, i % n)
                i = i // n
            body(tuple(index))
            return 0

        lax.fori_loop(0, total, step, 0)

    def core_start(self, keep=None, sem=None):
        self.exchange = self.net.send(self.half(1 - self.core), self.mine, 1)
        self.keep = self.half(self.core)
        self.load = None
        if keep is not None:
            self.load = pltpu.make_async_copy(self.keep, keep, sem)
            self.load.start()
            self.keep = keep

    def add(self, into, other):
        def body(index):
            value = into[index].astype(jnp.float32) + other[index].astype(jnp.float32)
            into[index] = value.astype(into.dtype)

        self.each(into, body)

    def core_finish(self):
        self.exchange.wait_recv()
        if self.load is not None:
            self.load.wait()
        self.add(self.mine, self.keep)

    def copy(self, up, p, slot):
        first = 0 if up else 8
        return pltpu.make_async_remote_copy(
            src_ref=self.piece(self.mine, p),
            dst_ref=self.arrive.at[slot],
            send_sem=self.sems.at[first + p],
            recv_sem=self.sems.at[first + 4 + p],
            device_id={"bucket": self.plane + (1 if up else -1)},
            device_id_type=MESH_IDS,
        )

    def moves(self, t):
        up = self.plane + 3 - t
        down = self.plane - 3 + t
        return (
            (True, up, up, self.plane <= t, self.plane >= 1),
            (False, down, 4 if t == 2 else down, self.plane >= 3 - t, self.plane <= 2),
        )

    def step(self, t):
        for up, p, slot, sends, inner in self.moves(t):

            @pl.when(sends)
            def _(up=up, p=p, slot=slot, inner=inner):
                @pl.when(inner)
                def _():
                    self.copy(up, p, p).wait_recv()
                    self.add(self.piece(self.mine, p), self.arrive.at[p])

                self.copy(up, p, slot).start()

    def finish(self):
        own = self.piece(self.mine, self.plane)

        def first(index):
            self.total[index] = own[index].astype(jnp.float32)

        self.each(self.total, first)
        for up, slot, inner in ((True, self.plane, self.plane >= 1), (False, 4, self.plane <= 2)):

            @pl.when(inner)
            def _(up=up, slot=slot):
                self.copy(up, self.plane, slot).wait_recv()
                self.add(self.total, self.arrive.at[slot])

    def close(self):
        for t in range(3):
            for up, p, slot, sends, inner in self.moves(t):

                @pl.when(sends)
                def _(up=up, p=p, slot=slot):
                    self.copy(up, p, slot).wait_send()


def chain_scratch(columns, shape, width):
    low = jnp.bfloat16
    if columns:
        n, rows = shape
        return [
            pltpu.VMEM((n, 4, 4, rows, width), low),
            pltpu.VMEM((5, n, 4, rows, width), low),
            pltpu.VMEM((n, 4, rows, width), jnp.float32),
            pltpu.SemaphoreType.DMA((16,)),
        ]
    return [
        pltpu.VMEM((4, shape, width), low),
        pltpu.VMEM((5, shape, width), low),
        pltpu.VMEM((shape, width), jnp.float32),
        pltpu.SemaphoreType.DMA((16,)),
    ]


class Columns:
    def __init__(self, net, total, stage, wide, out):
        self.net, self.total, self.stage, self.wide, self.out = net, total, stage, wide, out

    def start(self):
        net = self.net
        chip = net.me // 2
        n, _, rows, width = self.total.shape
        parts = self.wide.shape[0]
        width = width // parts
        at = pl.ds(pl.multiple_of(chip * width, width), width)

        def cast(i, _):
            self.stage[i // 4, i % 4] = self.total[i // 4, i % 4].astype(jnp.bfloat16)
            return 0

        lax.fori_loop(0, n * 4, cast, 0)
        self.copies = [
            net.send(
                self.stage.at[0, net.peer(m) // 2, :, pl.ds(i * width, width)],
                self.wide.at[i, :, at],
                m,
            )
            for m in (2, 4, 6)
            for i in range(parts)
        ]
        for i in range(parts):
            self.wide[i, :, at] = self.stage[0, chip, :, i * width : i * width + width]

    def finish(self):
        for c in self.copies:
            c.wait_recv()
        for i in range(self.out.shape[0]):
            self.out[i] = self.wide[i].astype(jnp.float32)


def meet_all(net):
    plane = lax.axis_index("bucket")
    chip = net.me // 2
    sem = pltpu.get_barrier_semaphore()
    for mask in ALL_PEERS:
        pl.semaphore_signal(
            sem, inc=1, device_id={"fsdp": net.peer(mask)}, device_id_type=MESH_IDS
        )
    for inner, step in ((plane >= 1, -1), (plane <= 2, 1)):

        @pl.when(inner)
        def _(step=step):
            pl.semaphore_signal(
                sem, inc=1, device_id={"bucket": plane + step}, device_id_type=MESH_IDS
            )

    @pl.when(chip != plane)
    def _():
        pl.semaphore_signal(
            sem,
            inc=1,
            device_id={"bucket": chip, "fsdp": plane * 2 + net.me % 2},
            device_id_type=MESH_IDS,
        )

    one = jnp.int32(1)
    zero = jnp.int32(0)
    count = (
        7
        + jnp.where(plane >= 1, one, zero)
        + jnp.where(plane <= 2, one, zero)
        + jnp.where(chip != plane, one, zero)
    )
    pl.semaphore_wait(sem, count)


def transposed(net, src, dst, sems):
    plane = lax.axis_index("bucket")
    return pltpu.make_async_remote_copy(
        src_ref=src,
        dst_ref=dst,
        send_sem=sems.at[0],
        recv_sem=sems.at[1],
        device_id={"bucket": net.me // 2, "fsdp": plane * 2 + net.me % 2},
        device_id_type=MESH_IDS,
    )


def close_kernel(
    text_g, attn_g, out_g,
    text_o, attn_o, out_o,
    tm, ta, tt, ts, am, aa, at_, as_, om, oa, ot, os_,
    t_wide, a_wide, t_stage, a_stage, o_stage, o_got, o_sem, send_sems, recv_sems,
):
    net = Net(send_sems, recv_sems)
    meet_all(net)
    plane = lax.axis_index("bucket")
    chip = net.me // 2
    out = Chain(net, out_g, om, oa, ot, os_, False)
    attn = Chain(net, attn_g, am, aa, at_, as_, True)
    text = Chain(net, text_g, tm, ta, tt, ts, True)
    chains = [out, attn, text]
    for c in chains:
        c.core_start()
    for c in chains:
        c.core_finish()
        c.step(0)
    for t in (1, 2):
        for c in chains:
            c.step(t)
    out.finish()
    o_stage[...] = ot[...].astype(jnp.bfloat16)

    @pl.when(chip != plane)
    def _():
        transposed(net, o_stage, o_got, o_sem).start()

    attn.finish()
    attn_cols = Columns(net, at_, a_stage, a_wide, attn_o)
    attn_cols.start()

    @pl.when(chip != plane)
    def _():
        transposed(net, o_stage, o_got, o_sem).wait()
        out_o[...] = o_got[...].astype(jnp.float32)

    @pl.when(chip == plane)
    def _():
        out_o[...] = ot[...]

    attn_cols.finish()
    text.finish()
    text_cols = Columns(net, tt, t_stage, t_wide, text_o)
    text_cols.start()
    text_cols.finish()
    for c in chains:
        c.close()
    net.close()


def close_layer(text_g, attn_g, out_g):
    low = jnp.bfloat16
    full = jnp.float32
    shape = jax.ShapeDtypeStruct
    V = VMEM_SPEC
    tr, tw = text_g.shape[-2], text_g.shape[-1] // 2
    ar, aw = attn_g.shape[-2], attn_g.shape[-1] // 3
    orow, ow = out_g.shape[-2:]
    return pl.pallas_call(
        close_kernel,
        in_specs=[V] * 3,
        out_specs=[V] * 3,
        out_shape=[
            shape((2, tr, 4 * tw), full),
            shape((3, ar, 4 * aw), full),
            shape((orow, ow), full),
        ],
        scratch_shapes=[
            *chain_scratch(True, (1, tr), 2 * tw),
            *chain_scratch(True, (1, ar), 3 * aw),
            *chain_scratch(False, orow, ow),
            pltpu.VMEM((2, tr, 4 * tw), low),
            pltpu.VMEM((3, ar, 4 * aw), low),
            pltpu.VMEM((1, 4, tr, 2 * tw), low),
            pltpu.VMEM((1, 4, ar, 3 * aw), low),
            pltpu.VMEM((orow, ow), low),
            pltpu.VMEM((orow, ow), low),
            pltpu.SemaphoreType.DMA((2,)),
            *net_scratch(32),
        ],
        compiler_params=pltpu.CompilerParams(
            collective_id=2, has_side_effects=True, vmem_limit_bytes=63 * 1024 * 1024
        ),
        cost_estimate=pl.CostEstimate(
            flops=1_000_000, bytes_accessed=400_000_000, transcendentals=0
        ),
    )(text_g, attn_g, out_g)


def column_of(v):
    return jnp.transpose(v)[:, 0:1]


def back_kernel(
    dh2_ref, fo_ref, x1_ref, branch_ref, cot_ref, w_ref, mod_ref, seg_ref, gain_ref, tok_ref,
    sr_ref, gs_ref, *rest,
):
    late, rest = rest[:LATE], rest[LATE:]
    places, rest = rest[-LATE - 1 : -1], rest[: -LATE - 1] + rest[-1:]
    loads = [
        pltpu.make_async_copy(src, dst, rest[-1].at[i])
        for i, (src, dst) in enumerate(zip(late, places))
    ]
    back_body(
        dh2_ref, fo_ref, x1_ref, branch_ref, cot_ref, w_ref, mod_ref, seg_ref, gain_ref, tok_ref,
        *places, sr_ref, gs_ref, *rest[:-1], loads,
    )


LATE = 17


def back_body(
    dh2_ref, fo_ref, x1_ref, branch_ref, cot_ref, w_ref, mod_ref, seg_ref, gain_ref, tok_ref,
    ow_ref, aw_ref, qr_ref, kr_ref, v_ref, tr_ref, tv_ref, cross_ref, q_ref, k_ref, tk_ref,
    iq_ref, ik_ref, it_ref, cos_ref, sin_ref, sc_ref, sr_ref, gs_ref, ffn_g, down_g,
    block_o, token_o, db_ref, dqkv_o, dtkv_o, dmod_o, gg_o, gs_o, ffn_o, down_o,
    dx_s, dc_s, dqf, dkf, dtf, part_s, sums, tsums, buf_a, far_a, buf_b, far_b, buf_c, far_c,
    fm, fa, ft, fs, dm, da, dt_c, ds_, f_wide, f_stage, d_stage, d_got, d_sem,
    f_keep, d_keep, keep_sem, send_sems, recv_sems, loads,
):
    low = jnp.bfloat16
    full = jnp.float32
    net = Net(send_sems, recv_sems)
    meet_all(net)
    plane = lax.axis_index("bucket")
    chip = net.me // 2
    ffn = Chain(net, ffn_g, fm, fa, ft, fs, True)
    down = Chain(net, down_g, dm, da, dt_c, ds_, False)
    ffn.core_start(f_keep, keep_sem.at[0])
    down.core_start(d_keep, keep_sem.at[1])
    for c in loads:
        c.start()

    def rows_of(ref):
        half = ROW // 2
        return lambda j, i: ref[pl.ds(j * ROW + i * half, half), :].astype(full)

    middle, finish = collect4(net, rows_of(dh2_ref), buf_a, far_a)
    middle()
    ffn.core_finish()
    ffn.step(0)
    down.core_finish()
    down.step(0)
    half = ROW // 2
    for i in (0, 1):
        dx_s[pl.ds(i * half, half), :] = finish(i)
    part_s[pl.ds(0, ROW), :] = dx_s[...]
    block = 32
    weight = w_ref[0:1, 0:1]

    def second_norm(at):
        x1 = x1_ref[at, :]
        inverse = lax.rsqrt(jnp.mean(x1 * x1, axis=-1, keepdims=True) + EPS)
        scale = pick_rows(mod_ref[:, :D], seg_ref[at, :], 4)
        return x1 * inverse, inverse, scale

    def to_branch(b, _):
        at = pl.ds(pl.multiple_of(b * block, block), block)
        normed, inverse, scale = second_norm(at)
        dn = dx_s[at, :] * gain_ref[1:2, :] * (1.0 + scale)
        back = inverse * (dn - normed * jnp.mean(dn * normed, axis=-1, keepdims=True))
        dx = cot_ref[at, :].astype(full) * weight + back
        dx_s[at, :] = dx
        gate = jnp.tanh(pick_rows(mod_ref[:, D:], seg_ref[at, :], 0))
        db_ref[0, at, :] = (dx * gate).astype(low)
        return 0

    lax.fori_loop(0, ROW // block, to_branch, 0)
    bx, by = share4_start(net, db_ref)

    def by_image(value, seg, row, lo):
        for i in range(IMGS):
            dmod_o[row + i : row + i + 1, lo : lo + D] += jnp.sum(
                jnp.where(seg == i, value, 0.0), axis=0, keepdims=True
            )

    dmod_o[...] = jnp.zeros(dmod_o.shape, full)
    gg_o[...] = jnp.zeros(gg_o.shape, full)

    def second_sums(b, _):
        at = pl.ds(pl.multiple_of(b * block, block), block)
        normed, inverse, scale = second_norm(at)
        seg = seg_ref[at, :]
        dh = part_s[at, :] * normed
        gg_o[1:2, :] += jnp.sum(dh * (1.0 + scale), axis=0, keepdims=True)
        by_image(dh * gain_ref[1:2, :], seg, 4, 0)
        gate = jnp.tanh(pick_rows(mod_ref[:, D:], seg, 0))
        by_image(dx_s[at, :] * branch_ref[at, :] * (1.0 - gate * gate), seg, 0, D)
        return 0

    lax.fori_loop(0, ROW // block, second_sums, 0)
    far = share4_relay(net, db_ref, bx, by)
    middle_b, finish_b = collect4(net, rows_of(fo_ref), buf_b, far_b)
    gs_o[...] = jnp.zeros(gs_o.shape, full)
    for c in loads:
        c.wait()
    cap = IMGS * TXT

    def attention_row(j, _):
        @pl.when(j == 3)
        def _():
            for c in far:
                c.wait_recv()

        @pl.when(j == 1)
        def _():
            ffn.step(1)
            down.step(1)

        @pl.when(j == 3)
        def _():
            ffn.step(2)
            down.step(2)

        rows = pl.ds(pl.multiple_of(j * ROW, ROW), ROW)
        text = pl.ds(pl.multiple_of(j * cap, cap), cap)
        dc_s[...] = dot_t(db_ref[j], ow_ref[...])
        dqv, dkv, dtv = dqf.at[rows], dkf.at[rows], dtf.at[text]
        attend_back_kernel(
            qr_ref.at[rows], kr_ref.at[rows], v_ref.at[rows], tr_ref.at[text], tv_ref.at[text],
            dc_s, cross_ref.at[rows], q_ref.at[rows], k_ref.at[rows], tk_ref.at[text],
            iq_ref.at[rows], ik_ref.at[rows], it_ref.at[text], cos_ref.at[rows], sin_ref.at[rows],
            sc_ref.at[rows], sr_ref.at[j], gs_ref,
            dqv, dkv, dqkv_o.at[rows, pl.ds(2 * HW, HW)], dtv, dtkv_o.at[text, pl.ds(HW, HW)], gs_o,
        )
        sums[0, :, rows] = row_sums(
            dqv[...] * (q_ref[rows, :] * iq_ref[rows, :]),
            dkv[...] * (k_ref[rows, :] * ik_ref[rows, :]),
        )
        tsums[0, :, text] = row_sums(dtv[...] * (tk_ref[text, :] * it_ref[text, :]), None)
        return 0

    lax.fori_loop(0, CHIPS, attention_row, 0)
    sum_io = []
    for i, m in ((1, 2), (2, 4), (3, 6)):
        sum_io.append(net.send(sums.at[0], sums.at[i], m))
        sum_io.append(net.send(tsums.at[0], tsums.at[i], m))
    middle_b()
    for i in (0, 1):
        part_s[pl.ds(i * half, half), :] = finish_b(i)

    def block_rows(b, _):
        at = pl.ds(pl.multiple_of(b * block, block), block)
        seg = seg_ref[at, :]
        gate = jnp.tanh(pick_rows(mod_ref[:, D:], seg, 4))
        out = part_s[at, :]
        block_o[at, :] = (x1_ref[at, :] + gate * out).astype(low)
        grad = cot_ref[at, :].astype(full) * weight
        by_image(grad * out * (1.0 - gate * gate), seg, 4, D)
        return 0

    for c in sum_io:
        c.wait_recv()
    for j in range(CHIPS):
        rows = pl.ds(j * ROW, ROW)
        text = pl.ds(j * cap, cap)
        total = sums[0, :, rows]
        words = tsums[0, :, text]
        for i in (1, 2, 3):
            total = total + sums[i, :, pl.ds((j ^ i) * ROW, ROW)]
            words = words + tsums[i, :, pl.ds((j ^ i) * cap, cap)]
        mean = jnp.transpose(total / D)
        iq, ik, it = iq_ref[rows, :], ik_ref[rows, :], it_ref[text, :]
        dqkv_o[rows, :HW] = (iq * (dqf[rows, :] - q_ref[rows, :] * iq * mean[:, 0:1])).astype(low)
        dqkv_o[rows, HW : 2 * HW] = (ik * (dkf[rows, :] - k_ref[rows, :] * ik * mean[:, 4:5])).astype(low)
        mean = jnp.transpose(words / D)
        dtkv_o[text, :HW] = (it * (dtf[text, :] - tk_ref[text, :] * it * mean[:, 0:1])).astype(low)

    lax.fori_loop(0, ROW // block, block_rows, 0)
    wide = 256

    def first_grad(n, _):
        at = pl.ds(pl.multiple_of(n * wide, wide), wide)
        part_s[:, at] = dot_t(dqkv_o[...], aw_ref[at, :])
        return 0

    lax.fori_loop(0, D // wide, first_grad, 0)
    middle_c, finish_c = collect4(net, rows_of(part_s), buf_c, far_c)
    ffn.finish()
    f_cols = Columns(net, ft, f_stage, f_wide, ffn_o)
    middle_c()
    f_cols.start()
    down.finish()
    d_stage[...] = dt_c[...].astype(low)

    @pl.when(chip != plane)
    def _():
        transposed(net, d_stage, d_got, d_sem).start()

    for i in (0, 1):
        part_s[pl.ds(i * half, half), :] = finish_c(i)

    def first_rows(b, _):
        at = pl.ds(pl.multiple_of(b * block, block), block)
        x = tok_ref[at, :].astype(full)
        inverse = lax.rsqrt(jnp.mean(x * x, axis=-1, keepdims=True) + EPS)
        normed = x * inverse
        seg = seg_ref[at, :]
        scale = pick_rows(mod_ref[:, :D], seg, 0)
        dh = part_s[at, :]
        gg_o[0:1, :] += jnp.sum(dh * normed * (1.0 + scale), axis=0, keepdims=True)
        by_image(dh * normed * gain_ref[0:1, :], seg, 0, 0)
        dn = dh * gain_ref[0:1, :] * (1.0 + scale)
        token_o[at, :] = dx_s[at, :] + inverse * (
            dn - normed * jnp.mean(dn * normed, axis=-1, keepdims=True)
        )
        return 0

    lax.fori_loop(0, ROW // block, first_rows, 0)
    f_cols.finish()

    @pl.when(chip != plane)
    def _():
        transposed(net, d_stage, d_got, d_sem).wait()
        down_o[...] = d_got[...].astype(full)

    @pl.when(chip == plane)
    def _():
        down_o[...] = dt_c[...]

    ffn.close()
    down.close()
    net.close()


def back_layer(early, late, ffn_g, down_g):
    low = jnp.bfloat16
    full = jnp.float32
    shape = jax.ShapeDtypeStruct
    V = VMEM_SPEC
    cap = IMGS * TXT
    fr, fw = ffn_g.shape[-2], ffn_g.shape[-1] // 2
    dr, dw = down_g.shape[-2:]
    tok = CHIPS * ROW
    reduce_scratch = [pltpu.VMEM((5, ROW, D), low), pltpu.VMEM((2, ROW // 2, D), low)]
    return pl.pallas_call(
        back_kernel,
        in_specs=[V] * len(early) + [ANY_SPEC] * (LATE + 2),
        out_specs=[V] * 10,
        out_shape=[
            shape((ROW, D), low),
            shape((ROW, D), full),
            shape((CHIPS, ROW, D), low),
            shape((tok, 3 * HW), low),
            shape((CHIPS * cap, 2 * HW), low),
            shape((8, 2 * D), full),
            shape((8, D), full),
            shape((8, HW), full),
            shape((2, fr, 4 * fw), full),
            shape((dr, dw), full),
        ],
        scratch_shapes=[
            pltpu.VMEM((ROW, D), full),
            pltpu.VMEM((ROW, HW), full),
            pltpu.VMEM((tok, HW), full),
            pltpu.VMEM((tok, HW), full),
            pltpu.VMEM((CHIPS * cap, HW), full),
            pltpu.VMEM((tok, D), full),
            pltpu.VMEM((CHIPS, 8, tok), full),
            pltpu.VMEM((CHIPS, 8, CHIPS * cap), full),
            *reduce_scratch, *reduce_scratch, *reduce_scratch,
            *chain_scratch(True, (1, fr), 2 * fw),
            *chain_scratch(False, dr, dw),
            pltpu.VMEM((2, fr, 4 * fw), low),
            pltpu.VMEM((1, 4, fr, 2 * fw), low),
            pltpu.VMEM((dr, dw), low),
            pltpu.VMEM((dr, dw), low),
            pltpu.SemaphoreType.DMA((2,)),
            pltpu.VMEM((1, 4, 4, fr, 2 * fw), low),
            pltpu.VMEM((4, dr, dw), low),
            pltpu.SemaphoreType.DMA((2,)),
            *net_scratch(48),
            *[pltpu.VMEM(v.shape, v.dtype) for v in late],
            pltpu.SemaphoreType.DMA((LATE,)),
        ],
        compiler_params=pltpu.CompilerParams(
            collective_id=3, has_side_effects=True, vmem_limit_bytes=63 * 1024 * 1024
        ),
        cost_estimate=pl.CostEstimate(
            flops=10_000_000_000, bytes_accessed=400_000_000, transcendentals=0
        ),
    )(*early, *late, ffn_g, down_g)


def row_spec(rows, width):
    return pl.BlockSpec((rows, width), lambda i: (i, 0))


def forward_kernel(
    q_ref, k_ref, v_ref, iq_ref, ik_ref, cos_ref, sin_ref, tk_ref, it_ref, tv_ref, sc_ref, sr_ref,
    gs_ref, mod_ref, seg_ref, gain_ref, tok_ref, cot_ref, w_ref, outw_ref, ffnw_ref, downw_ref,
    comb_o, cross_o, qr_o, kr_o, tr_o, branch_o, x1_o, h_o, df_o, ow_o, fw_o, dw_o,
    part_s, buf, far, f_own, d_own, local_sems, send_sems, recv_sems,
):
    low = jnp.bfloat16
    full = jnp.float32
    net = Net(send_sems, recv_sems)
    net.meet((1, 2, 4, 6))
    me = net.me
    chip = me // 2
    width = fw_o.shape[1] // 2
    rows = outw_ref.shape[0]

    def local(src, dst, i):
        copy = pltpu.make_async_copy(src, dst, local_sems.at[i])
        copy.start()
        return copy

    def own(ref, count):
        return ref.at[pl.ds(pl.multiple_of((me % 2) * count, count), count), :]

    out_here = local(outw_ref, own(ow_o, rows), 0)
    out_core = net.send(outw_ref, own(ow_o, rows), 1)
    down_rows = downw_ref.shape[0]
    down_here = local(downw_ref, d_own, 1)
    down_core = net.send(downw_ref, own(dw_o, down_rows), 1)
    f_rows = ffnw_ref.shape[1]
    place = [2]

    def stage(src, dst):
        i = place[0]
        place[0] += 1
        return local(src, f_own.at[:, pl.ds((i - 2) * width, width)], i)

    f_here, f_core, f_away, f_pass = spread(net, ffnw_ref, fw_o, width, stage)
    f_x, f_y = f_away(2), f_away(4)
    block = 32
    weight = w_ref[0:1, 0:1]

    def ffn_grad(b, _):
        at = pl.ds(pl.multiple_of(b * block, block), block)
        gate = jnp.tanh(pick_rows(mod_ref[:, D:], seg_ref[at, :], 4))
        df_o[0, at, :] = (cot_ref[at, :].astype(full) * weight * gate).astype(low)
        return 0

    lax.fori_loop(0, ROW // block, ffn_grad, 0)
    out_here.wait()
    out_core.wait_recv()
    cap = IMGS * TXT

    def attention_row(i, _):
        j = 3 - i
        at = pl.ds(pl.multiple_of(j * ROW, ROW), ROW)
        text = pl.ds(pl.multiple_of(j * cap, cap), cap)
        attend_kernel(
            q_ref.at[at], k_ref.at[at], v_ref.at[at], iq_ref.at[at], ik_ref.at[at],
            cos_ref.at[at], sin_ref.at[at], tk_ref.at[text], it_ref.at[text], tv_ref.at[text],
            sc_ref.at[at], sr_ref.at[j], gs_ref,
            comb_o.at[at], cross_o.at[at], qr_o.at[at], kr_o.at[at], tr_o.at[text],
        )
        part_s[at, :] = jnp.dot(comb_o[at, :], ow_o[...], preferred_element_type=full)
        return 0

    lax.fori_loop(0, CHIPS, attention_row, 0)
    half = ROW // 2
    middle, finish = collect4(
        net, lambda j, i: part_s[pl.ds(j * ROW + i * half, half), :], buf, far
    )
    f_far = f_away(6)
    dx, dy = share4_start(net, df_o)

    down_here.wait()
    down_out = local(d_own, own(dw_o, down_rows), 4)
    for c in f_here:
        c.wait()
    f_out = local(f_own, fw_o.at[pl.ds(pl.multiple_of(me * f_rows, f_rows), f_rows), :], 5)
    middle()
    for i in (0, 1):
        branch_o[pl.ds(i * half, half), :] = finish(i)

    def second(b, _):
        at = pl.ds(pl.multiple_of(b * block, block), block)
        seg = seg_ref[at, :]
        gate = jnp.tanh(pick_rows(mod_ref[:, D:], seg, 0))
        x1 = tok_ref[at, :].astype(full) + gate * branch_o[at, :]
        x1_o[at, :] = x1
        normed = x1 * lax.rsqrt(jnp.mean(x1 * x1, axis=-1, keepdims=True) + EPS)
        scale = pick_rows(mod_ref[:, :D], seg, 4)
        h_o[0, at, :] = (normed * gain_ref[1:2, :] * (1.0 + scale)).astype(low)
        return 0

    lax.fori_loop(0, ROW // block, second, 0)
    hx, hy = share4_start(net, h_o)
    last = [f_pass(f_x, 2), f_pass(f_y, 4)]
    last += share4_relay(net, df_o, dx, dy)
    last += share4_relay(net, h_o, hx, hy)
    last.append(f_pass(f_far, 6))
    for c in last + [down_core] + f_core:
        c.wait_recv()
    down_out.wait()
    f_out.wait()
    net.close()


def forward_layer(*args):
    low = jnp.bfloat16
    full = jnp.float32
    shape = jax.ShapeDtypeStruct
    V = VMEM_SPEC
    cap = IMGS * TXT
    tok = CHIPS * ROW
    out_w, ffn_w, down_w = args[-3:]
    width = ffn_w.shape[2] // CHIPS
    return pl.pallas_call(
        forward_kernel,
        in_specs=[V] * (len(args) - 3) + [ANY_SPEC] * 3,
        out_specs=[V] * 10 + [ANY_SPEC] * 2,
        out_shape=[
            shape((tok, HW), low),
            shape((tok, HW), full),
            shape((tok, HW), low),
            shape((tok, HW), low),
            shape((CHIPS * cap, HW), low),
            shape((ROW, D), full),
            shape((ROW, D), full),
            shape((CHIPS, ROW, D), low),
            shape((CHIPS, ROW, D), low),
            shape((2 * out_w.shape[0], D), low),
            shape((D, 2 * width), low),
            shape((2 * down_w.shape[0], D), low),
        ],
        scratch_shapes=[
            pltpu.VMEM((tok, D), full),
            pltpu.VMEM((5, ROW, D), low),
            pltpu.VMEM((2, ROW // 2, D), low),
            pltpu.VMEM((ffn_w.shape[1], 2 * width), low),
            pltpu.VMEM(down_w.shape, low),
            pltpu.SemaphoreType.DMA((6,)),
            *net_scratch(40),
        ],
        compiler_params=pltpu.CompilerParams(
            collective_id=4, has_side_effects=True, vmem_limit_bytes=56 * 1024 * 1024
        ),
        cost_estimate=pl.CostEstimate(
            flops=5_000_000_000, bytes_accessed=200_000_000, transcendentals=0
        ),
    )(*args)


def per_device(
    tokens,
    cond,
    text,
    segments,
    positions,
    counts,
    ada_weight,
    ada_bias,
    gains,
    attn_weight,
    out_weight,
    text_weight,
    ffn_weight,
    down_weight,
    cotangent,
):
    low = jnp.bfloat16
    full = jnp.float32
    plane = lax.axis_index("bucket")
    slot = lax.axis_index("fsdp")
    core = slot % 2
    chip = slot // 2
    ff = ffn_weight.shape[2] // CHIPS

    gain_pad = lax.dynamic_update_slice_in_dim(
        jnp.zeros((8, D), full), jnp.pad(gains.astype(full), ((0, 2), (0, 0))), slot * 192, axis=1
    )
    bias = lax.dynamic_update_slice_in_dim(
        jnp.zeros((ada_weight.shape[1],), full), ada_bias.astype(full), slot * ada_bias.shape[0], 0
    )
    bias_pad = jnp.repeat(bias.reshape(2, 3072), 4, axis=0)
    seg = segments[0]
    idx = jnp.concatenate([seg[None, :], positions[0], jnp.zeros((5, ROW), jnp.int32)], axis=0)
    (
        mod, gain_f, h_rows, idx_all, attn_w, text_rows, query, keyed, valued, text_keys, text_vals,
        inv_qk, inv_t,
    ) = open_layer(
        jnp.concatenate([cond[0], cond[0]], axis=0), gain_pad, bias_pad, ada_weight, tokens[0],
        seg[:, None], idx, attn_weight, text_weight, text[0],
    )
    cond_act = silu(cond[0].astype(full)).astype(low)
    h_all = h_rows.reshape(CHIPS * ROW, D)
    text_all = text_rows.reshape(CHIPS * IMGS * TXT, -1)
    inv_qk = jnp.stack([inv_qk[0], inv_qk[4]])[:, :, None]
    inv_t = inv_t[0][:, None]
    seg_all = idx_all[:, 0]
    pos_all = idx_all[:, 1:3]
    seg_col = seg_all.reshape(CHIPS * ROW, 1)
    seg_row = seg_all.reshape(CHIPS, 1, ROW)
    lane = jnp.arange(128, dtype=jnp.int32)
    quarter = HDIM // 4
    freq = (10000.0 ** (-jnp.arange(quarter, dtype=full) / quarter))[lane % quarter]
    where_row = ((lane // 32) % 2 == 0)[None, None, :]
    pos_lane = jnp.where(where_row, pos_all[:, 0, :, None], pos_all[:, 1, :, None]).astype(full)
    angle = (pos_lane * freq[None, None, :]).reshape(CHIPS * ROW, 128)
    cosine = jnp.cos(angle)
    sine = jnp.where(((lane // quarter) % 2 == 0)[None, :], -1.0, 1.0) * jnp.sin(angle)

    gain_s = lax.dynamic_slice_in_dim(gain_f, chip * HW, HW, axis=1)[:6]

    totals = counts.astype(full)
    here = jnp.sum(jnp.where(jnp.arange(totals.shape[0], dtype=jnp.int32) == plane, totals, 0.0))
    weight = lax.axis_size("bucket") * here / jnp.sum(totals)
    weight_row = jnp.full((1, 128), weight, full)
    (
        comb, cross_out, q_rot, k_rot, text_rot, branch, x_one, h_two_rows, d_ffn_rows, out_w, ffn_w,
        down_w,
    ) = forward_layer(
        query, keyed, valued, inv_qk[0], inv_qk[1], cosine, sine, text_keys, inv_t, text_vals,
        seg_col, seg_row, gain_s, mod, seg[:, None], gain_f, tokens[0], cotangent[0], weight_row,
        out_weight, ffn_weight, down_weight,
    )
    h_two_all = h_two_rows.reshape(CHIPS * ROW, D)
    d_ffn_all = d_ffn_rows.reshape(CHIPS * ROW, D)
    both = mult(h_two_all, ffn_w)
    gate_pre = both[:, :ff]
    upper = both[:, ff:]
    d_hidden = dot_t(d_ffn_all, down_w)
    sigm = jax.nn.sigmoid(gate_pre)
    silu_pre = gate_pre * sigm
    hidden = (silu_pre * upper).astype(low)
    d_pre = (d_hidden * upper * sigm * (1.0 + gate_pre * (1.0 - sigm))).astype(low)
    d_up = (d_hidden * silu_pre).astype(low)
    d_both = jnp.concatenate([d_pre, d_up], axis=1)
    d_h_two = dot_t(d_both, ffn_w).astype(low)
    ffn_out = mult(hidden, down_w).astype(low)
    g_down = t_dot(hidden, d_ffn_all).astype(low)
    g_ffn = t_dot(h_two_all, d_both).astype(low)

    (
        block_out, token_grad, d_branch_rows, d_qkv, d_text, d_mod, gg_full, gg_slice, s_ffn, s_down,
    ) = back_layer(
        [
            d_h_two, ffn_out, x_one, branch, cotangent[0], weight_row, mod,
            seg[:, None], gain_f, tokens[0], seg_row, gain_s,
        ],
        [
            out_w, attn_w, q_rot, k_rot, valued, text_rot, text_vals, cross_out, query, keyed,
            text_keys, inv_qk[0], inv_qk[1], inv_t, cosine, sine, seg_col,
        ],
        g_ffn.reshape(1, 4, 4, 2, 48, 2 * ff),
        g_down.reshape(4, 2, 128, D),
    )
    d_branch_all = d_branch_rows.reshape(CHIPS * ROW, D)
    g_text = t_dot(text_all, d_text).astype(low)
    g_attn = t_dot(h_all, d_qkv).astype(low)
    g_out = t_dot(comb, d_branch_all).astype(low)
    s_text, s_attn, s_out = close_layer(
        g_text.reshape(1, 4, 4, 2, 128, 2 * HW),
        g_attn.reshape(1, 4, 4, 2, 48, 3 * HW),
        g_out.reshape(4, 2, 48, D),
    )

    d_mod = jnp.concatenate([d_mod[:IMGS], d_mod[IMGS:]], axis=1)

    gg = gg_slice[:4]
    cross_gate = jnp.tanh(gain_s[5])
    gg = gg.at[3].multiply(1.0 - cross_gate * cross_gate)
    spread = lax.dynamic_update_slice_in_dim(jnp.zeros((4, D), full), gg, chip * HW, axis=1)
    small = jnp.concatenate(
        [gg_full[:2], spread, jnp.sum(d_mod, axis=0).reshape(4, D)], axis=0
    )
    small = small + at_core(small)
    small = sum4(small)
    small = small + lax.ppermute(small, "bucket", [(i, i ^ 1) for i in range(4)])
    small = small + lax.ppermute(small, "bucket", [(i, i ^ 2) for i in range(4)])
    rank = plane * 8 + slot
    s_gains = lax.dynamic_slice_in_dim(small[:6], rank * 48, 48, axis=1)
    s_ada_b = lax.dynamic_slice_in_dim(small[6:].reshape(-1), rank * 192, 192, axis=0)

    mod_low = d_mod.astype(low)
    mods = jnp.concatenate(gather4(mod_low), axis=0)
    planes_m = [mods]
    for shift in (1, 2, 3):
        planes_m.append(
            lax.ppermute(mods, "bucket", [(i, i ^ shift) for i in range(4)])
        )
    mods = jnp.concatenate(planes_m, axis=0)
    mods = jnp.concatenate([mods, at_core(mods)], axis=0)
    conds_all = jnp.concatenate(gather4(cond_act), axis=0)
    planes_c = [conds_all]
    for shift in (1, 2, 3):
        planes_c.append(
            lax.ppermute(conds_all, "bucket", [(i, i ^ shift) for i in range(4)])
        )
    conds_all = jnp.concatenate(planes_c, axis=0)
    conds_all = jnp.concatenate([conds_all, at_core(conds_all)], axis=0)
    s_ada_w = t_dot(lax.dynamic_slice_in_dim(conds_all, rank * 32, 32, axis=1), mods)

    return (
        block_out[None],
        token_grad[None],
        s_ada_w,
        s_ada_b,
        s_gains,
        s_attn,
        s_out,
        s_text,
        s_ffn,
        s_down,
    )


def solution(mesh):
    in_specs = (
        P(("bucket", "fsdp"), None, None),
        P(("bucket", "fsdp"), None, None),
        P(("bucket", "fsdp"), None, None),
        P(("bucket", "fsdp"), None),
        P(("bucket", "fsdp"), None, None),
        P(),
        P("fsdp", None),
        P("fsdp"),
        P(None, "fsdp"),
        P(None, "fsdp", None),
        P("fsdp", None),
        P(None, "fsdp", None),
        P(None, "fsdp", None),
        P("fsdp", None),
        P(("bucket", "fsdp"), None, None),
    )
    out_specs = (
        P(("bucket", "fsdp"), None, None),
        P(("bucket", "fsdp"), None, None),
        P(("bucket", "fsdp"), None),
        P(("bucket", "fsdp")),
        P(None, ("bucket", "fsdp")),
        P(None, ("bucket", "fsdp"), None),
        P(("bucket", "fsdp"), None),
        P(None, ("bucket", "fsdp"), None),
        P(None, ("bucket", "fsdp"), None),
        P(("bucket", "fsdp"), None),
    )
    fast = mesh.shape["fsdp"] == 8 and mesh.shape["bucket"] == 4
    return jax.shard_map(
        per_device if fast else per_device_general, mesh=mesh, in_specs=in_specs, out_specs=out_specs, check_vma=False
    )
```

```python
import jax
import jax.numpy as jnp
from jax import lax
from jax.experimental import pallas as pl
from jax.experimental.pallas import tpu as pltpu
from jax.sharding import PartitionSpec as P

D = 1536
HEADS = 24
HDIM = 64
IMGS = 4
TXT = 64


EPS = 1e-06
NEGATIVE = -1e30
HIGH = lax.Precision.HIGHEST


def silu(v):
    return v * jax.nn.sigmoid(v)


def norm_rows(v):
    inverse = lax.rsqrt(jnp.mean(v * v, axis=-1, keepdims=True) + EPS)
    return (v * inverse, inverse)


def norm_back(grad, normed, inverse):
    return inverse * (grad - normed * jnp.mean(grad * normed, axis=-1, keepdims=True))


def rotary_tables(pos):
    quarter = HDIM // 4
    freq = 10000.0 ** (-jnp.arange(quarter, dtype=jnp.float32) / quarter)
    angle = jnp.transpose(pos.astype(jnp.float32), (1, 0))[:, :, None] * freq[None, None, :]
    return (jnp.cos(angle), jnp.sin(angle))


def rotate(v, cosine, sine):
    rows = v.shape[0]
    parts = v.reshape(rows, HEADS, 2, 2, HDIM // 4)
    first = parts[:, :, :, 0]
    second = parts[:, :, :, 1]
    cosine = cosine[:, None]
    sine = sine[:, None]
    turned = jnp.stack([first * cosine - second * sine, first * sine + second * cosine], axis=3)
    return turned.reshape(rows, HEADS * HDIM)


def to_pairs(v):
    return jnp.transpose(v.reshape(v.shape[0], HEADS // 2, 2 * HDIM), (1, 0, 2))


def from_pairs(v):
    return jnp.transpose(v, (1, 0, 2)).reshape(v.shape[1], HEADS * HDIM)


def pair_scores(query, keys):
    q_heads = query.reshape(query.shape[0], 2, HDIM)
    k_heads = keys.reshape(keys.shape[0], 2, HDIM)
    return jnp.einsum(
        "rhd,khd->hrk", q_heads, k_heads, preferred_element_type=jnp.float32
    ) * HDIM ** (-0.5)


def attend_forward(q_b, k_b, v_b, allowed):

    def one_pair(item):
        query, keys, values = item
        scores = jnp.where(allowed[None], pair_scores(query, keys), NEGATIVE)
        top = jnp.max(scores, axis=-1, keepdims=True)
        expo = jnp.exp(scores - top)
        total = jnp.sum(expo, axis=-1, keepdims=True)
        probs = (expo / total).astype(jnp.bfloat16)
        result = jnp.einsum(
            "hrk,khd->rhd",
            probs,
            values.reshape(values.shape[0], 2, HDIM),
            preferred_element_type=jnp.float32,
        )
        return (result.reshape(query.shape[0], 2 * HDIM), (top + jnp.log(total))[..., 0])

    outputs, saved = lax.map(one_pair, (to_pairs(q_b), to_pairs(k_b), to_pairs(v_b)))
    return (from_pairs(outputs), saved)


def attend_back(q_b, k_b, v_b, saved, grad_b, allowed):

    def one_pair(item):
        query, keys, values, lse_pair, grad = item
        rows = query.shape[0]
        count = keys.shape[0]
        scores = jnp.where(allowed[None], pair_scores(query, keys), NEGATIVE)
        probs = jnp.exp(scores - lse_pair[..., None])
        probs_b = probs.astype(jnp.bfloat16)
        grad_heads = grad.reshape(rows, 2, HDIM)
        dprob = jnp.einsum(
            "rhd,khd->hrk",
            grad_heads,
            values.reshape(count, 2, HDIM),
            preferred_element_type=jnp.float32,
        )
        dscore = (probs * (dprob - jnp.sum(probs * dprob, axis=-1, keepdims=True))).astype(
            jnp.bfloat16
        )
        factor = HDIM ** (-0.5)
        dquery = (
            jnp.einsum(
                "hrk,khd->rhd",
                dscore,
                keys.reshape(count, 2, HDIM),
                preferred_element_type=jnp.float32,
            )
            * factor
        )
        dkeys = (
            jnp.einsum(
                "hrk,rhd->khd",
                dscore,
                query.reshape(rows, 2, HDIM),
                preferred_element_type=jnp.float32,
            )
            * factor
        )
        dvalues = jnp.einsum(
            "hrk,rhd->khd", probs_b, grad_heads, preferred_element_type=jnp.float32
        )
        return (
            dquery.reshape(rows, 2 * HDIM),
            dkeys.reshape(count, 2 * HDIM),
            dvalues.reshape(count, 2 * HDIM),
        )

    d_query, d_keys, d_values = lax.map(
        one_pair, (to_pairs(q_b), to_pairs(k_b), to_pairs(v_b), saved, to_pairs(grad_b))
    )
    return (from_pairs(d_query), from_pairs(d_keys), from_pairs(d_values))


def mult(left, right):
    return jnp.dot(left, right, preferred_element_type=jnp.float32)


def per_device_general(
    tokens,
    cond,
    text,
    segments,
    positions,
    counts,
    ada_weight,
    ada_bias,
    gains,
    attn_weight,
    out_weight,
    text_weight,
    ffn_weight,
    down_weight,
    cotangent,
):
    ada_w, ada_b, gain_rows, attn_w, out_w, text_w = (
        lax.all_gather(ada_weight, "fsdp", axis=0, tiled=True),
        lax.all_gather(ada_bias, "fsdp", axis=0, tiled=True),
        lax.all_gather(gains, "fsdp", axis=1, tiled=True),
        lax.all_gather(attn_weight, "fsdp", axis=1, tiled=True),
        lax.all_gather(out_weight, "fsdp", axis=0, tiled=True),
        lax.all_gather(text_weight, "fsdp", axis=1, tiled=True),
    )
    gain_f = gain_rows.astype(jnp.float32)
    x = tokens[0].astype(jnp.float32)
    seg = segments[0]
    cosine, sine = rotary_tables(positions[0])
    text_b = text[0]
    cond_act = silu(cond[0].astype(jnp.float32)).astype(jnp.bfloat16)
    mod = mult(cond_act, ada_w) + ada_b.astype(jnp.float32)[None, :]
    pick = (seg[:, None] == jnp.arange(IMGS, dtype=jnp.int32)[None, :]).astype(jnp.float32)
    per_token = jnp.dot(pick, mod, precision=HIGH)
    scale1 = per_token[:, :D]
    gate1 = per_token[:, D : 2 * D]
    scale2 = per_token[:, 2 * D : 3 * D]
    gate2 = per_token[:, 3 * D :]
    normed1, inverse1 = norm_rows(x)
    h_one = (normed1 * gain_f[0] * (1.0 + scale1)).astype(jnp.bfloat16)
    query = mult(h_one, attn_w[0])
    keyed = mult(h_one, attn_w[1])
    valued = mult(h_one, attn_w[2]).astype(jnp.bfloat16)
    q_norm, q_inv = norm_rows(query)
    k_norm, k_inv = norm_rows(keyed)
    q_rot = rotate(q_norm * gain_f[2], cosine, sine).astype(jnp.bfloat16)
    k_rot = rotate(k_norm * gain_f[3], cosine, sine).astype(jnp.bfloat16)
    text_keys = mult(text_b, text_w[0])
    text_vals = mult(text_b, text_w[1]).astype(jnp.bfloat16)
    t_norm, t_inv = norm_rows(text_keys)
    text_rot = (t_norm * gain_f[4]).astype(jnp.bfloat16)
    same = seg[:, None] == seg[None, :]
    owner = jnp.arange(IMGS * TXT, dtype=jnp.int32) // TXT
    mine = seg[:, None] == owner[None, :]
    self_out, self_lse = attend_forward(q_rot, k_rot, valued, same)
    cross_out, cross_lse = attend_forward(q_rot, text_rot, text_vals, mine)
    cross_gate = jnp.tanh(gain_f[5])
    comb = (self_out + cross_gate * cross_out).astype(jnp.bfloat16)
    branch = mult(comb, out_w)
    tanh_one = jnp.tanh(gate1)
    x_one = x + tanh_one * branch
    normed2, inverse2 = norm_rows(x_one)
    h_two = (normed2 * gain_f[1] * (1.0 + scale2)).astype(jnp.bfloat16)
    ffn_w, down_w = (
        lax.all_gather(ffn_weight, "fsdp", axis=1, tiled=True),
        lax.all_gather(down_weight, "fsdp", axis=0, tiled=True),
    )
    gate_pre = mult(h_two, ffn_w[0])
    upper = mult(h_two, ffn_w[1])
    sigm = jax.nn.sigmoid(gate_pre)
    silu_pre = gate_pre * sigm
    hidden = (silu_pre * upper).astype(jnp.bfloat16)
    ffn_out = mult(hidden, down_w)
    tanh_two = jnp.tanh(gate2)
    block_out = (x_one + tanh_two * ffn_out).astype(jnp.bfloat16)
    totals = counts.astype(jnp.float32)
    here = jnp.sum(
        jnp.where(
            jnp.arange(totals.shape[0], dtype=jnp.int32) == lax.axis_index("bucket"), totals, 0.0
        )
    )
    weight = lax.axis_size("bucket") * here / jnp.sum(totals)
    grad = cotangent[0].astype(jnp.float32) * weight
    back_ffn, back_down = (
        lax.all_gather(ffn_weight, "fsdp", axis=1, tiled=True),
        lax.all_gather(down_weight, "fsdp", axis=0, tiled=True),
    )
    d_gate2 = grad * ffn_out * (1.0 - tanh_two * tanh_two)
    d_ffn = (grad * tanh_two).astype(jnp.bfloat16)
    d_hidden = mult(d_ffn, back_down.T)
    g_down = mult(hidden.T, d_ffn)
    d_pre = (d_hidden * upper * sigm * (1.0 + gate_pre * (1.0 - sigm))).astype(jnp.bfloat16)
    d_up = (d_hidden * silu_pre).astype(jnp.bfloat16)
    d_h_two = mult(d_pre, back_ffn[0].T) + mult(d_up, back_ffn[1].T)
    g_ffn = jnp.stack([mult(h_two.T, d_pre), mult(h_two.T, d_up)])
    s_ffn, s_down = (
        lax.psum_scatter(g_ffn, ("bucket", "fsdp"), scatter_dimension=1, tiled=True),
        lax.psum_scatter(g_down, ("bucket", "fsdp"), scatter_dimension=0, tiled=True),
    )
    back_attn, back_out = (
        lax.all_gather(attn_weight, "fsdp", axis=1, tiled=True),
        lax.all_gather(out_weight, "fsdp", axis=0, tiled=True),
    )
    g_gain_one = jnp.sum(d_h_two * normed2 * (1.0 + scale2), axis=0)
    d_scale2 = d_h_two * normed2 * gain_f[1]
    d_x_one = grad + norm_back(d_h_two * gain_f[1] * (1.0 + scale2), normed2, inverse2)
    d_gate1 = d_x_one * branch * (1.0 - tanh_one * tanh_one)
    d_branch = (d_x_one * tanh_one).astype(jnp.bfloat16)
    d_comb = mult(d_branch, back_out.T)
    g_out = mult(comb.T, d_branch)
    g_gain_five = jnp.sum(d_comb * cross_out, axis=0) * (1.0 - cross_gate * cross_gate)
    d_self = d_comb.astype(jnp.bfloat16)
    d_cross = (d_comb * cross_gate).astype(jnp.bfloat16)
    dq_self, dk_self, dv_self = attend_back(q_rot, k_rot, valued, self_lse, d_self, same)
    dq_cross, dk_text, dv_text = attend_back(q_rot, text_rot, text_vals, cross_lse, d_cross, mine)
    d_q_norm = rotate(dq_self + dq_cross, cosine, -sine)
    g_gain_two = jnp.sum(d_q_norm * q_norm, axis=0)
    d_query = norm_back(d_q_norm * gain_f[2], q_norm, q_inv).astype(jnp.bfloat16)
    d_k_norm = rotate(dk_self, cosine, -sine)
    g_gain_three = jnp.sum(d_k_norm * k_norm, axis=0)
    d_keyed = norm_back(d_k_norm * gain_f[3], k_norm, k_inv).astype(jnp.bfloat16)
    d_valued = dv_self.astype(jnp.bfloat16)
    g_gain_four = jnp.sum(dk_text * t_norm, axis=0)
    d_text_keys = norm_back(dk_text * gain_f[4], t_norm, t_inv).astype(jnp.bfloat16)
    d_text_vals = dv_text.astype(jnp.bfloat16)
    g_text = jnp.stack([mult(text_b.T, d_text_keys), mult(text_b.T, d_text_vals)])
    d_h_one = (
        mult(d_query, back_attn[0].T)
        + mult(d_keyed, back_attn[1].T)
        + mult(d_valued, back_attn[2].T)
    )
    g_attn = jnp.stack([mult(h_one.T, d_query), mult(h_one.T, d_keyed), mult(h_one.T, d_valued)])
    g_gain_zero = jnp.sum(d_h_one * normed1 * (1.0 + scale1), axis=0)
    d_scale1 = d_h_one * normed1 * gain_f[0]
    token_grad = d_x_one + norm_back(d_h_one * gain_f[0] * (1.0 + scale1), normed1, inverse1)
    d_token_mod = jnp.concatenate([d_scale1, d_gate1, d_scale2, d_gate2], axis=1)
    d_mod = jnp.dot(pick.T, d_token_mod, precision=HIGH)
    g_ada_b = jnp.sum(d_mod, axis=0)
    g_ada_w = mult(cond_act.T, d_mod.astype(jnp.bfloat16))
    g_gains = jnp.stack(
        [g_gain_zero, g_gain_one, g_gain_two, g_gain_three, g_gain_four, g_gain_five]
    )
    s_ada_w, s_ada_b, s_gains, s_attn, s_out, s_text = (
        lax.psum_scatter(g_ada_w, ("bucket", "fsdp"), scatter_dimension=0, tiled=True),
        lax.psum_scatter(g_ada_b, ("bucket", "fsdp"), scatter_dimension=0, tiled=True),
        lax.psum_scatter(g_gains, ("bucket", "fsdp"), scatter_dimension=1, tiled=True),
        lax.psum_scatter(g_attn, ("bucket", "fsdp"), scatter_dimension=1, tiled=True),
        lax.psum_scatter(g_out, ("bucket", "fsdp"), scatter_dimension=0, tiled=True),
        lax.psum_scatter(g_text, ("bucket", "fsdp"), scatter_dimension=1, tiled=True),
    )
    return (
        block_out[None],
        token_grad[None],
        s_ada_w,
        s_ada_b,
        s_gains,
        s_attn,
        s_out,
        s_text,
        s_ffn,
        s_down,
    )


ROW = 128
CHIPS = 4
HW = D // CHIPS
PAIRS = HW // 128


def partner(u):
    lane = lax.broadcasted_iota(jnp.int32, u.shape, 1)
    ahead = pltpu.roll(u, u.shape[1] - 16, 1)
    behind = pltpu.roll(u, 16, 1)
    return jnp.where((lane // 16) % 2 == 0, ahead, behind)


def dot_t(a, b):
    return lax.dot_general(a, b, (((1,), (1,)), ((), ())), preferred_element_type=jnp.float32)


def dot_n(a, b):
    return lax.dot_general(a, b, (((1,), (0,)), ((), ())), preferred_element_type=jnp.float32)


def t_dot(a, b):
    return lax.dot_general(a, b, (((0,), (0,)), ((), ())), preferred_element_type=jnp.float32)


def softmax_of(scores, allowed):
    scores = jnp.where(allowed, scores * HDIM ** (-0.5), NEGATIVE)
    top = jnp.max(scores, axis=-1, keepdims=True)
    expo = jnp.exp(scores - top)
    return expo / jnp.sum(expo, axis=-1, keepdims=True)


def head_mask(v, head):
    lane = lax.broadcasted_iota(jnp.int32, v.shape, 1)
    return jnp.where((lane // HDIM) == head, v, jnp.zeros_like(v))


def masks_of(seg_col, seg_row, captions):
    same = seg_col == seg_row
    owner = lax.broadcasted_iota(jnp.int32, (seg_col.shape[0], captions), 1) // TXT
    return same, seg_col == owner


def attend_kernel(
    q_ref, k_ref, v_ref, iq_ref, ik_ref, cos_ref, sin_ref, tk_ref, it_ref, tv_ref, sc_ref, sr_ref,
    g_ref, comb_ref, cross_ref, qr_ref, kr_ref, tr_ref,
):
    same, mine = masks_of(sc_ref[...], sr_ref[...], tk_ref.shape[0])
    cosine = cos_ref[...]
    sine = sin_ref[...]
    low = jnp.bfloat16
    for pair in range(PAIRS):
        at = pl.ds(pair * 128, 128)
        qn = q_ref[:, at] * iq_ref[...] * g_ref[2:3, at]
        kn = k_ref[:, at] * ik_ref[...] * g_ref[3:4, at]
        qr = (qn * cosine + partner(qn) * sine).astype(low)
        kr = (kn * cosine + partner(kn) * sine).astype(low)
        tr = (tk_ref[:, at] * it_ref[...] * g_ref[4:5, at]).astype(low)
        qr_ref[:, at] = qr
        kr_ref[:, at] = kr
        tr_ref[:, at] = tr
        vv = v_ref[:, at]
        tv = tv_ref[:, at]
        self_out = jnp.zeros(qn.shape, jnp.float32)
        cross_out = jnp.zeros(qn.shape, jnp.float32)
        for head in range(2):
            qh = head_mask(qr, head)
            probs = softmax_of(dot_t(qh, kr), same).astype(low)
            self_out = self_out + head_mask(dot_n(probs, vv), head)
            probs = softmax_of(dot_t(qh, tr), mine).astype(low)
            cross_out = cross_out + head_mask(dot_n(probs, tv), head)
        cross_ref[:, at] = cross_out
        comb_ref[:, at] = (self_out + jnp.tanh(g_ref[5:6, at]) * cross_out).astype(low)


def attend_back_kernel(
    qr_ref, kr_ref, v_ref, tr_ref, tv_ref, dc_ref, cross_ref, q_ref, k_ref, tk_ref, iq_ref, ik_ref,
    it_ref, cos_ref, sin_ref, sc_ref, sr_ref, g_ref,
    dq_ref, dk_ref, dv_ref, dt_ref, dtv_ref, gg_ref,
):
    same, mine = masks_of(sc_ref[...], sr_ref[...], tk_ref.shape[0])
    cosine = cos_ref[...]
    sine = sin_ref[...]
    low = jnp.bfloat16
    factor = HDIM ** (-0.5)
    for pair in range(PAIRS):
        at = pl.ds(pair * 128, 128)
        qr = qr_ref[:, at]
        kr = kr_ref[:, at]
        vv = v_ref[:, at]
        tr = tr_ref[:, at]
        tv = tv_ref[:, at]
        dcomb = dc_ref[:, at]
        d_self = dcomb.astype(low)
        d_cross = (dcomb * jnp.tanh(g_ref[5:6, at])).astype(low)
        dq = jnp.zeros(dcomb.shape, jnp.float32)
        dk = jnp.zeros(dcomb.shape, jnp.float32)
        dv = jnp.zeros(dcomb.shape, jnp.float32)
        dt = jnp.zeros((tr.shape[0], 128), jnp.float32)
        dtv = jnp.zeros((tr.shape[0], 128), jnp.float32)
        for head in range(2):
            qh = head_mask(qr, head)
            probs = softmax_of(dot_t(qh, kr), same)
            grad = head_mask(d_self, head)
            dprob = dot_t(grad, vv)
            dscore = probs * (dprob - jnp.sum(probs * dprob, axis=-1, keepdims=True))
            dscore = dscore.astype(low)
            dq = dq + dot_n(dscore, head_mask(kr, head))
            dk = dk + t_dot(dscore, qh)
            dv = dv + t_dot(probs.astype(low), grad)
            probs = softmax_of(dot_t(qh, tr), mine)
            grad = head_mask(d_cross, head)
            dprob = dot_t(grad, tv)
            dscore = probs * (dprob - jnp.sum(probs * dprob, axis=-1, keepdims=True))
            dscore = dscore.astype(low)
            dq = dq + dot_n(dscore, head_mask(tr, head))
            dt = dt + t_dot(dscore, qh)
            dtv = dtv + t_dot(probs.astype(low), grad)
        dq = dq * factor
        dk = dk * factor
        dt = dt * factor
        dq = dq * cosine - partner(dq) * sine
        dk = dk * cosine - partner(dk) * sine
        q_norm = q_ref[:, at] * iq_ref[...]
        k_norm = k_ref[:, at] * ik_ref[...]
        t_norm = tk_ref[:, at] * it_ref[...]
        gg_ref[0:1, at] += jnp.sum(dq * q_norm, axis=0, keepdims=True)
        gg_ref[1:2, at] += jnp.sum(dk * k_norm, axis=0, keepdims=True)
        gg_ref[2:3, at] += jnp.sum(dt * t_norm, axis=0, keepdims=True)
        gg_ref[3:4, at] += jnp.sum(dcomb * cross_ref[:, at], axis=0, keepdims=True)
        dq = dq * g_ref[2:3, at]
        dk = dk * g_ref[3:4, at]
        dt = dt * g_ref[4:5, at]
        dq_ref[:, at] = dq
        dk_ref[:, at] = dk
        dv_ref[:, at] = dv.astype(low)
        dt_ref[:, at] = dt
        dtv_ref[:, at] = dtv.astype(low)


MESH_IDS = pl.DeviceIdType.MESH
VMEM_SPEC = pl.BlockSpec(memory_space=pltpu.VMEM)
ANY_SPEC = pl.BlockSpec(memory_space=pl.ANY)


def to_row_owner(block):
    pairs = [
        (a * 8 + b * 2 + k, b * 8 + a * 2 + k) for a in range(4) for b in range(4) for k in range(2)
    ]
    return lax.ppermute(block, ("bucket", "fsdp"), pairs).astype(jnp.float32)


class Net:
    def __init__(self, send_sems, recv_sems):
        self.me = lax.axis_index("fsdp")
        self.send_sems = send_sems
        self.recv_sems = recv_sems
        self.count = 0
        self.all = []

    def peer(self, mask):
        out = self.me
        for bit in (1, 2, 4):
            if mask & bit:
                out = out + bit * (1 - 2 * ((self.me // bit) % 2))
        return out

    def meet(self, masks):
        sem = pltpu.get_barrier_semaphore()
        for mask in masks:
            pl.semaphore_signal(
                sem, inc=1, device_id={"fsdp": self.peer(mask)}, device_id_type=MESH_IDS
            )
        pl.semaphore_wait(sem, len(masks))

    def send(self, src, dst, mask):
        assert self.count < self.send_sems.shape[0]
        copy = pltpu.make_async_remote_copy(
            src_ref=src,
            dst_ref=dst,
            send_sem=self.send_sems.at[self.count],
            recv_sem=self.recv_sems.at[self.count],
            device_id={"fsdp": self.peer(mask)},
            device_id_type=MESH_IDS,
        )
        self.count += 1
        copy.start()
        self.all.append(copy)
        return copy

    def close(self):
        for copy in self.all:
            copy.wait_send()


def net_scratch(count):
    return [pltpu.SemaphoreType.DMA((count,)), pltpu.SemaphoreType.DMA((count,))]


def share4_start(net, out):
    return net.send(out.at[0], out.at[1], 2), net.send(out.at[0], out.at[2], 4)


def share4_relay(net, out, by_x, by_y):
    half = out.shape[1] // 2
    top, bottom = pl.ds(0, half), pl.ds(half, half)
    by_x.wait_recv()
    first = net.send(out.at[1, top], out.at[3, top], 4)
    by_y.wait_recv()
    second = net.send(out.at[2, bottom], out.at[3, bottom], 2)
    return first, second


def collect4(net, part, buf, far):
    half = far.shape[1]
    rows = (pl.ds(0, half), pl.ds(half, half))
    low = jnp.bfloat16
    full = jnp.float32
    for i in (0, 1):
        buf[2, rows[i]] = part(3, i).astype(low)
    far_x = net.send(buf.at[2, rows[0]], far.at[0], 2)
    far_y = net.send(buf.at[2, rows[1]], far.at[1], 4)
    buf[0, rows[0]] = part(1, 0).astype(low)
    one_a = net.send(buf.at[0, rows[0]], buf.at[3, rows[0]], 2)
    buf[1, rows[1]] = part(2, 1).astype(low)
    two_b = net.send(buf.at[1, rows[1]], buf.at[4, rows[1]], 4)
    later = []

    def middle():
        far_x.wait_recv()
        buf[1, rows[0]] = (part(2, 0) + far[0].astype(full)).astype(low)
        later.append(net.send(buf.at[1, rows[0]], buf.at[4, rows[0]], 4))
        far_y.wait_recv()
        buf[0, rows[1]] = (part(1, 1) + far[1].astype(full)).astype(low)
        later.append(net.send(buf.at[0, rows[1]], buf.at[3, rows[1]], 2))

    def finish(i):
        (one_a, two_b)[i].wait_recv()
        later[i].wait_recv()
        return part(0, i) + buf[3, rows[i]].astype(full) + buf[4, rows[i]].astype(full)

    return middle, finish


def pick_rows(table, seg, first):
    out = table[first + IMGS - 1 : first + IMGS]
    for i in range(IMGS - 2, -1, -1):
        out = jnp.where(seg == i, table[first + i : first + i + 1], out)
    return out


def row_sums(a, b):
    ones = jnp.ones((8, a.shape[1]), jnp.float32)

    def one(v):
        return lax.dot_general(
            ones, v, (((1,), (1,)), ((), ())), precision=HIGH, preferred_element_type=jnp.float32
        )

    if b is None:
        return one(a)
    got = one(a)
    return jnp.where(lax.broadcasted_iota(jnp.int32, got.shape, 0) < 4, got, one(b))


def spread(net, src, dst, width, local):
    count, rows, _ = src.shape

    def cut(i, c):
        return src.at[i, :, pl.ds(pl.multiple_of(c * width, 128), width)]

    def put(i, f):
        return dst.at[pl.ds(pl.multiple_of(f * rows, rows), rows), pl.ds(i * width, width)]

    chip = net.me // 2
    ids = range(count)
    here = [local(cut(i, chip), put(i, net.me)) for i in ids]
    core = [net.send(cut(i, chip), put(i, net.me), 1) for i in ids]

    def away(m):
        return [net.send(cut(i, net.peer(m) // 2), put(i, net.me), m) for i in ids]

    def whole(f):
        return dst.at[pl.ds(pl.multiple_of(f * rows, rows), rows), :]

    def pass_on(copies, m):
        for c in copies:
            c.wait_recv()
        return net.send(whole(net.peer(m)), whole(net.peer(m)), 1)

    return here, core, away, pass_on


ALL_PEERS = (1, 2, 3, 4, 5, 6, 7)


def open_kernel(
    cond_ref, gain_ref, bias_ref, ada_ref, tok_ref, seg_ref, idx_ref, attn_ref, textw_ref, text_ref,
    mod_ref, gains_ref, h_ref, idxs_ref, aw_ref, ta_out, q_ref, k_ref, v_ref, tk_ref, tv_ref,
    iqk_ref, it_ref,
    conds, parts, mods, gbuf, tw_ref, ta_ref, sums, tsums, local_sems, out_sems, send_sems,
    recv_sems,
):
    low = jnp.bfloat16
    full = jnp.float32
    net = Net(send_sems, recv_sems)
    me = net.me
    chip = me // 2
    net.meet(ALL_PEERS)

    act = cond_ref[...].astype(full)
    act = (act * jax.nn.sigmoid(act)).astype(low).astype(full)
    for j in range(8):
        gbuf[8, :, 128 * j : 128 * j + 128] = act[:, 128 * j : 128 * j + 128]
    waits = []
    for m in ALL_PEERS:
        at = pl.ds(pl.multiple_of(net.peer(m) * 128, 128), 128)
        waits.append(net.send(gbuf.at[8, :, at], conds.at[m], m))
    conds[0] = gbuf[8, :, pl.ds(pl.multiple_of(me * 128, 128), 128)]
    gwaits = [net.send(gain_ref, gbuf.at[m], m) for m in ALL_PEERS]
    iwaits = [net.send(idx_ref, idxs_ref.at[i], m) for i, m in ((1, 2), (2, 4), (3, 6))]
    idxs_ref[0] = idx_ref[...]

    for w in waits:
        w.wait_recv()
    lhs = jnp.concatenate([conds[m] for m in range(8)], axis=0).astype(low)
    half_cols = 3072
    step = 512

    def mod_cols(i, _):
        lo = pl.ds(pl.multiple_of(i * step, step), step)
        hi = pl.ds(pl.multiple_of(half_cols + i * step, step), step)
        a = jnp.dot(lhs, ada_ref[:, lo], preferred_element_type=full)
        b = jnp.dot(lhs, ada_ref[:, hi], preferred_element_type=full)
        row = lax.broadcasted_iota(jnp.int32, (8, step), 0)
        for m in range(8):
            parts[m, :, lo] = (
                jnp.where(row < 4, a[8 * m : 8 * m + 8], b[8 * m : 8 * m + 8]) + bias_ref[:, lo]
            )
        return 0

    lax.fori_loop(0, half_cols // step, mod_cols, 0)
    waits = [net.send(parts.at[m], mods.at[m], m) for m in ALL_PEERS]

    def local(slot):
        def go(src, dst):
            copy = pltpu.make_async_copy(src, dst, local_sems.at[slot[0]])
            slot[0] += 1
            copy.start()
            return copy

        return go

    slot = [3]
    attn_io = spread(net, attn_ref, aw_ref, HW, local(slot))
    attn_away = [attn_io[2](m) for m in (2, 4, 6)]
    text_io = spread(net, textw_ref, tw_ref, HW, local(slot))
    text_away = [text_io[2](m) for m in (2, 4, 6)]
    own_text = pltpu.make_async_copy(text_ref, ta_ref.at[0], local_sems.at[2])
    own_text.start()
    for w in gwaits:
        w.wait_recv()
    gains = gain_ref[...]
    for m in ALL_PEERS:
        gains = gains + gbuf[m]
    gains_ref[...] = gains
    for w in waits:
        w.wait_recv()

    def mod_sum(i, _):
        at = pl.ds(pl.multiple_of(i * step, step), step)
        total = parts[0, :, at]
        for m in ALL_PEERS:
            total = total + mods[m, :, at]
        mod_ref[:, at] = total
        return 0

    lax.fori_loop(0, half_cols // step, mod_sum, 0)

    block = 32

    def first_norm(i, _):
        at = pl.ds(pl.multiple_of(i * block, block), block)
        x = tok_ref[at, :].astype(full)
        normed = x * lax.rsqrt(jnp.mean(x * x, axis=-1, keepdims=True) + EPS)
        scale = pick_rows(mod_ref[:, :D], seg_ref[at, :], 0)
        h_ref[0, at, :] = (normed * gains_ref[0:1, :] * (1.0 + scale)).astype(low)
        return 0

    lax.fori_loop(0, ROW // block, first_norm, 0)
    hx, hy = share4_start(net, h_ref)

    def all_in(io, away):
        for c in io[0]:
            c.wait()
        return io[1] + [io[3](c, m) for c, m in zip(away, (2, 4, 6))]

    attn_core = all_in(attn_io, attn_away)
    text_core = all_in(text_io, text_away)
    h_far = share4_relay(net, h_ref, hx, hy)
    own_text.wait()

    def keep(j):
        copy = pltpu.make_async_copy(ta_ref.at[j], ta_out.at[j], out_sems.at[j])
        copy.start()
        return copy

    kept = [keep(0)]
    chunks = 4
    size = ta_ref.shape[1] // chunks
    tx, ty = [None] * chunks, [None] * chunks
    for s in range(chunks):
        i, j = s, (s + chunks // 2) % chunks
        at = pl.ds(i * size, size)
        tx[i] = net.send(ta_ref.at[0, at], ta_ref.at[1, at], 2)
        at = pl.ds(j * size, size)
        ty[j] = net.send(ta_ref.at[0, at], ta_ref.at[2, at], 4)

    for c in attn_core:
        c.wait_recv()
    for c in h_far:
        c.wait_recv()

    for j in range(CHIPS):
        h = h_ref[j]
        at = pl.ds(j * ROW, ROW)
        qv = jnp.dot(h, aw_ref[:, :HW], preferred_element_type=full)
        q_ref[at, :] = qv
        kv = jnp.dot(h, aw_ref[:, HW : 2 * HW], preferred_element_type=full)
        k_ref[at, :] = kv
        v_ref[at, :] = jnp.dot(h, aw_ref[:, 2 * HW :], preferred_element_type=full).astype(low)
        sums[0, :, at] = row_sums(qv * qv, kv * kv)
    sum_io = [net.send(sums.at[0], sums.at[i], m) for i, m in ((1, 2), (2, 4), (3, 6))]

    for c in text_core:
        c.wait_recv()

    def text_rows(j, lo, count):
        kt = 1024

        def body(i, acc):
            at = pl.ds(pl.multiple_of(i * kt, kt), kt)
            rows = ta_ref[j, pl.ds(lo, count), at]
            return acc + jnp.dot(rows, tw_ref[at, :], preferred_element_type=full)

        both = lax.fori_loop(0, ta_ref.shape[2] // kt, body, jnp.zeros((count, 2 * HW), full))
        keys, vals = both[:, :HW], both[:, HW:]
        at = pl.ds(j * ta_ref.shape[1] + lo, count)
        tk_ref[at, :] = keys
        tv_ref[at, :] = vals.astype(low)
        tsums[0, :, at] = row_sums(keys * keys, None)

    cap = ta_ref.shape[1]
    half = cap // 2
    for lo in (0, half):
        text_rows(0, lo, half)
    relays = []
    for s in range(chunks // 2):
        i, j = s, s + chunks // 2
        tx[i].wait_recv()
        at = pl.ds(i * size, size)
        relays.append(net.send(ta_ref.at[1, at], ta_ref.at[3, at], 4))
        ty[j].wait_recv()
        at = pl.ds(j * size, size)
        relays.append(net.send(ta_ref.at[2, at], ta_ref.at[3, at], 2))
    for i, c in enumerate(sum_io):
        c.wait_recv()
    for j in range(CHIPS):
        total = sums[0, :, pl.ds(j * ROW, ROW)]
        for i in (1, 2, 3):
            total = total + sums[i, :, pl.ds((j ^ i) * ROW, ROW)]
        iqk_ref[:, pl.ds(j * ROW, ROW)] = lax.rsqrt(total / D + EPS)
    text_rows(1, 0, half)
    text_rows(2, half, half)
    for s in range(chunks // 2):
        tx[s + chunks // 2].wait_recv()
        ty[s].wait_recv()
    kept += [keep(1), keep(2)]
    text_rows(1, half, half)
    text_rows(2, 0, half)
    for c in relays:
        c.wait_recv()
    kept.append(keep(3))
    for lo in (0, half):
        text_rows(3, lo, half)
    sum_io = [net.send(tsums.at[0], tsums.at[i], m) for i, m in ((1, 2), (2, 4), (3, 6))]
    for c in sum_io:
        c.wait_recv()
    for j in range(CHIPS):
        total = tsums[0, :, pl.ds(j * cap, cap)]
        for i in (1, 2, 3):
            total = total + tsums[i, :, pl.ds((j ^ i) * cap, cap)]
        it_ref[:, pl.ds(j * cap, cap)] = lax.rsqrt(total / D + EPS)
    for c in iwaits:
        c.wait_recv()
    for c in kept:
        c.wait()
    net.close()


def open_layer(cond8, gain_pad, bias_pad, ada, tok, seg_col, idx, attn, textw, text):
    low = jnp.bfloat16
    full = jnp.float32
    shape = jax.ShapeDtypeStruct
    cap, txtd = text.shape
    V = VMEM_SPEC
    return pl.pallas_call(
        open_kernel,
        in_specs=[V, V, V, V, V, V, V, ANY_SPEC, ANY_SPEC, ANY_SPEC],
        out_specs=[V] * 5 + [ANY_SPEC] + [V] * 7,
        out_shape=[
            shape((8, 3072), full),
            shape((8, D), full),
            shape((CHIPS, ROW, D), low),
            shape((CHIPS, 8, ROW), jnp.int32),
            shape((D, 3 * HW), low),
            shape((CHIPS, cap, txtd), low),
            shape((CHIPS * ROW, HW), full),
            shape((CHIPS * ROW, HW), full),
            shape((CHIPS * ROW, HW), low),
            shape((CHIPS * cap, HW), full),
            shape((CHIPS * cap, HW), low),
            shape((8, CHIPS * ROW), full),
            shape((8, CHIPS * cap), full),
        ],
        scratch_shapes=[
            pltpu.VMEM((8, 8, 128), full),
            pltpu.VMEM((8, 8, 3072), full),
            pltpu.VMEM((8, 8, 3072), full),
            pltpu.VMEM((9, 8, D), full),
            pltpu.VMEM((txtd, 2 * HW), low),
            pltpu.VMEM((CHIPS, cap, txtd), low),
            pltpu.VMEM((CHIPS, 8, CHIPS * ROW), full),
            pltpu.VMEM((CHIPS, 8, CHIPS * cap), full),
            pltpu.SemaphoreType.DMA((8,)),
            pltpu.SemaphoreType.DMA((CHIPS,)),
            *net_scratch(80),
        ],
        compiler_params=pltpu.CompilerParams(
            collective_id=1, has_side_effects=True, vmem_limit_bytes=56 * 1024 * 1024
        ),
        cost_estimate=pl.CostEstimate(
            flops=10_000_000_000, bytes_accessed=400_000_000, transcendentals=0
        ),
    )(cond8, gain_pad, bias_pad, ada, tok, seg_col, idx, attn, textw, text)


class Chain:
    def __init__(self, net, grad, mine, arrive, total, sems, columns):
        self.net = net
        self.grad = grad
        self.mine = mine
        self.arrive = arrive
        self.total = total
        self.sems = sems
        self.columns = columns
        self.plane = lax.axis_index("bucket")
        self.core = net.me % 2

    def piece(self, ref, p):
        return ref.at[:, p] if self.columns else ref.at[p]

    def half(self, core):
        return self.grad.at[:, :, :, core] if self.columns else self.grad.at[:, core]

    def each(self, ref, body):
        lead = ref.shape[:-2]
        if not lead:
            body(())
            return
        total = 1
        for n in lead:
            total *= n

        def step(i, _):
            index = []
            for n in reversed(lead):
                index.insert(0, i % n)
                i = i // n
            body(tuple(index))
            return 0

        lax.fori_loop(0, total, step, 0)

    def core_start(self, keep=None, sem=None):
        self.exchange = self.net.send(self.half(1 - self.core), self.mine, 1)
        self.keep = self.half(self.core)
        self.load = None
        if keep is not None:
            self.load = pltpu.make_async_copy(self.keep, keep, sem)
            self.load.start()
            self.keep = keep

    def add(self, into, other):
        def body(index):
            value = into[index].astype(jnp.float32) + other[index].astype(jnp.float32)
            into[index] = value.astype(into.dtype)

        self.each(into, body)

    def core_finish(self):
        self.exchange.wait_recv()
        if self.load is not None:
            self.load.wait()
        self.add(self.mine, self.keep)

    def copy(self, up, p, slot):
        first = 0 if up else 8
        return pltpu.make_async_remote_copy(
            src_ref=self.piece(self.mine, p),
            dst_ref=self.arrive.at[slot],
            send_sem=self.sems.at[first + p],
            recv_sem=self.sems.at[first + 4 + p],
            device_id={"bucket": self.plane + (1 if up else -1)},
            device_id_type=MESH_IDS,
        )

    def moves(self, t):
        up = self.plane + 3 - t
        down = self.plane - 3 + t
        return (
            (True, up, up, self.plane <= t, self.plane >= 1),
            (False, down, 4 if t == 2 else down, self.plane >= 3 - t, self.plane <= 2),
        )

    def step(self, t):
        for up, p, slot, sends, inner in self.moves(t):

            @pl.when(sends)
            def _(up=up, p=p, slot=slot, inner=inner):
                @pl.when(inner)
                def _():
                    self.copy(up, p, p).wait_recv()
                    self.add(self.piece(self.mine, p), self.arrive.at[p])

                self.copy(up, p, slot).start()

    def finish(self):
        own = self.piece(self.mine, self.plane)

        def first(index):
            self.total[index] = own[index].astype(jnp.float32)

        self.each(self.total, first)
        for up, slot, inner in ((True, self.plane, self.plane >= 1), (False, 4, self.plane <= 2)):

            @pl.when(inner)
            def _(up=up, slot=slot):
                self.copy(up, self.plane, slot).wait_recv()
                self.add(self.total, self.arrive.at[slot])

    def close(self):
        for t in range(3):
            for up, p, slot, sends, inner in self.moves(t):

                @pl.when(sends)
                def _(up=up, p=p, slot=slot):
                    self.copy(up, p, slot).wait_send()


def chain_scratch(columns, shape, width):
    low = jnp.bfloat16
    if columns:
        n, rows = shape
        return [
            pltpu.VMEM((n, 4, 4, rows, width), low),
            pltpu.VMEM((5, n, 4, rows, width), low),
            pltpu.VMEM((n, 4, rows, width), jnp.float32),
            pltpu.SemaphoreType.DMA((16,)),
        ]
    return [
        pltpu.VMEM((4, shape, width), low),
        pltpu.VMEM((5, shape, width), low),
        pltpu.VMEM((shape, width), jnp.float32),
        pltpu.SemaphoreType.DMA((16,)),
    ]


class Columns:
    def __init__(self, net, total, stage, wide, out):
        self.net, self.total, self.stage, self.wide, self.out = net, total, stage, wide, out

    def start(self):
        net = self.net
        chip = net.me // 2
        n, _, rows, width = self.stage.shape
        parts = self.wide.shape[0]
        width = width // parts
        at = pl.ds(pl.multiple_of(chip * width, width), width)

        def cast(i, _):
            self.stage[i // 4, i % 4] = self.total[i // 4, i % 4].astype(jnp.bfloat16)
            return 0

        if self.total is not None:
            lax.fori_loop(0, n * 4, cast, 0)
        self.copies = [
            net.send(
                self.stage.at[0, net.peer(m) // 2, :, pl.ds(i * width, width)],
                self.wide.at[i, :, at],
                m,
            )
            for m in (2, 4, 6)
            for i in range(parts)
        ]
        for i in range(parts):
            self.wide[i, :, at] = self.stage[0, chip, :, i * width : i * width + width]

    def finish(self):
        for c in self.copies:
            c.wait_recv()
        for i in range(self.out.shape[0]):
            self.out[i] = self.wide[i].astype(jnp.float32)


def meet_all(net, far=False):
    plane = lax.axis_index("bucket")
    chip = net.me // 2
    sem = pltpu.get_barrier_semaphore()
    for mask in ALL_PEERS:
        pl.semaphore_signal(
            sem, inc=1, device_id={"fsdp": net.peer(mask)}, device_id_type=MESH_IDS
        )
    for inner, step in ((plane >= 1, -1), (plane <= 2, 1)):

        @pl.when(inner)
        def _(step=step):
            pl.semaphore_signal(
                sem, inc=1, device_id={"bucket": plane + step}, device_id_type=MESH_IDS
            )

    @pl.when(chip != plane)
    def _():
        pl.semaphore_signal(
            sem,
            inc=1,
            device_id={"bucket": chip, "fsdp": plane * 2 + net.me % 2},
            device_id_type=MESH_IDS,
        )

    if far:
        pl.semaphore_signal(
            sem,
            inc=1,
            device_id={"bucket": plane + 2 - 4 * (plane // 2)},
            device_id_type=MESH_IDS,
        )
    one = jnp.int32(1)
    zero = jnp.int32(0)
    count = (
        (8 if far else 7)
        + jnp.where(plane >= 1, one, zero)
        + jnp.where(plane <= 2, one, zero)
        + jnp.where(chip != plane, one, zero)
    )
    pl.semaphore_wait(sem, count)


def transposed(net, src, dst, sems):
    plane = lax.axis_index("bucket")
    return pltpu.make_async_remote_copy(
        src_ref=src,
        dst_ref=dst,
        send_sem=sems.at[0],
        recv_sem=sems.at[1],
        device_id={"bucket": net.me // 2, "fsdp": plane * 2 + net.me % 2},
        device_id_type=MESH_IDS,
    )


class Spread:
    def __init__(self, buf, sems):
        self.buf, self.sems = buf, sems
        self.plane = lax.axis_index("bucket")

    def copy(self, up, slab):
        first = 0 if up else 8
        return pltpu.make_async_remote_copy(
            src_ref=self.buf.at[slab],
            dst_ref=self.buf.at[slab],
            send_sem=self.sems.at[first + slab],
            recv_sem=self.sems.at[first + 4 + slab],
            device_id={"bucket": self.plane + (1 if up else -1)},
            device_id_type=MESH_IDS,
        )

    def hop(self, h):
        for up in (True, False):
            slab = self.plane - h if up else self.plane + h
            there = (slab >= 0) if up else (slab <= 3)
            sends = (self.plane <= 2) if up else (self.plane >= 1)

            @pl.when(there)
            def _(up=up, slab=slab, sends=sends):
                if h > 0:
                    self.copy(up, slab).wait_recv()

                @pl.when(sends)
                def _():
                    self.copy(up, slab).start()

    def close(self):
        for h in range(4):
            for up in (True, False):
                slab = self.plane - h if up else self.plane + h
                there = (slab >= 0) if up else (slab <= 3)
                sends = (self.plane <= 2) if up else (self.plane >= 1)

                @pl.when(there & sends)
                def _(up=up, slab=slab):
                    self.copy(up, slab).wait_send()


def close_kernel(
    text_g, attn_g, out_g, ffn_t, dmod_ref, gg_ref, gs_ref, cond_ref,
    text_o, attn_o, out_o, ffn_o, ada_o, small_o,
    tm, ta, tt, ts, am, aa, at_, as_, om, oa, ot, os_,
    t_wide, a_wide, f_wide, t_stage, a_stage, o_stage, o_got, o_sem,
    mods, mods_other, mod_sems, smalls, got, z_sems, ada_s, send_sems, recv_sems,
):
    low = jnp.bfloat16
    full = jnp.float32
    net = Net(send_sems, recv_sems)
    meet_all(net, True)
    plane = lax.axis_index("bucket")
    me = net.me
    chip = me // 2
    out = Chain(net, out_g, om, oa, ot, os_, False)
    attn = Chain(net, attn_g, am, aa, at_, as_, True)
    text = Chain(net, text_g, tm, ta, tt, ts, True)
    chains = [out, text, attn]
    for c in chains:
        c.core_start()

    act = cond_ref[...].astype(full)
    mods[plane, 0, :, 2 * D :] = (act * jax.nn.sigmoid(act)).astype(low)
    mods[plane, 0, :, : 2 * D] = dmod_ref[...].astype(low)
    mine = mods.at[plane, 0]
    mod_io = [net.send(mine, mods.at[plane, i], m) for i, m in ((1, 2), (2, 4), (3, 6))]

    smalls[...] = jnp.zeros(smalls.shape, full)
    smalls[0:2, :] = gg_ref[0:2, :]
    smalls[2:6, pl.ds(pl.multiple_of(chip * HW, 128), HW)] = gs_ref[0:4, :]
    for p in range(4):
        rows = dmod_ref[4 * (p // 2) : 4 * (p // 2) + 4, (p % 2) * D : (p % 2 + 1) * D]
        smalls[8 + p : 9 + p, :] = jnp.sum(rows, axis=0, keepdims=True)
    order = [None]

    def small_send(i):
        if i < 3:
            order[0] = net.send(smalls, got.at[i], (1, 2, 4)[i])
            return
        there = plane + 1 - 2 * (plane % 2) if i == 3 else plane + 2 - 4 * (plane // 2)
        copy = pltpu.make_async_remote_copy(
            src_ref=smalls,
            dst_ref=got.at[i],
            send_sem=z_sems.at[2 * (i - 3)],
            recv_sem=z_sems.at[2 * (i - 3) + 1],
            device_id={"bucket": there},
            device_id_type=MESH_IDS,
        )
        copy.start()
        order[0] = copy

    def small_add(i):
        order[0].wait()
        net.all = [c for c in net.all if c is not order[0]]
        smalls[...] = smalls[...] + got[i]

    small_send(0)
    f_cols = Columns(net, None, ffn_t, f_wide, ffn_o)
    f_cols.start()
    for c in chains:
        c.core_finish()
        c.step(0)
    small_add(0)
    small_send(1)
    for c in mod_io:
        c.wait_recv()
    lines = Spread(mods, mod_sems)
    lines.hop(0)
    small_add(1)
    small_send(2)
    for c in chains:
        c.step(1)
    lines.hop(1)
    small_add(2)
    small_send(3)
    f_cols.finish()
    for c in chains:
        c.step(2)
    lines.hop(2)
    small_add(3)
    small_send(4)
    lines.hop(3)
    other = net.send(mods, mods_other, 1)
    small_add(4)
    small_o[...] = smalls[...]
    out.finish()
    o_stage[...] = ot[...].astype(low)

    @pl.when(chip != plane)
    def _():
        transposed(net, o_stage, o_got, o_sem).start()

    other.wait_recv()
    rank = plane * 8 + me
    lanes = pl.ds(pl.multiple_of(2 * D + (rank // 4) * 128, 128), 128)
    total = 128
    both = []
    for ref in (mods, mods_other):
        acts = ref[:, :, :, lanes].astype(full).reshape(total, 128)
        both.append(acts)
    acts = jnp.concatenate(both, axis=0)
    upper = (lax.broadcasted_iota(jnp.int32, acts.shape, 0) % 8) < 4
    parts = (jnp.where(upper, acts, 0.0).astype(low), jnp.where(upper, 0.0, acts).astype(low))
    wide = 512

    def ada_cols(i, _):
        at = pl.ds(pl.multiple_of(i * wide, wide), wide)
        rows = jnp.concatenate(
            [r[:, :, :, at].astype(full).reshape(total, wide) for r in (mods, mods_other)], axis=0
        ).astype(low)
        for p in range(2):
            ada_s[...] = t_dot(parts[p], rows)
            to = pl.ds(pl.multiple_of(p * 2 * D + i * wide, wide), wide)
            ada_o[:, to] = ada_s[pl.ds(pl.multiple_of((rank % 4) * 32, 32), 32), :]
        return 0

    lax.fori_loop(0, 2 * D // wide, ada_cols, 0)
    text.finish()
    text_cols = Columns(net, tt, t_stage, t_wide, text_o)
    text_cols.start()

    @pl.when(chip != plane)
    def _():
        transposed(net, o_stage, o_got, o_sem).wait()
        out_o[...] = o_got[...].astype(jnp.float32)

    @pl.when(chip == plane)
    def _():
        out_o[...] = ot[...]

    attn.finish()
    attn_cols = Columns(net, at_, a_stage, a_wide, attn_o)
    attn_cols.start()
    text_cols.finish()
    attn_cols.finish()
    for c in chains:
        c.close()
    lines.close()
    net.close()


def close_layer(text_g, attn_g, out_g, ffn_t, dmod, gg, gs, cond8):
    low = jnp.bfloat16
    full = jnp.float32
    shape = jax.ShapeDtypeStruct
    V = VMEM_SPEC
    tr, tw = text_g.shape[-2], text_g.shape[-1] // 2
    ar, aw = attn_g.shape[-2], attn_g.shape[-1] // 3
    orow, ow = out_g.shape[-2:]
    fr, fw = ffn_t.shape[-2], ffn_t.shape[-1] // 2
    return pl.pallas_call(
        close_kernel,
        in_specs=[V] * 8,
        out_specs=[V] * 6,
        out_shape=[
            shape((2, tr, 4 * tw), full),
            shape((3, ar, 4 * aw), full),
            shape((orow, ow), full),
            shape((2, fr, 4 * fw), full),
            shape((32, 4 * D), full),
            shape((16, D), full),
        ],
        scratch_shapes=[
            *chain_scratch(True, (1, tr), 2 * tw),
            *chain_scratch(True, (1, ar), 3 * aw),
            *chain_scratch(False, orow, ow),
            pltpu.VMEM((2, tr, 4 * tw), low),
            pltpu.VMEM((3, ar, 4 * aw), low),
            pltpu.VMEM((2, fr, 4 * fw), low),
            pltpu.VMEM((1, 4, tr, 2 * tw), low),
            pltpu.VMEM((1, 4, ar, 3 * aw), low),
            pltpu.VMEM((orow, ow), low),
            pltpu.VMEM((orow, ow), low),
            pltpu.SemaphoreType.DMA((2,)),
            pltpu.VMEM((4, CHIPS, 8, 2 * D + cond8.shape[1]), low),
            pltpu.VMEM((4, CHIPS, 8, 2 * D + cond8.shape[1]), low),
            pltpu.SemaphoreType.DMA((16,)),
            pltpu.VMEM((16, D), full),
            pltpu.VMEM((5, 16, D), full),
            pltpu.SemaphoreType.DMA((4,)),
            pltpu.VMEM((128, 512), full),
            *net_scratch(40),
        ],
        compiler_params=pltpu.CompilerParams(
            collective_id=2, has_side_effects=True, vmem_limit_bytes=60 * 1024 * 1024
        ),
        cost_estimate=pl.CostEstimate(
            flops=1_000_000, bytes_accessed=400_000_000, transcendentals=0
        ),
    )(text_g, attn_g, out_g, ffn_t, dmod, gg, gs, cond8)


def back_kernel(
    dh2_ref, fo_ref, x1_ref, branch_ref, cot_ref, w_ref, mod_ref, seg_ref, gain_ref, tok_ref,
    sr_ref, gs_ref, *rest,
):
    late, rest = rest[:LATE], rest[LATE:]
    places, rest = rest[-LATE - 1 : -1], rest[: -LATE - 1] + rest[-1:]
    loads = [
        pltpu.make_async_copy(src, dst, rest[-1].at[i])
        for i, (src, dst) in enumerate(zip(late, places))
    ]
    back_body(
        dh2_ref, fo_ref, x1_ref, branch_ref, cot_ref, w_ref, mod_ref, seg_ref, gain_ref, tok_ref,
        *places, sr_ref, gs_ref, *rest[:-1], loads,
    )


LATE = 17


def back_body(
    dh2_ref, fo_ref, x1_ref, branch_ref, cot_ref, w_ref, mod_ref, seg_ref, gain_ref, tok_ref,
    ow_ref, aw_ref, qr_ref, kr_ref, v_ref, tr_ref, tv_ref, cross_ref, q_ref, k_ref, tk_ref,
    iq_ref, ik_ref, it_ref, cos_ref, sin_ref, sc_ref, sr_ref, gs_ref, ffn_g, down_g,
    block_o, token_o, db_ref, dqkv_o, dtkv_o, dmod_o, gg_o, gs_o, ffn_o, down_o,
    dx_s, dc_s, dqf, dkf, dtf, part_s, sums, tsums, buf_a, far_a, buf_b, far_b, buf_c, far_c,
    fm, fa, ft, fs, dm, da, dt_c, ds_, f_keep, d_keep, keep_sem, send_sems, recv_sems, loads,
):
    low = jnp.bfloat16
    full = jnp.float32
    net = Net(send_sems, recv_sems)
    meet_all(net)
    plane = lax.axis_index("bucket")
    chip = net.me // 2
    ffn = Chain(net, ffn_g, fm, fa, ft, fs, True)
    down = Chain(net, down_g, dm, da, dt_c, ds_, False)
    ffn.core_start(f_keep, keep_sem.at[0])
    down.core_start(d_keep, keep_sem.at[1])
    for c in loads:
        c.start()

    def rows_of(ref):
        half = ROW // 2
        return lambda j, i: ref[pl.ds(j * ROW + i * half, half), :].astype(full)

    middle, finish = collect4(net, rows_of(dh2_ref), buf_a, far_a)
    middle()
    ffn.core_finish()
    ffn.step(0)
    down.core_finish()
    down.step(0)
    half = ROW // 2
    for i in (0, 1):
        dx_s[pl.ds(i * half, half), :] = finish(i)
    part_s[pl.ds(0, ROW), :] = dx_s[...]
    block = 32
    weight = w_ref[0:1, 0:1]

    def second_norm(at):
        x1 = x1_ref[at, :]
        inverse = lax.rsqrt(jnp.mean(x1 * x1, axis=-1, keepdims=True) + EPS)
        scale = pick_rows(mod_ref[:, :D], seg_ref[at, :], 4)
        return x1 * inverse, inverse, scale

    def to_branch(b, _):
        at = pl.ds(pl.multiple_of(b * block, block), block)
        normed, inverse, scale = second_norm(at)
        dn = dx_s[at, :] * gain_ref[1:2, :] * (1.0 + scale)
        back = inverse * (dn - normed * jnp.mean(dn * normed, axis=-1, keepdims=True))
        dx = cot_ref[at, :].astype(full) * weight + back
        dx_s[at, :] = dx
        gate = jnp.tanh(pick_rows(mod_ref[:, D:], seg_ref[at, :], 0))
        db_ref[0, at, :] = (dx * gate).astype(low)
        return 0

    lax.fori_loop(0, ROW // block, to_branch, 0)
    bx, by = share4_start(net, db_ref)

    def by_image(value, seg, row, lo):
        for i in range(IMGS):
            dmod_o[row + i : row + i + 1, lo : lo + D] += jnp.sum(
                jnp.where(seg == i, value, 0.0), axis=0, keepdims=True
            )

    dmod_o[...] = jnp.zeros(dmod_o.shape, full)
    gg_o[...] = jnp.zeros(gg_o.shape, full)

    def second_sums(b, _):
        at = pl.ds(pl.multiple_of(b * block, block), block)
        normed, inverse, scale = second_norm(at)
        seg = seg_ref[at, :]
        dh = part_s[at, :] * normed
        gg_o[1:2, :] += jnp.sum(dh * (1.0 + scale), axis=0, keepdims=True)
        by_image(dh * gain_ref[1:2, :], seg, 4, 0)
        gate = jnp.tanh(pick_rows(mod_ref[:, D:], seg, 0))
        by_image(dx_s[at, :] * branch_ref[at, :] * (1.0 - gate * gate), seg, 0, D)
        return 0

    lax.fori_loop(0, ROW // block, second_sums, 0)
    far = share4_relay(net, db_ref, bx, by)
    middle_b, finish_b = collect4(net, rows_of(fo_ref), buf_b, far_b)
    gs_o[...] = jnp.zeros(gs_o.shape, full)
    for c in loads:
        c.wait()
    cap = IMGS * TXT

    def attention_row(j, _):
        @pl.when(j == 3)
        def _():
            for c in far:
                c.wait_recv()

        @pl.when(j == 1)
        def _():
            ffn.step(1)
            down.step(1)

        @pl.when(j == 3)
        def _():
            ffn.step(2)
            down.step(2)

        rows = pl.ds(pl.multiple_of(j * ROW, ROW), ROW)
        text = pl.ds(pl.multiple_of(j * cap, cap), cap)
        dc_s[...] = dot_t(db_ref[j], ow_ref[...])
        dqv, dkv, dtv = dqf.at[rows], dkf.at[rows], dtf.at[text]
        attend_back_kernel(
            qr_ref.at[rows], kr_ref.at[rows], v_ref.at[rows], tr_ref.at[text], tv_ref.at[text],
            dc_s, cross_ref.at[rows], q_ref.at[rows], k_ref.at[rows], tk_ref.at[text],
            iq_ref.at[rows], ik_ref.at[rows], it_ref.at[text], cos_ref.at[rows], sin_ref.at[rows],
            sc_ref.at[rows], sr_ref.at[j], gs_ref,
            dqv, dkv, dqkv_o.at[rows, pl.ds(2 * HW, HW)], dtv, dtkv_o.at[text, pl.ds(HW, HW)], gs_o,
        )
        sums[0, :, rows] = row_sums(
            dqv[...] * (q_ref[rows, :] * iq_ref[rows, :]),
            dkv[...] * (k_ref[rows, :] * ik_ref[rows, :]),
        )
        tsums[0, :, text] = row_sums(dtv[...] * (tk_ref[text, :] * it_ref[text, :]), None)
        return 0

    lax.fori_loop(0, CHIPS, attention_row, 0)
    sum_io = []
    for i, m in ((1, 2), (2, 4), (3, 6)):
        sum_io.append(net.send(sums.at[0], sums.at[i], m))
        sum_io.append(net.send(tsums.at[0], tsums.at[i], m))
    middle_b()
    for i in (0, 1):
        part_s[pl.ds(i * half, half), :] = finish_b(i)

    def block_rows(b, _):
        at = pl.ds(pl.multiple_of(b * block, block), block)
        seg = seg_ref[at, :]
        gate = jnp.tanh(pick_rows(mod_ref[:, D:], seg, 4))
        out = part_s[at, :]
        block_o[at, :] = (x1_ref[at, :] + gate * out).astype(low)
        grad = cot_ref[at, :].astype(full) * weight
        by_image(grad * out * (1.0 - gate * gate), seg, 4, D)
        return 0

    for c in sum_io:
        c.wait_recv()
    for j in range(CHIPS):
        rows = pl.ds(j * ROW, ROW)
        text = pl.ds(j * cap, cap)
        total = sums[0, :, rows]
        words = tsums[0, :, text]
        for i in (1, 2, 3):
            total = total + sums[i, :, pl.ds((j ^ i) * ROW, ROW)]
            words = words + tsums[i, :, pl.ds((j ^ i) * cap, cap)]
        mean = jnp.transpose(total / D)
        iq, ik, it = iq_ref[rows, :], ik_ref[rows, :], it_ref[text, :]
        dqkv_o[rows, :HW] = (iq * (dqf[rows, :] - q_ref[rows, :] * iq * mean[:, 0:1])).astype(low)
        dqkv_o[rows, HW : 2 * HW] = (ik * (dkf[rows, :] - k_ref[rows, :] * ik * mean[:, 4:5])).astype(low)
        mean = jnp.transpose(words / D)
        dtkv_o[text, :HW] = (it * (dtf[text, :] - tk_ref[text, :] * it * mean[:, 0:1])).astype(low)

    lax.fori_loop(0, ROW // block, block_rows, 0)
    wide = 256

    def first_grad(n, _):
        at = pl.ds(pl.multiple_of(n * wide, wide), wide)
        part_s[:, at] = dot_t(dqkv_o[...], aw_ref[at, :])
        return 0

    lax.fori_loop(0, D // wide, first_grad, 0)
    middle_c, finish_c = collect4(net, rows_of(part_s), buf_c, far_c)
    ffn.finish()
    middle_c()

    def ffn_cast(i, _):
        ffn_o[0, i] = ft[0, i].astype(low)
        return 0

    lax.fori_loop(0, 4, ffn_cast, 0)
    down.finish()
    down_o[...] = dt_c[...].astype(low)
    gate = jnp.tanh(gs_ref[5:6, :])
    gs_o[3:4, :] = gs_o[3:4, :] * (1.0 - gate * gate)
    for i in (0, 1):
        part_s[pl.ds(i * half, half), :] = finish_c(i)

    def first_rows(b, _):
        at = pl.ds(pl.multiple_of(b * block, block), block)
        x = tok_ref[at, :].astype(full)
        inverse = lax.rsqrt(jnp.mean(x * x, axis=-1, keepdims=True) + EPS)
        normed = x * inverse
        seg = seg_ref[at, :]
        scale = pick_rows(mod_ref[:, :D], seg, 0)
        dh = part_s[at, :]
        gg_o[0:1, :] += jnp.sum(dh * normed * (1.0 + scale), axis=0, keepdims=True)
        by_image(dh * normed * gain_ref[0:1, :], seg, 0, 0)
        dn = dh * gain_ref[0:1, :] * (1.0 + scale)
        token_o[at, :] = dx_s[at, :] + inverse * (
            dn - normed * jnp.mean(dn * normed, axis=-1, keepdims=True)
        )
        return 0

    lax.fori_loop(0, ROW // block, first_rows, 0)
    ffn.close()
    down.close()
    net.close()


def back_layer(early, late, ffn_g, down_g):
    low = jnp.bfloat16
    full = jnp.float32
    shape = jax.ShapeDtypeStruct
    V = VMEM_SPEC
    cap = IMGS * TXT
    fr, fw = ffn_g.shape[-2], ffn_g.shape[-1] // 2
    dr, dw = down_g.shape[-2:]
    tok = CHIPS * ROW
    reduce_scratch = [pltpu.VMEM((5, ROW, D), low), pltpu.VMEM((2, ROW // 2, D), low)]
    return pl.pallas_call(
        back_kernel,
        in_specs=[V] * len(early) + [ANY_SPEC] * (LATE + 2),
        out_specs=[V] * 10,
        out_shape=[
            shape((ROW, D), low),
            shape((ROW, D), full),
            shape((CHIPS, ROW, D), low),
            shape((tok, 3 * HW), low),
            shape((CHIPS * cap, 2 * HW), low),
            shape((8, 2 * D), full),
            shape((8, D), full),
            shape((8, HW), full),
            shape((1, 4, fr, 2 * fw), low),
            shape((dr, dw), low),
        ],
        scratch_shapes=[
            pltpu.VMEM((ROW, D), full),
            pltpu.VMEM((ROW, HW), full),
            pltpu.VMEM((tok, HW), full),
            pltpu.VMEM((tok, HW), full),
            pltpu.VMEM((CHIPS * cap, HW), full),
            pltpu.VMEM((tok, D), full),
            pltpu.VMEM((CHIPS, 8, tok), full),
            pltpu.VMEM((CHIPS, 8, CHIPS * cap), full),
            *reduce_scratch, *reduce_scratch, *reduce_scratch,
            *chain_scratch(True, (1, fr), 2 * fw),
            *chain_scratch(False, dr, dw),
            pltpu.VMEM((1, 4, 4, fr, 2 * fw), low),
            pltpu.VMEM((4, dr, dw), low),
            pltpu.SemaphoreType.DMA((2,)),
            *net_scratch(48),
            *[pltpu.VMEM(v.shape, v.dtype) for v in late],
            pltpu.SemaphoreType.DMA((LATE,)),
        ],
        compiler_params=pltpu.CompilerParams(
            collective_id=3, has_side_effects=True, vmem_limit_bytes=63 * 1024 * 1024
        ),
        cost_estimate=pl.CostEstimate(
            flops=10_000_000_000, bytes_accessed=400_000_000, transcendentals=0
        ),
    )(*early, *late, ffn_g, down_g)


def row_spec(rows, width):
    return pl.BlockSpec((rows, width), lambda i: (i, 0))


def forward_kernel(
    q_ref, k_ref, v_ref, iq_ref, ik_ref, cos_ref, sin_ref, tk_ref, it_ref, tv_ref, sc_ref, sr_ref,
    gs_ref, mod_ref, seg_ref, gain_ref, tok_ref, cot_ref, w_ref, outw_ref, ffnw_ref, downw_ref,
    comb_o, cross_o, qr_o, kr_o, tr_o, branch_o, x1_o, h_o, df_o, ow_o, fw_o, dw_o,
    part_s, buf, far, f_own, d_own, local_sems, send_sems, recv_sems,
):
    low = jnp.bfloat16
    full = jnp.float32
    net = Net(send_sems, recv_sems)
    net.meet((1, 2, 4, 6))
    me = net.me
    chip = me // 2
    width = fw_o.shape[1] // 2
    rows = outw_ref.shape[0]

    def local(src, dst, i):
        copy = pltpu.make_async_copy(src, dst, local_sems.at[i])
        copy.start()
        return copy

    def own(ref, count):
        return ref.at[pl.ds(pl.multiple_of((me % 2) * count, count), count), :]

    out_here = local(outw_ref, own(ow_o, rows), 0)
    out_core = net.send(outw_ref, own(ow_o, rows), 1)
    down_rows = downw_ref.shape[0]
    down_here = local(downw_ref, d_own, 1)
    down_core = net.send(downw_ref, own(dw_o, down_rows), 1)
    f_rows = ffnw_ref.shape[1]
    place = [2]

    def stage(src, dst):
        i = place[0]
        place[0] += 1
        return local(src, f_own.at[:, pl.ds((i - 2) * width, width)], i)

    f_here, f_core, f_away, f_pass = spread(net, ffnw_ref, fw_o, width, stage)
    f_x, f_y = f_away(2), f_away(4)
    block = 32
    weight = w_ref[0:1, 0:1]

    def ffn_grad(b, _):
        at = pl.ds(pl.multiple_of(b * block, block), block)
        gate = jnp.tanh(pick_rows(mod_ref[:, D:], seg_ref[at, :], 4))
        df_o[0, at, :] = (cot_ref[at, :].astype(full) * weight * gate).astype(low)
        return 0

    lax.fori_loop(0, ROW // block, ffn_grad, 0)
    out_here.wait()
    out_core.wait_recv()
    cap = IMGS * TXT

    def attention_row(i, _):
        j = 3 - i
        at = pl.ds(pl.multiple_of(j * ROW, ROW), ROW)
        text = pl.ds(pl.multiple_of(j * cap, cap), cap)
        attend_kernel(
            q_ref.at[at], k_ref.at[at], v_ref.at[at], iq_ref.at[at], ik_ref.at[at],
            cos_ref.at[at], sin_ref.at[at], tk_ref.at[text], it_ref.at[text], tv_ref.at[text],
            sc_ref.at[at], sr_ref.at[j], gs_ref,
            comb_o.at[at], cross_o.at[at], qr_o.at[at], kr_o.at[at], tr_o.at[text],
        )
        part_s[at, :] = jnp.dot(comb_o[at, :], ow_o[...], preferred_element_type=full)
        return 0

    lax.fori_loop(0, CHIPS, attention_row, 0)
    half = ROW // 2
    middle, finish = collect4(
        net, lambda j, i: part_s[pl.ds(j * ROW + i * half, half), :], buf, far
    )
    f_far = f_away(6)
    dx, dy = share4_start(net, df_o)

    down_here.wait()
    down_out = local(d_own, own(dw_o, down_rows), 4)
    for c in f_here:
        c.wait()
    f_out = local(f_own, fw_o.at[pl.ds(pl.multiple_of(me * f_rows, f_rows), f_rows), :], 5)
    middle()
    for i in (0, 1):
        branch_o[pl.ds(i * half, half), :] = finish(i)

    def second(b, _):
        at = pl.ds(pl.multiple_of(b * block, block), block)
        seg = seg_ref[at, :]
        gate = jnp.tanh(pick_rows(mod_ref[:, D:], seg, 0))
        x1 = tok_ref[at, :].astype(full) + gate * branch_o[at, :]
        x1_o[at, :] = x1
        normed = x1 * lax.rsqrt(jnp.mean(x1 * x1, axis=-1, keepdims=True) + EPS)
        scale = pick_rows(mod_ref[:, :D], seg, 4)
        h_o[0, at, :] = (normed * gain_ref[1:2, :] * (1.0 + scale)).astype(low)
        return 0

    lax.fori_loop(0, ROW // block, second, 0)
    hx, hy = share4_start(net, h_o)
    last = [f_pass(f_x, 2), f_pass(f_y, 4)]
    last += share4_relay(net, df_o, dx, dy)
    last += share4_relay(net, h_o, hx, hy)
    last.append(f_pass(f_far, 6))
    for c in last + [down_core] + f_core:
        c.wait_recv()
    down_out.wait()
    f_out.wait()
    net.close()


def forward_layer(*args):
    low = jnp.bfloat16
    full = jnp.float32
    shape = jax.ShapeDtypeStruct
    V = VMEM_SPEC
    cap = IMGS * TXT
    tok = CHIPS * ROW
    out_w, ffn_w, down_w = args[-3:]
    width = ffn_w.shape[2] // CHIPS
    return pl.pallas_call(
        forward_kernel,
        in_specs=[V] * (len(args) - 3) + [ANY_SPEC] * 3,
        out_specs=[V] * 10 + [ANY_SPEC] * 2,
        out_shape=[
            shape((tok, HW), low),
            shape((tok, HW), full),
            shape((tok, HW), low),
            shape((tok, HW), low),
            shape((CHIPS * cap, HW), low),
            shape((ROW, D), full),
            shape((ROW, D), full),
            shape((CHIPS, ROW, D), low),
            shape((CHIPS, ROW, D), low),
            shape((2 * out_w.shape[0], D), low),
            shape((D, 2 * width), low),
            shape((2 * down_w.shape[0], D), low),
        ],
        scratch_shapes=[
            pltpu.VMEM((tok, D), full),
            pltpu.VMEM((5, ROW, D), low),
            pltpu.VMEM((2, ROW // 2, D), low),
            pltpu.VMEM((ffn_w.shape[1], 2 * width), low),
            pltpu.VMEM(down_w.shape, low),
            pltpu.SemaphoreType.DMA((6,)),
            *net_scratch(40),
        ],
        compiler_params=pltpu.CompilerParams(
            collective_id=4, has_side_effects=True, vmem_limit_bytes=56 * 1024 * 1024
        ),
        cost_estimate=pl.CostEstimate(
            flops=5_000_000_000, bytes_accessed=200_000_000, transcendentals=0
        ),
    )(*args)


def per_device(
    tokens,
    cond,
    text,
    segments,
    positions,
    counts,
    ada_weight,
    ada_bias,
    gains,
    attn_weight,
    out_weight,
    text_weight,
    ffn_weight,
    down_weight,
    cotangent,
):
    low = jnp.bfloat16
    full = jnp.float32
    plane = lax.axis_index("bucket")
    slot = lax.axis_index("fsdp")
    core = slot % 2
    chip = slot // 2
    ff = ffn_weight.shape[2] // CHIPS

    gain_pad = lax.dynamic_update_slice_in_dim(
        jnp.zeros((8, D), full), jnp.pad(gains.astype(full), ((0, 2), (0, 0))), slot * 192, axis=1
    )
    bias = lax.dynamic_update_slice_in_dim(
        jnp.zeros((ada_weight.shape[1],), full), ada_bias.astype(full), slot * ada_bias.shape[0], 0
    )
    bias_pad = jnp.repeat(bias.reshape(2, 3072), 4, axis=0)
    cond8 = jnp.concatenate([cond[0], cond[0]], axis=0)
    seg = segments[0]
    idx = jnp.concatenate([seg[None, :], positions[0], jnp.zeros((5, ROW), jnp.int32)], axis=0)
    (
        mod, gain_f, h_rows, idx_all, attn_w, text_rows, query, keyed, valued, text_keys, text_vals,
        inv_qk, inv_t,
    ) = open_layer(
        cond8, gain_pad, bias_pad, ada_weight, tokens[0],
        seg[:, None], idx, attn_weight, text_weight, text[0],
    )
    h_all = h_rows.reshape(CHIPS * ROW, D)
    text_all = text_rows.reshape(CHIPS * IMGS * TXT, -1)
    inv_qk = jnp.stack([inv_qk[0], inv_qk[4]])[:, :, None]
    inv_t = inv_t[0][:, None]
    seg_all = idx_all[:, 0]
    pos_all = idx_all[:, 1:3]
    seg_col = seg_all.reshape(CHIPS * ROW, 1)
    seg_row = seg_all.reshape(CHIPS, 1, ROW)
    lane = jnp.arange(128, dtype=jnp.int32)
    quarter = HDIM // 4
    freq = (10000.0 ** (-jnp.arange(quarter, dtype=full) / quarter))[lane % quarter]
    where_row = ((lane // 32) % 2 == 0)[None, None, :]
    pos_lane = jnp.where(where_row, pos_all[:, 0, :, None], pos_all[:, 1, :, None]).astype(full)
    angle = (pos_lane * freq[None, None, :]).reshape(CHIPS * ROW, 128)
    cosine = jnp.cos(angle)
    sine = jnp.where(((lane // quarter) % 2 == 0)[None, :], -1.0, 1.0) * jnp.sin(angle)

    gain_s = lax.dynamic_slice_in_dim(gain_f, chip * HW, HW, axis=1)[:6]

    totals = counts.astype(full)
    here = jnp.sum(jnp.where(jnp.arange(totals.shape[0], dtype=jnp.int32) == plane, totals, 0.0))
    weight = lax.axis_size("bucket") * here / jnp.sum(totals)
    weight_row = jnp.full((1, 128), weight, full)
    (
        comb, cross_out, q_rot, k_rot, text_rot, branch, x_one, h_two_rows, d_ffn_rows, out_w, ffn_w,
        down_w,
    ) = forward_layer(
        query, keyed, valued, inv_qk[0], inv_qk[1], cosine, sine, text_keys, inv_t, text_vals,
        seg_col, seg_row, gain_s, mod, seg[:, None], gain_f, tokens[0], cotangent[0], weight_row,
        out_weight, ffn_weight, down_weight,
    )
    h_two_all = h_two_rows.reshape(CHIPS * ROW, D)
    d_ffn_all = d_ffn_rows.reshape(CHIPS * ROW, D)
    both = mult(h_two_all, ffn_w)
    gate_pre = both[:, :ff]
    upper = both[:, ff:]
    d_hidden = dot_t(d_ffn_all, down_w)
    sigm = jax.nn.sigmoid(gate_pre)
    silu_pre = gate_pre * sigm
    hidden = (silu_pre * upper).astype(low)
    d_pre = (d_hidden * upper * sigm * (1.0 + gate_pre * (1.0 - sigm))).astype(low)
    d_up = (d_hidden * silu_pre).astype(low)
    d_both = jnp.concatenate([d_pre, d_up], axis=1)
    d_h_two = dot_t(d_both, ffn_w).astype(low)
    ffn_out = mult(hidden, down_w).astype(low)
    g_down = t_dot(hidden, d_ffn_all).astype(low)
    g_ffn = t_dot(h_two_all, d_both).astype(low)

    (
        block_out, token_grad, d_branch_rows, d_qkv, d_text, d_mod, gg_full, gg_slice, ffn_sum, down_sum,
    ) = back_layer(
        [
            d_h_two, ffn_out, x_one, branch, cotangent[0], weight_row, mod,
            seg[:, None], gain_f, tokens[0], seg_row, gain_s,
        ],
        [
            out_w, attn_w, q_rot, k_rot, valued, text_rot, text_vals, cross_out, query, keyed,
            text_keys, inv_qk[0], inv_qk[1], inv_t, cosine, sine, seg_col,
        ],
        g_ffn.reshape(1, 4, 4, 2, 48, 2 * ff),
        g_down.reshape(4, 2, 128, D),
    )
    d_branch_all = d_branch_rows.reshape(CHIPS * ROW, D)
    g_text = t_dot(text_all, d_text).astype(low)
    g_attn = t_dot(h_all, d_qkv).astype(low)
    g_out = t_dot(comb, d_branch_all).astype(low)
    s_down = to_row_owner(down_sum)
    s_text, s_attn, s_out, s_ffn, s_ada_w, small = close_layer(
        g_text.reshape(1, 4, 4, 2, 128, 2 * HW),
        g_attn.reshape(1, 4, 4, 2, 48, 3 * HW),
        g_out.reshape(4, 2, 48, D),
        ffn_sum,
        d_mod,
        gg_full,
        gg_slice,
        cond8,
    )
    rank = plane * 8 + slot
    s_gains = lax.dynamic_slice_in_dim(small[:6], rank * 48, 48, axis=1)
    s_ada_b = lax.dynamic_slice_in_dim(small[8:12].reshape(-1), rank * 192, 192, axis=0)
    return (
        block_out[None],
        token_grad[None],
        s_ada_w,
        s_ada_b,
        s_gains,
        s_attn,
        s_out,
        s_text,
        s_ffn,
        s_down,
    )


def solution(mesh):
    in_specs = (
        P(("bucket", "fsdp"), None, None),
        P(("bucket", "fsdp"), None, None),
        P(("bucket", "fsdp"), None, None),
        P(("bucket", "fsdp"), None),
        P(("bucket", "fsdp"), None, None),
        P(),
        P("fsdp", None),
        P("fsdp"),
        P(None, "fsdp"),
        P(None, "fsdp", None),
        P("fsdp", None),
        P(None, "fsdp", None),
        P(None, "fsdp", None),
        P("fsdp", None),
        P(("bucket", "fsdp"), None, None),
    )
    out_specs = (
        P(("bucket", "fsdp"), None, None),
        P(("bucket", "fsdp"), None, None),
        P(("bucket", "fsdp"), None),
        P(("bucket", "fsdp")),
        P(None, ("bucket", "fsdp")),
        P(None, ("bucket", "fsdp"), None),
        P(("bucket", "fsdp"), None),
        P(None, ("bucket", "fsdp"), None),
        P(None, ("bucket", "fsdp"), None),
        P(("bucket", "fsdp"), None),
    )
    fast = mesh.shape["fsdp"] == 8 and mesh.shape["bucket"] == 4
    return jax.shard_map(
        per_device if fast else per_device_general, mesh=mesh, in_specs=in_specs, out_specs=out_specs, check_vma=False
    )
```

```python
import jax
import jax.numpy as jnp
import numpy as np
from jax import lax
from jax.experimental import pallas as pl
from jax.experimental.pallas import tpu as pltpu
from jax.sharding import PartitionSpec as P

D = 1536
HEADS = 24
HDIM = 64
IMGS = 4
TXT = 64


EPS = 1e-06
NEGATIVE = -1e30
HIGH = lax.Precision.HIGHEST


def silu(v):
    return v * jax.nn.sigmoid(v)


def norm_rows(v):
    inverse = lax.rsqrt(jnp.mean(v * v, axis=-1, keepdims=True) + EPS)
    return (v * inverse, inverse)


def norm_back(grad, normed, inverse):
    return inverse * (grad - normed * jnp.mean(grad * normed, axis=-1, keepdims=True))


def rotary_tables(pos):
    quarter = HDIM // 4
    freq = 10000.0 ** (-jnp.arange(quarter, dtype=jnp.float32) / quarter)
    angle = jnp.transpose(pos.astype(jnp.float32), (1, 0))[:, :, None] * freq[None, None, :]
    return (jnp.cos(angle), jnp.sin(angle))


def rotate(v, cosine, sine):
    rows = v.shape[0]
    parts = v.reshape(rows, HEADS, 2, 2, HDIM // 4)
    first = parts[:, :, :, 0]
    second = parts[:, :, :, 1]
    cosine = cosine[:, None]
    sine = sine[:, None]
    turned = jnp.stack([first * cosine - second * sine, first * sine + second * cosine], axis=3)
    return turned.reshape(rows, HEADS * HDIM)


def to_pairs(v):
    return jnp.transpose(v.reshape(v.shape[0], HEADS // 2, 2 * HDIM), (1, 0, 2))


def from_pairs(v):
    return jnp.transpose(v, (1, 0, 2)).reshape(v.shape[1], HEADS * HDIM)


def pair_scores(query, keys):
    q_heads = query.reshape(query.shape[0], 2, HDIM)
    k_heads = keys.reshape(keys.shape[0], 2, HDIM)
    return jnp.einsum(
        "rhd,khd->hrk", q_heads, k_heads, preferred_element_type=jnp.float32
    ) * HDIM ** (-0.5)


def attend_forward(q_b, k_b, v_b, allowed):

    def one_pair(item):
        query, keys, values = item
        scores = jnp.where(allowed[None], pair_scores(query, keys), NEGATIVE)
        top = jnp.max(scores, axis=-1, keepdims=True)
        expo = jnp.exp(scores - top)
        total = jnp.sum(expo, axis=-1, keepdims=True)
        probs = (expo / total).astype(jnp.bfloat16)
        result = jnp.einsum(
            "hrk,khd->rhd",
            probs,
            values.reshape(values.shape[0], 2, HDIM),
            preferred_element_type=jnp.float32,
        )
        return (result.reshape(query.shape[0], 2 * HDIM), (top + jnp.log(total))[..., 0])

    outputs, saved = lax.map(one_pair, (to_pairs(q_b), to_pairs(k_b), to_pairs(v_b)))
    return (from_pairs(outputs), saved)


def attend_back(q_b, k_b, v_b, saved, grad_b, allowed):

    def one_pair(item):
        query, keys, values, lse_pair, grad = item
        rows = query.shape[0]
        count = keys.shape[0]
        scores = jnp.where(allowed[None], pair_scores(query, keys), NEGATIVE)
        probs = jnp.exp(scores - lse_pair[..., None])
        probs_b = probs.astype(jnp.bfloat16)
        grad_heads = grad.reshape(rows, 2, HDIM)
        dprob = jnp.einsum(
            "rhd,khd->hrk",
            grad_heads,
            values.reshape(count, 2, HDIM),
            preferred_element_type=jnp.float32,
        )
        dscore = (probs * (dprob - jnp.sum(probs * dprob, axis=-1, keepdims=True))).astype(
            jnp.bfloat16
        )
        factor = HDIM ** (-0.5)
        dquery = (
            jnp.einsum(
                "hrk,khd->rhd",
                dscore,
                keys.reshape(count, 2, HDIM),
                preferred_element_type=jnp.float32,
            )
            * factor
        )
        dkeys = (
            jnp.einsum(
                "hrk,rhd->khd",
                dscore,
                query.reshape(rows, 2, HDIM),
                preferred_element_type=jnp.float32,
            )
            * factor
        )
        dvalues = jnp.einsum(
            "hrk,rhd->khd", probs_b, grad_heads, preferred_element_type=jnp.float32
        )
        return (
            dquery.reshape(rows, 2 * HDIM),
            dkeys.reshape(count, 2 * HDIM),
            dvalues.reshape(count, 2 * HDIM),
        )

    d_query, d_keys, d_values = lax.map(
        one_pair, (to_pairs(q_b), to_pairs(k_b), to_pairs(v_b), saved, to_pairs(grad_b))
    )
    return (from_pairs(d_query), from_pairs(d_keys), from_pairs(d_values))


def mult(left, right):
    return jnp.dot(left, right, preferred_element_type=jnp.float32)


def per_device_general(
    tokens,
    cond,
    text,
    segments,
    positions,
    counts,
    ada_weight,
    ada_bias,
    gains,
    attn_weight,
    out_weight,
    text_weight,
    ffn_weight,
    down_weight,
    cotangent,
):
    ada_w, ada_b, gain_rows, attn_w, out_w, text_w = (
        lax.all_gather(ada_weight, "fsdp", axis=0, tiled=True),
        lax.all_gather(ada_bias, "fsdp", axis=0, tiled=True),
        lax.all_gather(gains, "fsdp", axis=1, tiled=True),
        lax.all_gather(attn_weight, "fsdp", axis=1, tiled=True),
        lax.all_gather(out_weight, "fsdp", axis=0, tiled=True),
        lax.all_gather(text_weight, "fsdp", axis=1, tiled=True),
    )
    gain_f = gain_rows.astype(jnp.float32)
    x = tokens[0].astype(jnp.float32)
    seg = segments[0]
    cosine, sine = rotary_tables(positions[0])
    text_b = text[0]
    cond_act = silu(cond[0].astype(jnp.float32)).astype(jnp.bfloat16)
    mod = mult(cond_act, ada_w) + ada_b.astype(jnp.float32)[None, :]
    pick = (seg[:, None] == jnp.arange(IMGS, dtype=jnp.int32)[None, :]).astype(jnp.float32)
    per_token = jnp.dot(pick, mod, precision=HIGH)
    scale1 = per_token[:, :D]
    gate1 = per_token[:, D : 2 * D]
    scale2 = per_token[:, 2 * D : 3 * D]
    gate2 = per_token[:, 3 * D :]
    normed1, inverse1 = norm_rows(x)
    h_one = (normed1 * gain_f[0] * (1.0 + scale1)).astype(jnp.bfloat16)
    query = mult(h_one, attn_w[0])
    keyed = mult(h_one, attn_w[1])
    valued = mult(h_one, attn_w[2]).astype(jnp.bfloat16)
    q_norm, q_inv = norm_rows(query)
    k_norm, k_inv = norm_rows(keyed)
    q_rot = rotate(q_norm * gain_f[2], cosine, sine).astype(jnp.bfloat16)
    k_rot = rotate(k_norm * gain_f[3], cosine, sine).astype(jnp.bfloat16)
    text_keys = mult(text_b, text_w[0])
    text_vals = mult(text_b, text_w[1]).astype(jnp.bfloat16)
    t_norm, t_inv = norm_rows(text_keys)
    text_rot = (t_norm * gain_f[4]).astype(jnp.bfloat16)
    same = seg[:, None] == seg[None, :]
    owner = jnp.arange(IMGS * TXT, dtype=jnp.int32) // TXT
    mine = seg[:, None] == owner[None, :]
    self_out, self_lse = attend_forward(q_rot, k_rot, valued, same)
    cross_out, cross_lse = attend_forward(q_rot, text_rot, text_vals, mine)
    cross_gate = jnp.tanh(gain_f[5])
    comb = (self_out + cross_gate * cross_out).astype(jnp.bfloat16)
    branch = mult(comb, out_w)
    tanh_one = jnp.tanh(gate1)
    x_one = x + tanh_one * branch
    normed2, inverse2 = norm_rows(x_one)
    h_two = (normed2 * gain_f[1] * (1.0 + scale2)).astype(jnp.bfloat16)
    ffn_w, down_w = (
        lax.all_gather(ffn_weight, "fsdp", axis=1, tiled=True),
        lax.all_gather(down_weight, "fsdp", axis=0, tiled=True),
    )
    gate_pre = mult(h_two, ffn_w[0])
    upper = mult(h_two, ffn_w[1])
    sigm = jax.nn.sigmoid(gate_pre)
    silu_pre = gate_pre * sigm
    hidden = (silu_pre * upper).astype(jnp.bfloat16)
    ffn_out = mult(hidden, down_w)
    tanh_two = jnp.tanh(gate2)
    block_out = (x_one + tanh_two * ffn_out).astype(jnp.bfloat16)
    totals = counts.astype(jnp.float32)
    here = jnp.sum(
        jnp.where(
            jnp.arange(totals.shape[0], dtype=jnp.int32) == lax.axis_index("bucket"), totals, 0.0
        )
    )
    weight = lax.axis_size("bucket") * here / jnp.sum(totals)
    grad = cotangent[0].astype(jnp.float32) * weight
    back_ffn, back_down = (
        lax.all_gather(ffn_weight, "fsdp", axis=1, tiled=True),
        lax.all_gather(down_weight, "fsdp", axis=0, tiled=True),
    )
    d_gate2 = grad * ffn_out * (1.0 - tanh_two * tanh_two)
    d_ffn = (grad * tanh_two).astype(jnp.bfloat16)
    d_hidden = mult(d_ffn, back_down.T)
    g_down = mult(hidden.T, d_ffn)
    d_pre = (d_hidden * upper * sigm * (1.0 + gate_pre * (1.0 - sigm))).astype(jnp.bfloat16)
    d_up = (d_hidden * silu_pre).astype(jnp.bfloat16)
    d_h_two = mult(d_pre, back_ffn[0].T) + mult(d_up, back_ffn[1].T)
    g_ffn = jnp.stack([mult(h_two.T, d_pre), mult(h_two.T, d_up)])
    s_ffn, s_down = (
        lax.psum_scatter(g_ffn, ("bucket", "fsdp"), scatter_dimension=1, tiled=True),
        lax.psum_scatter(g_down, ("bucket", "fsdp"), scatter_dimension=0, tiled=True),
    )
    back_attn, back_out = (
        lax.all_gather(attn_weight, "fsdp", axis=1, tiled=True),
        lax.all_gather(out_weight, "fsdp", axis=0, tiled=True),
    )
    g_gain_one = jnp.sum(d_h_two * normed2 * (1.0 + scale2), axis=0)
    d_scale2 = d_h_two * normed2 * gain_f[1]
    d_x_one = grad + norm_back(d_h_two * gain_f[1] * (1.0 + scale2), normed2, inverse2)
    d_gate1 = d_x_one * branch * (1.0 - tanh_one * tanh_one)
    d_branch = (d_x_one * tanh_one).astype(jnp.bfloat16)
    d_comb = mult(d_branch, back_out.T)
    g_out = mult(comb.T, d_branch)
    g_gain_five = jnp.sum(d_comb * cross_out, axis=0) * (1.0 - cross_gate * cross_gate)
    d_self = d_comb.astype(jnp.bfloat16)
    d_cross = (d_comb * cross_gate).astype(jnp.bfloat16)
    dq_self, dk_self, dv_self = attend_back(q_rot, k_rot, valued, self_lse, d_self, same)
    dq_cross, dk_text, dv_text = attend_back(q_rot, text_rot, text_vals, cross_lse, d_cross, mine)
    d_q_norm = rotate(dq_self + dq_cross, cosine, -sine)
    g_gain_two = jnp.sum(d_q_norm * q_norm, axis=0)
    d_query = norm_back(d_q_norm * gain_f[2], q_norm, q_inv).astype(jnp.bfloat16)
    d_k_norm = rotate(dk_self, cosine, -sine)
    g_gain_three = jnp.sum(d_k_norm * k_norm, axis=0)
    d_keyed = norm_back(d_k_norm * gain_f[3], k_norm, k_inv).astype(jnp.bfloat16)
    d_valued = dv_self.astype(jnp.bfloat16)
    g_gain_four = jnp.sum(dk_text * t_norm, axis=0)
    d_text_keys = norm_back(dk_text * gain_f[4], t_norm, t_inv).astype(jnp.bfloat16)
    d_text_vals = dv_text.astype(jnp.bfloat16)
    g_text = jnp.stack([mult(text_b.T, d_text_keys), mult(text_b.T, d_text_vals)])
    d_h_one = (
        mult(d_query, back_attn[0].T)
        + mult(d_keyed, back_attn[1].T)
        + mult(d_valued, back_attn[2].T)
    )
    g_attn = jnp.stack([mult(h_one.T, d_query), mult(h_one.T, d_keyed), mult(h_one.T, d_valued)])
    g_gain_zero = jnp.sum(d_h_one * normed1 * (1.0 + scale1), axis=0)
    d_scale1 = d_h_one * normed1 * gain_f[0]
    token_grad = d_x_one + norm_back(d_h_one * gain_f[0] * (1.0 + scale1), normed1, inverse1)
    d_token_mod = jnp.concatenate([d_scale1, d_gate1, d_scale2, d_gate2], axis=1)
    d_mod = jnp.dot(pick.T, d_token_mod, precision=HIGH)
    g_ada_b = jnp.sum(d_mod, axis=0)
    g_ada_w = mult(cond_act.T, d_mod.astype(jnp.bfloat16))
    g_gains = jnp.stack(
        [g_gain_zero, g_gain_one, g_gain_two, g_gain_three, g_gain_four, g_gain_five]
    )
    s_ada_w, s_ada_b, s_gains, s_attn, s_out, s_text = (
        lax.psum_scatter(g_ada_w, ("bucket", "fsdp"), scatter_dimension=0, tiled=True),
        lax.psum_scatter(g_ada_b, ("bucket", "fsdp"), scatter_dimension=0, tiled=True),
        lax.psum_scatter(g_gains, ("bucket", "fsdp"), scatter_dimension=1, tiled=True),
        lax.psum_scatter(g_attn, ("bucket", "fsdp"), scatter_dimension=1, tiled=True),
        lax.psum_scatter(g_out, ("bucket", "fsdp"), scatter_dimension=0, tiled=True),
        lax.psum_scatter(g_text, ("bucket", "fsdp"), scatter_dimension=1, tiled=True),
    )
    return (
        block_out[None],
        token_grad[None],
        s_ada_w,
        s_ada_b,
        s_gains,
        s_attn,
        s_out,
        s_text,
        s_ffn,
        s_down,
    )


ROW = 128
CHIPS = 4
HW = D // CHIPS
PAIRS = HW // 128


def partner(u):
    lane = lax.broadcasted_iota(jnp.int32, u.shape, 1)
    ahead = pltpu.roll(u, u.shape[1] - 16, 1)
    behind = pltpu.roll(u, 16, 1)
    return jnp.where((lane // 16) % 2 == 0, ahead, behind)


def dot_t(a, b):
    return lax.dot_general(a, b, (((1,), (1,)), ((), ())), preferred_element_type=jnp.float32)


def dot_n(a, b):
    return lax.dot_general(a, b, (((1,), (0,)), ((), ())), preferred_element_type=jnp.float32)


def t_dot(a, b):
    return lax.dot_general(a, b, (((0,), (0,)), ((), ())), preferred_element_type=jnp.float32)


def softmax_of(scores, allowed):
    scores = jnp.where(allowed, scores * HDIM ** (-0.5), NEGATIVE)
    top = jnp.max(scores, axis=-1, keepdims=True)
    expo = jnp.exp(scores - top)
    return expo / jnp.sum(expo, axis=-1, keepdims=True)


def head_mask(v, head):
    lane = lax.broadcasted_iota(jnp.int32, v.shape, 1)
    return jnp.where((lane // HDIM) == head, v, jnp.zeros_like(v))


def masks_of(seg_col, seg_row, captions):
    same = seg_col == seg_row
    owner = lax.broadcasted_iota(jnp.int32, (seg_col.shape[0], captions), 1) // TXT
    return same, seg_col == owner


def attend_kernel(
    q_ref, k_ref, v_ref, iq_ref, ik_ref, cos_ref, sin_ref, tk_ref, it_ref, tv_ref, sc_ref, sr_ref,
    g_ref, comb_ref, cross_ref, qr_ref, kr_ref, tr_ref,
):
    same, mine = masks_of(sc_ref[...], sr_ref[...], tk_ref.shape[0])
    cosine = cos_ref[...]
    sine = sin_ref[...]
    low = jnp.bfloat16
    for pair in range(PAIRS):
        at = pl.ds(pair * 128, 128)
        qn = q_ref[:, at] * iq_ref[...] * g_ref[2:3, at]
        kn = k_ref[:, at] * ik_ref[...] * g_ref[3:4, at]
        qr = (qn * cosine + partner(qn) * sine).astype(low)
        kr = (kn * cosine + partner(kn) * sine).astype(low)
        tr = (tk_ref[:, at] * it_ref[...] * g_ref[4:5, at]).astype(low)
        qr_ref[:, at] = qr
        kr_ref[:, at] = kr
        tr_ref[:, at] = tr
        vv = v_ref[:, at]
        tv = tv_ref[:, at]
        self_out = jnp.zeros(qn.shape, jnp.float32)
        cross_out = jnp.zeros(qn.shape, jnp.float32)
        for head in range(2):
            qh = head_mask(qr, head)
            probs = softmax_of(dot_t(qh, kr), same).astype(low)
            self_out = self_out + head_mask(dot_n(probs, vv), head)
            probs = softmax_of(dot_t(qh, tr), mine).astype(low)
            cross_out = cross_out + head_mask(dot_n(probs, tv), head)
        cross_ref[:, at] = cross_out
        comb_ref[:, at] = (self_out + jnp.tanh(g_ref[5:6, at]) * cross_out).astype(low)


def attend_back_kernel(
    qr_ref, kr_ref, v_ref, tr_ref, tv_ref, dc_ref, cross_ref, q_ref, k_ref, tk_ref, iq_ref, ik_ref,
    it_ref, cos_ref, sin_ref, sc_ref, sr_ref, g_ref,
    dq_ref, dk_ref, dv_ref, dt_ref, dtv_ref, gg_ref,
):
    same, mine = masks_of(sc_ref[...], sr_ref[...], tk_ref.shape[0])
    cosine = cos_ref[...]
    sine = sin_ref[...]
    low = jnp.bfloat16
    factor = HDIM ** (-0.5)
    for pair in range(PAIRS):
        at = pl.ds(pair * 128, 128)
        qr = qr_ref[:, at]
        kr = kr_ref[:, at]
        vv = v_ref[:, at]
        tr = tr_ref[:, at]
        tv = tv_ref[:, at]
        dcomb = dc_ref[:, at]
        d_self = dcomb.astype(low)
        d_cross = (dcomb * jnp.tanh(g_ref[5:6, at])).astype(low)
        dq = jnp.zeros(dcomb.shape, jnp.float32)
        dk = jnp.zeros(dcomb.shape, jnp.float32)
        dv = jnp.zeros(dcomb.shape, jnp.float32)
        dt = jnp.zeros((tr.shape[0], 128), jnp.float32)
        dtv = jnp.zeros((tr.shape[0], 128), jnp.float32)
        for head in range(2):
            qh = head_mask(qr, head)
            probs = softmax_of(dot_t(qh, kr), same)
            grad = head_mask(d_self, head)
            dprob = dot_t(grad, vv)
            dscore = probs * (dprob - jnp.sum(probs * dprob, axis=-1, keepdims=True))
            dscore = dscore.astype(low)
            dq = dq + dot_n(dscore, head_mask(kr, head))
            dk = dk + t_dot(dscore, qh)
            dv = dv + t_dot(probs.astype(low), grad)
            probs = softmax_of(dot_t(qh, tr), mine)
            grad = head_mask(d_cross, head)
            dprob = dot_t(grad, tv)
            dscore = probs * (dprob - jnp.sum(probs * dprob, axis=-1, keepdims=True))
            dscore = dscore.astype(low)
            dq = dq + dot_n(dscore, head_mask(tr, head))
            dt = dt + t_dot(dscore, qh)
            dtv = dtv + t_dot(probs.astype(low), grad)
        dq = dq * factor
        dk = dk * factor
        dt = dt * factor
        dq = dq * cosine - partner(dq) * sine
        dk = dk * cosine - partner(dk) * sine
        q_norm = q_ref[:, at] * iq_ref[...]
        k_norm = k_ref[:, at] * ik_ref[...]
        t_norm = tk_ref[:, at] * it_ref[...]
        gg_ref[0:1, at] += jnp.sum(dq * q_norm, axis=0, keepdims=True)
        gg_ref[1:2, at] += jnp.sum(dk * k_norm, axis=0, keepdims=True)
        gg_ref[2:3, at] += jnp.sum(dt * t_norm, axis=0, keepdims=True)
        gg_ref[3:4, at] += jnp.sum(dcomb * cross_ref[:, at], axis=0, keepdims=True)
        dq = dq * g_ref[2:3, at]
        dk = dk * g_ref[3:4, at]
        dt = dt * g_ref[4:5, at]
        dq_ref[:, at] = dq
        dk_ref[:, at] = dk
        dv_ref[:, at] = dv.astype(low)
        dt_ref[:, at] = dt
        dtv_ref[:, at] = dtv.astype(low)


MESH_IDS = pl.DeviceIdType.MESH
VMEM_SPEC = pl.BlockSpec(memory_space=pltpu.VMEM)
ANY_SPEC = pl.BlockSpec(memory_space=pl.ANY)


def to_row_owner(block):
    pairs = [
        (a * 8 + b * 2 + k, b * 8 + a * 2 + k) for a in range(4) for b in range(4) for k in range(2)
    ]
    return lax.ppermute(block, ("bucket", "fsdp"), pairs).astype(jnp.float32)


class Net:
    def __init__(self, send_sems, recv_sems):
        self.me = lax.axis_index("fsdp")
        self.send_sems = send_sems
        self.recv_sems = recv_sems
        self.count = 0
        self.all = []

    def peer(self, mask):
        out = self.me
        for bit in (1, 2, 4):
            if mask & bit:
                out = out + bit * (1 - 2 * ((self.me // bit) % 2))
        return out

    def meet(self, masks):
        sem = pltpu.get_barrier_semaphore()
        for mask in masks:
            pl.semaphore_signal(
                sem, inc=1, device_id={"fsdp": self.peer(mask)}, device_id_type=MESH_IDS
            )
        pl.semaphore_wait(sem, len(masks))

    def send(self, src, dst, mask):
        assert self.count < self.send_sems.shape[0]
        copy = pltpu.make_async_remote_copy(
            src_ref=src,
            dst_ref=dst,
            send_sem=self.send_sems.at[self.count],
            recv_sem=self.recv_sems.at[self.count],
            device_id={"fsdp": self.peer(mask)},
            device_id_type=MESH_IDS,
        )
        self.count += 1
        copy.start()
        self.all.append(copy)
        return copy

    def close(self):
        for copy in self.all:
            copy.wait_send()


def net_scratch(count):
    return [pltpu.SemaphoreType.DMA((count,)), pltpu.SemaphoreType.DMA((count,))]


def share4_start(net, out):
    return net.send(out.at[0], out.at[1], 2), net.send(out.at[0], out.at[2], 4)


def share4_relay(net, out, by_x, by_y):
    half = out.shape[1] // 2
    top, bottom = pl.ds(0, half), pl.ds(half, half)
    by_x.wait_recv()
    first = net.send(out.at[1, top], out.at[3, top], 4)
    by_y.wait_recv()
    second = net.send(out.at[2, bottom], out.at[3, bottom], 2)
    return first, second


def collect4(net, part, buf, far):
    half = far.shape[1]
    rows = (pl.ds(0, half), pl.ds(half, half))
    low = jnp.bfloat16
    full = jnp.float32
    for i in (0, 1):
        buf[2, rows[i]] = part(3, i).astype(low)
    far_x = net.send(buf.at[2, rows[0]], far.at[0], 2)
    far_y = net.send(buf.at[2, rows[1]], far.at[1], 4)
    buf[0, rows[0]] = part(1, 0).astype(low)
    one_a = net.send(buf.at[0, rows[0]], buf.at[3, rows[0]], 2)
    buf[1, rows[1]] = part(2, 1).astype(low)
    two_b = net.send(buf.at[1, rows[1]], buf.at[4, rows[1]], 4)
    later = []

    def middle():
        far_x.wait_recv()
        buf[1, rows[0]] = (part(2, 0) + far[0].astype(full)).astype(low)
        later.append(net.send(buf.at[1, rows[0]], buf.at[4, rows[0]], 4))
        far_y.wait_recv()
        buf[0, rows[1]] = (part(1, 1) + far[1].astype(full)).astype(low)
        later.append(net.send(buf.at[0, rows[1]], buf.at[3, rows[1]], 2))

    def finish(i):
        (one_a, two_b)[i].wait_recv()
        later[i].wait_recv()
        return part(0, i) + buf[3, rows[i]].astype(full) + buf[4, rows[i]].astype(full)

    return middle, finish


def pick_rows(table, seg, first):
    out = table[first + IMGS - 1 : first + IMGS]
    for i in range(IMGS - 2, -1, -1):
        out = jnp.where(seg == i, table[first + i : first + i + 1], out)
    return out


def row_sums(a, b):
    ones = jnp.ones((8, a.shape[1]), jnp.float32)

    def one(v):
        return lax.dot_general(
            ones, v, (((1,), (1,)), ((), ())), precision=HIGH, preferred_element_type=jnp.float32
        )

    if b is None:
        return one(a)
    got = one(a)
    return jnp.where(lax.broadcasted_iota(jnp.int32, got.shape, 0) < 4, got, one(b))


class Lines:
    MASKS = (2, 4, 6)

    def __init__(self, net, src, dst, width, sems, local):
        self.net, self.src, self.dst, self.width, self.sems = net, src, dst, width, sems
        self.plane = lax.axis_index("bucket")
        self.chip = net.me // 2
        self.core = net.me % 2
        self.local = local
        self.ids = range(src.shape[0])

    def columns(self, c):
        return pl.ds(pl.multiple_of(c * self.width, 128), self.width)

    def lanes(self, i):
        return pl.ds(i * self.width, self.width)

    def away_start(self):
        own = self.dst.at[self.chip, self.core, self.plane]
        self.away = [
            self.net.send(
                self.src.at[i, self.plane, :, self.columns(self.net.peer(m) // 2)],
                own.at[:, self.lanes(i)],
                m,
            )
            for m in self.MASKS
            for i in self.ids
        ]

    def own_start(self):
        own = self.dst.at[self.chip, self.core]
        cuts = [self.src.at[i, :, :, self.columns(self.chip)] for i in self.ids]
        puts = [own.at[:, :, self.lanes(i)] for i in self.ids]
        self.ready = [self.net.send(a, b, 1) for a, b in zip(cuts, puts)]
        self.here = [self.local(i, a, b) for i, (a, b) in enumerate(zip(cuts, puts))]

    def copy(self, up, k, slab):
        at = self.dst.at[self.net.peer(self.MASKS[k]) // 2, self.core, slab]
        first = ((k * 2 + (0 if up else 1)) * 4 + slab) * 2
        return pltpu.make_async_remote_copy(
            src_ref=at,
            dst_ref=at,
            send_sem=self.sems.at[first],
            recv_sem=self.sems.at[first + 1],
            device_id={"bucket": self.plane + (1 if up else -1)},
            device_id_type=MESH_IDS,
        )

    def moves(self, h):
        for up in (True, False):
            slab = self.plane - h if up else self.plane + h
            there = (slab >= 0) if up else (slab <= 3)
            sends = (self.plane <= 2) if up else (self.plane >= 1)
            yield up, slab, there, sends

    def hop(self, h):
        if h == 0:
            for c in self.away:
                c.wait_recv()
        for up, slab, there, sends in self.moves(h):

            @pl.when(there)
            def _(up=up, slab=slab, sends=sends):
                for k in range(3):
                    if h > 0:
                        self.copy(up, k, slab).wait_recv()
                    if h < 3:

                        @pl.when(sends)
                        def _(k=k):
                            self.copy(up, k, slab).start()

    def finish(self):
        self.hop(3)
        for m in self.MASKS:
            at = self.dst.at[self.net.peer(m) // 2, self.core]
            self.ready.append(self.net.send(at, at, 1))

    def wait(self):
        for c in self.ready:
            c.wait_recv()

    def close(self):
        for h in range(3):
            for up, slab, there, sends in self.moves(h):

                @pl.when(there & sends)
                def _(up=up, slab=slab):
                    for k in range(3):
                        self.copy(up, k, slab).wait_send()


def meet_line(net, masks):
    plane = lax.axis_index("bucket")
    sem = pltpu.get_barrier_semaphore()
    for mask in masks:
        pl.semaphore_signal(
            sem, inc=1, device_id={"fsdp": net.peer(mask)}, device_id_type=MESH_IDS
        )
    for inner, step in ((plane >= 1, -1), (plane <= 2, 1)):

        @pl.when(inner)
        def _(step=step):
            pl.semaphore_signal(
                sem, inc=1, device_id={"bucket": plane + step}, device_id_type=MESH_IDS
            )

    one = jnp.int32(1)
    zero = jnp.int32(0)
    pl.semaphore_wait(
        sem, len(masks) + jnp.where(plane >= 1, one, zero) + jnp.where(plane <= 2, one, zero)
    )


ALL_PEERS = (1, 2, 3, 4, 5, 6, 7)


def open_kernel(
    cond_ref, gain_ref, bias_ref, ada_ref, tok_ref, seg_ref, idx_ref, freq_ref, attn_ref, textw_ref,
    text_ref,
    mod_ref, gains_ref, h_ref, idxs_ref, aw_ref, ta_out, q_ref, k_ref, v_ref, tk_ref, tv_ref,
    iq_ref, ik_ref, it_ref, cos_ref, sin_ref, sc_ref, gs_ref,
    conds, parts, mods, gbuf, tw_ref, ta_ref, sums, tsums, local_sems, out_sems, attn_sems, text_sems,
    send_sems, recv_sems,
):
    low = jnp.bfloat16
    full = jnp.float32
    net = Net(send_sems, recv_sems)
    me = net.me
    chip = me // 2
    meet_line(net, ALL_PEERS)

    act = cond_ref[...].astype(full)
    act = (act * jax.nn.sigmoid(act)).astype(low).astype(full)
    for j in range(8):
        gbuf[8, :, 128 * j : 128 * j + 128] = act[:, 128 * j : 128 * j + 128]
    waits = []
    for m in ALL_PEERS:
        at = pl.ds(pl.multiple_of(net.peer(m) * 128, 128), 128)
        waits.append(net.send(gbuf.at[8, :, at], conds.at[m], m))
    conds[0] = gbuf[8, :, pl.ds(pl.multiple_of(me * 128, 128), 128)]
    gwaits = [net.send(gain_ref, gbuf.at[m], m) for m in ALL_PEERS]
    iwaits = [net.send(idx_ref, idxs_ref.at[i], m) for i, m in ((1, 2), (2, 4), (3, 6))]
    idxs_ref[0] = idx_ref[...]

    def local(first):
        def go(i, src, dst):
            copy = pltpu.make_async_copy(src, dst, local_sems.at[first + i])
            copy.start()
            return copy

        return go

    attn_io = Lines(net, attn_ref, aw_ref, HW, attn_sems, local(3))
    text_io = Lines(net, textw_ref, tw_ref, HW, text_sems, local(6))
    attn_io.away_start()
    text_io.away_start()
    own_text = local(2)(0, text_ref, ta_ref.at[0])

    for w in waits:
        w.wait_recv()
    lhs = jnp.concatenate([conds[m] for m in range(8)], axis=0).astype(low)
    half_cols = 3072
    step = 512

    def mod_cols(i, _):
        lo = pl.ds(pl.multiple_of(i * step, step), step)
        hi = pl.ds(pl.multiple_of(half_cols + i * step, step), step)
        a = jnp.dot(lhs, ada_ref[:, lo], preferred_element_type=full)
        b = jnp.dot(lhs, ada_ref[:, hi], preferred_element_type=full)
        row = lax.broadcasted_iota(jnp.int32, (8, step), 0)
        for m in range(8):
            parts[m, :, lo] = (
                jnp.where(row < 4, a[8 * m : 8 * m + 8], b[8 * m : 8 * m + 8]) + bias_ref[:, lo]
            )
        return 0

    lax.fori_loop(0, half_cols // step, mod_cols, 0)
    waits = [net.send(parts.at[m], mods.at[m], m) for m in ALL_PEERS]

    attn_io.own_start()
    text_io.own_start()
    own_text.wait()

    def keep(j):
        copy = pltpu.make_async_copy(ta_ref.at[j], ta_out.at[j], out_sems.at[j])
        copy.start()
        return copy

    kept = [keep(0)]
    chunks = 4
    size = ta_ref.shape[1] // chunks
    tx, ty = [None] * chunks, [None] * chunks

    def text_send(s):
        i, j = s, (s + chunks // 2) % chunks
        at = pl.ds(i * size, size)
        tx[i] = net.send(ta_ref.at[0, at], ta_ref.at[1, at], 2)
        at = pl.ds(j * size, size)
        ty[j] = net.send(ta_ref.at[0, at], ta_ref.at[2, at], 4)

    text_send(0)
    attn_io.hop(0)
    text_io.hop(0)
    for w in gwaits:
        w.wait_recv()
    gains = gain_ref[...]
    for m in ALL_PEERS:
        gains = gains + gbuf[m]
    gains_ref[...] = gains
    for w in waits:
        w.wait_recv()

    def mod_sum(i, _):
        at = pl.ds(pl.multiple_of(i * step, step), step)
        total = parts[0, :, at]
        for m in ALL_PEERS:
            total = total + mods[m, :, at]
        mod_ref[:, at] = total
        return 0

    lax.fori_loop(0, half_cols // step, mod_sum, 0)

    block = 32

    def first_norm(i, _):
        at = pl.ds(pl.multiple_of(i * block, block), block)
        x = tok_ref[at, :].astype(full)
        normed = x * lax.rsqrt(jnp.mean(x * x, axis=-1, keepdims=True) + EPS)
        scale = pick_rows(mod_ref[:, :D], seg_ref[at, :], 0)
        h_ref[0, at, :] = (normed * gains_ref[0:1, :] * (1.0 + scale)).astype(low)
        return 0

    lax.fori_loop(0, ROW // block, first_norm, 0)
    hx, hy = share4_start(net, h_ref)

    text_send(1)
    attn_io.hop(1)
    h_far = share4_relay(net, h_ref, hx, hy)
    for i in range(2, chunks):
        text_send(i)
    text_io.hop(1)
    attn_io.hop(2)
    attn_io.finish()
    text_io.hop(2)
    relays = []
    for s in range(chunks // 2):
        i, j = s, s + chunks // 2
        tx[i].wait_recv()
        at = pl.ds(i * size, size)
        relays.append(net.send(ta_ref.at[1, at], ta_ref.at[3, at], 4))
        ty[j].wait_recv()
        at = pl.ds(j * size, size)
        relays.append(net.send(ta_ref.at[2, at], ta_ref.at[3, at], 2))

    for c in iwaits:
        c.wait_recv()
    gs_ref[...] = gains_ref[:, pl.ds(pl.multiple_of(chip * HW, 128), HW)]
    lane = lax.broadcasted_iota(jnp.int32, (ROW, 128), 1)
    sign = jnp.where((lane // 16) % 2 == 0, -1.0, 1.0)
    for j in range(CHIPS):
        at = pl.ds(j * ROW, ROW)
        cols = jnp.transpose(idxs_ref[j].astype(full))
        sc_ref[at, :] = cols[:, 0:1].astype(jnp.int32)
        place = jnp.where((lane // 32) % 2 == 0, cols[:, 1:2], cols[:, 2:3])
        angle = place * freq_ref[0:1, :]
        cos_ref[at, :] = jnp.cos(angle)
        sin_ref[at, :] = sign * jnp.sin(angle)

    attn_io.wait()
    for c in attn_io.here:
        c.wait()
    for c in h_far:
        c.wait_recv()

    def columns(lo, hi):
        return aw_ref[:, :, :, :, lo:hi].reshape(D, hi - lo)

    for j in range(CHIPS):
        h = h_ref[j]
        at = pl.ds(j * ROW, ROW)
        qv = jnp.dot(h, columns(0, HW), preferred_element_type=full)
        q_ref[at, :] = qv
        kv = jnp.dot(h, columns(HW, 2 * HW), preferred_element_type=full)
        k_ref[at, :] = kv
        v_ref[at, :] = jnp.dot(h, columns(2 * HW, 3 * HW), preferred_element_type=full).astype(low)
        sums[0, :, at] = row_sums(qv * qv, kv * kv)
    sum_io = [net.send(sums.at[0], sums.at[i], m) for i, m in ((1, 2), (2, 4), (3, 6))]

    text_io.finish()
    text_io.wait()
    for c in text_io.here:
        c.wait()

    def text_rows(j, lo, count):
        kt = 1024

        def body(i, acc):
            at = pl.ds(pl.multiple_of(i * kt, kt), kt)
            rows = ta_ref[j, pl.ds(lo, count), at]
            return acc + jnp.dot(rows, tw_ref[i].reshape(kt, 2 * HW), preferred_element_type=full)

        both = lax.fori_loop(0, ta_ref.shape[2] // kt, body, jnp.zeros((count, 2 * HW), full))
        keys, vals = both[:, :HW], both[:, HW:]
        at = pl.ds(j * ta_ref.shape[1] + lo, count)
        tk_ref[at, :] = keys
        tv_ref[at, :] = vals.astype(low)
        tsums[0, :, at] = row_sums(keys * keys, None)

    cap = ta_ref.shape[1]
    half = cap // 2
    for lo in (0, half):
        text_rows(0, lo, half)
    for i, c in enumerate(sum_io):
        c.wait_recv()
    for j in range(CHIPS):
        total = sums[0, :, pl.ds(j * ROW, ROW)]
        for i in (1, 2, 3):
            total = total + sums[i, :, pl.ds((j ^ i) * ROW, ROW)]
        both = jnp.transpose(lax.rsqrt(total / D + EPS))
        iq_ref[pl.ds(j * ROW, ROW), :] = both[:, 0:1]
        ik_ref[pl.ds(j * ROW, ROW), :] = both[:, 4:5]
    text_rows(1, 0, half)
    text_rows(2, half, half)
    for s in range(chunks // 2):
        tx[s + chunks // 2].wait_recv()
        ty[s].wait_recv()
    kept += [keep(1), keep(2)]
    text_rows(1, half, half)
    text_rows(2, 0, half)
    for c in relays:
        c.wait_recv()
    kept.append(keep(3))
    for lo in (0, half):
        text_rows(3, lo, half)
    sum_io = [net.send(tsums.at[0], tsums.at[i], m) for i, m in ((1, 2), (2, 4), (3, 6))]
    for c in sum_io:
        c.wait_recv()
    for j in range(CHIPS):
        total = tsums[0, :, pl.ds(j * cap, cap)]
        for i in (1, 2, 3):
            total = total + tsums[i, :, pl.ds((j ^ i) * cap, cap)]
        it_ref[pl.ds(j * cap, cap), :] = jnp.transpose(lax.rsqrt(total / D + EPS))[:, 0:1]
    for c in kept:
        c.wait()
    attn_io.close()
    text_io.close()
    net.close()


def open_layer(cond8, gain_pad, bias_pad, ada, tok, seg_col, idx, freq, attn, textw, text):
    low = jnp.bfloat16
    full = jnp.float32
    shape = jax.ShapeDtypeStruct
    cap, txtd = text.shape
    V = VMEM_SPEC
    return pl.pallas_call(
        open_kernel,
        in_specs=[V] * 8 + [ANY_SPEC] * 3,
        out_specs=[V] * 5 + [ANY_SPEC] + [V] * 12,
        out_shape=[
            shape((8, 3072), full),
            shape((8, D), full),
            shape((CHIPS, ROW, D), low),
            shape((CHIPS, 8, ROW), jnp.int32),
            shape((CHIPS, 2, *attn.shape[1:3], 3 * HW), low),
            shape((CHIPS, cap, txtd), low),
            shape((CHIPS * ROW, HW), full),
            shape((CHIPS * ROW, HW), full),
            shape((CHIPS * ROW, HW), low),
            shape((CHIPS * cap, HW), full),
            shape((CHIPS * cap, HW), low),
            shape((CHIPS * ROW, 1), full),
            shape((CHIPS * ROW, 1), full),
            shape((CHIPS * cap, 1), full),
            shape((CHIPS * ROW, 128), full),
            shape((CHIPS * ROW, 128), full),
            shape((CHIPS * ROW, 1), jnp.int32),
            shape((8, HW), full),
        ],
        scratch_shapes=[
            pltpu.VMEM((8, 8, 128), full),
            pltpu.VMEM((8, 8, 3072), full),
            pltpu.VMEM((8, 8, 3072), full),
            pltpu.VMEM((9, 8, D), full),
            pltpu.VMEM((CHIPS, 2, *textw.shape[1:3], 2 * HW), low),
            pltpu.VMEM((CHIPS, cap, txtd), low),
            pltpu.VMEM((CHIPS, 8, CHIPS * ROW), full),
            pltpu.VMEM((CHIPS, 8, CHIPS * cap), full),
            pltpu.SemaphoreType.DMA((8,)),
            pltpu.SemaphoreType.DMA((CHIPS,)),
            pltpu.SemaphoreType.DMA((48,)),
            pltpu.SemaphoreType.DMA((48,)),
            *net_scratch(80),
        ],
        compiler_params=pltpu.CompilerParams(
            collective_id=1, has_side_effects=True, vmem_limit_bytes=56 * 1024 * 1024
        ),
        cost_estimate=pl.CostEstimate(
            flops=10_000_000_000, bytes_accessed=400_000_000, transcendentals=0
        ),
    )(cond8, gain_pad, bias_pad, ada, tok, seg_col, idx, freq, attn, textw, text)


class Chain:
    def __init__(self, net, grad, mine, arrive, total, sems, columns):
        self.net = net
        self.grad = grad
        self.mine = mine
        self.arrive = arrive
        self.total = total
        self.sems = sems
        self.columns = columns
        self.plane = lax.axis_index("bucket")
        self.core = net.me % 2

    def piece(self, ref, p):
        return ref.at[:, p] if self.columns else ref.at[p]

    def half(self, core):
        return self.grad.at[:, :, :, core] if self.columns else self.grad.at[:, core]

    def each(self, ref, body):
        lead = ref.shape[:-2]
        if not lead:
            body(())
            return
        total = 1
        for n in lead:
            total *= n

        def step(i, _):
            index = []
            for n in reversed(lead):
                index.insert(0, i % n)
                i = i // n
            body(tuple(index))
            return 0

        lax.fori_loop(0, total, step, 0)

    def core_start(self, keep=None, sem=None):
        self.exchange = self.net.send(self.half(1 - self.core), self.mine, 1)
        self.keep = self.half(self.core)
        self.load = None
        if keep is not None:
            self.load = pltpu.make_async_copy(self.keep, keep, sem)
            self.load.start()
            self.keep = keep

    def add(self, into, other):
        def body(index):
            value = into[index].astype(jnp.float32) + other[index].astype(jnp.float32)
            into[index] = value.astype(into.dtype)

        self.each(into, body)

    def core_finish(self):
        self.exchange.wait_recv()
        if self.load is not None:
            self.load.wait()
        self.add(self.mine, self.keep)

    def copy(self, up, p, slot):
        first = 0 if up else 8
        return pltpu.make_async_remote_copy(
            src_ref=self.piece(self.mine, p),
            dst_ref=self.arrive.at[slot],
            send_sem=self.sems.at[first + p],
            recv_sem=self.sems.at[first + 4 + p],
            device_id={"bucket": self.plane + (1 if up else -1)},
            device_id_type=MESH_IDS,
        )

    def moves(self, t):
        up = self.plane + 3 - t
        down = self.plane - 3 + t
        return (
            (True, up, up, self.plane <= t, self.plane >= 1),
            (False, down, 4 if t == 2 else down, self.plane >= 3 - t, self.plane <= 2),
        )

    def step(self, t):
        for up, p, slot, sends, inner in self.moves(t):

            @pl.when(sends)
            def _(up=up, p=p, slot=slot, inner=inner):
                @pl.when(inner)
                def _():
                    self.copy(up, p, p).wait_recv()
                    self.add(self.piece(self.mine, p), self.arrive.at[p])

                self.copy(up, p, slot).start()

    def finish(self):
        own = self.piece(self.mine, self.plane)

        def first(index):
            self.total[index] = own[index].astype(jnp.float32)

        self.each(self.total, first)
        for up, slot, inner in ((True, self.plane, self.plane >= 1), (False, 4, self.plane <= 2)):

            @pl.when(inner)
            def _(up=up, slot=slot):
                self.copy(up, self.plane, slot).wait_recv()
                self.add(self.total, self.arrive.at[slot])

    def close(self):
        for t in range(3):
            for up, p, slot, sends, inner in self.moves(t):

                @pl.when(sends)
                def _(up=up, p=p, slot=slot):
                    self.copy(up, p, slot).wait_send()


def chain_scratch(columns, shape, width):
    low = jnp.bfloat16
    if columns:
        n, rows = shape
        return [
            pltpu.VMEM((n, 4, 4, rows, width), low),
            pltpu.VMEM((5, n, 4, rows, width), low),
            pltpu.VMEM((n, 4, rows, width), jnp.float32),
            pltpu.SemaphoreType.DMA((16,)),
        ]
    return [
        pltpu.VMEM((4, shape, width), low),
        pltpu.VMEM((5, shape, width), low),
        pltpu.VMEM((shape, width), jnp.float32),
        pltpu.SemaphoreType.DMA((16,)),
    ]


class Columns:
    def __init__(self, net, total, stage, wide, out):
        self.net, self.total, self.stage, self.wide, self.out = net, total, stage, wide, out

    def start(self):
        net = self.net
        chip = net.me // 2
        n, _, rows, width = self.stage.shape
        parts = self.wide.shape[0]
        width = width // parts
        at = pl.ds(pl.multiple_of(chip * width, width), width)

        def cast(i, _):
            self.stage[i // 4, i % 4] = self.total[i // 4, i % 4].astype(jnp.bfloat16)
            return 0

        if self.total is not None:
            lax.fori_loop(0, n * 4, cast, 0)
        self.copies = [
            net.send(
                self.stage.at[0, net.peer(m) // 2, :, pl.ds(i * width, width)],
                self.wide.at[i, :, at],
                m,
            )
            for m in (2, 4, 6)
            for i in range(parts)
        ]
        for i in range(parts):
            self.wide[i, :, at] = self.stage[0, chip, :, i * width : i * width + width]

    def finish(self):
        for c in self.copies:
            c.wait_recv()
        for i in range(self.out.shape[0]):
            self.out[i] = self.wide[i].astype(jnp.float32)


def meet_all(net, far=False):
    plane = lax.axis_index("bucket")
    chip = net.me // 2
    sem = pltpu.get_barrier_semaphore()
    for mask in ALL_PEERS:
        pl.semaphore_signal(
            sem, inc=1, device_id={"fsdp": net.peer(mask)}, device_id_type=MESH_IDS
        )
    for inner, step in ((plane >= 1, -1), (plane <= 2, 1)):

        @pl.when(inner)
        def _(step=step):
            pl.semaphore_signal(
                sem, inc=1, device_id={"bucket": plane + step}, device_id_type=MESH_IDS
            )

    @pl.when(chip != plane)
    def _():
        pl.semaphore_signal(
            sem,
            inc=1,
            device_id={"bucket": chip, "fsdp": plane * 2 + net.me % 2},
            device_id_type=MESH_IDS,
        )

    if far:
        pl.semaphore_signal(
            sem,
            inc=1,
            device_id={"bucket": plane + 2 - 4 * (plane // 2)},
            device_id_type=MESH_IDS,
        )
    one = jnp.int32(1)
    zero = jnp.int32(0)
    count = (
        (8 if far else 7)
        + jnp.where(plane >= 1, one, zero)
        + jnp.where(plane <= 2, one, zero)
        + jnp.where(chip != plane, one, zero)
    )
    pl.semaphore_wait(sem, count)


def transposed(net, src, dst, sems):
    plane = lax.axis_index("bucket")
    return pltpu.make_async_remote_copy(
        src_ref=src,
        dst_ref=dst,
        send_sem=sems.at[0],
        recv_sem=sems.at[1],
        device_id={"bucket": net.me // 2, "fsdp": plane * 2 + net.me % 2},
        device_id_type=MESH_IDS,
    )


class Spread:
    def __init__(self, buf, sems):
        self.buf, self.sems = buf, sems
        self.plane = lax.axis_index("bucket")

    def copy(self, up, slab):
        first = 0 if up else 8
        return pltpu.make_async_remote_copy(
            src_ref=self.buf.at[slab],
            dst_ref=self.buf.at[slab],
            send_sem=self.sems.at[first + slab],
            recv_sem=self.sems.at[first + 4 + slab],
            device_id={"bucket": self.plane + (1 if up else -1)},
            device_id_type=MESH_IDS,
        )

    def hop(self, h):
        for up in (True, False):
            slab = self.plane - h if up else self.plane + h
            there = (slab >= 0) if up else (slab <= 3)
            sends = (self.plane <= 2) if up else (self.plane >= 1)

            @pl.when(there)
            def _(up=up, slab=slab, sends=sends):
                if h > 0:
                    self.copy(up, slab).wait_recv()

                @pl.when(sends)
                def _():
                    self.copy(up, slab).start()

    def close(self):
        for h in range(4):
            for up in (True, False):
                slab = self.plane - h if up else self.plane + h
                there = (slab >= 0) if up else (slab <= 3)
                sends = (self.plane <= 2) if up else (self.plane >= 1)

                @pl.when(there & sends)
                def _(up=up, slab=slab):
                    self.copy(up, slab).wait_send()


def close_kernel(
    text_g, attn_g, out_g, ffn_t, dmod_ref, gg_ref, gs_ref, cond_ref,
    text_o, attn_o, out_o, ffn_o, ada_o, small_o,
    tm, ta, tt, ts, am, aa, at_, as_, om, oa, ot, os_,
    t_wide, a_wide, f_wide, t_stage, a_stage, o_stage, o_got, o_sem,
    mods, mods_other, mod_sems, smalls, got, z_sems, ada_s, send_sems, recv_sems,
):
    low = jnp.bfloat16
    full = jnp.float32
    net = Net(send_sems, recv_sems)
    meet_all(net, True)
    plane = lax.axis_index("bucket")
    me = net.me
    chip = me // 2
    out = Chain(net, out_g, om, oa, ot, os_, False)
    attn = Chain(net, attn_g, am, aa, at_, as_, True)
    text = Chain(net, text_g, tm, ta, tt, ts, True)
    chains = [out, text, attn]
    for c in chains:
        c.core_start()

    act = cond_ref[...].astype(full)
    mods[plane, 0, :, 2 * D :] = (act * jax.nn.sigmoid(act)).astype(low)
    mods[plane, 0, :, : 2 * D] = dmod_ref[...].astype(low)
    mine = mods.at[plane, 0]
    mod_io = [net.send(mine, mods.at[plane, i], m) for i, m in ((1, 2), (2, 4), (3, 6))]

    smalls[...] = jnp.zeros(smalls.shape, full)
    smalls[0:2, :] = gg_ref[0:2, :]
    smalls[2:6, pl.ds(pl.multiple_of(chip * HW, 128), HW)] = gs_ref[0:4, :]
    for p in range(4):
        rows = dmod_ref[4 * (p // 2) : 4 * (p // 2) + 4, (p % 2) * D : (p % 2 + 1) * D]
        smalls[8 + p : 9 + p, :] = jnp.sum(rows, axis=0, keepdims=True)
    order = [None]

    def small_send(i):
        if i < 3:
            order[0] = net.send(smalls, got.at[i], (1, 2, 4)[i])
            return
        there = plane + 1 - 2 * (plane % 2) if i == 3 else plane + 2 - 4 * (plane // 2)
        copy = pltpu.make_async_remote_copy(
            src_ref=smalls,
            dst_ref=got.at[i],
            send_sem=z_sems.at[2 * (i - 3)],
            recv_sem=z_sems.at[2 * (i - 3) + 1],
            device_id={"bucket": there},
            device_id_type=MESH_IDS,
        )
        copy.start()
        order[0] = copy

    def small_add(i):
        order[0].wait()
        net.all = [c for c in net.all if c is not order[0]]
        smalls[...] = smalls[...] + got[i]

    small_send(0)
    f_cols = Columns(net, None, ffn_t, f_wide, ffn_o)
    f_cols.start()
    for c in chains:
        c.core_finish()
        c.step(0)
    small_add(0)
    small_send(1)
    for c in mod_io:
        c.wait_recv()
    lines = Spread(mods, mod_sems)
    lines.hop(0)
    small_add(1)
    small_send(2)
    for c in chains:
        c.step(1)
    lines.hop(1)
    small_add(2)
    small_send(3)
    f_cols.finish()
    for c in chains:
        c.step(2)
    lines.hop(2)
    small_add(3)
    small_send(4)
    lines.hop(3)
    other = net.send(mods, mods_other, 1)
    small_add(4)
    small_o[...] = smalls[...]
    out.finish()
    o_stage[...] = ot[...].astype(low)

    @pl.when(chip != plane)
    def _():
        transposed(net, o_stage, o_got, o_sem).start()

    other.wait_recv()
    rank = plane * 8 + me
    lanes = pl.ds(pl.multiple_of(2 * D + (rank // 4) * 128, 128), 128)
    total = 128
    both = []
    for ref in (mods, mods_other):
        acts = ref[:, :, :, lanes].astype(full).reshape(total, 128)
        both.append(acts)
    acts = jnp.concatenate(both, axis=0)
    upper = (lax.broadcasted_iota(jnp.int32, acts.shape, 0) % 8) < 4
    parts = (jnp.where(upper, acts, 0.0).astype(low), jnp.where(upper, 0.0, acts).astype(low))
    wide = 512

    def ada_cols(i, _):
        at = pl.ds(pl.multiple_of(i * wide, wide), wide)
        rows = jnp.concatenate(
            [r[:, :, :, at].astype(full).reshape(total, wide) for r in (mods, mods_other)], axis=0
        ).astype(low)
        for p in range(2):
            ada_s[...] = t_dot(parts[p], rows)
            to = pl.ds(pl.multiple_of(p * 2 * D + i * wide, wide), wide)
            ada_o[:, to] = ada_s[pl.ds(pl.multiple_of((rank % 4) * 32, 32), 32), :]
        return 0

    lax.fori_loop(0, 2 * D // wide, ada_cols, 0)
    text.finish()
    text_cols = Columns(net, tt, t_stage, t_wide, text_o)
    text_cols.start()

    @pl.when(chip != plane)
    def _():
        transposed(net, o_stage, o_got, o_sem).wait()
        out_o[...] = o_got[...].astype(jnp.float32)

    @pl.when(chip == plane)
    def _():
        out_o[...] = ot[...]

    attn.finish()
    attn_cols = Columns(net, at_, a_stage, a_wide, attn_o)
    attn_cols.start()
    text_cols.finish()
    attn_cols.finish()
    for c in chains:
        c.close()
    lines.close()
    net.close()


def close_layer(text_g, attn_g, out_g, ffn_t, dmod, gg, gs, cond8):
    low = jnp.bfloat16
    full = jnp.float32
    shape = jax.ShapeDtypeStruct
    V = VMEM_SPEC
    tr, tw = text_g.shape[-2], text_g.shape[-1] // 2
    ar, aw = attn_g.shape[-2], attn_g.shape[-1] // 3
    orow, ow = out_g.shape[-2:]
    fr, fw = ffn_t.shape[-2], ffn_t.shape[-1] // 2
    return pl.pallas_call(
        close_kernel,
        in_specs=[V] * 8,
        out_specs=[V] * 6,
        out_shape=[
            shape((2, tr, 4 * tw), full),
            shape((3, ar, 4 * aw), full),
            shape((orow, ow), full),
            shape((2, fr, 4 * fw), full),
            shape((32, 4 * D), full),
            shape((16, D), full),
        ],
        scratch_shapes=[
            *chain_scratch(True, (1, tr), 2 * tw),
            *chain_scratch(True, (1, ar), 3 * aw),
            *chain_scratch(False, orow, ow),
            pltpu.VMEM((2, tr, 4 * tw), low),
            pltpu.VMEM((3, ar, 4 * aw), low),
            pltpu.VMEM((2, fr, 4 * fw), low),
            pltpu.VMEM((1, 4, tr, 2 * tw), low),
            pltpu.VMEM((1, 4, ar, 3 * aw), low),
            pltpu.VMEM((orow, ow), low),
            pltpu.VMEM((orow, ow), low),
            pltpu.SemaphoreType.DMA((2,)),
            pltpu.VMEM((4, CHIPS, 8, 2 * D + cond8.shape[1]), low),
            pltpu.VMEM((4, CHIPS, 8, 2 * D + cond8.shape[1]), low),
            pltpu.SemaphoreType.DMA((16,)),
            pltpu.VMEM((16, D), full),
            pltpu.VMEM((5, 16, D), full),
            pltpu.SemaphoreType.DMA((4,)),
            pltpu.VMEM((128, 512), full),
            *net_scratch(40),
        ],
        compiler_params=pltpu.CompilerParams(
            collective_id=2, has_side_effects=True, vmem_limit_bytes=60 * 1024 * 1024
        ),
        cost_estimate=pl.CostEstimate(
            flops=1_000_000, bytes_accessed=400_000_000, transcendentals=0
        ),
    )(text_g, attn_g, out_g, ffn_t, dmod, gg, gs, cond8)


def back_kernel(
    dh2_ref, fo_ref, x1_ref, branch_ref, cot_ref, w_ref, mod_ref, seg_ref, gain_ref, tok_ref,
    sr_ref, gs_ref, *rest,
):
    late, rest = rest[:LATE], rest[LATE:]
    places, rest = rest[-LATE - 1 : -1], rest[: -LATE - 1] + rest[-1:]
    loads = [
        pltpu.make_async_copy(src, dst, rest[-1].at[i])
        for i, (src, dst) in enumerate(zip(late, places))
    ]
    back_body(
        dh2_ref, fo_ref, x1_ref, branch_ref, cot_ref, w_ref, mod_ref, seg_ref, gain_ref, tok_ref,
        *places, sr_ref, gs_ref, *rest[:-1], loads,
    )


LATE = 17


def back_body(
    dh2_ref, fo_ref, x1_ref, branch_ref, cot_ref, w_ref, mod_ref, seg_ref, gain_ref, tok_ref,
    ow_ref, aw_ref, qr_ref, kr_ref, v_ref, tr_ref, tv_ref, cross_ref, q_ref, k_ref, tk_ref,
    iq_ref, ik_ref, it_ref, cos_ref, sin_ref, sc_ref, sr_ref, gs_ref, ffn_g, down_g,
    block_o, token_o, db_ref, dqkv_o, dtkv_o, dmod_o, gg_o, gs_o, ffn_o, down_o,
    dx_s, dc_s, dqf, dkf, dtf, part_s, sums, tsums, buf_a, far_a, buf_b, far_b, buf_c, far_c,
    fm, fa, ft, fs, dm, da, dt_c, ds_, f_keep, d_keep, keep_sem, send_sems, recv_sems, loads,
):
    low = jnp.bfloat16
    full = jnp.float32
    net = Net(send_sems, recv_sems)
    meet_all(net)
    plane = lax.axis_index("bucket")
    chip = net.me // 2
    ffn = Chain(net, ffn_g, fm, fa, ft, fs, True)
    down = Chain(net, down_g, dm, da, dt_c, ds_, False)
    ffn.core_start(f_keep, keep_sem.at[0])
    down.core_start(d_keep, keep_sem.at[1])
    for c in loads:
        c.start()

    def rows_of(ref):
        half = ROW // 2
        return lambda j, i: ref[pl.ds(j * ROW + i * half, half), :].astype(full)

    middle, finish = collect4(net, rows_of(dh2_ref), buf_a, far_a)
    middle()
    ffn.core_finish()
    ffn.step(0)
    down.core_finish()
    down.step(0)
    half = ROW // 2
    for i in (0, 1):
        dx_s[pl.ds(i * half, half), :] = finish(i)
    part_s[pl.ds(0, ROW), :] = dx_s[...]
    block = 32
    weight = w_ref[0:1, 0:1]

    def second_norm(at):
        x1 = x1_ref[at, :]
        inverse = lax.rsqrt(jnp.mean(x1 * x1, axis=-1, keepdims=True) + EPS)
        scale = pick_rows(mod_ref[:, :D], seg_ref[at, :], 4)
        return x1 * inverse, inverse, scale

    def to_branch(b, _):
        at = pl.ds(pl.multiple_of(b * block, block), block)
        normed, inverse, scale = second_norm(at)
        dn = dx_s[at, :] * gain_ref[1:2, :] * (1.0 + scale)
        back = inverse * (dn - normed * jnp.mean(dn * normed, axis=-1, keepdims=True))
        dx = cot_ref[at, :].astype(full) * weight + back
        dx_s[at, :] = dx
        gate = jnp.tanh(pick_rows(mod_ref[:, D:], seg_ref[at, :], 0))
        db_ref[0, at, :] = (dx * gate).astype(low)
        return 0

    lax.fori_loop(0, ROW // block, to_branch, 0)
    bx, by = share4_start(net, db_ref)

    def by_image(value, seg, row, lo):
        for i in range(IMGS):
            dmod_o[row + i : row + i + 1, lo : lo + D] += jnp.sum(
                jnp.where(seg == i, value, 0.0), axis=0, keepdims=True
            )

    dmod_o[...] = jnp.zeros(dmod_o.shape, full)
    gg_o[...] = jnp.zeros(gg_o.shape, full)

    def second_sums(b, _):
        at = pl.ds(pl.multiple_of(b * block, block), block)
        normed, inverse, scale = second_norm(at)
        seg = seg_ref[at, :]
        dh = part_s[at, :] * normed
        gg_o[1:2, :] += jnp.sum(dh * (1.0 + scale), axis=0, keepdims=True)
        by_image(dh * gain_ref[1:2, :], seg, 4, 0)
        gate = jnp.tanh(pick_rows(mod_ref[:, D:], seg, 0))
        by_image(dx_s[at, :] * branch_ref[at, :] * (1.0 - gate * gate), seg, 0, D)
        return 0

    lax.fori_loop(0, ROW // block, second_sums, 0)
    far = share4_relay(net, db_ref, bx, by)
    middle_b, finish_b = collect4(net, rows_of(fo_ref), buf_b, far_b)
    gs_o[...] = jnp.zeros(gs_o.shape, full)
    for c in loads:
        c.wait()
    cap = IMGS * TXT

    def attention_row(j, _):
        @pl.when(j == 3)
        def _():
            for c in far:
                c.wait_recv()

        @pl.when(j == 1)
        def _():
            ffn.step(1)
            down.step(1)

        @pl.when(j == 3)
        def _():
            ffn.step(2)
            down.step(2)

        rows = pl.ds(pl.multiple_of(j * ROW, ROW), ROW)
        text = pl.ds(pl.multiple_of(j * cap, cap), cap)
        dc_s[...] = dot_t(db_ref[j], ow_ref[...])
        dqv, dkv, dtv = dqf.at[rows], dkf.at[rows], dtf.at[text]
        attend_back_kernel(
            qr_ref.at[rows], kr_ref.at[rows], v_ref.at[rows], tr_ref.at[text], tv_ref.at[text],
            dc_s, cross_ref.at[rows], q_ref.at[rows], k_ref.at[rows], tk_ref.at[text],
            iq_ref.at[rows], ik_ref.at[rows], it_ref.at[text], cos_ref.at[rows], sin_ref.at[rows],
            sc_ref.at[rows], sr_ref.at[j, pl.ds(0, 1)], gs_ref,
            dqv, dkv, dqkv_o.at[rows, pl.ds(2 * HW, HW)], dtv, dtkv_o.at[text, pl.ds(HW, HW)], gs_o,
        )
        sums[0, :, rows] = row_sums(
            dqv[...] * (q_ref[rows, :] * iq_ref[rows, :]),
            dkv[...] * (k_ref[rows, :] * ik_ref[rows, :]),
        )
        tsums[0, :, text] = row_sums(dtv[...] * (tk_ref[text, :] * it_ref[text, :]), None)
        return 0

    lax.fori_loop(0, CHIPS, attention_row, 0)
    sum_io = []
    for i, m in ((1, 2), (2, 4), (3, 6)):
        sum_io.append(net.send(sums.at[0], sums.at[i], m))
        sum_io.append(net.send(tsums.at[0], tsums.at[i], m))
    middle_b()
    for i in (0, 1):
        part_s[pl.ds(i * half, half), :] = finish_b(i)

    def block_rows(b, _):
        at = pl.ds(pl.multiple_of(b * block, block), block)
        seg = seg_ref[at, :]
        gate = jnp.tanh(pick_rows(mod_ref[:, D:], seg, 4))
        out = part_s[at, :]
        block_o[at, :] = (x1_ref[at, :] + gate * out).astype(low)
        grad = cot_ref[at, :].astype(full) * weight
        by_image(grad * out * (1.0 - gate * gate), seg, 4, D)
        return 0

    for c in sum_io:
        c.wait_recv()
    for j in range(CHIPS):
        rows = pl.ds(j * ROW, ROW)
        text = pl.ds(j * cap, cap)
        total = sums[0, :, rows]
        words = tsums[0, :, text]
        for i in (1, 2, 3):
            total = total + sums[i, :, pl.ds((j ^ i) * ROW, ROW)]
            words = words + tsums[i, :, pl.ds((j ^ i) * cap, cap)]
        mean = jnp.transpose(total / D)
        iq, ik, it = iq_ref[rows, :], ik_ref[rows, :], it_ref[text, :]
        dqkv_o[rows, :HW] = (iq * (dqf[rows, :] - q_ref[rows, :] * iq * mean[:, 0:1])).astype(low)
        dqkv_o[rows, HW : 2 * HW] = (ik * (dkf[rows, :] - k_ref[rows, :] * ik * mean[:, 4:5])).astype(low)
        mean = jnp.transpose(words / D)
        dtkv_o[text, :HW] = (it * (dtf[text, :] - tk_ref[text, :] * it * mean[:, 0:1])).astype(low)

    lax.fori_loop(0, ROW // block, block_rows, 0)
    wide = 256

    def first_grad(n, _):
        at = pl.ds(pl.multiple_of(n * wide, wide), wide)
        part_s[:, at] = dot_t(dqkv_o[...], aw_ref[at, :])
        return 0

    lax.fori_loop(0, D // wide, first_grad, 0)
    middle_c, finish_c = collect4(net, rows_of(part_s), buf_c, far_c)
    ffn.finish()
    middle_c()

    def ffn_cast(i, _):
        ffn_o[0, i] = ft[0, i].astype(low)
        return 0

    lax.fori_loop(0, 4, ffn_cast, 0)
    down.finish()
    down_o[...] = dt_c[...].astype(low)
    gate = jnp.tanh(gs_ref[5:6, :])
    gs_o[3:4, :] = gs_o[3:4, :] * (1.0 - gate * gate)
    for i in (0, 1):
        part_s[pl.ds(i * half, half), :] = finish_c(i)

    def first_rows(b, _):
        at = pl.ds(pl.multiple_of(b * block, block), block)
        x = tok_ref[at, :].astype(full)
        inverse = lax.rsqrt(jnp.mean(x * x, axis=-1, keepdims=True) + EPS)
        normed = x * inverse
        seg = seg_ref[at, :]
        scale = pick_rows(mod_ref[:, :D], seg, 0)
        dh = part_s[at, :]
        gg_o[0:1, :] += jnp.sum(dh * normed * (1.0 + scale), axis=0, keepdims=True)
        by_image(dh * normed * gain_ref[0:1, :], seg, 0, 0)
        dn = dh * gain_ref[0:1, :] * (1.0 + scale)
        token_o[at, :] = dx_s[at, :] + inverse * (
            dn - normed * jnp.mean(dn * normed, axis=-1, keepdims=True)
        )
        return 0

    lax.fori_loop(0, ROW // block, first_rows, 0)
    ffn.close()
    down.close()
    net.close()


def back_layer(early, late, ffn_g, down_g):
    low = jnp.bfloat16
    full = jnp.float32
    shape = jax.ShapeDtypeStruct
    V = VMEM_SPEC
    cap = IMGS * TXT
    fr, fw = ffn_g.shape[-2], ffn_g.shape[-1] // 2
    dr, dw = down_g.shape[-2:]
    tok = CHIPS * ROW
    reduce_scratch = [pltpu.VMEM((5, ROW, D), low), pltpu.VMEM((2, ROW // 2, D), low)]
    return pl.pallas_call(
        back_kernel,
        in_specs=[V] * len(early) + [ANY_SPEC] * (LATE + 2),
        out_specs=[V] * 10,
        out_shape=[
            shape((ROW, D), low),
            shape((ROW, D), full),
            shape((CHIPS, ROW, D), low),
            shape((tok, 3 * HW), low),
            shape((CHIPS * cap, 2 * HW), low),
            shape((8, 2 * D), full),
            shape((8, D), full),
            shape((8, HW), full),
            shape((1, 4, fr, 2 * fw), low),
            shape((dr, dw), low),
        ],
        scratch_shapes=[
            pltpu.VMEM((ROW, D), full),
            pltpu.VMEM((ROW, HW), full),
            pltpu.VMEM((tok, HW), full),
            pltpu.VMEM((tok, HW), full),
            pltpu.VMEM((CHIPS * cap, HW), full),
            pltpu.VMEM((tok, D), full),
            pltpu.VMEM((CHIPS, 8, tok), full),
            pltpu.VMEM((CHIPS, 8, CHIPS * cap), full),
            *reduce_scratch, *reduce_scratch, *reduce_scratch,
            *chain_scratch(True, (1, fr), 2 * fw),
            *chain_scratch(False, dr, dw),
            pltpu.VMEM((1, 4, 4, fr, 2 * fw), low),
            pltpu.VMEM((4, dr, dw), low),
            pltpu.SemaphoreType.DMA((2,)),
            *net_scratch(48),
            *[pltpu.VMEM(v.shape, v.dtype) for v in late],
            pltpu.SemaphoreType.DMA((LATE,)),
        ],
        compiler_params=pltpu.CompilerParams(
            collective_id=3, has_side_effects=True, vmem_limit_bytes=63 * 1024 * 1024
        ),
        cost_estimate=pl.CostEstimate(
            flops=10_000_000_000, bytes_accessed=400_000_000, transcendentals=0
        ),
    )(*early, *late, ffn_g, down_g)


def row_spec(rows, width):
    return pl.BlockSpec((rows, width), lambda i: (i, 0))


def forward_kernel(
    q_ref, k_ref, v_ref, iq_ref, ik_ref, cos_ref, sin_ref, tk_ref, it_ref, tv_ref, sc_ref, sr_ref,
    gs_ref, mod_ref, seg_ref, gain_ref, tok_ref, cot_ref, w_ref, outw_ref, ffnw_ref, downw_ref,
    comb_o, cross_o, qr_o, kr_o, tr_o, branch_o, x1_o, h_o, df_o, ow_o, fw_o, dw_o,
    part_s, buf, far, f_own, d_own, local_sems, line_sems, send_sems, recv_sems,
):
    low = jnp.bfloat16
    full = jnp.float32
    net = Net(send_sems, recv_sems)
    meet_line(net, (1, 2, 4, 6))
    me = net.me
    chip = me // 2
    width = fw_o.shape[4] // 2
    rows = outw_ref.shape[0]

    def local(src, dst, i):
        copy = pltpu.make_async_copy(src, dst, local_sems.at[i])
        copy.start()
        return copy

    def own(ref, count):
        return ref.at[pl.ds(pl.multiple_of((me % 2) * count, count), count), :]

    out_here = local(outw_ref, own(ow_o, rows), 0)
    out_core = net.send(outw_ref, own(ow_o, rows), 1)
    down_rows = downw_ref.shape[0]
    down_here = local(downw_ref, d_own, 1)
    down_core = net.send(downw_ref, own(dw_o, down_rows), 1)

    def stage(i, src, dst):
        return local(src, f_own.at[:, :, pl.ds(i * width, width)], 2 + i)

    ffn_io = Lines(net, ffnw_ref, fw_o, width, line_sems, stage)
    ffn_io.away_start()
    ffn_io.own_start()
    block = 32
    weight = w_ref[0:1, 0:1]

    def ffn_grad(b, _):
        at = pl.ds(pl.multiple_of(b * block, block), block)
        gate = jnp.tanh(pick_rows(mod_ref[:, D:], seg_ref[at, :], 4))
        df_o[0, at, :] = (cot_ref[at, :].astype(full) * weight * gate).astype(low)
        return 0

    lax.fori_loop(0, ROW // block, ffn_grad, 0)
    dx, dy = share4_start(net, df_o)
    out_here.wait()
    out_core.wait_recv()
    cap = IMGS * TXT

    def attention_row(i, _):
        @pl.when(i == 1)
        def _():
            ffn_io.hop(0)

        @pl.when(i == 3)
        def _():
            ffn_io.hop(1)

        j = 3 - i
        at = pl.ds(pl.multiple_of(j * ROW, ROW), ROW)
        text = pl.ds(pl.multiple_of(j * cap, cap), cap)
        attend_kernel(
            q_ref.at[at], k_ref.at[at], v_ref.at[at], iq_ref.at[at], ik_ref.at[at],
            cos_ref.at[at], sin_ref.at[at], tk_ref.at[text], it_ref.at[text], tv_ref.at[text],
            sc_ref.at[at], sr_ref.at[j, pl.ds(0, 1)], gs_ref,
            comb_o.at[at], cross_o.at[at], qr_o.at[at], kr_o.at[at], tr_o.at[text],
        )
        part_s[at, :] = jnp.dot(comb_o[at, :], ow_o[...], preferred_element_type=full)
        return 0

    lax.fori_loop(0, CHIPS, attention_row, 0)
    half = ROW // 2
    middle, finish = collect4(
        net, lambda j, i: part_s[pl.ds(j * ROW + i * half, half), :], buf, far
    )
    df_far = share4_relay(net, df_o, dx, dy)

    down_here.wait()
    down_out = local(d_own, own(dw_o, down_rows), 4)
    for c in ffn_io.here:
        c.wait()
    f_out = local(f_own, fw_o.at[chip, me % 2], 5)
    middle()
    ffn_io.hop(2)
    for i in (0, 1):
        branch_o[pl.ds(i * half, half), :] = finish(i)

    def second(b, _):
        at = pl.ds(pl.multiple_of(b * block, block), block)
        seg = seg_ref[at, :]
        gate = jnp.tanh(pick_rows(mod_ref[:, D:], seg, 0))
        x1 = tok_ref[at, :].astype(full) + gate * branch_o[at, :]
        x1_o[at, :] = x1
        normed = x1 * lax.rsqrt(jnp.mean(x1 * x1, axis=-1, keepdims=True) + EPS)
        scale = pick_rows(mod_ref[:, :D], seg, 4)
        h_o[0, at, :] = (normed * gain_ref[1:2, :] * (1.0 + scale)).astype(low)
        return 0

    lax.fori_loop(0, ROW // block, second, 0)
    hx, hy = share4_start(net, h_o)
    ffn_io.finish()
    last = share4_relay(net, h_o, hx, hy)
    for c in (*df_far, *last, down_core):
        c.wait_recv()
    ffn_io.wait()
    down_out.wait()
    f_out.wait()
    ffn_io.close()
    net.close()


def forward_layer(*args):
    low = jnp.bfloat16
    full = jnp.float32
    shape = jax.ShapeDtypeStruct
    V = VMEM_SPEC
    cap = IMGS * TXT
    tok = CHIPS * ROW
    out_w, ffn_w, down_w = args[-3:]
    width = ffn_w.shape[3] // CHIPS
    return pl.pallas_call(
        forward_kernel,
        in_specs=[V] * (len(args) - 3) + [ANY_SPEC] * 3,
        out_specs=[V] * 10 + [ANY_SPEC] * 2,
        out_shape=[
            shape((tok, HW), low),
            shape((tok, HW), full),
            shape((tok, HW), low),
            shape((tok, HW), low),
            shape((CHIPS * cap, HW), low),
            shape((ROW, D), full),
            shape((ROW, D), full),
            shape((CHIPS, ROW, D), low),
            shape((CHIPS, ROW, D), low),
            shape((2 * out_w.shape[0], D), low),
            shape((CHIPS, 2, *ffn_w.shape[1:3], 2 * width), low),
            shape((2 * down_w.shape[0], D), low),
        ],
        scratch_shapes=[
            pltpu.VMEM((tok, D), full),
            pltpu.VMEM((5, ROW, D), low),
            pltpu.VMEM((2, ROW // 2, D), low),
            pltpu.VMEM((*ffn_w.shape[1:3], 2 * width), low),
            pltpu.VMEM(down_w.shape, low),
            pltpu.SemaphoreType.DMA((6,)),
            pltpu.SemaphoreType.DMA((48,)),
            *net_scratch(40),
        ],
        compiler_params=pltpu.CompilerParams(
            collective_id=4, has_side_effects=True, vmem_limit_bytes=56 * 1024 * 1024
        ),
        cost_estimate=pl.CostEstimate(
            flops=5_000_000_000, bytes_accessed=200_000_000, transcendentals=0
        ),
    )(*args)


def quarters(w):
    n, rows, columns = w.shape
    return w.reshape(n, 4, rows // 4, columns)


def per_device(
    tokens,
    cond,
    text,
    segments,
    positions,
    counts,
    ada_weight,
    ada_bias,
    gains,
    attn_weight,
    out_weight,
    text_weight,
    ffn_weight,
    down_weight,
    cotangent,
):
    low = jnp.bfloat16
    full = jnp.float32
    plane = lax.axis_index("bucket")
    slot = lax.axis_index("fsdp")
    core = slot % 2
    chip = slot // 2
    ff = ffn_weight.shape[2] // CHIPS

    gain_pad = lax.dynamic_update_slice_in_dim(
        jnp.zeros((8, D), full), jnp.pad(gains.astype(full), ((0, 2), (0, 0))), slot * 192, axis=1
    )
    bias = lax.dynamic_update_slice_in_dim(
        jnp.zeros((ada_weight.shape[1],), full), ada_bias.astype(full), slot * ada_bias.shape[0], 0
    )
    bias_pad = jnp.repeat(bias.reshape(2, 3072), 4, axis=0)
    cond8 = jnp.concatenate([cond[0], cond[0]], axis=0)
    seg = segments[0]
    idx = jnp.concatenate([seg[None, :], positions[0], jnp.zeros((5, ROW), jnp.int32)], axis=0)
    quarter = HDIM // 4
    freq = np.tile(10000.0 ** (-np.arange(quarter) / quarter), (8, 128 // quarter))
    freq_row = jnp.asarray(freq.astype(np.float32))
    (
        mod, gain_f, h_rows, idx_all, attn_w, text_rows, query, keyed, valued, text_keys, text_vals,
        inv_q, inv_k, inv_t, cosine, sine, seg_col, gain_s,
    ) = open_layer(
        cond8, gain_pad, bias_pad, ada_weight, tokens[0],
        seg[:, None], idx, freq_row, quarters(attn_weight), quarters(text_weight), text[0],
    )
    attn_w = attn_w.reshape(D, 3 * HW)
    h_all = h_rows.reshape(CHIPS * ROW, D)
    text_all = text_rows.reshape(CHIPS * IMGS * TXT, -1)
    totals = counts.astype(full)
    here = jnp.sum(jnp.where(jnp.arange(totals.shape[0], dtype=jnp.int32) == plane, totals, 0.0))
    weight = lax.axis_size("bucket") * here / jnp.sum(totals)
    weight_row = jnp.full((1, 128), weight, full)
    (
        comb, cross_out, q_rot, k_rot, text_rot, branch, x_one, h_two_rows, d_ffn_rows, out_w, ffn_w,
        down_w,
    ) = forward_layer(
        query, keyed, valued, inv_q, inv_k, cosine, sine, text_keys, inv_t, text_vals,
        seg_col, idx_all, gain_s, mod, seg[:, None], gain_f, tokens[0], cotangent[0], weight_row,
        out_weight, quarters(ffn_weight), down_weight,
    )
    ffn_w = ffn_w.reshape(D, 2 * ff)
    h_two_all = h_two_rows.reshape(CHIPS * ROW, D)
    d_ffn_all = d_ffn_rows.reshape(CHIPS * ROW, D)
    both = mult(h_two_all, ffn_w)
    gate_pre = both[:, :ff]
    upper = both[:, ff:]
    d_hidden = dot_t(d_ffn_all, down_w)
    sigm = jax.nn.sigmoid(gate_pre)
    silu_pre = gate_pre * sigm
    hidden = (silu_pre * upper).astype(low)
    d_pre = (d_hidden * upper * sigm * (1.0 + gate_pre * (1.0 - sigm))).astype(low)
    d_up = (d_hidden * silu_pre).astype(low)
    d_both = jnp.concatenate([d_pre, d_up], axis=1)
    d_h_two = dot_t(d_both, ffn_w).astype(low)
    ffn_out = mult(hidden, down_w).astype(low)
    g_down = t_dot(hidden, d_ffn_all).astype(low)
    g_ffn = t_dot(h_two_all, d_both).astype(low)

    (
        block_out, token_grad, d_branch_rows, d_qkv, d_text, d_mod, gg_full, gg_slice, ffn_sum, down_sum,
    ) = back_layer(
        [
            d_h_two, ffn_out, x_one, branch, cotangent[0], weight_row, mod,
            seg[:, None], gain_f, tokens[0], idx_all, gain_s,
        ],
        [
            out_w, attn_w, q_rot, k_rot, valued, text_rot, text_vals, cross_out, query, keyed,
            text_keys, inv_q, inv_k, inv_t, cosine, sine, seg_col,
        ],
        g_ffn.reshape(1, 4, 4, 2, 48, 2 * ff),
        g_down.reshape(4, 2, 128, D),
    )
    d_branch_all = d_branch_rows.reshape(CHIPS * ROW, D)
    g_text = t_dot(text_all, d_text).astype(low)
    g_attn = t_dot(h_all, d_qkv).astype(low)
    g_out = t_dot(comb, d_branch_all).astype(low)
    s_down = to_row_owner(down_sum)
    s_text, s_attn, s_out, s_ffn, s_ada_w, small = close_layer(
        g_text.reshape(1, 4, 4, 2, 128, 2 * HW),
        g_attn.reshape(1, 4, 4, 2, 48, 3 * HW),
        g_out.reshape(4, 2, 48, D),
        ffn_sum,
        d_mod,
        gg_full,
        gg_slice,
        cond8,
    )
    rank = plane * 8 + slot
    s_gains = lax.dynamic_slice_in_dim(small[:6], rank * 48, 48, axis=1)
    s_ada_b = lax.dynamic_slice_in_dim(small[8:12].reshape(-1), rank * 192, 192, axis=0)
    return (
        block_out[None],
        token_grad[None],
        s_ada_w,
        s_ada_b,
        s_gains,
        s_attn,
        s_out,
        s_text,
        s_ffn,
        s_down,
    )


def solution(mesh):
    in_specs = (
        P(("bucket", "fsdp"), None, None),
        P(("bucket", "fsdp"), None, None),
        P(("bucket", "fsdp"), None, None),
        P(("bucket", "fsdp"), None),
        P(("bucket", "fsdp"), None, None),
        P(),
        P("fsdp", None),
        P("fsdp"),
        P(None, "fsdp"),
        P(None, "fsdp", None),
        P("fsdp", None),
        P(None, "fsdp", None),
        P(None, "fsdp", None),
        P("fsdp", None),
        P(("bucket", "fsdp"), None, None),
    )
    out_specs = (
        P(("bucket", "fsdp"), None, None),
        P(("bucket", "fsdp"), None, None),
        P(("bucket", "fsdp"), None),
        P(("bucket", "fsdp")),
        P(None, ("bucket", "fsdp")),
        P(None, ("bucket", "fsdp"), None),
        P(("bucket", "fsdp"), None),
        P(None, ("bucket", "fsdp"), None),
        P(None, ("bucket", "fsdp"), None),
        P(("bucket", "fsdp"), None),
    )
    fast = mesh.shape["fsdp"] == 8 and mesh.shape["bucket"] == 4
    return jax.shard_map(
        per_device if fast else per_device_general, mesh=mesh, in_specs=in_specs, out_specs=out_specs, check_vma=False
    )
```

```python
import jax
import jax.numpy as jnp
import numpy as np
from jax import lax
from jax.experimental import pallas as pl
from jax.experimental.pallas import tpu as pltpu
from jax.sharding import PartitionSpec as P

D = 1536
HEADS = 24
HDIM = 64
IMGS = 4
TXT = 64


EPS = 1e-06
NEGATIVE = -1e30
HIGH = lax.Precision.HIGHEST


def silu(v):
    return v * jax.nn.sigmoid(v)


def norm_rows(v):
    inverse = lax.rsqrt(jnp.mean(v * v, axis=-1, keepdims=True) + EPS)
    return (v * inverse, inverse)


def norm_back(grad, normed, inverse):
    return inverse * (grad - normed * jnp.mean(grad * normed, axis=-1, keepdims=True))


def rotary_tables(pos):
    quarter = HDIM // 4
    freq = 10000.0 ** (-jnp.arange(quarter, dtype=jnp.float32) / quarter)
    angle = jnp.transpose(pos.astype(jnp.float32), (1, 0))[:, :, None] * freq[None, None, :]
    return (jnp.cos(angle), jnp.sin(angle))


def rotate(v, cosine, sine):
    rows = v.shape[0]
    parts = v.reshape(rows, HEADS, 2, 2, HDIM // 4)
    first = parts[:, :, :, 0]
    second = parts[:, :, :, 1]
    cosine = cosine[:, None]
    sine = sine[:, None]
    turned = jnp.stack([first * cosine - second * sine, first * sine + second * cosine], axis=3)
    return turned.reshape(rows, HEADS * HDIM)


def to_pairs(v):
    return jnp.transpose(v.reshape(v.shape[0], HEADS // 2, 2 * HDIM), (1, 0, 2))


def from_pairs(v):
    return jnp.transpose(v, (1, 0, 2)).reshape(v.shape[1], HEADS * HDIM)


def pair_scores(query, keys):
    q_heads = query.reshape(query.shape[0], 2, HDIM)
    k_heads = keys.reshape(keys.shape[0], 2, HDIM)
    return jnp.einsum(
        "rhd,khd->hrk", q_heads, k_heads, preferred_element_type=jnp.float32
    ) * HDIM ** (-0.5)


def attend_forward(q_b, k_b, v_b, allowed):

    def one_pair(item):
        query, keys, values = item
        scores = jnp.where(allowed[None], pair_scores(query, keys), NEGATIVE)
        top = jnp.max(scores, axis=-1, keepdims=True)
        expo = jnp.exp(scores - top)
        total = jnp.sum(expo, axis=-1, keepdims=True)
        probs = (expo / total).astype(jnp.bfloat16)
        result = jnp.einsum(
            "hrk,khd->rhd",
            probs,
            values.reshape(values.shape[0], 2, HDIM),
            preferred_element_type=jnp.float32,
        )
        return (result.reshape(query.shape[0], 2 * HDIM), (top + jnp.log(total))[..., 0])

    outputs, saved = lax.map(one_pair, (to_pairs(q_b), to_pairs(k_b), to_pairs(v_b)))
    return (from_pairs(outputs), saved)


def attend_back(q_b, k_b, v_b, saved, grad_b, allowed):

    def one_pair(item):
        query, keys, values, lse_pair, grad = item
        rows = query.shape[0]
        count = keys.shape[0]
        scores = jnp.where(allowed[None], pair_scores(query, keys), NEGATIVE)
        probs = jnp.exp(scores - lse_pair[..., None])
        probs_b = probs.astype(jnp.bfloat16)
        grad_heads = grad.reshape(rows, 2, HDIM)
        dprob = jnp.einsum(
            "rhd,khd->hrk",
            grad_heads,
            values.reshape(count, 2, HDIM),
            preferred_element_type=jnp.float32,
        )
        dscore = (probs * (dprob - jnp.sum(probs * dprob, axis=-1, keepdims=True))).astype(
            jnp.bfloat16
        )
        factor = HDIM ** (-0.5)
        dquery = (
            jnp.einsum(
                "hrk,khd->rhd",
                dscore,
                keys.reshape(count, 2, HDIM),
                preferred_element_type=jnp.float32,
            )
            * factor
        )
        dkeys = (
            jnp.einsum(
                "hrk,rhd->khd",
                dscore,
                query.reshape(rows, 2, HDIM),
                preferred_element_type=jnp.float32,
            )
            * factor
        )
        dvalues = jnp.einsum(
            "hrk,rhd->khd", probs_b, grad_heads, preferred_element_type=jnp.float32
        )
        return (
            dquery.reshape(rows, 2 * HDIM),
            dkeys.reshape(count, 2 * HDIM),
            dvalues.reshape(count, 2 * HDIM),
        )

    d_query, d_keys, d_values = lax.map(
        one_pair, (to_pairs(q_b), to_pairs(k_b), to_pairs(v_b), saved, to_pairs(grad_b))
    )
    return (from_pairs(d_query), from_pairs(d_keys), from_pairs(d_values))


def mult(left, right):
    return jnp.dot(left, right, preferred_element_type=jnp.float32)


def per_device_general(
    tokens,
    cond,
    text,
    segments,
    positions,
    counts,
    ada_weight,
    ada_bias,
    gains,
    attn_weight,
    out_weight,
    text_weight,
    ffn_weight,
    down_weight,
    cotangent,
):
    ada_w, ada_b, gain_rows, attn_w, out_w, text_w = (
        lax.all_gather(ada_weight, "fsdp", axis=0, tiled=True),
        lax.all_gather(ada_bias, "fsdp", axis=0, tiled=True),
        lax.all_gather(gains, "fsdp", axis=1, tiled=True),
        lax.all_gather(attn_weight, "fsdp", axis=1, tiled=True),
        lax.all_gather(out_weight, "fsdp", axis=0, tiled=True),
        lax.all_gather(text_weight, "fsdp", axis=1, tiled=True),
    )
    gain_f = gain_rows.astype(jnp.float32)
    x = tokens[0].astype(jnp.float32)
    seg = segments[0]
    cosine, sine = rotary_tables(positions[0])
    text_b = text[0]
    cond_act = silu(cond[0].astype(jnp.float32)).astype(jnp.bfloat16)
    mod = mult(cond_act, ada_w) + ada_b.astype(jnp.float32)[None, :]
    pick = (seg[:, None] == jnp.arange(IMGS, dtype=jnp.int32)[None, :]).astype(jnp.float32)
    per_token = jnp.dot(pick, mod, precision=HIGH)
    scale1 = per_token[:, :D]
    gate1 = per_token[:, D : 2 * D]
    scale2 = per_token[:, 2 * D : 3 * D]
    gate2 = per_token[:, 3 * D :]
    normed1, inverse1 = norm_rows(x)
    h_one = (normed1 * gain_f[0] * (1.0 + scale1)).astype(jnp.bfloat16)
    query = mult(h_one, attn_w[0])
    keyed = mult(h_one, attn_w[1])
    valued = mult(h_one, attn_w[2]).astype(jnp.bfloat16)
    q_norm, q_inv = norm_rows(query)
    k_norm, k_inv = norm_rows(keyed)
    q_rot = rotate(q_norm * gain_f[2], cosine, sine).astype(jnp.bfloat16)
    k_rot = rotate(k_norm * gain_f[3], cosine, sine).astype(jnp.bfloat16)
    text_keys = mult(text_b, text_w[0])
    text_vals = mult(text_b, text_w[1]).astype(jnp.bfloat16)
    t_norm, t_inv = norm_rows(text_keys)
    text_rot = (t_norm * gain_f[4]).astype(jnp.bfloat16)
    same = seg[:, None] == seg[None, :]
    owner = jnp.arange(IMGS * TXT, dtype=jnp.int32) // TXT
    mine = seg[:, None] == owner[None, :]
    self_out, self_lse = attend_forward(q_rot, k_rot, valued, same)
    cross_out, cross_lse = attend_forward(q_rot, text_rot, text_vals, mine)
    cross_gate = jnp.tanh(gain_f[5])
    comb = (self_out + cross_gate * cross_out).astype(jnp.bfloat16)
    branch = mult(comb, out_w)
    tanh_one = jnp.tanh(gate1)
    x_one = x + tanh_one * branch
    normed2, inverse2 = norm_rows(x_one)
    h_two = (normed2 * gain_f[1] * (1.0 + scale2)).astype(jnp.bfloat16)
    ffn_w, down_w = (
        lax.all_gather(ffn_weight, "fsdp", axis=1, tiled=True),
        lax.all_gather(down_weight, "fsdp", axis=0, tiled=True),
    )
    gate_pre = mult(h_two, ffn_w[0])
    upper = mult(h_two, ffn_w[1])
    sigm = jax.nn.sigmoid(gate_pre)
    silu_pre = gate_pre * sigm
    hidden = (silu_pre * upper).astype(jnp.bfloat16)
    ffn_out = mult(hidden, down_w)
    tanh_two = jnp.tanh(gate2)
    block_out = (x_one + tanh_two * ffn_out).astype(jnp.bfloat16)
    totals = counts.astype(jnp.float32)
    here = jnp.sum(
        jnp.where(
            jnp.arange(totals.shape[0], dtype=jnp.int32) == lax.axis_index("bucket"), totals, 0.0
        )
    )
    weight = lax.axis_size("bucket") * here / jnp.sum(totals)
    grad = cotangent[0].astype(jnp.float32) * weight
    back_ffn, back_down = (
        lax.all_gather(ffn_weight, "fsdp", axis=1, tiled=True),
        lax.all_gather(down_weight, "fsdp", axis=0, tiled=True),
    )
    d_gate2 = grad * ffn_out * (1.0 - tanh_two * tanh_two)
    d_ffn = (grad * tanh_two).astype(jnp.bfloat16)
    d_hidden = mult(d_ffn, back_down.T)
    g_down = mult(hidden.T, d_ffn)
    d_pre = (d_hidden * upper * sigm * (1.0 + gate_pre * (1.0 - sigm))).astype(jnp.bfloat16)
    d_up = (d_hidden * silu_pre).astype(jnp.bfloat16)
    d_h_two = mult(d_pre, back_ffn[0].T) + mult(d_up, back_ffn[1].T)
    g_ffn = jnp.stack([mult(h_two.T, d_pre), mult(h_two.T, d_up)])
    s_ffn, s_down = (
        lax.psum_scatter(g_ffn, ("bucket", "fsdp"), scatter_dimension=1, tiled=True),
        lax.psum_scatter(g_down, ("bucket", "fsdp"), scatter_dimension=0, tiled=True),
    )
    back_attn, back_out = (
        lax.all_gather(attn_weight, "fsdp", axis=1, tiled=True),
        lax.all_gather(out_weight, "fsdp", axis=0, tiled=True),
    )
    g_gain_one = jnp.sum(d_h_two * normed2 * (1.0 + scale2), axis=0)
    d_scale2 = d_h_two * normed2 * gain_f[1]
    d_x_one = grad + norm_back(d_h_two * gain_f[1] * (1.0 + scale2), normed2, inverse2)
    d_gate1 = d_x_one * branch * (1.0 - tanh_one * tanh_one)
    d_branch = (d_x_one * tanh_one).astype(jnp.bfloat16)
    d_comb = mult(d_branch, back_out.T)
    g_out = mult(comb.T, d_branch)
    g_gain_five = jnp.sum(d_comb * cross_out, axis=0) * (1.0 - cross_gate * cross_gate)
    d_self = d_comb.astype(jnp.bfloat16)
    d_cross = (d_comb * cross_gate).astype(jnp.bfloat16)
    dq_self, dk_self, dv_self = attend_back(q_rot, k_rot, valued, self_lse, d_self, same)
    dq_cross, dk_text, dv_text = attend_back(q_rot, text_rot, text_vals, cross_lse, d_cross, mine)
    d_q_norm = rotate(dq_self + dq_cross, cosine, -sine)
    g_gain_two = jnp.sum(d_q_norm * q_norm, axis=0)
    d_query = norm_back(d_q_norm * gain_f[2], q_norm, q_inv).astype(jnp.bfloat16)
    d_k_norm = rotate(dk_self, cosine, -sine)
    g_gain_three = jnp.sum(d_k_norm * k_norm, axis=0)
    d_keyed = norm_back(d_k_norm * gain_f[3], k_norm, k_inv).astype(jnp.bfloat16)
    d_valued = dv_self.astype(jnp.bfloat16)
    g_gain_four = jnp.sum(dk_text * t_norm, axis=0)
    d_text_keys = norm_back(dk_text * gain_f[4], t_norm, t_inv).astype(jnp.bfloat16)
    d_text_vals = dv_text.astype(jnp.bfloat16)
    g_text = jnp.stack([mult(text_b.T, d_text_keys), mult(text_b.T, d_text_vals)])
    d_h_one = (
        mult(d_query, back_attn[0].T)
        + mult(d_keyed, back_attn[1].T)
        + mult(d_valued, back_attn[2].T)
    )
    g_attn = jnp.stack([mult(h_one.T, d_query), mult(h_one.T, d_keyed), mult(h_one.T, d_valued)])
    g_gain_zero = jnp.sum(d_h_one * normed1 * (1.0 + scale1), axis=0)
    d_scale1 = d_h_one * normed1 * gain_f[0]
    token_grad = d_x_one + norm_back(d_h_one * gain_f[0] * (1.0 + scale1), normed1, inverse1)
    d_token_mod = jnp.concatenate([d_scale1, d_gate1, d_scale2, d_gate2], axis=1)
    d_mod = jnp.dot(pick.T, d_token_mod, precision=HIGH)
    g_ada_b = jnp.sum(d_mod, axis=0)
    g_ada_w = mult(cond_act.T, d_mod.astype(jnp.bfloat16))
    g_gains = jnp.stack(
        [g_gain_zero, g_gain_one, g_gain_two, g_gain_three, g_gain_four, g_gain_five]
    )
    s_ada_w, s_ada_b, s_gains, s_attn, s_out, s_text = (
        lax.psum_scatter(g_ada_w, ("bucket", "fsdp"), scatter_dimension=0, tiled=True),
        lax.psum_scatter(g_ada_b, ("bucket", "fsdp"), scatter_dimension=0, tiled=True),
        lax.psum_scatter(g_gains, ("bucket", "fsdp"), scatter_dimension=1, tiled=True),
        lax.psum_scatter(g_attn, ("bucket", "fsdp"), scatter_dimension=1, tiled=True),
        lax.psum_scatter(g_out, ("bucket", "fsdp"), scatter_dimension=0, tiled=True),
        lax.psum_scatter(g_text, ("bucket", "fsdp"), scatter_dimension=1, tiled=True),
    )
    return (
        block_out[None],
        token_grad[None],
        s_ada_w,
        s_ada_b,
        s_gains,
        s_attn,
        s_out,
        s_text,
        s_ffn,
        s_down,
    )


ROW = 128
CHIPS = 4
HW = D // CHIPS
PAIRS = HW // 128


def partner(u):
    lane = lax.broadcasted_iota(jnp.int32, u.shape, 1)
    ahead = pltpu.roll(u, u.shape[1] - 16, 1)
    behind = pltpu.roll(u, 16, 1)
    return jnp.where((lane // 16) % 2 == 0, ahead, behind)


def dot_t(a, b):
    return lax.dot_general(a, b, (((1,), (1,)), ((), ())), preferred_element_type=jnp.float32)


def dot_n(a, b):
    return lax.dot_general(a, b, (((1,), (0,)), ((), ())), preferred_element_type=jnp.float32)


def t_dot(a, b):
    return lax.dot_general(a, b, (((0,), (0,)), ((), ())), preferred_element_type=jnp.float32)


def softmax_of(scores, allowed):
    scores = jnp.where(allowed, scores * HDIM ** (-0.5), NEGATIVE)
    top = jnp.max(scores, axis=-1, keepdims=True)
    expo = jnp.exp(scores - top)
    return expo / jnp.sum(expo, axis=-1, keepdims=True)


def head_mask(v, head):
    lane = lax.broadcasted_iota(jnp.int32, v.shape, 1)
    return jnp.where((lane // HDIM) == head, v, jnp.zeros_like(v))


def masks_of(seg_col, seg_row, captions):
    same = seg_col == seg_row
    owner = lax.broadcasted_iota(jnp.int32, (seg_col.shape[0], captions), 1) // TXT
    return same, seg_col == owner


def attend_kernel(
    q_ref, k_ref, v_ref, iq_ref, ik_ref, cos_ref, sin_ref, tk_ref, it_ref, tv_ref, sc_ref, sr_ref,
    g_ref, comb_ref, cross_ref, qr_ref, kr_ref, tr_ref,
):
    same, mine = masks_of(sc_ref[...], sr_ref[...], tk_ref.shape[0])
    cosine = cos_ref[...]
    sine = sin_ref[...]
    low = jnp.bfloat16
    for pair in range(PAIRS):
        at = pl.ds(pair * 128, 128)
        qn = q_ref[:, at] * iq_ref[...] * g_ref[2:3, at]
        kn = k_ref[:, at] * ik_ref[...] * g_ref[3:4, at]
        qr = (qn * cosine + partner(qn) * sine).astype(low)
        kr = (kn * cosine + partner(kn) * sine).astype(low)
        tr = (tk_ref[:, at] * it_ref[...] * g_ref[4:5, at]).astype(low)
        qr_ref[:, at] = qr
        kr_ref[:, at] = kr
        tr_ref[:, at] = tr
        vv = v_ref[:, at]
        tv = tv_ref[:, at]
        self_out = jnp.zeros(qn.shape, jnp.float32)
        cross_out = jnp.zeros(qn.shape, jnp.float32)
        for head in range(2):
            qh = head_mask(qr, head)
            probs = softmax_of(dot_t(qh, kr), same).astype(low)
            self_out = self_out + head_mask(dot_n(probs, vv), head)
            probs = softmax_of(dot_t(qh, tr), mine).astype(low)
            cross_out = cross_out + head_mask(dot_n(probs, tv), head)
        cross_ref[:, at] = cross_out
        comb_ref[:, at] = (self_out + jnp.tanh(g_ref[5:6, at]) * cross_out).astype(low)


def attend_back_kernel(
    qr_ref, kr_ref, v_ref, tr_ref, tv_ref, dc_ref, cross_ref, q_ref, k_ref, tk_ref, iq_ref, ik_ref,
    it_ref, cos_ref, sin_ref, sc_ref, sr_ref, g_ref,
    dq_ref, dk_ref, dv_ref, dt_ref, dtv_ref, gg_ref,
):
    same, mine = masks_of(sc_ref[...], sr_ref[...], tk_ref.shape[0])
    cosine = cos_ref[...]
    sine = sin_ref[...]
    low = jnp.bfloat16
    factor = HDIM ** (-0.5)
    for pair in range(PAIRS):
        at = pl.ds(pair * 128, 128)
        qr = qr_ref[:, at]
        kr = kr_ref[:, at]
        vv = v_ref[:, at]
        tr = tr_ref[:, at]
        tv = tv_ref[:, at]
        dcomb = dc_ref[:, at]
        d_self = dcomb.astype(low)
        d_cross = (dcomb * jnp.tanh(g_ref[5:6, at])).astype(low)
        dq = jnp.zeros(dcomb.shape, jnp.float32)
        dk = jnp.zeros(dcomb.shape, jnp.float32)
        dv = jnp.zeros(dcomb.shape, jnp.float32)
        dt = jnp.zeros((tr.shape[0], 128), jnp.float32)
        dtv = jnp.zeros((tr.shape[0], 128), jnp.float32)
        for head in range(2):
            qh = head_mask(qr, head)
            probs = softmax_of(dot_t(qh, kr), same)
            grad = head_mask(d_self, head)
            dprob = dot_t(grad, vv)
            dscore = probs * (dprob - jnp.sum(probs * dprob, axis=-1, keepdims=True))
            dscore = dscore.astype(low)
            dq = dq + dot_n(dscore, head_mask(kr, head))
            dk = dk + t_dot(dscore, qh)
            dv = dv + t_dot(probs.astype(low), grad)
            probs = softmax_of(dot_t(qh, tr), mine)
            grad = head_mask(d_cross, head)
            dprob = dot_t(grad, tv)
            dscore = probs * (dprob - jnp.sum(probs * dprob, axis=-1, keepdims=True))
            dscore = dscore.astype(low)
            dq = dq + dot_n(dscore, head_mask(tr, head))
            dt = dt + t_dot(dscore, qh)
            dtv = dtv + t_dot(probs.astype(low), grad)
        dq = dq * factor
        dk = dk * factor
        dt = dt * factor
        dq = dq * cosine - partner(dq) * sine
        dk = dk * cosine - partner(dk) * sine
        q_norm = q_ref[:, at] * iq_ref[...]
        k_norm = k_ref[:, at] * ik_ref[...]
        t_norm = tk_ref[:, at] * it_ref[...]
        gg_ref[0:1, at] += jnp.sum(dq * q_norm, axis=0, keepdims=True)
        gg_ref[1:2, at] += jnp.sum(dk * k_norm, axis=0, keepdims=True)
        gg_ref[2:3, at] += jnp.sum(dt * t_norm, axis=0, keepdims=True)
        gg_ref[3:4, at] += jnp.sum(dcomb * cross_ref[:, at], axis=0, keepdims=True)
        dq = dq * g_ref[2:3, at]
        dk = dk * g_ref[3:4, at]
        dt = dt * g_ref[4:5, at]
        dq_ref[:, at] = dq
        dk_ref[:, at] = dk
        dv_ref[:, at] = dv.astype(low)
        dt_ref[:, at] = dt
        dtv_ref[:, at] = dtv.astype(low)


MESH_IDS = pl.DeviceIdType.MESH
VMEM_SPEC = pl.BlockSpec(memory_space=pltpu.VMEM)
ANY_SPEC = pl.BlockSpec(memory_space=pl.ANY)


def to_row_owner(block):
    pairs = [
        (a * 8 + b * 2 + k, b * 8 + a * 2 + k) for a in range(4) for b in range(4) for k in range(2)
    ]
    return lax.ppermute(block, ("bucket", "fsdp"), pairs).astype(jnp.float32)


class Net:
    def __init__(self, send_sems, recv_sems):
        self.me = lax.axis_index("fsdp")
        self.send_sems = send_sems
        self.recv_sems = recv_sems
        self.count = 0
        self.all = []

    def peer(self, mask):
        out = self.me
        for bit in (1, 2, 4):
            if mask & bit:
                out = out + bit * (1 - 2 * ((self.me // bit) % 2))
        return out

    def meet(self, masks):
        sem = pltpu.get_barrier_semaphore()
        for mask in masks:
            pl.semaphore_signal(
                sem, inc=1, device_id={"fsdp": self.peer(mask)}, device_id_type=MESH_IDS
            )
        pl.semaphore_wait(sem, len(masks))

    def send(self, src, dst, mask):
        assert self.count < self.send_sems.shape[0]
        copy = pltpu.make_async_remote_copy(
            src_ref=src,
            dst_ref=dst,
            send_sem=self.send_sems.at[self.count],
            recv_sem=self.recv_sems.at[self.count],
            device_id={"fsdp": self.peer(mask)},
            device_id_type=MESH_IDS,
        )
        self.count += 1
        copy.start()
        self.all.append(copy)
        return copy

    def close(self):
        for copy in self.all:
            copy.wait_send()


def net_scratch(count):
    return [pltpu.SemaphoreType.DMA((count,)), pltpu.SemaphoreType.DMA((count,))]


def share4_start(net, out):
    return net.send(out.at[0], out.at[1], 2), net.send(out.at[0], out.at[2], 4)


def share4_relay(net, out, by_x, by_y):
    half = out.shape[1] // 2
    top, bottom = pl.ds(0, half), pl.ds(half, half)
    by_x.wait_recv()
    first = net.send(out.at[1, top], out.at[3, top], 4)
    by_y.wait_recv()
    second = net.send(out.at[2, bottom], out.at[3, bottom], 2)
    return first, second


def collect4(net, part, buf, far):
    half = far.shape[1]
    rows = (pl.ds(0, half), pl.ds(half, half))
    low = jnp.bfloat16
    full = jnp.float32
    for i in (0, 1):
        buf[2, rows[i]] = part(3, i).astype(low)
    far_x = net.send(buf.at[2, rows[0]], far.at[0], 2)
    far_y = net.send(buf.at[2, rows[1]], far.at[1], 4)
    buf[0, rows[0]] = part(1, 0).astype(low)
    one_a = net.send(buf.at[0, rows[0]], buf.at[3, rows[0]], 2)
    buf[1, rows[1]] = part(2, 1).astype(low)
    two_b = net.send(buf.at[1, rows[1]], buf.at[4, rows[1]], 4)
    later = []

    def middle():
        far_x.wait_recv()
        buf[1, rows[0]] = (part(2, 0) + far[0].astype(full)).astype(low)
        later.append(net.send(buf.at[1, rows[0]], buf.at[4, rows[0]], 4))
        far_y.wait_recv()
        buf[0, rows[1]] = (part(1, 1) + far[1].astype(full)).astype(low)
        later.append(net.send(buf.at[0, rows[1]], buf.at[3, rows[1]], 2))

    def finish(i):
        (one_a, two_b)[i].wait_recv()
        later[i].wait_recv()
        return part(0, i) + buf[3, rows[i]].astype(full) + buf[4, rows[i]].astype(full)

    return middle, finish


def pick_rows(table, seg, first):
    out = table[first + IMGS - 1 : first + IMGS]
    for i in range(IMGS - 2, -1, -1):
        out = jnp.where(seg == i, table[first + i : first + i + 1], out)
    return out


def row_sums(a, b):
    ones = jnp.ones((8, a.shape[1]), jnp.float32)

    def one(v):
        return lax.dot_general(
            ones, v, (((1,), (1,)), ((), ())), precision=HIGH, preferred_element_type=jnp.float32
        )

    if b is None:
        return one(a)
    got = one(a)
    return jnp.where(lax.broadcasted_iota(jnp.int32, got.shape, 0) < 4, got, one(b))


class Lines:
    MASKS = (2, 4, 6)

    def __init__(self, net, src, dst, width, sems, local):
        self.net, self.src, self.dst, self.width, self.sems = net, src, dst, width, sems
        self.plane = lax.axis_index("bucket")
        self.chip = net.me // 2
        self.core = net.me % 2
        self.local = local
        self.ids = range(src.shape[0])

    def columns(self, c):
        return pl.ds(pl.multiple_of(c * self.width, 128), self.width)

    def lanes(self, i):
        return pl.ds(i * self.width, self.width)

    def away_start(self):
        own = self.dst.at[self.chip, self.core, self.plane]
        self.away = [
            self.net.send(
                self.src.at[i, self.plane, :, self.columns(self.net.peer(m) // 2)],
                own.at[:, self.lanes(i)],
                m,
            )
            for m in self.MASKS
            for i in self.ids
        ]

    def own_start(self):
        own = self.dst.at[self.chip, self.core]
        cuts = [self.src.at[i, :, :, self.columns(self.chip)] for i in self.ids]
        puts = [own.at[:, :, self.lanes(i)] for i in self.ids]
        self.ready = [self.net.send(a, b, 1) for a, b in zip(cuts, puts)]
        self.here = [self.local(i, a, b) for i, (a, b) in enumerate(zip(cuts, puts))]

    def copy(self, up, k, slab):
        at = self.dst.at[self.net.peer(self.MASKS[k]) // 2, self.core, slab]
        first = ((k * 2 + (0 if up else 1)) * 4 + slab) * 2
        return pltpu.make_async_remote_copy(
            src_ref=at,
            dst_ref=at,
            send_sem=self.sems.at[first],
            recv_sem=self.sems.at[first + 1],
            device_id={"bucket": self.plane + (1 if up else -1)},
            device_id_type=MESH_IDS,
        )

    def moves(self, h):
        for up in (True, False):
            slab = self.plane - h if up else self.plane + h
            there = (slab >= 0) if up else (slab <= 3)
            sends = (self.plane <= 2) if up else (self.plane >= 1)
            yield up, slab, there, sends

    def hop(self, h):
        if h == 0:
            for c in self.away:
                c.wait_recv()
        for up, slab, there, sends in self.moves(h):

            @pl.when(there)
            def _(up=up, slab=slab, sends=sends):
                for k in range(3):
                    if h > 0:
                        self.copy(up, k, slab).wait_recv()
                    if h < 3:

                        @pl.when(sends)
                        def _(k=k):
                            self.copy(up, k, slab).start()

    def finish(self):
        self.hop(3)
        for m in self.MASKS:
            at = self.dst.at[self.net.peer(m) // 2, self.core]
            self.ready.append(self.net.send(at, at, 1))

    def wait(self):
        for c in self.ready:
            c.wait_recv()

    def close(self):
        for h in range(3):
            for up, slab, there, sends in self.moves(h):

                @pl.when(there & sends)
                def _(up=up, slab=slab):
                    for k in range(3):
                        self.copy(up, k, slab).wait_send()


def meet_line(net, masks):
    plane = lax.axis_index("bucket")
    sem = pltpu.get_barrier_semaphore()
    for mask in masks:
        pl.semaphore_signal(
            sem, inc=1, device_id={"fsdp": net.peer(mask)}, device_id_type=MESH_IDS
        )
    for inner, step in ((plane >= 1, -1), (plane <= 2, 1)):

        @pl.when(inner)
        def _(step=step):
            pl.semaphore_signal(
                sem, inc=1, device_id={"bucket": plane + step}, device_id_type=MESH_IDS
            )

    one = jnp.int32(1)
    zero = jnp.int32(0)
    pl.semaphore_wait(
        sem, len(masks) + jnp.where(plane >= 1, one, zero) + jnp.where(plane <= 2, one, zero)
    )


ALL_PEERS = (1, 2, 3, 4, 5, 6, 7)


def open_kernel(
    cond_ref, gain_ref, bias_ref, ada_ref, tok_ref, counts_ref, idx_ref, freq_ref, attn_ref, textw_ref,
    text_ref,
    mod_ref, gains_ref, h_out, idxs_ref, aw_out, ta_out, q_out, k_out, v_out, tk_ref, tv_ref,
    iq_ref, ik_ref, it_ref, cos_ref, sin_ref, sc_ref, gs_ref,
    seg_ref, w_ref, h_ref, aw_ref, q_ref, k_ref, v_ref, conds, parts, mods, gbuf, tw_ref, ta_ref, sums, tsums, local_sems, out_sems, attn_sems, text_sems,
    send_sems, recv_sems,
):
    low = jnp.bfloat16
    full = jnp.float32
    net = Net(send_sems, recv_sems)
    me = net.me
    chip = me // 2
    meet_line(net, ALL_PEERS)

    act = cond_ref[...].astype(full)
    act = (act * jax.nn.sigmoid(act)).astype(low).astype(full)
    act = jnp.concatenate([act, act], axis=0)
    for j in range(8):
        gbuf[8, :, 128 * j : 128 * j + 128] = act[:, 128 * j : 128 * j + 128]
    waits = []
    for m in ALL_PEERS:
        at = pl.ds(pl.multiple_of(net.peer(m) * 128, 128), 128)
        waits.append(net.send(gbuf.at[8, :, at], conds.at[m], m))
    conds[0] = gbuf[8, :, pl.ds(pl.multiple_of(me * 128, 128), 128)]
    gwaits = [net.send(gain_ref, gbuf.at[m], m) for m in ALL_PEERS]
    iwaits = [net.send(idx_ref, idxs_ref.at[i], m) for i, m in ((1, 2), (2, 4), (3, 6))]
    idxs_ref[0] = idx_ref[...]

    def local(first):
        def go(i, src, dst):
            copy = pltpu.make_async_copy(src, dst, local_sems.at[first + i])
            copy.start()
            return copy

        return go

    attn_io = Lines(net, attn_ref, aw_ref, HW, attn_sems, local(3))
    text_io = Lines(net, textw_ref, tw_ref, HW, text_sems, local(6))
    attn_io.away_start()
    text_io.away_start()
    own_text = local(2)(0, text_ref, ta_ref.at[0])

    for w in waits:
        w.wait_recv()
    lhs = jnp.concatenate([conds[m] for m in range(8)], axis=0).astype(low)
    half_cols = 3072
    step = 512

    def mod_cols(i, _):
        lo = pl.ds(pl.multiple_of(i * step, step), step)
        hi = pl.ds(pl.multiple_of(half_cols + i * step, step), step)
        a = jnp.dot(lhs, ada_ref[:, lo], preferred_element_type=full)
        b = jnp.dot(lhs, ada_ref[:, hi], preferred_element_type=full)
        row = lax.broadcasted_iota(jnp.int32, (8, step), 0)
        for m in range(8):
            parts[m, :, lo] = (
                jnp.where(row < 4, a[8 * m : 8 * m + 8], b[8 * m : 8 * m + 8]) + bias_ref[:, lo]
            )
        return 0

    lax.fori_loop(0, half_cols // step, mod_cols, 0)
    waits = [net.send(parts.at[m], mods.at[m], m) for m in ALL_PEERS]

    attn_io.own_start()
    text_io.own_start()
    own_text.wait()

    def keep(j):
        copy = pltpu.make_async_copy(ta_ref.at[j], ta_out.at[j], out_sems.at[j])
        copy.start()
        return copy

    kept = [keep(0)]
    chunks = 4
    size = ta_ref.shape[1] // chunks
    tx, ty = [None] * chunks, [None] * chunks

    def text_send(s):
        i, j = s, (s + chunks // 2) % chunks
        at = pl.ds(i * size, size)
        tx[i] = net.send(ta_ref.at[0, at], ta_ref.at[1, at], 2)
        at = pl.ds(j * size, size)
        ty[j] = net.send(ta_ref.at[0, at], ta_ref.at[2, at], 4)

    text_send(0)
    attn_io.hop(0)
    text_io.hop(0)
    seg_ref[...] = jnp.transpose(idx_ref[...].astype(full))[:, 0:1].astype(jnp.int32)
    totals = counts_ref[...].astype(full)
    bucket = lax.broadcasted_iota(jnp.int32, totals.shape, 1) == lax.axis_index("bucket")
    here = jnp.sum(jnp.where(bucket, totals, 0.0), axis=-1, keepdims=True)
    weight = CHIPS * here / jnp.sum(totals, axis=-1, keepdims=True)
    w_ref[...] = jnp.broadcast_to(weight, w_ref.shape)
    for w in gwaits:
        w.wait_recv()
    gains = gain_ref[...]
    for m in ALL_PEERS:
        gains = gains + gbuf[m]
    gains_ref[...] = gains
    for w in waits:
        w.wait_recv()

    def mod_sum(i, _):
        at = pl.ds(pl.multiple_of(i * step, step), step)
        total = parts[0, :, at]
        for m in ALL_PEERS:
            total = total + mods[m, :, at]
        mod_ref[:, at] = total
        return 0

    lax.fori_loop(0, half_cols // step, mod_sum, 0)

    block = 32

    def first_norm(i, _):
        at = pl.ds(pl.multiple_of(i * block, block), block)
        x = tok_ref[at, :].astype(full)
        normed = x * lax.rsqrt(jnp.mean(x * x, axis=-1, keepdims=True) + EPS)
        scale = pick_rows(mod_ref[:, :D], seg_ref[at, :], 0)
        h_ref[0, at, :] = (normed * gains_ref[0:1, :] * (1.0 + scale)).astype(low)
        return 0

    lax.fori_loop(0, ROW // block, first_norm, 0)
    hx, hy = share4_start(net, h_ref)

    text_send(1)
    attn_io.hop(1)
    h_far = share4_relay(net, h_ref, hx, hy)
    for i in range(2, chunks):
        text_send(i)
    text_io.hop(1)
    attn_io.hop(2)
    attn_io.finish()
    text_io.hop(2)
    relays = []
    for s in range(chunks // 2):
        i, j = s, s + chunks // 2
        tx[i].wait_recv()
        at = pl.ds(i * size, size)
        relays.append(net.send(ta_ref.at[1, at], ta_ref.at[3, at], 4))
        ty[j].wait_recv()
        at = pl.ds(j * size, size)
        relays.append(net.send(ta_ref.at[2, at], ta_ref.at[3, at], 2))

    for c in iwaits:
        c.wait_recv()
    gs_ref[...] = gains_ref[:, pl.ds(pl.multiple_of(chip * HW, 128), HW)]
    lane = lax.broadcasted_iota(jnp.int32, (ROW, 128), 1)
    sign = jnp.where((lane // 16) % 2 == 0, -1.0, 1.0)
    for j in range(CHIPS):
        at = pl.ds(j * ROW, ROW)
        cols = jnp.transpose(idxs_ref[j].astype(full))
        sc_ref[at, :] = cols[:, 0:1].astype(jnp.int32)
        place = jnp.where((lane // 32) % 2 == 0, cols[:, 1:2], cols[:, 2:3])
        angle = place * freq_ref[0:1, :]
        cos_ref[at, :] = jnp.cos(angle)
        sin_ref[at, :] = sign * jnp.sin(angle)

    attn_io.wait()
    for c in attn_io.here:
        c.wait()
    for c in h_far:
        c.wait_recv()

    def columns(lo, hi):
        return aw_ref[:, :, :, :, lo:hi].reshape(D, hi - lo)

    for j in range(CHIPS):
        h = h_ref[j]
        at = pl.ds(j * ROW, ROW)
        qv = jnp.dot(h, columns(0, HW), preferred_element_type=full)
        q_ref[at, :] = qv
        kv = jnp.dot(h, columns(HW, 2 * HW), preferred_element_type=full)
        k_ref[at, :] = kv
        v_ref[at, :] = jnp.dot(h, columns(2 * HW, 3 * HW), preferred_element_type=full).astype(low)
        sums[0, :, at] = row_sums(qv * qv, kv * kv)
    sum_io = [net.send(sums.at[0], sums.at[i], m) for i, m in ((1, 2), (2, 4), (3, 6))]
    early = ((h_ref, h_out), (aw_ref, aw_out), (q_ref, q_out), (k_ref, k_out), (v_ref, v_out))
    for i, (src, dst) in enumerate(early):
        kept.append(pltpu.make_async_copy(src, dst, out_sems.at[CHIPS + i]))
        kept[-1].start()

    text_io.finish()
    text_io.wait()
    for c in text_io.here:
        c.wait()

    def text_rows(j, lo, count):
        kt = 1024

        def body(i, acc):
            at = pl.ds(pl.multiple_of(i * kt, kt), kt)
            rows = ta_ref[j, pl.ds(lo, count), at]
            return acc + jnp.dot(rows, tw_ref[i].reshape(kt, 2 * HW), preferred_element_type=full)

        both = lax.fori_loop(0, ta_ref.shape[2] // kt, body, jnp.zeros((count, 2 * HW), full))
        keys, vals = both[:, :HW], both[:, HW:]
        at = pl.ds(j * ta_ref.shape[1] + lo, count)
        tk_ref[at, :] = keys
        tv_ref[at, :] = vals.astype(low)
        tsums[0, :, at] = row_sums(keys * keys, None)

    cap = ta_ref.shape[1]
    half = cap // 2
    text_rows(0, 0, cap)
    for i, c in enumerate(sum_io):
        c.wait_recv()
    for j in range(CHIPS):
        total = sums[0, :, pl.ds(j * ROW, ROW)]
        for i in (1, 2, 3):
            total = total + sums[i, :, pl.ds((j ^ i) * ROW, ROW)]
        both = jnp.transpose(lax.rsqrt(total / D + EPS))
        iq_ref[pl.ds(j * ROW, ROW), :] = both[:, 0:1]
        ik_ref[pl.ds(j * ROW, ROW), :] = both[:, 4:5]
    text_rows(1, 0, half)
    text_rows(2, half, half)
    for s in range(chunks // 2):
        tx[s + chunks // 2].wait_recv()
        ty[s].wait_recv()
    kept += [keep(1), keep(2)]
    text_rows(1, half, half)
    text_rows(2, 0, half)
    for c in relays:
        c.wait_recv()
    kept.append(keep(3))
    text_rows(3, 0, cap)
    sum_io = [net.send(tsums.at[0], tsums.at[i], m) for i, m in ((1, 2), (2, 4), (3, 6))]
    for c in sum_io:
        c.wait_recv()
    for j in range(CHIPS):
        total = tsums[0, :, pl.ds(j * cap, cap)]
        for i in (1, 2, 3):
            total = total + tsums[i, :, pl.ds((j ^ i) * cap, cap)]
        it_ref[pl.ds(j * cap, cap), :] = jnp.transpose(lax.rsqrt(total / D + EPS))[:, 0:1]
    for c in kept:
        c.wait()
    attn_io.close()
    text_io.close()
    net.close()


def open_layer(cond, gain_pad, bias_pad, ada, tok, counts, idx, freq, attn, textw, text):
    low = jnp.bfloat16
    full = jnp.float32
    shape = jax.ShapeDtypeStruct
    cap, txtd = text.shape
    V = VMEM_SPEC
    return pl.pallas_call(
        open_kernel,
        in_specs=[V] * 8 + [ANY_SPEC] * 3,
        out_specs=[V, V, ANY_SPEC, V] + [ANY_SPEC] * 5 + [V] * 11,
        out_shape=[
            shape((8, 3072), full),
            shape((8, D), full),
            shape((CHIPS, ROW, D), low),
            shape((CHIPS, 8, ROW), jnp.int32),
            shape((CHIPS, 2, *attn.shape[1:3], 3 * HW), low),
            shape((CHIPS, cap, txtd), low),
            shape((CHIPS * ROW, HW), full),
            shape((CHIPS * ROW, HW), full),
            shape((CHIPS * ROW, HW), low),
            shape((CHIPS * cap, HW), full),
            shape((CHIPS * cap, HW), low),
            shape((CHIPS * ROW, 1), full),
            shape((CHIPS * ROW, 1), full),
            shape((CHIPS * cap, 1), full),
            shape((CHIPS * ROW, 128), full),
            shape((CHIPS * ROW, 128), full),
            shape((CHIPS * ROW, 1), jnp.int32),
            shape((8, HW), full),
            shape((ROW, 1), jnp.int32),
            shape((8, 128), full),
        ],
        scratch_shapes=[
            pltpu.VMEM((CHIPS, ROW, D), low),
            pltpu.VMEM((CHIPS, 2, *attn.shape[1:3], 3 * HW), low),
            pltpu.VMEM((CHIPS * ROW, HW), full),
            pltpu.VMEM((CHIPS * ROW, HW), full),
            pltpu.VMEM((CHIPS * ROW, HW), low),
            pltpu.VMEM((8, 8, 128), full),
            pltpu.VMEM((8, 8, 3072), full),
            pltpu.VMEM((8, 8, 3072), full),
            pltpu.VMEM((9, 8, D), full),
            pltpu.VMEM((CHIPS, 2, *textw.shape[1:3], 2 * HW), low),
            pltpu.VMEM((CHIPS, cap, txtd), low),
            pltpu.VMEM((CHIPS, 8, CHIPS * ROW), full),
            pltpu.VMEM((CHIPS, 8, CHIPS * cap), full),
            pltpu.SemaphoreType.DMA((8,)),
            pltpu.SemaphoreType.DMA((CHIPS + 5,)),
            pltpu.SemaphoreType.DMA((48,)),
            pltpu.SemaphoreType.DMA((48,)),
            *net_scratch(80),
        ],
        compiler_params=pltpu.CompilerParams(
            collective_id=1, has_side_effects=True, vmem_limit_bytes=56 * 1024 * 1024
        ),
        cost_estimate=pl.CostEstimate(
            flops=10_000_000_000, bytes_accessed=400_000_000, transcendentals=0
        ),
    )(cond, gain_pad, bias_pad, ada, tok, counts, idx, freq, attn, textw, text)


class Chain:
    def __init__(self, net, grad, mine, arrive, total, sems, columns):
        self.net = net
        self.grad = grad
        self.mine = mine
        self.arrive = arrive
        self.total = total
        self.sems = sems
        self.columns = columns
        self.plane = lax.axis_index("bucket")
        self.core = net.me % 2

    def piece(self, ref, p):
        return ref.at[:, p] if self.columns else ref.at[p]

    def half(self, core):
        return self.grad.at[:, :, :, core] if self.columns else self.grad.at[:, core]

    def each(self, ref, body):
        lead = ref.shape[:-2]
        if not lead:
            body(())
            return
        total = 1
        for n in lead:
            total *= n

        def step(i, _):
            index = []
            for n in reversed(lead):
                index.insert(0, i % n)
                i = i // n
            body(tuple(index))
            return 0

        lax.fori_loop(0, total, step, 0)

    def core_start(self, keep=None, sem=None):
        self.exchange = self.net.send(self.half(1 - self.core), self.mine, 1)
        self.keep = self.half(self.core)
        self.load = None
        if keep is not None:
            self.load = pltpu.make_async_copy(self.keep, keep, sem)
            self.load.start()
            self.keep = keep

    def add(self, into, other):
        def body(index):
            value = into[index].astype(jnp.float32) + other[index].astype(jnp.float32)
            into[index] = value.astype(into.dtype)

        self.each(into, body)

    def core_finish(self):
        self.exchange.wait_recv()
        if self.load is not None:
            self.load.wait()
        self.add(self.mine, self.keep)

    def copy(self, up, p, slot):
        first = 0 if up else 8
        return pltpu.make_async_remote_copy(
            src_ref=self.piece(self.mine, p),
            dst_ref=self.arrive.at[slot],
            send_sem=self.sems.at[first + p],
            recv_sem=self.sems.at[first + 4 + p],
            device_id={"bucket": self.plane + (1 if up else -1)},
            device_id_type=MESH_IDS,
        )

    def moves(self, t):
        up = self.plane + 3 - t
        down = self.plane - 3 + t
        return (
            (True, up, up, self.plane <= t, self.plane >= 1),
            (False, down, 4 if t == 2 else down, self.plane >= 3 - t, self.plane <= 2),
        )

    def step(self, t):
        for up, p, slot, sends, inner in self.moves(t):

            @pl.when(sends)
            def _(up=up, p=p, slot=slot, inner=inner):
                @pl.when(inner)
                def _():
                    self.copy(up, p, p).wait_recv()
                    self.add(self.piece(self.mine, p), self.arrive.at[p])

                self.copy(up, p, slot).start()

    def finish(self):
        own = self.piece(self.mine, self.plane)

        def first(index):
            self.total[index] = own[index].astype(jnp.float32)

        self.each(self.total, first)
        for up, slot, inner in ((True, self.plane, self.plane >= 1), (False, 4, self.plane <= 2)):

            @pl.when(inner)
            def _(up=up, slot=slot):
                self.copy(up, self.plane, slot).wait_recv()
                self.add(self.total, self.arrive.at[slot])

    def close(self):
        for t in range(3):
            for up, p, slot, sends, inner in self.moves(t):

                @pl.when(sends)
                def _(up=up, p=p, slot=slot):
                    self.copy(up, p, slot).wait_send()


def chain_scratch(columns, shape, width):
    low = jnp.bfloat16
    if columns:
        n, rows = shape
        return [
            pltpu.VMEM((n, 4, 4, rows, width), low),
            pltpu.VMEM((5, n, 4, rows, width), low),
            pltpu.VMEM((n, 4, rows, width), jnp.float32),
            pltpu.SemaphoreType.DMA((16,)),
        ]
    return [
        pltpu.VMEM((4, shape, width), low),
        pltpu.VMEM((5, shape, width), low),
        pltpu.VMEM((shape, width), jnp.float32),
        pltpu.SemaphoreType.DMA((16,)),
    ]


class Columns:
    def __init__(self, net, total, stage, wide):
        self.net, self.total, self.stage, self.wide = net, total, stage, wide

    def start(self):
        net = self.net
        chip = net.me // 2
        n, _, rows, width = self.stage.shape
        parts = self.wide.shape[0]
        width = width // parts
        at = pl.ds(pl.multiple_of(chip * width, width), width)

        def cast(i, _):
            self.stage[i // 4, i % 4] = self.total[i // 4, i % 4].astype(jnp.bfloat16)
            return 0

        if self.total is not None:
            lax.fori_loop(0, n * 4, cast, 0)
        self.copies = [
            net.send(
                self.stage.at[0, net.peer(m) // 2, :, pl.ds(i * width, width)],
                self.wide.at[i, :, at],
                m,
            )
            for m in (2, 4, 6)
            for i in range(parts)
        ]
        for i in range(parts):
            self.wide[i, :, at] = self.stage[0, chip, :, i * width : i * width + width]

    def finish(self):
        for c in self.copies:
            c.wait_recv()


def meet_all(net, far=False):
    plane = lax.axis_index("bucket")
    chip = net.me // 2
    sem = pltpu.get_barrier_semaphore()
    for mask in ALL_PEERS:
        pl.semaphore_signal(
            sem, inc=1, device_id={"fsdp": net.peer(mask)}, device_id_type=MESH_IDS
        )
    for inner, step in ((plane >= 1, -1), (plane <= 2, 1)):

        @pl.when(inner)
        def _(step=step):
            pl.semaphore_signal(
                sem, inc=1, device_id={"bucket": plane + step}, device_id_type=MESH_IDS
            )

    @pl.when(chip != plane)
    def _():
        pl.semaphore_signal(
            sem,
            inc=1,
            device_id={"bucket": chip, "fsdp": plane * 2 + net.me % 2},
            device_id_type=MESH_IDS,
        )

    if far:
        pl.semaphore_signal(
            sem,
            inc=1,
            device_id={"bucket": plane + 2 - 4 * (plane // 2)},
            device_id_type=MESH_IDS,
        )
    one = jnp.int32(1)
    zero = jnp.int32(0)
    count = (
        (8 if far else 7)
        + jnp.where(plane >= 1, one, zero)
        + jnp.where(plane <= 2, one, zero)
        + jnp.where(chip != plane, one, zero)
    )
    pl.semaphore_wait(sem, count)


def transposed(net, src, dst, sems):
    plane = lax.axis_index("bucket")
    return pltpu.make_async_remote_copy(
        src_ref=src,
        dst_ref=dst,
        send_sem=sems.at[0],
        recv_sem=sems.at[1],
        device_id={"bucket": net.me // 2, "fsdp": plane * 2 + net.me % 2},
        device_id_type=MESH_IDS,
    )


class Spread:
    def __init__(self, buf, sems):
        self.buf, self.sems = buf, sems
        self.plane = lax.axis_index("bucket")

    def copy(self, up, slab):
        first = 0 if up else 8
        return pltpu.make_async_remote_copy(
            src_ref=self.buf.at[slab],
            dst_ref=self.buf.at[slab],
            send_sem=self.sems.at[first + slab],
            recv_sem=self.sems.at[first + 4 + slab],
            device_id={"bucket": self.plane + (1 if up else -1)},
            device_id_type=MESH_IDS,
        )

    def hop(self, h):
        for up in (True, False):
            slab = self.plane - h if up else self.plane + h
            there = (slab >= 0) if up else (slab <= 3)
            sends = (self.plane <= 2) if up else (self.plane >= 1)

            @pl.when(there)
            def _(up=up, slab=slab, sends=sends):
                if h > 0:
                    self.copy(up, slab).wait_recv()

                @pl.when(sends)
                def _():
                    self.copy(up, slab).start()

    def close(self):
        for h in range(4):
            for up in (True, False):
                slab = self.plane - h if up else self.plane + h
                there = (slab >= 0) if up else (slab <= 3)
                sends = (self.plane <= 2) if up else (self.plane >= 1)

                @pl.when(there & sends)
                def _(up=up, slab=slab):
                    self.copy(up, slab).wait_send()


def close_kernel(
    text_g, attn_g, out_g, ffn_t, dmod_ref, gg_ref, gs_ref, cond_ref,
    t_wide, a_wide, out_o, f_wide, ada_o, small_o,
    tm, ta, tt, ts, am, aa, at_, as_, om, oa, ot, os_,
    t_stage, a_stage, o_stage, o_got, o_sem,
    mods, mods_other, mod_sems, smalls, got, z_sems, ada_s, send_sems, recv_sems,
):
    low = jnp.bfloat16
    full = jnp.float32
    net = Net(send_sems, recv_sems)
    meet_all(net, True)
    plane = lax.axis_index("bucket")
    me = net.me
    chip = me // 2
    out = Chain(net, out_g, om, oa, ot, os_, False)
    attn = Chain(net, attn_g, am, aa, at_, as_, True)
    text = Chain(net, text_g, tm, ta, tt, ts, True)
    chains = [out, text, attn]
    for c in chains:
        c.core_start()

    act = cond_ref[...].astype(full)
    act = act * jax.nn.sigmoid(act)
    mods[plane, 0, :, 2 * D :] = jnp.concatenate([act, act], axis=0).astype(low)
    mods[plane, 0, :, : 2 * D] = dmod_ref[...].astype(low)
    mine = mods.at[plane, 0]
    mod_io = [net.send(mine, mods.at[plane, i], m) for i, m in ((1, 2), (2, 4), (3, 6))]

    smalls[...] = jnp.zeros(smalls.shape, full)
    smalls[0:2, :] = gg_ref[0:2, :]
    smalls[2:6, pl.ds(pl.multiple_of(chip * HW, 128), HW)] = gs_ref[0:4, :]
    for p in range(4):
        rows = dmod_ref[4 * (p // 2) : 4 * (p // 2) + 4, (p % 2) * D : (p % 2 + 1) * D]
        smalls[8 + p : 9 + p, :] = jnp.sum(rows, axis=0, keepdims=True)
    order = [None]

    def small_send(i):
        if i < 3:
            order[0] = net.send(smalls, got.at[i], (1, 2, 4)[i])
            return
        there = plane + 1 - 2 * (plane % 2) if i == 3 else plane + 2 - 4 * (plane // 2)
        copy = pltpu.make_async_remote_copy(
            src_ref=smalls,
            dst_ref=got.at[i],
            send_sem=z_sems.at[2 * (i - 3)],
            recv_sem=z_sems.at[2 * (i - 3) + 1],
            device_id={"bucket": there},
            device_id_type=MESH_IDS,
        )
        copy.start()
        order[0] = copy

    def small_add(i):
        order[0].wait()
        net.all = [c for c in net.all if c is not order[0]]
        smalls[...] = smalls[...] + got[i]

    small_send(0)
    f_cols = Columns(net, None, ffn_t, f_wide)
    f_cols.start()
    for c in chains:
        c.core_finish()
        c.step(0)
    small_add(0)
    small_send(1)
    for c in mod_io:
        c.wait_recv()
    lines = Spread(mods, mod_sems)
    lines.hop(0)
    small_add(1)
    small_send(2)
    for c in chains:
        c.step(1)
    lines.hop(1)
    small_add(2)
    small_send(3)
    f_cols.finish()
    for c in chains:
        c.step(2)
    lines.hop(2)
    small_add(3)
    small_send(4)
    lines.hop(3)
    other = net.send(mods, mods_other, 1)
    small_add(4)
    small_o[...] = smalls[...]
    out.finish()
    o_stage[...] = ot[...].astype(low)

    @pl.when(chip != plane)
    def _():
        transposed(net, o_stage, o_got, o_sem).start()

    other.wait_recv()
    rank = plane * 8 + me
    lanes = pl.ds(pl.multiple_of(2 * D + (rank // 4) * 128, 128), 128)
    total = 128
    both = []
    for ref in (mods, mods_other):
        acts = ref[:, :, :, lanes].astype(full).reshape(total, 128)
        both.append(acts)
    acts = jnp.concatenate(both, axis=0)
    upper = (lax.broadcasted_iota(jnp.int32, acts.shape, 0) % 8) < 4
    parts = (jnp.where(upper, acts, 0.0).astype(low), jnp.where(upper, 0.0, acts).astype(low))
    wide = 512

    def ada_cols(i, _):
        at = pl.ds(pl.multiple_of(i * wide, wide), wide)
        rows = jnp.concatenate(
            [r[:, :, :, at].astype(full).reshape(total, wide) for r in (mods, mods_other)], axis=0
        ).astype(low)
        for p in range(2):
            ada_s[...] = t_dot(parts[p], rows)
            to = pl.ds(pl.multiple_of(p * 2 * D + i * wide, wide), wide)
            ada_o[:, to] = ada_s[pl.ds(pl.multiple_of((rank % 4) * 32, 32), 32), :]
        return 0

    lax.fori_loop(0, 2 * D // wide, ada_cols, 0)
    text.finish()
    text_cols = Columns(net, tt, t_stage, t_wide)
    text_cols.start()

    @pl.when(chip != plane)
    def _():
        transposed(net, o_stage, o_got, o_sem).wait()
        out_o[...] = o_got[...]

    @pl.when(chip == plane)
    def _():
        out_o[...] = o_stage[...]

    attn.finish()
    attn_cols = Columns(net, at_, a_stage, a_wide)
    attn_cols.start()
    text_cols.finish()
    attn_cols.finish()
    for c in chains:
        c.close()
    lines.close()
    net.close()


def close_layer(text_g, attn_g, out_g, ffn_t, dmod, gg, gs, cond8):
    low = jnp.bfloat16
    full = jnp.float32
    shape = jax.ShapeDtypeStruct
    V = VMEM_SPEC
    tr, tw = text_g.shape[-2], text_g.shape[-1] // 2
    ar, aw = attn_g.shape[-2], attn_g.shape[-1] // 3
    orow, ow = out_g.shape[-2:]
    fr, fw = ffn_t.shape[-2], ffn_t.shape[-1] // 2
    return pl.pallas_call(
        close_kernel,
        in_specs=[V] * 8,
        out_specs=[V] * 6,
        out_shape=[
            shape((2, tr, 4 * tw), low),
            shape((3, ar, 4 * aw), low),
            shape((orow, ow), low),
            shape((2, fr, 4 * fw), low),
            shape((32, 4 * D), full),
            shape((16, D), full),
        ],
        scratch_shapes=[
            *chain_scratch(True, (1, tr), 2 * tw),
            *chain_scratch(True, (1, ar), 3 * aw),
            *chain_scratch(False, orow, ow),
            pltpu.VMEM((1, 4, tr, 2 * tw), low),
            pltpu.VMEM((1, 4, ar, 3 * aw), low),
            pltpu.VMEM((orow, ow), low),
            pltpu.VMEM((orow, ow), low),
            pltpu.SemaphoreType.DMA((2,)),
            pltpu.VMEM((4, CHIPS, 8, 2 * D + cond8.shape[1]), low),
            pltpu.VMEM((4, CHIPS, 8, 2 * D + cond8.shape[1]), low),
            pltpu.SemaphoreType.DMA((16,)),
            pltpu.VMEM((16, D), full),
            pltpu.VMEM((5, 16, D), full),
            pltpu.SemaphoreType.DMA((4,)),
            pltpu.VMEM((128, 512), full),
            *net_scratch(40),
        ],
        compiler_params=pltpu.CompilerParams(
            collective_id=2, has_side_effects=True, vmem_limit_bytes=60 * 1024 * 1024
        ),
        cost_estimate=pl.CostEstimate(
            flops=1_000_000, bytes_accessed=400_000_000, transcendentals=0
        ),
    )(text_g, attn_g, out_g, ffn_t, dmod, gg, gs, cond8)


def back_kernel(
    dh2_ref, fo_ref, x1_ref, branch_ref, cot_ref, w_ref, mod_ref, seg_ref, gain_ref, tok_ref,
    sr_ref, gs_ref, *rest,
):
    late, rest = rest[:LATE], rest[LATE:]
    places, rest = rest[-LATE - 1 : -1], rest[: -LATE - 1] + rest[-1:]
    loads = [
        pltpu.make_async_copy(src, dst, rest[-1].at[i])
        for i, (src, dst) in enumerate(zip(late, places))
    ]
    back_body(
        dh2_ref, fo_ref, x1_ref, branch_ref, cot_ref, w_ref, mod_ref, seg_ref, gain_ref, tok_ref,
        *places, sr_ref, gs_ref, *rest[:-1], loads,
    )


LATE = 17


def back_body(
    dh2_ref, fo_ref, x1_ref, branch_ref, cot_ref, w_ref, mod_ref, seg_ref, gain_ref, tok_ref,
    ow_ref, aw_ref, qr_ref, kr_ref, v_ref, tr_ref, tv_ref, cross_ref, q_ref, k_ref, tk_ref,
    iq_ref, ik_ref, it_ref, cos_ref, sin_ref, sc_ref, sr_ref, gs_ref, ffn_g, down_g,
    block_o, token_o, db_ref, dqkv_o, dtkv_o, dmod_o, gg_o, gs_o, ffn_o, down_o,
    dx_s, dc_s, dqf, dkf, dtf, part_s, sums, tsums, buf_a, far_a, buf_b, far_b, buf_c, far_c,
    fm, fa, ft, fs, dm, da, dt_c, ds_, f_keep, d_keep, keep_sem, send_sems, recv_sems, loads,
):
    low = jnp.bfloat16
    full = jnp.float32
    net = Net(send_sems, recv_sems)
    meet_all(net)
    plane = lax.axis_index("bucket")
    chip = net.me // 2
    ffn = Chain(net, ffn_g, fm, fa, ft, fs, True)
    down = Chain(net, down_g, dm, da, dt_c, ds_, False)
    ffn.core_start(f_keep, keep_sem.at[0])
    down.core_start(d_keep, keep_sem.at[1])
    for c in loads:
        c.start()

    def rows_of(ref):
        half = ROW // 2
        return lambda j, i: ref[pl.ds(j * ROW + i * half, half), :].astype(full)

    middle, finish = collect4(net, rows_of(dh2_ref), buf_a, far_a)
    middle()
    ffn.core_finish()
    ffn.step(0)
    down.core_finish()
    down.step(0)
    half = ROW // 2
    for i in (0, 1):
        dx_s[pl.ds(i * half, half), :] = finish(i)
    part_s[pl.ds(0, ROW), :] = dx_s[...]
    block = 32
    weight = w_ref[0:1, 0:1]

    def second_norm(at):
        x1 = x1_ref[at, :]
        inverse = lax.rsqrt(jnp.mean(x1 * x1, axis=-1, keepdims=True) + EPS)
        scale = pick_rows(mod_ref[:, :D], seg_ref[at, :], 4)
        return x1 * inverse, inverse, scale

    def to_branch(b, _):
        at = pl.ds(pl.multiple_of(b * block, block), block)
        normed, inverse, scale = second_norm(at)
        dn = dx_s[at, :] * gain_ref[1:2, :] * (1.0 + scale)
        back = inverse * (dn - normed * jnp.mean(dn * normed, axis=-1, keepdims=True))
        dx = cot_ref[at, :].astype(full) * weight + back
        dx_s[at, :] = dx
        gate = jnp.tanh(pick_rows(mod_ref[:, D:], seg_ref[at, :], 0))
        db_ref[0, at, :] = (dx * gate).astype(low)
        return 0

    lax.fori_loop(0, ROW // block, to_branch, 0)
    bx, by = share4_start(net, db_ref)

    def by_image(value, seg, row, lo):
        for i in range(IMGS):
            dmod_o[row + i : row + i + 1, lo : lo + D] += jnp.sum(
                jnp.where(seg == i, value, 0.0), axis=0, keepdims=True
            )

    dmod_o[...] = jnp.zeros(dmod_o.shape, full)
    gg_o[...] = jnp.zeros(gg_o.shape, full)

    def second_sums(b, _):
        at = pl.ds(pl.multiple_of(b * block, block), block)
        normed, inverse, scale = second_norm(at)
        seg = seg_ref[at, :]
        dh = part_s[at, :] * normed
        gg_o[1:2, :] += jnp.sum(dh * (1.0 + scale), axis=0, keepdims=True)
        by_image(dh * gain_ref[1:2, :], seg, 4, 0)
        gate = jnp.tanh(pick_rows(mod_ref[:, D:], seg, 0))
        by_image(dx_s[at, :] * branch_ref[at, :] * (1.0 - gate * gate), seg, 0, D)
        return 0

    lax.fori_loop(0, ROW // block, second_sums, 0)
    far = share4_relay(net, db_ref, bx, by)
    middle_b, finish_b = collect4(net, rows_of(fo_ref), buf_b, far_b)
    gs_o[...] = jnp.zeros(gs_o.shape, full)
    for c in loads:
        c.wait()
    cap = IMGS * TXT

    def attention_row(j, _):
        @pl.when(j == 3)
        def _():
            for c in far:
                c.wait_recv()

        @pl.when(j == 1)
        def _():
            ffn.step(1)
            down.step(1)

        @pl.when(j == 3)
        def _():
            ffn.step(2)
            down.step(2)

        rows = pl.ds(pl.multiple_of(j * ROW, ROW), ROW)
        text = pl.ds(pl.multiple_of(j * cap, cap), cap)
        dc_s[...] = dot_t(db_ref[j], ow_ref[...])
        dqv, dkv, dtv = dqf.at[rows], dkf.at[rows], dtf.at[text]
        attend_back_kernel(
            qr_ref.at[rows], kr_ref.at[rows], v_ref.at[rows], tr_ref.at[text], tv_ref.at[text],
            dc_s, cross_ref.at[rows], q_ref.at[rows], k_ref.at[rows], tk_ref.at[text],
            iq_ref.at[rows], ik_ref.at[rows], it_ref.at[text], cos_ref.at[rows], sin_ref.at[rows],
            sc_ref.at[rows], sr_ref.at[j, pl.ds(0, 1)], gs_ref,
            dqv, dkv, dqkv_o.at[rows, pl.ds(2 * HW, HW)], dtv, dtkv_o.at[text, pl.ds(HW, HW)], gs_o,
        )
        sums[0, :, rows] = row_sums(
            dqv[...] * (q_ref[rows, :] * iq_ref[rows, :]),
            dkv[...] * (k_ref[rows, :] * ik_ref[rows, :]),
        )
        tsums[0, :, text] = row_sums(dtv[...] * (tk_ref[text, :] * it_ref[text, :]), None)
        return 0

    lax.fori_loop(0, CHIPS, attention_row, 0)
    sum_io = []
    for i, m in ((1, 2), (2, 4), (3, 6)):
        sum_io.append(net.send(sums.at[0], sums.at[i], m))
        sum_io.append(net.send(tsums.at[0], tsums.at[i], m))
    middle_b()
    for i in (0, 1):
        part_s[pl.ds(i * half, half), :] = finish_b(i)

    def block_rows(b, _):
        at = pl.ds(pl.multiple_of(b * block, block), block)
        seg = seg_ref[at, :]
        gate = jnp.tanh(pick_rows(mod_ref[:, D:], seg, 4))
        out = part_s[at, :]
        block_o[at, :] = (x1_ref[at, :] + gate * out).astype(low)
        grad = cot_ref[at, :].astype(full) * weight
        by_image(grad * out * (1.0 - gate * gate), seg, 4, D)
        return 0

    for c in sum_io:
        c.wait_recv()
    for j in range(CHIPS):
        rows = pl.ds(j * ROW, ROW)
        text = pl.ds(j * cap, cap)
        total = sums[0, :, rows]
        words = tsums[0, :, text]
        for i in (1, 2, 3):
            total = total + sums[i, :, pl.ds((j ^ i) * ROW, ROW)]
            words = words + tsums[i, :, pl.ds((j ^ i) * cap, cap)]
        mean = jnp.transpose(total / D)
        iq, ik, it = iq_ref[rows, :], ik_ref[rows, :], it_ref[text, :]
        dqkv_o[rows, :HW] = (iq * (dqf[rows, :] - q_ref[rows, :] * iq * mean[:, 0:1])).astype(low)
        dqkv_o[rows, HW : 2 * HW] = (ik * (dkf[rows, :] - k_ref[rows, :] * ik * mean[:, 4:5])).astype(low)
        mean = jnp.transpose(words / D)
        dtkv_o[text, :HW] = (it * (dtf[text, :] - tk_ref[text, :] * it * mean[:, 0:1])).astype(low)

    lax.fori_loop(0, ROW // block, block_rows, 0)
    wide = 256

    def first_grad(n, _):
        at = pl.ds(pl.multiple_of(n * wide, wide), wide)
        part_s[:, at] = dot_t(dqkv_o[...], aw_ref[at, :])
        return 0

    lax.fori_loop(0, D // wide, first_grad, 0)
    middle_c, finish_c = collect4(net, rows_of(part_s), buf_c, far_c)
    ffn.finish()
    middle_c()

    def ffn_cast(i, _):
        ffn_o[0, i] = ft[0, i].astype(low)
        return 0

    lax.fori_loop(0, 4, ffn_cast, 0)
    down.finish()
    down_o[...] = dt_c[...].astype(low)
    gate = jnp.tanh(gs_ref[5:6, :])
    gs_o[3:4, :] = gs_o[3:4, :] * (1.0 - gate * gate)
    for i in (0, 1):
        part_s[pl.ds(i * half, half), :] = finish_c(i)

    def first_rows(b, _):
        at = pl.ds(pl.multiple_of(b * block, block), block)
        x = tok_ref[at, :].astype(full)
        inverse = lax.rsqrt(jnp.mean(x * x, axis=-1, keepdims=True) + EPS)
        normed = x * inverse
        seg = seg_ref[at, :]
        scale = pick_rows(mod_ref[:, :D], seg, 0)
        dh = part_s[at, :]
        gg_o[0:1, :] += jnp.sum(dh * normed * (1.0 + scale), axis=0, keepdims=True)
        by_image(dh * normed * gain_ref[0:1, :], seg, 0, 0)
        dn = dh * gain_ref[0:1, :] * (1.0 + scale)
        token_o[at, :] = dx_s[at, :] + inverse * (
            dn - normed * jnp.mean(dn * normed, axis=-1, keepdims=True)
        )
        return 0

    lax.fori_loop(0, ROW // block, first_rows, 0)
    ffn.close()
    down.close()
    net.close()


def back_layer(early, late, ffn_g, down_g):
    low = jnp.bfloat16
    full = jnp.float32
    shape = jax.ShapeDtypeStruct
    V = VMEM_SPEC
    cap = IMGS * TXT
    fr, fw = ffn_g.shape[-2], ffn_g.shape[-1] // 2
    dr, dw = down_g.shape[-2:]
    tok = CHIPS * ROW
    reduce_scratch = [pltpu.VMEM((5, ROW, D), low), pltpu.VMEM((2, ROW // 2, D), low)]
    return pl.pallas_call(
        back_kernel,
        in_specs=[V] * len(early) + [ANY_SPEC] * (LATE + 2),
        out_specs=[V] * 10,
        out_shape=[
            shape((ROW, D), low),
            shape((ROW, D), full),
            shape((CHIPS, ROW, D), low),
            shape((tok, 3 * HW), low),
            shape((CHIPS * cap, 2 * HW), low),
            shape((8, 2 * D), full),
            shape((8, D), full),
            shape((8, HW), full),
            shape((1, 4, fr, 2 * fw), low),
            shape((dr, dw), low),
        ],
        scratch_shapes=[
            pltpu.VMEM((ROW, D), full),
            pltpu.VMEM((ROW, HW), full),
            pltpu.VMEM((tok, HW), full),
            pltpu.VMEM((tok, HW), full),
            pltpu.VMEM((CHIPS * cap, HW), full),
            pltpu.VMEM((tok, D), full),
            pltpu.VMEM((CHIPS, 8, tok), full),
            pltpu.VMEM((CHIPS, 8, CHIPS * cap), full),
            *reduce_scratch, *reduce_scratch, *reduce_scratch,
            *chain_scratch(True, (1, fr), 2 * fw),
            *chain_scratch(False, dr, dw),
            pltpu.VMEM((1, 4, 4, fr, 2 * fw), low),
            pltpu.VMEM((4, dr, dw), low),
            pltpu.SemaphoreType.DMA((2,)),
            *net_scratch(48),
            *[pltpu.VMEM(v.shape, v.dtype) for v in late],
            pltpu.SemaphoreType.DMA((LATE,)),
        ],
        compiler_params=pltpu.CompilerParams(
            collective_id=3, has_side_effects=True, vmem_limit_bytes=63 * 1024 * 1024
        ),
        cost_estimate=pl.CostEstimate(
            flops=10_000_000_000, bytes_accessed=400_000_000, transcendentals=0
        ),
    )(*early, *late, ffn_g, down_g)


def row_spec(rows, width):
    return pl.BlockSpec((rows, width), lambda i: (i, 0))


def forward_kernel(
    q_ref, k_ref, v_ref, iq_ref, ik_ref, cos_ref, sin_ref, tk_ref, it_ref, tv_ref, sc_ref, sr_ref,
    gs_ref, mod_ref, seg_ref, gain_ref, tok_ref, cot_ref, w_ref, outw_ref, ffnw_ref, downw_ref,
    comb_o, cross_o, qr_o, kr_o, tr_o, branch_o, x1_o, h_o, df_o, ow_o, fw_o, dw_o,
    part_s, buf, far, f_own, d_own, local_sems, line_sems, send_sems, recv_sems,
):
    low = jnp.bfloat16
    full = jnp.float32
    net = Net(send_sems, recv_sems)
    meet_line(net, (1, 2, 4, 6))
    me = net.me
    chip = me // 2
    width = fw_o.shape[4] // 2
    rows = outw_ref.shape[0]

    def local(src, dst, i):
        copy = pltpu.make_async_copy(src, dst, local_sems.at[i])
        copy.start()
        return copy

    def own(ref, count):
        return ref.at[pl.ds(pl.multiple_of((me % 2) * count, count), count), :]

    out_here = local(outw_ref, own(ow_o, rows), 0)
    out_core = net.send(outw_ref, own(ow_o, rows), 1)
    down_rows = downw_ref.shape[0]
    down_here = local(downw_ref, d_own, 1)
    down_core = net.send(downw_ref, own(dw_o, down_rows), 1)

    def stage(i, src, dst):
        return local(src, f_own.at[:, :, pl.ds(i * width, width)], 2 + i)

    ffn_io = Lines(net, ffnw_ref, fw_o, width, line_sems, stage)
    ffn_io.away_start()
    ffn_io.own_start()
    block = 32
    weight = w_ref[0:1, 0:1]

    def ffn_grad(b, _):
        at = pl.ds(pl.multiple_of(b * block, block), block)
        gate = jnp.tanh(pick_rows(mod_ref[:, D:], seg_ref[at, :], 4))
        df_o[0, at, :] = (cot_ref[at, :].astype(full) * weight * gate).astype(low)
        return 0

    lax.fori_loop(0, ROW // block, ffn_grad, 0)
    dx, dy = share4_start(net, df_o)
    out_here.wait()
    out_core.wait_recv()
    cap = IMGS * TXT

    def attention_row(i, _):
        @pl.when(i == 1)
        def _():
            ffn_io.hop(0)

        @pl.when(i == 3)
        def _():
            ffn_io.hop(1)

        j = 3 - i
        at = pl.ds(pl.multiple_of(j * ROW, ROW), ROW)
        text = pl.ds(pl.multiple_of(j * cap, cap), cap)
        attend_kernel(
            q_ref.at[at], k_ref.at[at], v_ref.at[at], iq_ref.at[at], ik_ref.at[at],
            cos_ref.at[at], sin_ref.at[at], tk_ref.at[text], it_ref.at[text], tv_ref.at[text],
            sc_ref.at[at], sr_ref.at[j, pl.ds(0, 1)], gs_ref,
            comb_o.at[at], cross_o.at[at], qr_o.at[at], kr_o.at[at], tr_o.at[text],
        )
        part_s[at, :] = jnp.dot(comb_o[at, :], ow_o[...], preferred_element_type=full)
        return 0

    lax.fori_loop(0, CHIPS, attention_row, 0)
    half = ROW // 2
    middle, finish = collect4(
        net, lambda j, i: part_s[pl.ds(j * ROW + i * half, half), :], buf, far
    )
    df_far = share4_relay(net, df_o, dx, dy)

    down_here.wait()
    down_out = local(d_own, own(dw_o, down_rows), 4)
    for c in ffn_io.here:
        c.wait()
    f_out = local(f_own, fw_o.at[chip, me % 2], 5)
    middle()
    ffn_io.hop(2)
    for i in (0, 1):
        branch_o[pl.ds(i * half, half), :] = finish(i)

    def second(b, _):
        at = pl.ds(pl.multiple_of(b * block, block), block)
        seg = seg_ref[at, :]
        gate = jnp.tanh(pick_rows(mod_ref[:, D:], seg, 0))
        x1 = tok_ref[at, :].astype(full) + gate * branch_o[at, :]
        x1_o[at, :] = x1
        normed = x1 * lax.rsqrt(jnp.mean(x1 * x1, axis=-1, keepdims=True) + EPS)
        scale = pick_rows(mod_ref[:, :D], seg, 4)
        h_o[0, at, :] = (normed * gain_ref[1:2, :] * (1.0 + scale)).astype(low)
        return 0

    lax.fori_loop(0, ROW // block, second, 0)
    hx, hy = share4_start(net, h_o)
    ffn_io.finish()
    last = share4_relay(net, h_o, hx, hy)
    for c in (*df_far, *last, down_core):
        c.wait_recv()
    ffn_io.wait()
    down_out.wait()
    f_out.wait()
    ffn_io.close()
    net.close()


def forward_layer(*args):
    low = jnp.bfloat16
    full = jnp.float32
    shape = jax.ShapeDtypeStruct
    V = VMEM_SPEC
    cap = IMGS * TXT
    tok = CHIPS * ROW
    out_w, ffn_w, down_w = args[-3:]
    width = ffn_w.shape[3] // CHIPS
    return pl.pallas_call(
        forward_kernel,
        in_specs=[V] * (len(args) - 3) + [ANY_SPEC] * 3,
        out_specs=[V] * 10 + [ANY_SPEC] * 2,
        out_shape=[
            shape((tok, HW), low),
            shape((tok, HW), full),
            shape((tok, HW), low),
            shape((tok, HW), low),
            shape((CHIPS * cap, HW), low),
            shape((ROW, D), full),
            shape((ROW, D), full),
            shape((CHIPS, ROW, D), low),
            shape((CHIPS, ROW, D), low),
            shape((2 * out_w.shape[0], D), low),
            shape((CHIPS, 2, *ffn_w.shape[1:3], 2 * width), low),
            shape((2 * down_w.shape[0], D), low),
        ],
        scratch_shapes=[
            pltpu.VMEM((tok, D), full),
            pltpu.VMEM((5, ROW, D), low),
            pltpu.VMEM((2, ROW // 2, D), low),
            pltpu.VMEM((*ffn_w.shape[1:3], 2 * width), low),
            pltpu.VMEM(down_w.shape, low),
            pltpu.SemaphoreType.DMA((6,)),
            pltpu.SemaphoreType.DMA((48,)),
            *net_scratch(40),
        ],
        compiler_params=pltpu.CompilerParams(
            collective_id=4, has_side_effects=True, vmem_limit_bytes=56 * 1024 * 1024
        ),
        cost_estimate=pl.CostEstimate(
            flops=5_000_000_000, bytes_accessed=200_000_000, transcendentals=0
        ),
    )(*args)


def quarters(w):
    n, rows, columns = w.shape
    return w.reshape(n, 4, rows // 4, columns)


def per_device(
    tokens,
    cond,
    text,
    segments,
    positions,
    counts,
    ada_weight,
    ada_bias,
    gains,
    attn_weight,
    out_weight,
    text_weight,
    ffn_weight,
    down_weight,
    cotangent,
):
    low = jnp.bfloat16
    full = jnp.float32
    plane = lax.axis_index("bucket")
    slot = lax.axis_index("fsdp")
    core = slot % 2
    chip = slot // 2
    ff = ffn_weight.shape[2] // CHIPS

    gain_pad = lax.dynamic_update_slice_in_dim(
        jnp.zeros((8, D), full), jnp.pad(gains.astype(full), ((0, 2), (0, 0))), slot * 192, axis=1
    )
    bias = lax.dynamic_update_slice_in_dim(
        jnp.zeros((ada_weight.shape[1],), full), ada_bias.astype(full), slot * ada_bias.shape[0], 0
    )
    bias_pad = jnp.repeat(bias.reshape(2, 3072), 4, axis=0)
    seg = segments[0]
    idx = jnp.concatenate([seg[None, :], positions[0], jnp.zeros((5, ROW), jnp.int32)], axis=0)
    quarter = HDIM // 4
    freq = np.tile(10000.0 ** (-np.arange(quarter) / quarter), (8, 128 // quarter))
    freq_row = jnp.asarray(freq.astype(np.float32))
    (
        mod, gain_f, h_rows, idx_all, attn_w, text_rows, query, keyed, valued, text_keys, text_vals,
        inv_q, inv_k, inv_t, cosine, sine, seg_col, gain_s, seg_own, weight_row,
    ) = open_layer(
        cond[0], gain_pad, bias_pad, ada_weight, tokens[0],
        counts[None, :], idx, freq_row, quarters(attn_weight), quarters(text_weight), text[0],
    )
    attn_w = attn_w.reshape(D, 3 * HW)
    h_all = h_rows.reshape(CHIPS * ROW, D)
    text_all = text_rows.reshape(CHIPS * IMGS * TXT, -1)
    (
        comb, cross_out, q_rot, k_rot, text_rot, branch, x_one, h_two_rows, d_ffn_rows, out_w, ffn_w,
        down_w,
    ) = forward_layer(
        query, keyed, valued, inv_q, inv_k, cosine, sine, text_keys, inv_t, text_vals,
        seg_col, idx_all, gain_s, mod, seg_own, gain_f, tokens[0], cotangent[0], weight_row,
        out_weight, quarters(ffn_weight), down_weight,
    )
    ffn_w = ffn_w.reshape(D, 2 * ff)
    h_two_all = h_two_rows.reshape(CHIPS * ROW, D)
    d_ffn_all = d_ffn_rows.reshape(CHIPS * ROW, D)
    both = mult(h_two_all, ffn_w)
    gate_pre = both[:, :ff]
    upper = both[:, ff:]
    d_hidden = dot_t(d_ffn_all, down_w)
    sigm = jax.nn.sigmoid(gate_pre)
    silu_pre = gate_pre * sigm
    hidden = (silu_pre * upper).astype(low)
    d_pre = (d_hidden * upper * sigm * (1.0 + gate_pre * (1.0 - sigm))).astype(low)
    d_up = (d_hidden * silu_pre).astype(low)
    d_both = jnp.concatenate([d_pre, d_up], axis=1)
    d_h_two = dot_t(d_both, ffn_w).astype(low)
    ffn_out = mult(hidden, down_w).astype(low)
    g_down = t_dot(hidden, d_ffn_all).astype(low)
    g_ffn = t_dot(h_two_all, d_both).astype(low)

    (
        block_out, token_grad, d_branch_rows, d_qkv, d_text, d_mod, gg_full, gg_slice, ffn_sum, down_sum,
    ) = back_layer(
        [
            d_h_two, ffn_out, x_one, branch, cotangent[0], weight_row, mod,
            seg_own, gain_f, tokens[0], idx_all, gain_s,
        ],
        [
            out_w, attn_w, q_rot, k_rot, valued, text_rot, text_vals, cross_out, query, keyed,
            text_keys, inv_q, inv_k, inv_t, cosine, sine, seg_col,
        ],
        g_ffn.reshape(1, 4, 4, 2, 48, 2 * ff),
        g_down.reshape(4, 2, 128, D),
    )
    d_branch_all = d_branch_rows.reshape(CHIPS * ROW, D)
    g_text = t_dot(text_all, d_text).astype(low)
    g_attn = t_dot(h_all, d_qkv).astype(low)
    g_out = t_dot(comb, d_branch_all).astype(low)
    s_down = to_row_owner(down_sum)
    s_text, s_attn, s_out, s_ffn, s_ada_w, small = close_layer(
        g_text.reshape(1, 4, 4, 2, 128, 2 * HW),
        g_attn.reshape(1, 4, 4, 2, 48, 3 * HW),
        g_out.reshape(4, 2, 48, D),
        ffn_sum,
        d_mod,
        gg_full,
        gg_slice,
        cond[0],
    )
    rank = plane * 8 + slot
    s_gains = lax.dynamic_slice_in_dim(small[:6], rank * 48, 48, axis=1)
    s_ada_b = lax.dynamic_slice_in_dim(small[8:12].reshape(-1), rank * 192, 192, axis=0)
    return (
        block_out[None],
        token_grad[None],
        s_ada_w,
        s_ada_b,
        s_gains,
        s_attn.astype(full),
        s_out.astype(full),
        s_text.astype(full),
        s_ffn.astype(full),
        s_down,
    )


def solution(mesh):
    in_specs = (
        P(("bucket", "fsdp"), None, None),
        P(("bucket", "fsdp"), None, None),
        P(("bucket", "fsdp"), None, None),
        P(("bucket", "fsdp"), None),
        P(("bucket", "fsdp"), None, None),
        P(),
        P("fsdp", None),
        P("fsdp"),
        P(None, "fsdp"),
        P(None, "fsdp", None),
        P("fsdp", None),
        P(None, "fsdp", None),
        P(None, "fsdp", None),
        P("fsdp", None),
        P(("bucket", "fsdp"), None, None),
    )
    out_specs = (
        P(("bucket", "fsdp"), None, None),
        P(("bucket", "fsdp"), None, None),
        P(("bucket", "fsdp"), None),
        P(("bucket", "fsdp")),
        P(None, ("bucket", "fsdp")),
        P(None, ("bucket", "fsdp"), None),
        P(("bucket", "fsdp"), None),
        P(None, ("bucket", "fsdp"), None),
        P(None, ("bucket", "fsdp"), None),
        P(("bucket", "fsdp"), None),
    )
    fast = mesh.shape["fsdp"] == 8 and mesh.shape["bucket"] == 4
    return jax.shard_map(
        per_device if fast else per_device_general, mesh=mesh, in_specs=in_specs, out_specs=out_specs, check_vma=False
    )
```

```python
import jax
import jax.numpy as jnp
import numpy as np
from jax import lax
from jax.experimental import pallas as pl
from jax.experimental.pallas import tpu as pltpu
from jax.sharding import PartitionSpec as P

D = 1536
HEADS = 24
HDIM = 64
IMGS = 4
TXT = 64


EPS = 1e-06
NEGATIVE = -1e30
HIGH = lax.Precision.HIGHEST


def silu(v):
    return v * jax.nn.sigmoid(v)


def norm_rows(v):
    inverse = lax.rsqrt(jnp.mean(v * v, axis=-1, keepdims=True) + EPS)
    return (v * inverse, inverse)


def norm_back(grad, normed, inverse):
    return inverse * (grad - normed * jnp.mean(grad * normed, axis=-1, keepdims=True))


def rotary_tables(pos):
    quarter = HDIM // 4
    freq = 10000.0 ** (-jnp.arange(quarter, dtype=jnp.float32) / quarter)
    angle = jnp.transpose(pos.astype(jnp.float32), (1, 0))[:, :, None] * freq[None, None, :]
    return (jnp.cos(angle), jnp.sin(angle))


def rotate(v, cosine, sine):
    rows = v.shape[0]
    parts = v.reshape(rows, HEADS, 2, 2, HDIM // 4)
    first = parts[:, :, :, 0]
    second = parts[:, :, :, 1]
    cosine = cosine[:, None]
    sine = sine[:, None]
    turned = jnp.stack([first * cosine - second * sine, first * sine + second * cosine], axis=3)
    return turned.reshape(rows, HEADS * HDIM)


def to_pairs(v):
    return jnp.transpose(v.reshape(v.shape[0], HEADS // 2, 2 * HDIM), (1, 0, 2))


def from_pairs(v):
    return jnp.transpose(v, (1, 0, 2)).reshape(v.shape[1], HEADS * HDIM)


def pair_scores(query, keys):
    q_heads = query.reshape(query.shape[0], 2, HDIM)
    k_heads = keys.reshape(keys.shape[0], 2, HDIM)
    return jnp.einsum(
        "rhd,khd->hrk", q_heads, k_heads, preferred_element_type=jnp.float32
    ) * HDIM ** (-0.5)


def attend_forward(q_b, k_b, v_b, allowed):

    def one_pair(item):
        query, keys, values = item
        scores = jnp.where(allowed[None], pair_scores(query, keys), NEGATIVE)
        top = jnp.max(scores, axis=-1, keepdims=True)
        expo = jnp.exp(scores - top)
        total = jnp.sum(expo, axis=-1, keepdims=True)
        probs = (expo / total).astype(jnp.bfloat16)
        result = jnp.einsum(
            "hrk,khd->rhd",
            probs,
            values.reshape(values.shape[0], 2, HDIM),
            preferred_element_type=jnp.float32,
        )
        return (result.reshape(query.shape[0], 2 * HDIM), (top + jnp.log(total))[..., 0])

    outputs, saved = lax.map(one_pair, (to_pairs(q_b), to_pairs(k_b), to_pairs(v_b)))
    return (from_pairs(outputs), saved)


def attend_back(q_b, k_b, v_b, saved, grad_b, allowed):

    def one_pair(item):
        query, keys, values, lse_pair, grad = item
        rows = query.shape[0]
        count = keys.shape[0]
        scores = jnp.where(allowed[None], pair_scores(query, keys), NEGATIVE)
        probs = jnp.exp(scores - lse_pair[..., None])
        probs_b = probs.astype(jnp.bfloat16)
        grad_heads = grad.reshape(rows, 2, HDIM)
        dprob = jnp.einsum(
            "rhd,khd->hrk",
            grad_heads,
            values.reshape(count, 2, HDIM),
            preferred_element_type=jnp.float32,
        )
        dscore = (probs * (dprob - jnp.sum(probs * dprob, axis=-1, keepdims=True))).astype(
            jnp.bfloat16
        )
        factor = HDIM ** (-0.5)
        dquery = (
            jnp.einsum(
                "hrk,khd->rhd",
                dscore,
                keys.reshape(count, 2, HDIM),
                preferred_element_type=jnp.float32,
            )
            * factor
        )
        dkeys = (
            jnp.einsum(
                "hrk,rhd->khd",
                dscore,
                query.reshape(rows, 2, HDIM),
                preferred_element_type=jnp.float32,
            )
            * factor
        )
        dvalues = jnp.einsum(
            "hrk,rhd->khd", probs_b, grad_heads, preferred_element_type=jnp.float32
        )
        return (
            dquery.reshape(rows, 2 * HDIM),
            dkeys.reshape(count, 2 * HDIM),
            dvalues.reshape(count, 2 * HDIM),
        )

    d_query, d_keys, d_values = lax.map(
        one_pair, (to_pairs(q_b), to_pairs(k_b), to_pairs(v_b), saved, to_pairs(grad_b))
    )
    return (from_pairs(d_query), from_pairs(d_keys), from_pairs(d_values))


def mult(left, right):
    return jnp.dot(left, right, preferred_element_type=jnp.float32)


def per_device_general(
    tokens,
    cond,
    text,
    segments,
    positions,
    counts,
    ada_weight,
    ada_bias,
    gains,
    attn_weight,
    out_weight,
    text_weight,
    ffn_weight,
    down_weight,
    cotangent,
):
    ada_w, ada_b, gain_rows, attn_w, out_w, text_w = (
        lax.all_gather(ada_weight, "fsdp", axis=0, tiled=True),
        lax.all_gather(ada_bias, "fsdp", axis=0, tiled=True),
        lax.all_gather(gains, "fsdp", axis=1, tiled=True),
        lax.all_gather(attn_weight, "fsdp", axis=1, tiled=True),
        lax.all_gather(out_weight, "fsdp", axis=0, tiled=True),
        lax.all_gather(text_weight, "fsdp", axis=1, tiled=True),
    )
    gain_f = gain_rows.astype(jnp.float32)
    x = tokens[0].astype(jnp.float32)
    seg = segments[0]
    cosine, sine = rotary_tables(positions[0])
    text_b = text[0]
    cond_act = silu(cond[0].astype(jnp.float32)).astype(jnp.bfloat16)
    mod = mult(cond_act, ada_w) + ada_b.astype(jnp.float32)[None, :]
    pick = (seg[:, None] == jnp.arange(IMGS, dtype=jnp.int32)[None, :]).astype(jnp.float32)
    per_token = jnp.dot(pick, mod, precision=HIGH)
    scale1 = per_token[:, :D]
    gate1 = per_token[:, D : 2 * D]
    scale2 = per_token[:, 2 * D : 3 * D]
    gate2 = per_token[:, 3 * D :]
    normed1, inverse1 = norm_rows(x)
    h_one = (normed1 * gain_f[0] * (1.0 + scale1)).astype(jnp.bfloat16)
    query = mult(h_one, attn_w[0])
    keyed = mult(h_one, attn_w[1])
    valued = mult(h_one, attn_w[2]).astype(jnp.bfloat16)
    q_norm, q_inv = norm_rows(query)
    k_norm, k_inv = norm_rows(keyed)
    q_rot = rotate(q_norm * gain_f[2], cosine, sine).astype(jnp.bfloat16)
    k_rot = rotate(k_norm * gain_f[3], cosine, sine).astype(jnp.bfloat16)
    text_keys = mult(text_b, text_w[0])
    text_vals = mult(text_b, text_w[1]).astype(jnp.bfloat16)
    t_norm, t_inv = norm_rows(text_keys)
    text_rot = (t_norm * gain_f[4]).astype(jnp.bfloat16)
    same = seg[:, None] == seg[None, :]
    owner = jnp.arange(IMGS * TXT, dtype=jnp.int32) // TXT
    mine = seg[:, None] == owner[None, :]
    self_out, self_lse = attend_forward(q_rot, k_rot, valued, same)
    cross_out, cross_lse = attend_forward(q_rot, text_rot, text_vals, mine)
    cross_gate = jnp.tanh(gain_f[5])
    comb = (self_out + cross_gate * cross_out).astype(jnp.bfloat16)
    branch = mult(comb, out_w)
    tanh_one = jnp.tanh(gate1)
    x_one = x + tanh_one * branch
    normed2, inverse2 = norm_rows(x_one)
    h_two = (normed2 * gain_f[1] * (1.0 + scale2)).astype(jnp.bfloat16)
    ffn_w, down_w = (
        lax.all_gather(ffn_weight, "fsdp", axis=1, tiled=True),
        lax.all_gather(down_weight, "fsdp", axis=0, tiled=True),
    )
    gate_pre = mult(h_two, ffn_w[0])
    upper = mult(h_two, ffn_w[1])
    sigm = jax.nn.sigmoid(gate_pre)
    silu_pre = gate_pre * sigm
    hidden = (silu_pre * upper).astype(jnp.bfloat16)
    ffn_out = mult(hidden, down_w)
    tanh_two = jnp.tanh(gate2)
    block_out = (x_one + tanh_two * ffn_out).astype(jnp.bfloat16)
    totals = counts.astype(jnp.float32)
    here = jnp.sum(
        jnp.where(
            jnp.arange(totals.shape[0], dtype=jnp.int32) == lax.axis_index("bucket"), totals, 0.0
        )
    )
    weight = lax.axis_size("bucket") * here / jnp.sum(totals)
    grad = cotangent[0].astype(jnp.float32) * weight
    back_ffn, back_down = (
        lax.all_gather(ffn_weight, "fsdp", axis=1, tiled=True),
        lax.all_gather(down_weight, "fsdp", axis=0, tiled=True),
    )
    d_gate2 = grad * ffn_out * (1.0 - tanh_two * tanh_two)
    d_ffn = (grad * tanh_two).astype(jnp.bfloat16)
    d_hidden = mult(d_ffn, back_down.T)
    g_down = mult(hidden.T, d_ffn)
    d_pre = (d_hidden * upper * sigm * (1.0 + gate_pre * (1.0 - sigm))).astype(jnp.bfloat16)
    d_up = (d_hidden * silu_pre).astype(jnp.bfloat16)
    d_h_two = mult(d_pre, back_ffn[0].T) + mult(d_up, back_ffn[1].T)
    g_ffn = jnp.stack([mult(h_two.T, d_pre), mult(h_two.T, d_up)])
    s_ffn, s_down = (
        lax.psum_scatter(g_ffn, ("bucket", "fsdp"), scatter_dimension=1, tiled=True),
        lax.psum_scatter(g_down, ("bucket", "fsdp"), scatter_dimension=0, tiled=True),
    )
    back_attn, back_out = (
        lax.all_gather(attn_weight, "fsdp", axis=1, tiled=True),
        lax.all_gather(out_weight, "fsdp", axis=0, tiled=True),
    )
    g_gain_one = jnp.sum(d_h_two * normed2 * (1.0 + scale2), axis=0)
    d_scale2 = d_h_two * normed2 * gain_f[1]
    d_x_one = grad + norm_back(d_h_two * gain_f[1] * (1.0 + scale2), normed2, inverse2)
    d_gate1 = d_x_one * branch * (1.0 - tanh_one * tanh_one)
    d_branch = (d_x_one * tanh_one).astype(jnp.bfloat16)
    d_comb = mult(d_branch, back_out.T)
    g_out = mult(comb.T, d_branch)
    g_gain_five = jnp.sum(d_comb * cross_out, axis=0) * (1.0 - cross_gate * cross_gate)
    d_self = d_comb.astype(jnp.bfloat16)
    d_cross = (d_comb * cross_gate).astype(jnp.bfloat16)
    dq_self, dk_self, dv_self = attend_back(q_rot, k_rot, valued, self_lse, d_self, same)
    dq_cross, dk_text, dv_text = attend_back(q_rot, text_rot, text_vals, cross_lse, d_cross, mine)
    d_q_norm = rotate(dq_self + dq_cross, cosine, -sine)
    g_gain_two = jnp.sum(d_q_norm * q_norm, axis=0)
    d_query = norm_back(d_q_norm * gain_f[2], q_norm, q_inv).astype(jnp.bfloat16)
    d_k_norm = rotate(dk_self, cosine, -sine)
    g_gain_three = jnp.sum(d_k_norm * k_norm, axis=0)
    d_keyed = norm_back(d_k_norm * gain_f[3], k_norm, k_inv).astype(jnp.bfloat16)
    d_valued = dv_self.astype(jnp.bfloat16)
    g_gain_four = jnp.sum(dk_text * t_norm, axis=0)
    d_text_keys = norm_back(dk_text * gain_f[4], t_norm, t_inv).astype(jnp.bfloat16)
    d_text_vals = dv_text.astype(jnp.bfloat16)
    g_text = jnp.stack([mult(text_b.T, d_text_keys), mult(text_b.T, d_text_vals)])
    d_h_one = (
        mult(d_query, back_attn[0].T)
        + mult(d_keyed, back_attn[1].T)
        + mult(d_valued, back_attn[2].T)
    )
    g_attn = jnp.stack([mult(h_one.T, d_query), mult(h_one.T, d_keyed), mult(h_one.T, d_valued)])
    g_gain_zero = jnp.sum(d_h_one * normed1 * (1.0 + scale1), axis=0)
    d_scale1 = d_h_one * normed1 * gain_f[0]
    token_grad = d_x_one + norm_back(d_h_one * gain_f[0] * (1.0 + scale1), normed1, inverse1)
    d_token_mod = jnp.concatenate([d_scale1, d_gate1, d_scale2, d_gate2], axis=1)
    d_mod = jnp.dot(pick.T, d_token_mod, precision=HIGH)
    g_ada_b = jnp.sum(d_mod, axis=0)
    g_ada_w = mult(cond_act.T, d_mod.astype(jnp.bfloat16))
    g_gains = jnp.stack(
        [g_gain_zero, g_gain_one, g_gain_two, g_gain_three, g_gain_four, g_gain_five]
    )
    s_ada_w, s_ada_b, s_gains, s_attn, s_out, s_text = (
        lax.psum_scatter(g_ada_w, ("bucket", "fsdp"), scatter_dimension=0, tiled=True),
        lax.psum_scatter(g_ada_b, ("bucket", "fsdp"), scatter_dimension=0, tiled=True),
        lax.psum_scatter(g_gains, ("bucket", "fsdp"), scatter_dimension=1, tiled=True),
        lax.psum_scatter(g_attn, ("bucket", "fsdp"), scatter_dimension=1, tiled=True),
        lax.psum_scatter(g_out, ("bucket", "fsdp"), scatter_dimension=0, tiled=True),
        lax.psum_scatter(g_text, ("bucket", "fsdp"), scatter_dimension=1, tiled=True),
    )
    return (
        block_out[None],
        token_grad[None],
        s_ada_w,
        s_ada_b,
        s_gains,
        s_attn,
        s_out,
        s_text,
        s_ffn,
        s_down,
    )


ROW = 128
CHIPS = 4
HW = D // CHIPS
PAIRS = HW // 128


def partner(u):
    lane = lax.broadcasted_iota(jnp.int32, u.shape, 1)
    ahead = pltpu.roll(u, u.shape[1] - 16, 1)
    behind = pltpu.roll(u, 16, 1)
    return jnp.where((lane // 16) % 2 == 0, ahead, behind)


def dot_t(a, b):
    return lax.dot_general(a, b, (((1,), (1,)), ((), ())), preferred_element_type=jnp.float32)


def dot_n(a, b):
    return lax.dot_general(a, b, (((1,), (0,)), ((), ())), preferred_element_type=jnp.float32)


def t_dot(a, b):
    return lax.dot_general(a, b, (((0,), (0,)), ((), ())), preferred_element_type=jnp.float32)


def softmax_of(scores, allowed):
    scores = jnp.where(allowed, scores * HDIM ** (-0.5), NEGATIVE)
    top = jnp.max(scores, axis=-1, keepdims=True)
    expo = jnp.exp(scores - top)
    return expo / jnp.sum(expo, axis=-1, keepdims=True)


def head_mask(v, head):
    lane = lax.broadcasted_iota(jnp.int32, v.shape, 1)
    return jnp.where((lane // HDIM) == head, v, jnp.zeros_like(v))


def masks_of(seg_col, seg_row, captions):
    same = seg_col == seg_row
    owner = lax.broadcasted_iota(jnp.int32, (seg_col.shape[0], captions), 1) // TXT
    return same, seg_col == owner


def attend_kernel(
    q_ref, k_ref, v_ref, iq_ref, ik_ref, cos_ref, sin_ref, tk_ref, it_ref, tv_ref, sc_ref, sr_ref,
    g_ref, comb_ref, cross_ref, qr_ref, kr_ref, tr_ref,
):
    same, mine = masks_of(sc_ref[...], sr_ref[...], tk_ref.shape[0])
    cosine = cos_ref[...]
    sine = sin_ref[...]
    low = jnp.bfloat16
    for pair in range(PAIRS):
        at = pl.ds(pair * 128, 128)
        qn = q_ref[:, at] * iq_ref[...] * g_ref[2:3, at]
        kn = k_ref[:, at] * ik_ref[...] * g_ref[3:4, at]
        qr = (qn * cosine + partner(qn) * sine).astype(low)
        kr = (kn * cosine + partner(kn) * sine).astype(low)
        tr = (tk_ref[:, at] * it_ref[...] * g_ref[4:5, at]).astype(low)
        qr_ref[:, at] = qr
        kr_ref[:, at] = kr
        tr_ref[:, at] = tr
        vv = v_ref[:, at]
        tv = tv_ref[:, at]
        self_out = jnp.zeros(qn.shape, jnp.float32)
        cross_out = jnp.zeros(qn.shape, jnp.float32)
        for head in range(2):
            qh = head_mask(qr, head)
            probs = softmax_of(dot_t(qh, kr), same).astype(low)
            self_out = self_out + head_mask(dot_n(probs, vv), head)
            probs = softmax_of(dot_t(qh, tr), mine).astype(low)
            cross_out = cross_out + head_mask(dot_n(probs, tv), head)
        cross_ref[:, at] = cross_out
        comb_ref[:, at] = (self_out + jnp.tanh(g_ref[5:6, at]) * cross_out).astype(low)


def attend_back_kernel(
    qr_ref, kr_ref, v_ref, tr_ref, tv_ref, dc_ref, cross_ref, q_ref, k_ref, tk_ref, iq_ref, ik_ref,
    it_ref, cos_ref, sin_ref, sc_ref, sr_ref, g_ref,
    dq_ref, dk_ref, dv_ref, dt_ref, dtv_ref, gg_ref,
):
    same, mine = masks_of(sc_ref[...], sr_ref[...], tk_ref.shape[0])
    cosine = cos_ref[...]
    sine = sin_ref[...]
    low = jnp.bfloat16
    factor = HDIM ** (-0.5)
    for pair in range(PAIRS):
        at = pl.ds(pair * 128, 128)
        qr = qr_ref[:, at]
        kr = kr_ref[:, at]
        vv = v_ref[:, at]
        tr = tr_ref[:, at]
        tv = tv_ref[:, at]
        dcomb = dc_ref[:, at]
        d_self = dcomb.astype(low)
        d_cross = (dcomb * jnp.tanh(g_ref[5:6, at])).astype(low)
        dq = jnp.zeros(dcomb.shape, jnp.float32)
        dk = jnp.zeros(dcomb.shape, jnp.float32)
        dv = jnp.zeros(dcomb.shape, jnp.float32)
        dt = jnp.zeros((tr.shape[0], 128), jnp.float32)
        dtv = jnp.zeros((tr.shape[0], 128), jnp.float32)
        for head in range(2):
            qh = head_mask(qr, head)
            probs = softmax_of(dot_t(qh, kr), same)
            grad = head_mask(d_self, head)
            dprob = dot_t(grad, vv)
            dscore = probs * (dprob - jnp.sum(probs * dprob, axis=-1, keepdims=True))
            dscore = dscore.astype(low)
            dq = dq + dot_n(dscore, head_mask(kr, head))
            dk = dk + t_dot(dscore, qh)
            dv = dv + t_dot(probs.astype(low), grad)
            probs = softmax_of(dot_t(qh, tr), mine)
            grad = head_mask(d_cross, head)
            dprob = dot_t(grad, tv)
            dscore = probs * (dprob - jnp.sum(probs * dprob, axis=-1, keepdims=True))
            dscore = dscore.astype(low)
            dq = dq + dot_n(dscore, head_mask(tr, head))
            dt = dt + t_dot(dscore, qh)
            dtv = dtv + t_dot(probs.astype(low), grad)
        dq = dq * factor
        dk = dk * factor
        dt = dt * factor
        dq = dq * cosine - partner(dq) * sine
        dk = dk * cosine - partner(dk) * sine
        q_norm = q_ref[:, at] * iq_ref[...]
        k_norm = k_ref[:, at] * ik_ref[...]
        t_norm = tk_ref[:, at] * it_ref[...]
        gg_ref[0:1, at] += jnp.sum(dq * q_norm, axis=0, keepdims=True)
        gg_ref[1:2, at] += jnp.sum(dk * k_norm, axis=0, keepdims=True)
        gg_ref[2:3, at] += jnp.sum(dt * t_norm, axis=0, keepdims=True)
        gg_ref[3:4, at] += jnp.sum(dcomb * cross_ref[:, at], axis=0, keepdims=True)
        dq = dq * g_ref[2:3, at]
        dk = dk * g_ref[3:4, at]
        dt = dt * g_ref[4:5, at]
        dq_ref[:, at] = dq
        dk_ref[:, at] = dk
        dv_ref[:, at] = dv.astype(low)
        dt_ref[:, at] = dt
        dtv_ref[:, at] = dtv.astype(low)


MESH_IDS = pl.DeviceIdType.MESH
VMEM_SPEC = pl.BlockSpec(memory_space=pltpu.VMEM)
ANY_SPEC = pl.BlockSpec(memory_space=pl.ANY)


def to_row_owner(block):
    pairs = [
        (a * 8 + b * 2 + k, b * 8 + a * 2 + k) for a in range(4) for b in range(4) for k in range(2)
    ]
    return lax.ppermute(block, ("bucket", "fsdp"), pairs).astype(jnp.float32)


class Net:
    def __init__(self, send_sems, recv_sems):
        self.me = lax.axis_index("fsdp")
        self.send_sems = send_sems
        self.recv_sems = recv_sems
        self.count = 0
        self.all = []

    def peer(self, mask):
        out = self.me
        for bit in (1, 2, 4):
            if mask & bit:
                out = out + bit * (1 - 2 * ((self.me // bit) % 2))
        return out

    def meet(self, masks):
        sem = pltpu.get_barrier_semaphore()
        for mask in masks:
            pl.semaphore_signal(
                sem, inc=1, device_id={"fsdp": self.peer(mask)}, device_id_type=MESH_IDS
            )
        pl.semaphore_wait(sem, len(masks))

    def send(self, src, dst, mask):
        assert self.count < self.send_sems.shape[0]
        copy = pltpu.make_async_remote_copy(
            src_ref=src,
            dst_ref=dst,
            send_sem=self.send_sems.at[self.count],
            recv_sem=self.recv_sems.at[self.count],
            device_id={"fsdp": self.peer(mask)},
            device_id_type=MESH_IDS,
        )
        self.count += 1
        copy.start()
        self.all.append(copy)
        return copy

    def close(self):
        for copy in self.all:
            copy.wait_send()


def net_scratch(count):
    return [pltpu.SemaphoreType.DMA((count,)), pltpu.SemaphoreType.DMA((count,))]


def share4_start(net, out):
    return net.send(out.at[0], out.at[1], 2), net.send(out.at[0], out.at[2], 4)


def share4_relay(net, out, by_x, by_y):
    half = out.shape[1] // 2
    top, bottom = pl.ds(0, half), pl.ds(half, half)
    by_x.wait_recv()
    first = net.send(out.at[1, top], out.at[3, top], 4)
    by_y.wait_recv()
    second = net.send(out.at[2, bottom], out.at[3, bottom], 2)
    return first, second


def collect4(net, part, buf, far):
    half = far.shape[1]
    rows = (pl.ds(0, half), pl.ds(half, half))
    low = jnp.bfloat16
    full = jnp.float32
    for i in (0, 1):
        buf[2, rows[i]] = part(3, i).astype(low)
    far_x = net.send(buf.at[2, rows[0]], far.at[0], 2)
    far_y = net.send(buf.at[2, rows[1]], far.at[1], 4)
    buf[0, rows[0]] = part(1, 0).astype(low)
    one_a = net.send(buf.at[0, rows[0]], buf.at[3, rows[0]], 2)
    buf[1, rows[1]] = part(2, 1).astype(low)
    two_b = net.send(buf.at[1, rows[1]], buf.at[4, rows[1]], 4)
    later = []

    def middle():
        far_x.wait_recv()
        buf[1, rows[0]] = (part(2, 0) + far[0].astype(full)).astype(low)
        later.append(net.send(buf.at[1, rows[0]], buf.at[4, rows[0]], 4))
        far_y.wait_recv()
        buf[0, rows[1]] = (part(1, 1) + far[1].astype(full)).astype(low)
        later.append(net.send(buf.at[0, rows[1]], buf.at[3, rows[1]], 2))

    def finish(i):
        (one_a, two_b)[i].wait_recv()
        later[i].wait_recv()
        return part(0, i) + buf[3, rows[i]].astype(full) + buf[4, rows[i]].astype(full)

    return middle, finish


def pick_rows(table, seg, first):
    out = table[first + IMGS - 1 : first + IMGS]
    for i in range(IMGS - 2, -1, -1):
        out = jnp.where(seg == i, table[first + i : first + i + 1], out)
    return out


def row_sums(a, b):
    ones = jnp.ones((8, a.shape[1]), jnp.float32)

    def one(v):
        return lax.dot_general(
            ones, v, (((1,), (1,)), ((), ())), precision=HIGH, preferred_element_type=jnp.float32
        )

    if b is None:
        return one(a)
    got = one(a)
    return jnp.where(lax.broadcasted_iota(jnp.int32, got.shape, 0) < 4, got, one(b))


class Lines:
    MASKS = (2, 4, 6)

    def __init__(self, net, src, dst, width, sems, local):
        self.net, self.src, self.dst, self.width, self.sems = net, src, dst, width, sems
        self.plane = lax.axis_index("bucket")
        self.chip = net.me // 2
        self.core = net.me % 2
        self.local = local
        self.ids = range(src.shape[0])

    def columns(self, c):
        return pl.ds(pl.multiple_of(c * self.width, 128), self.width)

    def lanes(self, i):
        return pl.ds(i * self.width, self.width)

    def away_start(self):
        own = self.dst.at[self.chip, self.core, self.plane]
        self.away = [
            self.net.send(
                self.src.at[i, self.plane, :, self.columns(self.net.peer(m) // 2)],
                own.at[:, self.lanes(i)],
                m,
            )
            for m in self.MASKS
            for i in self.ids
        ]

    def own_start(self):
        own = self.dst.at[self.chip, self.core]
        cuts = [self.src.at[i, :, :, self.columns(self.chip)] for i in self.ids]
        puts = [own.at[:, :, self.lanes(i)] for i in self.ids]
        self.ready = [self.net.send(a, b, 1) for a, b in zip(cuts, puts)]
        self.here = [self.local(i, a, b) for i, (a, b) in enumerate(zip(cuts, puts))]

    def copy(self, up, k, slab):
        at = self.dst.at[self.net.peer(self.MASKS[k]) // 2, self.core, slab]
        first = ((k * 2 + (0 if up else 1)) * 4 + slab) * 2
        return pltpu.make_async_remote_copy(
            src_ref=at,
            dst_ref=at,
            send_sem=self.sems.at[first],
            recv_sem=self.sems.at[first + 1],
            device_id={"bucket": self.plane + (1 if up else -1)},
            device_id_type=MESH_IDS,
        )

    def moves(self, h):
        for up in (True, False):
            slab = self.plane - h if up else self.plane + h
            there = (slab >= 0) if up else (slab <= 3)
            sends = (self.plane <= 2) if up else (self.plane >= 1)
            yield up, slab, there, sends

    def hop(self, h):
        if h == 0:
            for c in self.away:
                c.wait_recv()
        for up, slab, there, sends in self.moves(h):

            @pl.when(there)
            def _(up=up, slab=slab, sends=sends):
                for k in range(3):
                    if h > 0:
                        self.copy(up, k, slab).wait_recv()
                    if h < 3:

                        @pl.when(sends)
                        def _(k=k):
                            self.copy(up, k, slab).start()

    def finish(self):
        self.hop(3)
        for m in self.MASKS:
            at = self.dst.at[self.net.peer(m) // 2, self.core]
            self.ready.append(self.net.send(at, at, 1))

    def wait(self):
        for c in self.ready:
            c.wait_recv()

    def close(self):
        for h in range(3):
            for up, slab, there, sends in self.moves(h):

                @pl.when(there & sends)
                def _(up=up, slab=slab):
                    for k in range(3):
                        self.copy(up, k, slab).wait_send()


def meet_line(net, masks):
    plane = lax.axis_index("bucket")
    sem = pltpu.get_barrier_semaphore()
    for mask in masks:
        pl.semaphore_signal(
            sem, inc=1, device_id={"fsdp": net.peer(mask)}, device_id_type=MESH_IDS
        )
    for inner, step in ((plane >= 1, -1), (plane <= 2, 1)):

        @pl.when(inner)
        def _(step=step):
            pl.semaphore_signal(
                sem, inc=1, device_id={"bucket": plane + step}, device_id_type=MESH_IDS
            )

    one = jnp.int32(1)
    zero = jnp.int32(0)
    pl.semaphore_wait(
        sem, len(masks) + jnp.where(plane >= 1, one, zero) + jnp.where(plane <= 2, one, zero)
    )


ALL_PEERS = (1, 2, 3, 4, 5, 6, 7)


def open_kernel(
    cond_ref, gain_ref, bias_ref, ada_ref, tok_ref, counts_ref, idx_ref, freq_ref, attn_ref, textw_ref,
    text_ref,
    mod_ref, gains_ref, h_out, idxs_ref, aw_out, ta_out, q_out, k_out, v_out, tk_ref, tv_ref,
    iq_ref, ik_ref, it_ref, cos_ref, sin_ref, sc_ref, gs_ref,
    seg_ref, w_ref, h_ref, aw_ref, q_ref, k_ref, v_ref, conds, parts, mods, gbuf, tw_ref, ta_ref, sums, tsums, local_sems, out_sems, attn_sems, text_sems,
    send_sems, recv_sems,
):
    low = jnp.bfloat16
    full = jnp.float32
    net = Net(send_sems, recv_sems)
    me = net.me
    chip = me // 2
    meet_line(net, ALL_PEERS)

    act = cond_ref[...].astype(full)
    act = (act * jax.nn.sigmoid(act)).astype(low).astype(full)
    act = jnp.concatenate([act, act], axis=0)
    for j in range(8):
        gbuf[8, :, 128 * j : 128 * j + 128] = act[:, 128 * j : 128 * j + 128]
    waits = []
    for m in ALL_PEERS:
        at = pl.ds(pl.multiple_of(net.peer(m) * 128, 128), 128)
        waits.append(net.send(gbuf.at[8, :, at], conds.at[m], m))
    conds[0] = gbuf[8, :, pl.ds(pl.multiple_of(me * 128, 128), 128)]
    gwaits = [net.send(gain_ref, gbuf.at[m], m) for m in ALL_PEERS]
    iwaits = [net.send(idx_ref, idxs_ref.at[i], m) for i, m in ((1, 2), (2, 4), (3, 6))]
    idxs_ref[0] = idx_ref[...]

    def local(first):
        def go(i, src, dst):
            copy = pltpu.make_async_copy(src, dst, local_sems.at[first + i])
            copy.start()
            return copy

        return go

    attn_io = Lines(net, attn_ref, aw_ref, HW, attn_sems, local(3))
    text_io = Lines(net, textw_ref, tw_ref, HW, text_sems, local(6))
    attn_io.away_start()
    text_io.away_start()
    own_text = local(2)(0, text_ref, ta_ref.at[0])

    for w in waits:
        w.wait_recv()
    lhs = jnp.concatenate([conds[m] for m in range(8)], axis=0).astype(low)
    half_cols = 3072
    step = 512

    def mod_cols(i, _):
        lo = pl.ds(pl.multiple_of(i * step, step), step)
        hi = pl.ds(pl.multiple_of(half_cols + i * step, step), step)
        a = jnp.dot(lhs, ada_ref[:, lo], preferred_element_type=full)
        b = jnp.dot(lhs, ada_ref[:, hi], preferred_element_type=full)
        row = lax.broadcasted_iota(jnp.int32, (8, step), 0)
        for m in range(8):
            parts[m, :, lo] = (
                jnp.where(row < 4, a[8 * m : 8 * m + 8], b[8 * m : 8 * m + 8]) + bias_ref[:, lo]
            )
        return 0

    lax.fori_loop(0, half_cols // step, mod_cols, 0)
    waits = [net.send(parts.at[m], mods.at[m], m) for m in ALL_PEERS]

    attn_io.own_start()
    text_io.own_start()
    own_text.wait()

    def keep(j):
        copy = pltpu.make_async_copy(ta_ref.at[j], ta_out.at[j], out_sems.at[j])
        copy.start()
        return copy

    kept = [keep(0)]
    chunks = 4
    size = ta_ref.shape[1] // chunks
    tx, ty = [None] * chunks, [None] * chunks

    def text_send(s):
        i, j = s, (s + chunks // 2) % chunks
        at = pl.ds(i * size, size)
        tx[i] = net.send(ta_ref.at[0, at], ta_ref.at[1, at], 2)
        at = pl.ds(j * size, size)
        ty[j] = net.send(ta_ref.at[0, at], ta_ref.at[2, at], 4)

    text_send(0)
    attn_io.hop(0)
    text_io.hop(0)
    seg_ref[...] = jnp.transpose(idx_ref[...].astype(full))[:, 0:1].astype(jnp.int32)
    totals = counts_ref[...].astype(full)
    bucket = lax.broadcasted_iota(jnp.int32, totals.shape, 1) == lax.axis_index("bucket")
    here = jnp.sum(jnp.where(bucket, totals, 0.0), axis=-1, keepdims=True)
    weight = CHIPS * here / jnp.sum(totals, axis=-1, keepdims=True)
    w_ref[...] = jnp.broadcast_to(weight, w_ref.shape)
    for w in gwaits:
        w.wait_recv()
    gains = gain_ref[...]
    for m in ALL_PEERS:
        gains = gains + gbuf[m]
    gains_ref[...] = gains
    for w in waits:
        w.wait_recv()

    def mod_sum(i, _):
        at = pl.ds(pl.multiple_of(i * step, step), step)
        total = parts[0, :, at]
        for m in ALL_PEERS:
            total = total + mods[m, :, at]
        mod_ref[:, at] = total
        return 0

    lax.fori_loop(0, half_cols // step, mod_sum, 0)

    block = 32

    def first_norm(i, _):
        at = pl.ds(pl.multiple_of(i * block, block), block)
        x = tok_ref[at, :].astype(full)
        normed = x * lax.rsqrt(jnp.mean(x * x, axis=-1, keepdims=True) + EPS)
        scale = pick_rows(mod_ref[:, :D], seg_ref[at, :], 0)
        h_ref[0, at, :] = (normed * gains_ref[0:1, :] * (1.0 + scale)).astype(low)
        return 0

    lax.fori_loop(0, ROW // block, first_norm, 0)
    hx, hy = share4_start(net, h_ref)

    text_send(1)
    attn_io.hop(1)
    h_far = share4_relay(net, h_ref, hx, hy)
    for i in range(2, chunks):
        text_send(i)
    text_io.hop(1)
    attn_io.hop(2)
    attn_io.finish()
    text_io.hop(2)
    relays = []
    for s in range(chunks // 2):
        i, j = s, s + chunks // 2
        tx[i].wait_recv()
        at = pl.ds(i * size, size)
        relays.append(net.send(ta_ref.at[1, at], ta_ref.at[3, at], 4))
        ty[j].wait_recv()
        at = pl.ds(j * size, size)
        relays.append(net.send(ta_ref.at[2, at], ta_ref.at[3, at], 2))

    for c in iwaits:
        c.wait_recv()
    gs_ref[...] = gains_ref[:, pl.ds(pl.multiple_of(chip * HW, 128), HW)]
    lane = lax.broadcasted_iota(jnp.int32, (ROW, 128), 1)
    sign = jnp.where((lane // 16) % 2 == 0, -1.0, 1.0)
    for j in range(CHIPS):
        at = pl.ds(j * ROW, ROW)
        cols = jnp.transpose(idxs_ref[j].astype(full))
        sc_ref[at, :] = cols[:, 0:1].astype(jnp.int32)
        place = jnp.where((lane // 32) % 2 == 0, cols[:, 1:2], cols[:, 2:3])
        angle = place * freq_ref[0:1, :]
        cos_ref[at, :] = jnp.cos(angle)
        sin_ref[at, :] = sign * jnp.sin(angle)

    attn_io.wait()
    for c in attn_io.here:
        c.wait()
    for c in h_far:
        c.wait_recv()

    def columns(lo, hi):
        return aw_ref[:, :, :, :, lo:hi].reshape(D, hi - lo)

    for j in range(CHIPS):
        h = h_ref[j]
        at = pl.ds(j * ROW, ROW)
        qv = jnp.dot(h, columns(0, HW), preferred_element_type=full)
        q_ref[at, :] = qv
        kv = jnp.dot(h, columns(HW, 2 * HW), preferred_element_type=full)
        k_ref[at, :] = kv
        v_ref[at, :] = jnp.dot(h, columns(2 * HW, 3 * HW), preferred_element_type=full).astype(low)
        sums[0, :, at] = row_sums(qv * qv, kv * kv)
    sum_io = [net.send(sums.at[0], sums.at[i], m) for i, m in ((1, 2), (2, 4), (3, 6))]
    early = ((h_ref, h_out), (aw_ref, aw_out), (q_ref, q_out), (k_ref, k_out), (v_ref, v_out))
    for i, (src, dst) in enumerate(early):
        kept.append(pltpu.make_async_copy(src, dst, out_sems.at[CHIPS + i]))
        kept[-1].start()

    text_io.finish()
    text_io.wait()
    for c in text_io.here:
        c.wait()

    def text_rows(j, lo, count):
        kt = 1024

        def body(i, acc):
            at = pl.ds(pl.multiple_of(i * kt, kt), kt)
            rows = ta_ref[j, pl.ds(lo, count), at]
            return acc + jnp.dot(rows, tw_ref[i].reshape(kt, 2 * HW), preferred_element_type=full)

        both = lax.fori_loop(0, ta_ref.shape[2] // kt, body, jnp.zeros((count, 2 * HW), full))
        keys, vals = both[:, :HW], both[:, HW:]
        at = pl.ds(j * ta_ref.shape[1] + lo, count)
        tk_ref[at, :] = keys
        tv_ref[at, :] = vals.astype(low)
        tsums[0, :, at] = row_sums(keys * keys, None)

    cap = ta_ref.shape[1]
    half = cap // 2
    text_rows(0, 0, cap)
    for i, c in enumerate(sum_io):
        c.wait_recv()
    for j in range(CHIPS):
        total = sums[0, :, pl.ds(j * ROW, ROW)]
        for i in (1, 2, 3):
            total = total + sums[i, :, pl.ds((j ^ i) * ROW, ROW)]
        both = jnp.transpose(lax.rsqrt(total / D + EPS))
        iq_ref[pl.ds(j * ROW, ROW), :] = both[:, 0:1]
        ik_ref[pl.ds(j * ROW, ROW), :] = both[:, 4:5]
    text_rows(1, 0, half)
    text_rows(2, half, half)
    for s in range(chunks // 2):
        tx[s + chunks // 2].wait_recv()
        ty[s].wait_recv()
    kept += [keep(1), keep(2)]
    text_rows(1, half, half)
    text_rows(2, 0, half)
    for c in relays:
        c.wait_recv()
    kept.append(keep(3))
    text_rows(3, 0, cap)
    sum_io = [net.send(tsums.at[0], tsums.at[i], m) for i, m in ((1, 2), (2, 4), (3, 6))]
    for c in sum_io:
        c.wait_recv()
    for j in range(CHIPS):
        total = tsums[0, :, pl.ds(j * cap, cap)]
        for i in (1, 2, 3):
            total = total + tsums[i, :, pl.ds((j ^ i) * cap, cap)]
        it_ref[pl.ds(j * cap, cap), :] = jnp.transpose(lax.rsqrt(total / D + EPS))[:, 0:1]
    for c in kept:
        c.wait()
    attn_io.close()
    text_io.close()
    net.close()


def open_layer(cond, gain_pad, bias_pad, ada, tok, counts, idx, freq, attn, textw, text):
    low = jnp.bfloat16
    full = jnp.float32
    shape = jax.ShapeDtypeStruct
    cap, txtd = text.shape
    V = VMEM_SPEC
    return pl.pallas_call(
        open_kernel,
        in_specs=[V] * 8 + [ANY_SPEC] * 3,
        out_specs=[V, V, ANY_SPEC, V] + [ANY_SPEC] * 5 + [V] * 11,
        out_shape=[
            shape((8, 3072), full),
            shape((8, D), full),
            shape((CHIPS, ROW, D), low),
            shape((CHIPS, 8, ROW), jnp.int32),
            shape((CHIPS, 2, *attn.shape[1:3], 3 * HW), low),
            shape((CHIPS, cap, txtd), low),
            shape((CHIPS * ROW, HW), full),
            shape((CHIPS * ROW, HW), full),
            shape((CHIPS * ROW, HW), low),
            shape((CHIPS * cap, HW), full),
            shape((CHIPS * cap, HW), low),
            shape((CHIPS * ROW, 1), full),
            shape((CHIPS * ROW, 1), full),
            shape((CHIPS * cap, 1), full),
            shape((CHIPS * ROW, 128), full),
            shape((CHIPS * ROW, 128), full),
            shape((CHIPS * ROW, 1), jnp.int32),
            shape((8, HW), full),
            shape((ROW, 1), jnp.int32),
            shape((8, 128), full),
        ],
        scratch_shapes=[
            pltpu.VMEM((CHIPS, ROW, D), low),
            pltpu.VMEM((CHIPS, 2, *attn.shape[1:3], 3 * HW), low),
            pltpu.VMEM((CHIPS * ROW, HW), full),
            pltpu.VMEM((CHIPS * ROW, HW), full),
            pltpu.VMEM((CHIPS * ROW, HW), low),
            pltpu.VMEM((8, 8, 128), full),
            pltpu.VMEM((8, 8, 3072), full),
            pltpu.VMEM((8, 8, 3072), full),
            pltpu.VMEM((9, 8, D), full),
            pltpu.VMEM((CHIPS, 2, *textw.shape[1:3], 2 * HW), low),
            pltpu.VMEM((CHIPS, cap, txtd), low),
            pltpu.VMEM((CHIPS, 8, CHIPS * ROW), full),
            pltpu.VMEM((CHIPS, 8, CHIPS * cap), full),
            pltpu.SemaphoreType.DMA((8,)),
            pltpu.SemaphoreType.DMA((CHIPS + 5,)),
            pltpu.SemaphoreType.DMA((48,)),
            pltpu.SemaphoreType.DMA((48,)),
            *net_scratch(80),
        ],
        compiler_params=pltpu.CompilerParams(
            collective_id=1, has_side_effects=True, vmem_limit_bytes=56 * 1024 * 1024
        ),
        cost_estimate=pl.CostEstimate(
            flops=10_000_000_000, bytes_accessed=400_000_000, transcendentals=0
        ),
    )(cond, gain_pad, bias_pad, ada, tok, counts, idx, freq, attn, textw, text)


class Chain:
    def __init__(self, net, grad, mine, arrive, total, sems, columns):
        self.net = net
        self.grad = grad
        self.mine = mine
        self.arrive = arrive
        self.total = total
        self.sems = sems
        self.columns = columns
        self.plane = lax.axis_index("bucket")
        self.core = net.me % 2

    def piece(self, ref, p):
        return ref.at[:, p] if self.columns else ref.at[p]

    def half(self, core):
        return self.grad.at[:, :, :, core] if self.columns else self.grad.at[:, core]

    def each(self, ref, body):
        lead = ref.shape[:-2]
        if not lead:
            body(())
            return
        total = 1
        for n in lead:
            total *= n

        def step(i, _):
            index = []
            for n in reversed(lead):
                index.insert(0, i % n)
                i = i // n
            body(tuple(index))
            return 0

        lax.fori_loop(0, total, step, 0)

    def core_start(self, keep=None, sem=None):
        self.exchange = self.net.send(self.half(1 - self.core), self.mine, 1)
        self.keep = self.half(self.core)
        self.load = None
        if keep is not None:
            self.load = pltpu.make_async_copy(self.keep, keep, sem)
            self.load.start()
            self.keep = keep

    def add(self, into, other):
        def body(index):
            value = into[index].astype(jnp.float32) + other[index].astype(jnp.float32)
            into[index] = value.astype(into.dtype)

        self.each(into, body)

    def core_finish(self):
        self.exchange.wait_recv()
        if self.load is not None:
            self.load.wait()
        self.add(self.mine, self.keep)

    def copy(self, up, p, slot):
        first = 0 if up else 8
        return pltpu.make_async_remote_copy(
            src_ref=self.piece(self.mine, p),
            dst_ref=self.arrive.at[slot],
            send_sem=self.sems.at[first + p],
            recv_sem=self.sems.at[first + 4 + p],
            device_id={"bucket": self.plane + (1 if up else -1)},
            device_id_type=MESH_IDS,
        )

    def moves(self, t):
        up = self.plane + 3 - t
        down = self.plane - 3 + t
        return (
            (True, up, up, self.plane <= t, self.plane >= 1),
            (False, down, 4 if t == 2 else down, self.plane >= 3 - t, self.plane <= 2),
        )

    def step(self, t):
        for up, p, slot, sends, inner in self.moves(t):

            @pl.when(sends)
            def _(up=up, p=p, slot=slot, inner=inner):
                @pl.when(inner)
                def _():
                    self.copy(up, p, p).wait_recv()
                    self.add(self.piece(self.mine, p), self.arrive.at[p])

                self.copy(up, p, slot).start()

    def finish(self):
        own = self.piece(self.mine, self.plane)

        def first(index):
            self.total[index] = own[index].astype(jnp.float32)

        self.each(self.total, first)
        for up, slot, inner in ((True, self.plane, self.plane >= 1), (False, 4, self.plane <= 2)):

            @pl.when(inner)
            def _(up=up, slot=slot):
                self.copy(up, self.plane, slot).wait_recv()
                self.add(self.total, self.arrive.at[slot])

    def close(self):
        for t in range(3):
            for up, p, slot, sends, inner in self.moves(t):

                @pl.when(sends)
                def _(up=up, p=p, slot=slot):
                    self.copy(up, p, slot).wait_send()


def chain_scratch(columns, shape, width):
    low = jnp.bfloat16
    if columns:
        n, rows = shape
        return [
            pltpu.VMEM((n, 4, 4, rows, width), low),
            pltpu.VMEM((5, n, 4, rows, width), low),
            pltpu.VMEM((n, 4, rows, width), jnp.float32),
            pltpu.SemaphoreType.DMA((16,)),
        ]
    return [
        pltpu.VMEM((4, shape, width), low),
        pltpu.VMEM((5, shape, width), low),
        pltpu.VMEM((shape, width), jnp.float32),
        pltpu.SemaphoreType.DMA((16,)),
    ]


class Columns:
    def __init__(self, net, total, stage, wide):
        self.net, self.total, self.stage, self.wide = net, total, stage, wide

    def start(self):
        net = self.net
        chip = net.me // 2
        n, _, rows, width = self.stage.shape
        parts = self.wide.shape[0]
        width = width // parts
        at = pl.ds(pl.multiple_of(chip * width, width), width)

        def cast(i, _):
            self.stage[i // 4, i % 4] = self.total[i // 4, i % 4].astype(jnp.bfloat16)
            return 0

        if self.total is not None:
            lax.fori_loop(0, n * 4, cast, 0)
        self.copies = [
            net.send(
                self.stage.at[0, net.peer(m) // 2, :, pl.ds(i * width, width)],
                self.wide.at[i, :, at],
                m,
            )
            for m in (2, 4, 6)
            for i in range(parts)
        ]
        for i in range(parts):
            self.wide[i, :, at] = self.stage[0, chip, :, i * width : i * width + width]

    def finish(self):
        for c in self.copies:
            c.wait_recv()


def meet_all(net, far=False):
    plane = lax.axis_index("bucket")
    chip = net.me // 2
    sem = pltpu.get_barrier_semaphore()
    for mask in ALL_PEERS:
        pl.semaphore_signal(
            sem, inc=1, device_id={"fsdp": net.peer(mask)}, device_id_type=MESH_IDS
        )
    for inner, step in ((plane >= 1, -1), (plane <= 2, 1)):

        @pl.when(inner)
        def _(step=step):
            pl.semaphore_signal(
                sem, inc=1, device_id={"bucket": plane + step}, device_id_type=MESH_IDS
            )

    @pl.when(chip != plane)
    def _():
        pl.semaphore_signal(
            sem,
            inc=1,
            device_id={"bucket": chip, "fsdp": plane * 2 + net.me % 2},
            device_id_type=MESH_IDS,
        )

    if far:
        pl.semaphore_signal(
            sem,
            inc=1,
            device_id={"bucket": plane + 2 - 4 * (plane // 2)},
            device_id_type=MESH_IDS,
        )
    one = jnp.int32(1)
    zero = jnp.int32(0)
    count = (
        (8 if far else 7)
        + jnp.where(plane >= 1, one, zero)
        + jnp.where(plane <= 2, one, zero)
        + jnp.where(chip != plane, one, zero)
    )
    pl.semaphore_wait(sem, count)


def transposed(net, src, dst, sems):
    plane = lax.axis_index("bucket")
    return pltpu.make_async_remote_copy(
        src_ref=src,
        dst_ref=dst,
        send_sem=sems.at[0],
        recv_sem=sems.at[1],
        device_id={"bucket": net.me // 2, "fsdp": plane * 2 + net.me % 2},
        device_id_type=MESH_IDS,
    )


class Spread:
    def __init__(self, buf, sems):
        self.buf, self.sems = buf, sems
        self.plane = lax.axis_index("bucket")

    def copy(self, up, slab):
        first = 0 if up else 8
        return pltpu.make_async_remote_copy(
            src_ref=self.buf.at[slab],
            dst_ref=self.buf.at[slab],
            send_sem=self.sems.at[first + slab],
            recv_sem=self.sems.at[first + 4 + slab],
            device_id={"bucket": self.plane + (1 if up else -1)},
            device_id_type=MESH_IDS,
        )

    def hop(self, h):
        for up in (True, False):
            slab = self.plane - h if up else self.plane + h
            there = (slab >= 0) if up else (slab <= 3)
            sends = (self.plane <= 2) if up else (self.plane >= 1)

            @pl.when(there)
            def _(up=up, slab=slab, sends=sends):
                if h > 0:
                    self.copy(up, slab).wait_recv()

                @pl.when(sends)
                def _():
                    self.copy(up, slab).start()

    def close(self):
        for h in range(4):
            for up in (True, False):
                slab = self.plane - h if up else self.plane + h
                there = (slab >= 0) if up else (slab <= 3)
                sends = (self.plane <= 2) if up else (self.plane >= 1)

                @pl.when(there & sends)
                def _(up=up, slab=slab):
                    self.copy(up, slab).wait_send()


def close_kernel(
    ta_ref, dt_ref, attn_g, out_g, ffn_t, dmod_ref, gg_ref, gs_ref, cond_ref,
    t_wide, a_wide, out_o, f_wide, ada_o, small_o,
    tm, ta, tt, ts, am, aa, at_, as_, om, oa, ot, os_,
    t_stage, a_stage, o_stage, o_got, o_sem,
    mods, mods_other, mod_sems, smalls, got, z_sems, ada_s, ta_s, text_g, ta_sem, send_sems, recv_sems,
):
    low = jnp.bfloat16
    full = jnp.float32
    net = Net(send_sems, recv_sems)
    load = pltpu.make_async_copy(ta_ref, ta_s, ta_sem.at[0])
    load.start()
    meet_all(net, True)
    plane = lax.axis_index("bucket")
    me = net.me
    chip = me // 2
    out = Chain(net, out_g, om, oa, ot, os_, False)
    attn = Chain(net, attn_g, am, aa, at_, as_, True)
    text = Chain(net, text_g, tm, ta, tt, ts, True)
    chains = [out, attn, text]
    first = [out, attn]
    for c in first:
        c.core_start()

    def caption_grad(core):
        def block(i, _):
            at = (i // 4) * 1024 + (i % 4) * 256 + core * 128
            part = t_dot(ta_s[:, pl.ds(pl.multiple_of(at, 128), 128)], dt_ref[...])
            text_g[0, i // 4, i % 4, core] = part.astype(low)
            return 0

        lax.fori_loop(0, 16, block, 0)

    act = cond_ref[...].astype(full)
    act = act * jax.nn.sigmoid(act)
    mods[plane, 0, :, 2 * D :] = jnp.concatenate([act, act], axis=0).astype(low)
    mods[plane, 0, :, : 2 * D] = dmod_ref[...].astype(low)
    mine = mods.at[plane, 0]
    mod_io = [net.send(mine, mods.at[plane, i], m) for i, m in ((1, 2), (2, 4), (3, 6))]

    smalls[...] = jnp.zeros(smalls.shape, full)
    smalls[0:2, :] = gg_ref[0:2, :]
    smalls[2:6, pl.ds(pl.multiple_of(chip * HW, 128), HW)] = gs_ref[0:4, :]
    for p in range(4):
        rows = dmod_ref[4 * (p // 2) : 4 * (p // 2) + 4, (p % 2) * D : (p % 2 + 1) * D]
        smalls[8 + p : 9 + p, :] = jnp.sum(rows, axis=0, keepdims=True)
    order = [None]

    def small_send(i):
        if i < 3:
            order[0] = net.send(smalls, got.at[i], (1, 2, 4)[i])
            return
        there = plane + 1 - 2 * (plane % 2) if i == 3 else plane + 2 - 4 * (plane // 2)
        copy = pltpu.make_async_remote_copy(
            src_ref=smalls,
            dst_ref=got.at[i],
            send_sem=z_sems.at[2 * (i - 3)],
            recv_sem=z_sems.at[2 * (i - 3) + 1],
            device_id={"bucket": there},
            device_id_type=MESH_IDS,
        )
        copy.start()
        order[0] = copy

    def small_add(i):
        order[0].wait()
        net.all = [c for c in net.all if c is not order[0]]
        smalls[...] = smalls[...] + got[i]

    small_send(0)
    f_cols = Columns(net, None, ffn_t, f_wide)
    f_cols.start()
    for c in first:
        c.core_finish()
        c.step(0)
    load.wait()
    caption_grad(1 - me % 2)
    text.core_start()
    small_add(0)
    small_send(1)
    for c in first:
        c.step(1)
    for c in mod_io:
        c.wait_recv()
    lines = Spread(mods, mod_sems)
    lines.hop(0)
    caption_grad(me % 2)
    text.core_finish()
    text.step(0)
    small_add(1)
    small_send(2)
    for c in first:
        c.step(2)
    lines.hop(1)
    small_add(2)
    small_send(3)
    f_cols.finish()
    text.step(1)
    lines.hop(2)
    small_add(3)
    small_send(4)
    text.step(2)
    lines.hop(3)
    other = net.send(mods, mods_other, 1)
    small_add(4)
    small_o[...] = smalls[...]
    out.finish()
    o_stage[...] = ot[...].astype(low)

    @pl.when(chip != plane)
    def _():
        transposed(net, o_stage, o_got, o_sem).start()

    other.wait_recv()
    rank = plane * 8 + me
    lanes = pl.ds(pl.multiple_of(2 * D + (rank // 4) * 128, 128), 128)
    total = 128
    both = []
    for ref in (mods, mods_other):
        acts = ref[:, :, :, lanes].astype(full).reshape(total, 128)
        both.append(acts)
    acts = jnp.concatenate(both, axis=0)
    upper = (lax.broadcasted_iota(jnp.int32, acts.shape, 0) % 8) < 4
    parts = (jnp.where(upper, acts, 0.0).astype(low), jnp.where(upper, 0.0, acts).astype(low))
    wide = 512

    def ada_cols(i, _):
        at = pl.ds(pl.multiple_of(i * wide, wide), wide)
        rows = jnp.concatenate(
            [r[:, :, :, at].astype(full).reshape(total, wide) for r in (mods, mods_other)], axis=0
        ).astype(low)
        for p in range(2):
            ada_s[...] = t_dot(parts[p], rows)
            to = pl.ds(pl.multiple_of(p * 2 * D + i * wide, wide), wide)
            ada_o[:, to] = ada_s[pl.ds(pl.multiple_of((rank % 4) * 32, 32), 32), :]
        return 0

    lax.fori_loop(0, 2 * D // wide, ada_cols, 0)
    attn.finish()
    attn_cols = Columns(net, at_, a_stage, a_wide)
    attn_cols.start()

    @pl.when(chip != plane)
    def _():
        transposed(net, o_stage, o_got, o_sem).wait()
        out_o[...] = o_got[...]

    @pl.when(chip == plane)
    def _():
        out_o[...] = o_stage[...]

    text.finish()
    text_cols = Columns(net, tt, t_stage, t_wide)
    text_cols.start()
    attn_cols.finish()
    text_cols.finish()
    for c in chains:
        c.close()
    lines.close()
    net.close()


def close_layer(text_all, d_text, attn_g, out_g, ffn_t, dmod, gg, gs, cond):
    low = jnp.bfloat16
    full = jnp.float32
    shape = jax.ShapeDtypeStruct
    V = VMEM_SPEC
    tr, tw = text_all.shape[1] // 32, d_text.shape[1] // 2
    ar, aw = attn_g.shape[-2], attn_g.shape[-1] // 3
    orow, ow = out_g.shape[-2:]
    fr, fw = ffn_t.shape[-2], ffn_t.shape[-1] // 2
    return pl.pallas_call(
        close_kernel,
        in_specs=[ANY_SPEC] + [V] * 8,
        out_specs=[V] * 6,
        out_shape=[
            shape((2, tr, 4 * tw), low),
            shape((3, ar, 4 * aw), low),
            shape((orow, ow), low),
            shape((2, fr, 4 * fw), low),
            shape((32, 4 * D), full),
            shape((16, D), full),
        ],
        scratch_shapes=[
            *chain_scratch(True, (1, tr), 2 * tw),
            *chain_scratch(True, (1, ar), 3 * aw),
            *chain_scratch(False, orow, ow),
            pltpu.VMEM((1, 4, tr, 2 * tw), low),
            pltpu.VMEM((1, 4, ar, 3 * aw), low),
            pltpu.VMEM((orow, ow), low),
            pltpu.VMEM((orow, ow), low),
            pltpu.SemaphoreType.DMA((2,)),
            pltpu.VMEM((4, CHIPS, 8, 2 * D + cond.shape[1]), low),
            pltpu.VMEM((4, CHIPS, 8, 2 * D + cond.shape[1]), low),
            pltpu.SemaphoreType.DMA((16,)),
            pltpu.VMEM((16, D), full),
            pltpu.VMEM((5, 16, D), full),
            pltpu.SemaphoreType.DMA((4,)),
            pltpu.VMEM((128, 512), full),
            pltpu.VMEM(text_all.shape, low),
            pltpu.VMEM((1, 4, 4, 2, tr, 2 * tw), low),
            pltpu.SemaphoreType.DMA((1,)),
            *net_scratch(40),
        ],
        compiler_params=pltpu.CompilerParams(
            collective_id=2, has_side_effects=True, vmem_limit_bytes=60 * 1024 * 1024
        ),
        cost_estimate=pl.CostEstimate(
            flops=1_000_000, bytes_accessed=400_000_000, transcendentals=0
        ),
    )(text_all, d_text, attn_g, out_g, ffn_t, dmod, gg, gs, cond)


def back_kernel(
    dh2_ref, fo_ref, x1_ref, branch_ref, cot_ref, w_ref, mod_ref, seg_ref, gain_ref, tok_ref,
    sr_ref, gs_ref, *rest,
):
    late, rest = rest[:LATE], rest[LATE:]
    places, rest = rest[-LATE - 1 : -1], rest[: -LATE - 1] + rest[-1:]
    loads = [
        pltpu.make_async_copy(src, dst, rest[-1].at[i])
        for i, (src, dst) in enumerate(zip(late, places))
    ]
    back_body(
        dh2_ref, fo_ref, x1_ref, branch_ref, cot_ref, w_ref, mod_ref, seg_ref, gain_ref, tok_ref,
        *places, sr_ref, gs_ref, *rest[:-1], loads,
    )


LATE = 17


def back_body(
    dh2_ref, fo_ref, x1_ref, branch_ref, cot_ref, w_ref, mod_ref, seg_ref, gain_ref, tok_ref,
    ow_ref, aw_ref, qr_ref, kr_ref, v_ref, tr_ref, tv_ref, cross_ref, q_ref, k_ref, tk_ref,
    iq_ref, ik_ref, it_ref, cos_ref, sin_ref, sc_ref, sr_ref, gs_ref, ffn_g, down_g,
    block_o, token_o, db_ref, dqkv_o, dtkv_o, dmod_o, gg_o, gs_o, ffn_o, down_o,
    dx_s, dc_s, dqf, dkf, dtf, part_s, sums, tsums, buf_a, far_a, buf_b, far_b, buf_c, far_c,
    fm, fa, ft, fs, dm, da, dt_c, ds_, f_keep, d_keep, keep_sem, send_sems, recv_sems, loads,
):
    low = jnp.bfloat16
    full = jnp.float32
    net = Net(send_sems, recv_sems)
    meet_all(net)
    plane = lax.axis_index("bucket")
    chip = net.me // 2
    ffn = Chain(net, ffn_g, fm, fa, ft, fs, True)
    down = Chain(net, down_g, dm, da, dt_c, ds_, False)
    ffn.core_start(f_keep, keep_sem.at[0])
    down.core_start(d_keep, keep_sem.at[1])
    for c in loads:
        c.start()

    def rows_of(ref):
        half = ROW // 2
        return lambda j, i: ref[pl.ds(j * ROW + i * half, half), :].astype(full)

    middle, finish = collect4(net, rows_of(dh2_ref), buf_a, far_a)
    middle()
    ffn.core_finish()
    ffn.step(0)
    down.core_finish()
    down.step(0)
    half = ROW // 2
    for i in (0, 1):
        dx_s[pl.ds(i * half, half), :] = finish(i)
    part_s[pl.ds(0, ROW), :] = dx_s[...]
    block = 32
    weight = w_ref[0:1, 0:1]

    def second_norm(at):
        x1 = x1_ref[at, :]
        inverse = lax.rsqrt(jnp.mean(x1 * x1, axis=-1, keepdims=True) + EPS)
        scale = pick_rows(mod_ref[:, :D], seg_ref[at, :], 4)
        return x1 * inverse, inverse, scale

    def to_branch(b, _):
        at = pl.ds(pl.multiple_of(b * block, block), block)
        normed, inverse, scale = second_norm(at)
        dn = dx_s[at, :] * gain_ref[1:2, :] * (1.0 + scale)
        back = inverse * (dn - normed * jnp.mean(dn * normed, axis=-1, keepdims=True))
        dx = cot_ref[at, :].astype(full) * weight + back
        dx_s[at, :] = dx
        gate = jnp.tanh(pick_rows(mod_ref[:, D:], seg_ref[at, :], 0))
        db_ref[0, at, :] = (dx * gate).astype(low)
        return 0

    lax.fori_loop(0, ROW // block, to_branch, 0)
    bx, by = share4_start(net, db_ref)

    def by_image(value, seg, row, lo):
        for i in range(IMGS):
            dmod_o[row + i : row + i + 1, lo : lo + D] += jnp.sum(
                jnp.where(seg == i, value, 0.0), axis=0, keepdims=True
            )

    dmod_o[...] = jnp.zeros(dmod_o.shape, full)
    gg_o[...] = jnp.zeros(gg_o.shape, full)

    def second_sums(b, _):
        at = pl.ds(pl.multiple_of(b * block, block), block)
        normed, inverse, scale = second_norm(at)
        seg = seg_ref[at, :]
        dh = part_s[at, :] * normed
        gg_o[1:2, :] += jnp.sum(dh * (1.0 + scale), axis=0, keepdims=True)
        by_image(dh * gain_ref[1:2, :], seg, 4, 0)
        gate = jnp.tanh(pick_rows(mod_ref[:, D:], seg, 0))
        by_image(dx_s[at, :] * branch_ref[at, :] * (1.0 - gate * gate), seg, 0, D)
        return 0

    lax.fori_loop(0, ROW // block, second_sums, 0)
    far = share4_relay(net, db_ref, bx, by)
    middle_b, finish_b = collect4(net, rows_of(fo_ref), buf_b, far_b)
    gs_o[...] = jnp.zeros(gs_o.shape, full)
    for c in loads:
        c.wait()
    cap = IMGS * TXT

    def attention_row(j, _):
        @pl.when(j == 3)
        def _():
            for c in far:
                c.wait_recv()

        @pl.when(j == 1)
        def _():
            ffn.step(1)
            down.step(1)

        @pl.when(j == 3)
        def _():
            ffn.step(2)
            down.step(2)

        rows = pl.ds(pl.multiple_of(j * ROW, ROW), ROW)
        text = pl.ds(pl.multiple_of(j * cap, cap), cap)
        dc_s[...] = dot_t(db_ref[j], ow_ref[...])
        dqv, dkv, dtv = dqf.at[rows], dkf.at[rows], dtf.at[text]
        attend_back_kernel(
            qr_ref.at[rows], kr_ref.at[rows], v_ref.at[rows], tr_ref.at[text], tv_ref.at[text],
            dc_s, cross_ref.at[rows], q_ref.at[rows], k_ref.at[rows], tk_ref.at[text],
            iq_ref.at[rows], ik_ref.at[rows], it_ref.at[text], cos_ref.at[rows], sin_ref.at[rows],
            sc_ref.at[rows], sr_ref.at[j, pl.ds(0, 1)], gs_ref,
            dqv, dkv, dqkv_o.at[rows, pl.ds(2 * HW, HW)], dtv, dtkv_o.at[text, pl.ds(HW, HW)], gs_o,
        )
        sums[0, :, rows] = row_sums(
            dqv[...] * (q_ref[rows, :] * iq_ref[rows, :]),
            dkv[...] * (k_ref[rows, :] * ik_ref[rows, :]),
        )
        tsums[0, :, text] = row_sums(dtv[...] * (tk_ref[text, :] * it_ref[text, :]), None)
        return 0

    lax.fori_loop(0, CHIPS, attention_row, 0)
    sum_io = []
    for i, m in ((1, 2), (2, 4), (3, 6)):
        sum_io.append(net.send(sums.at[0], sums.at[i], m))
        sum_io.append(net.send(tsums.at[0], tsums.at[i], m))
    middle_b()
    for i in (0, 1):
        part_s[pl.ds(i * half, half), :] = finish_b(i)

    def block_rows(b, _):
        at = pl.ds(pl.multiple_of(b * block, block), block)
        seg = seg_ref[at, :]
        gate = jnp.tanh(pick_rows(mod_ref[:, D:], seg, 4))
        out = part_s[at, :]
        block_o[at, :] = (x1_ref[at, :] + gate * out).astype(low)
        grad = cot_ref[at, :].astype(full) * weight
        by_image(grad * out * (1.0 - gate * gate), seg, 4, D)
        return 0

    for c in sum_io:
        c.wait_recv()
    for j in range(CHIPS):
        rows = pl.ds(j * ROW, ROW)
        text = pl.ds(j * cap, cap)
        total = sums[0, :, rows]
        words = tsums[0, :, text]
        for i in (1, 2, 3):
            total = total + sums[i, :, pl.ds((j ^ i) * ROW, ROW)]
            words = words + tsums[i, :, pl.ds((j ^ i) * cap, cap)]
        mean = jnp.transpose(total / D)
        iq, ik, it = iq_ref[rows, :], ik_ref[rows, :], it_ref[text, :]
        dqkv_o[rows, :HW] = (iq * (dqf[rows, :] - q_ref[rows, :] * iq * mean[:, 0:1])).astype(low)
        dqkv_o[rows, HW : 2 * HW] = (ik * (dkf[rows, :] - k_ref[rows, :] * ik * mean[:, 4:5])).astype(low)
        mean = jnp.transpose(words / D)
        dtkv_o[text, :HW] = (it * (dtf[text, :] - tk_ref[text, :] * it * mean[:, 0:1])).astype(low)

    lax.fori_loop(0, ROW // block, block_rows, 0)
    wide = 256

    def first_grad(n, _):
        at = pl.ds(pl.multiple_of(n * wide, wide), wide)
        part_s[:, at] = dot_t(dqkv_o[...], aw_ref[at, :])
        return 0

    lax.fori_loop(0, D // wide, first_grad, 0)
    middle_c, finish_c = collect4(net, rows_of(part_s), buf_c, far_c)
    ffn.finish()
    middle_c()

    def ffn_cast(i, _):
        ffn_o[0, i] = ft[0, i].astype(low)
        return 0

    lax.fori_loop(0, 4, ffn_cast, 0)
    down.finish()
    down_o[...] = dt_c[...].astype(low)
    gate = jnp.tanh(gs_ref[5:6, :])
    gs_o[3:4, :] = gs_o[3:4, :] * (1.0 - gate * gate)
    for i in (0, 1):
        part_s[pl.ds(i * half, half), :] = finish_c(i)

    def first_rows(b, _):
        at = pl.ds(pl.multiple_of(b * block, block), block)
        x = tok_ref[at, :].astype(full)
        inverse = lax.rsqrt(jnp.mean(x * x, axis=-1, keepdims=True) + EPS)
        normed = x * inverse
        seg = seg_ref[at, :]
        scale = pick_rows(mod_ref[:, :D], seg, 0)
        dh = part_s[at, :]
        gg_o[0:1, :] += jnp.sum(dh * normed * (1.0 + scale), axis=0, keepdims=True)
        by_image(dh * normed * gain_ref[0:1, :], seg, 0, 0)
        dn = dh * gain_ref[0:1, :] * (1.0 + scale)
        token_o[at, :] = dx_s[at, :] + inverse * (
            dn - normed * jnp.mean(dn * normed, axis=-1, keepdims=True)
        )
        return 0

    lax.fori_loop(0, ROW // block, first_rows, 0)
    ffn.close()
    down.close()
    net.close()


def back_layer(early, late, ffn_g, down_g):
    low = jnp.bfloat16
    full = jnp.float32
    shape = jax.ShapeDtypeStruct
    V = VMEM_SPEC
    cap = IMGS * TXT
    fr, fw = ffn_g.shape[-2], ffn_g.shape[-1] // 2
    dr, dw = down_g.shape[-2:]
    tok = CHIPS * ROW
    reduce_scratch = [pltpu.VMEM((5, ROW, D), low), pltpu.VMEM((2, ROW // 2, D), low)]
    return pl.pallas_call(
        back_kernel,
        in_specs=[V] * len(early) + [ANY_SPEC] * (LATE + 2),
        out_specs=[V] * 10,
        out_shape=[
            shape((ROW, D), low),
            shape((ROW, D), full),
            shape((CHIPS, ROW, D), low),
            shape((tok, 3 * HW), low),
            shape((CHIPS * cap, 2 * HW), low),
            shape((8, 2 * D), full),
            shape((8, D), full),
            shape((8, HW), full),
            shape((1, 4, fr, 2 * fw), low),
            shape((dr, dw), low),
        ],
        scratch_shapes=[
            pltpu.VMEM((ROW, D), full),
            pltpu.VMEM((ROW, HW), full),
            pltpu.VMEM((tok, HW), full),
            pltpu.VMEM((tok, HW), full),
            pltpu.VMEM((CHIPS * cap, HW), full),
            pltpu.VMEM((tok, D), full),
            pltpu.VMEM((CHIPS, 8, tok), full),
            pltpu.VMEM((CHIPS, 8, CHIPS * cap), full),
            *reduce_scratch, *reduce_scratch, *reduce_scratch,
            *chain_scratch(True, (1, fr), 2 * fw),
            *chain_scratch(False, dr, dw),
            pltpu.VMEM((1, 4, 4, fr, 2 * fw), low),
            pltpu.VMEM((4, dr, dw), low),
            pltpu.SemaphoreType.DMA((2,)),
            *net_scratch(48),
            *[pltpu.VMEM(v.shape, v.dtype) for v in late],
            pltpu.SemaphoreType.DMA((LATE,)),
        ],
        compiler_params=pltpu.CompilerParams(
            collective_id=3, has_side_effects=True, vmem_limit_bytes=63 * 1024 * 1024
        ),
        cost_estimate=pl.CostEstimate(
            flops=10_000_000_000, bytes_accessed=400_000_000, transcendentals=0
        ),
    )(*early, *late, ffn_g, down_g)


def row_spec(rows, width):
    return pl.BlockSpec((rows, width), lambda i: (i, 0))


def forward_kernel(
    q_ref, k_ref, v_ref, iq_ref, ik_ref, cos_ref, sin_ref, tk_ref, it_ref, tv_ref, sc_ref, sr_ref,
    gs_ref, mod_ref, seg_ref, gain_ref, tok_ref, cot_ref, w_ref, outw_ref, ffnw_ref, downw_ref,
    comb_o, cross_o, qr_o, kr_o, tr_o, branch_o, x1_o, h_o, df_o, ow_o, fw_o, dw_o,
    part_s, buf, far, f_own, d_own, local_sems, line_sems, send_sems, recv_sems,
):
    low = jnp.bfloat16
    full = jnp.float32
    net = Net(send_sems, recv_sems)
    meet_line(net, (1, 2, 4, 6))
    me = net.me
    chip = me // 2
    width = fw_o.shape[4] // 2
    rows = outw_ref.shape[0]

    def local(src, dst, i):
        copy = pltpu.make_async_copy(src, dst, local_sems.at[i])
        copy.start()
        return copy

    def own(ref, count):
        return ref.at[pl.ds(pl.multiple_of((me % 2) * count, count), count), :]

    out_here = local(outw_ref, own(ow_o, rows), 0)
    out_core = net.send(outw_ref, own(ow_o, rows), 1)
    down_rows = downw_ref.shape[0]
    down_here = local(downw_ref, d_own, 1)
    down_core = net.send(downw_ref, own(dw_o, down_rows), 1)

    def stage(i, src, dst):
        return local(src, f_own.at[:, :, pl.ds(i * width, width)], 2 + i)

    ffn_io = Lines(net, ffnw_ref, fw_o, width, line_sems, stage)
    ffn_io.away_start()
    ffn_io.own_start()
    block = 32
    weight = w_ref[0:1, 0:1]

    def ffn_grad(b, _):
        at = pl.ds(pl.multiple_of(b * block, block), block)
        gate = jnp.tanh(pick_rows(mod_ref[:, D:], seg_ref[at, :], 4))
        df_o[0, at, :] = (cot_ref[at, :].astype(full) * weight * gate).astype(low)
        return 0

    lax.fori_loop(0, ROW // block, ffn_grad, 0)
    dx, dy = share4_start(net, df_o)
    out_here.wait()
    out_core.wait_recv()
    cap = IMGS * TXT

    def attention_row(i, _):
        @pl.when(i == 1)
        def _():
            ffn_io.hop(0)

        @pl.when(i == 3)
        def _():
            ffn_io.hop(1)

        j = 3 - i
        at = pl.ds(pl.multiple_of(j * ROW, ROW), ROW)
        text = pl.ds(pl.multiple_of(j * cap, cap), cap)
        attend_kernel(
            q_ref.at[at], k_ref.at[at], v_ref.at[at], iq_ref.at[at], ik_ref.at[at],
            cos_ref.at[at], sin_ref.at[at], tk_ref.at[text], it_ref.at[text], tv_ref.at[text],
            sc_ref.at[at], sr_ref.at[j, pl.ds(0, 1)], gs_ref,
            comb_o.at[at], cross_o.at[at], qr_o.at[at], kr_o.at[at], tr_o.at[text],
        )
        part_s[at, :] = jnp.dot(comb_o[at, :], ow_o[...], preferred_element_type=full)
        return 0

    lax.fori_loop(0, CHIPS, attention_row, 0)
    half = ROW // 2
    middle, finish = collect4(
        net, lambda j, i: part_s[pl.ds(j * ROW + i * half, half), :], buf, far
    )
    df_far = share4_relay(net, df_o, dx, dy)

    down_here.wait()
    down_out = local(d_own, own(dw_o, down_rows), 4)
    for c in ffn_io.here:
        c.wait()
    f_out = local(f_own, fw_o.at[chip, me % 2], 5)
    middle()
    ffn_io.hop(2)
    for i in (0, 1):
        branch_o[pl.ds(i * half, half), :] = finish(i)

    def second(b, _):
        at = pl.ds(pl.multiple_of(b * block, block), block)
        seg = seg_ref[at, :]
        gate = jnp.tanh(pick_rows(mod_ref[:, D:], seg, 0))
        x1 = tok_ref[at, :].astype(full) + gate * branch_o[at, :]
        x1_o[at, :] = x1
        normed = x1 * lax.rsqrt(jnp.mean(x1 * x1, axis=-1, keepdims=True) + EPS)
        scale = pick_rows(mod_ref[:, :D], seg, 4)
        h_o[0, at, :] = (normed * gain_ref[1:2, :] * (1.0 + scale)).astype(low)
        return 0

    lax.fori_loop(0, ROW // block, second, 0)
    hx, hy = share4_start(net, h_o)
    ffn_io.finish()
    last = share4_relay(net, h_o, hx, hy)
    for c in (*df_far, *last, down_core):
        c.wait_recv()
    ffn_io.wait()
    down_out.wait()
    f_out.wait()
    ffn_io.close()
    net.close()


def forward_layer(*args):
    low = jnp.bfloat16
    full = jnp.float32
    shape = jax.ShapeDtypeStruct
    V = VMEM_SPEC
    cap = IMGS * TXT
    tok = CHIPS * ROW
    out_w, ffn_w, down_w = args[-3:]
    width = ffn_w.shape[3] // CHIPS
    return pl.pallas_call(
        forward_kernel,
        in_specs=[V] * (len(args) - 3) + [ANY_SPEC] * 3,
        out_specs=[V] * 10 + [ANY_SPEC] * 2,
        out_shape=[
            shape((tok, HW), low),
            shape((tok, HW), full),
            shape((tok, HW), low),
            shape((tok, HW), low),
            shape((CHIPS * cap, HW), low),
            shape((ROW, D), full),
            shape((ROW, D), full),
            shape((CHIPS, ROW, D), low),
            shape((CHIPS, ROW, D), low),
            shape((2 * out_w.shape[0], D), low),
            shape((CHIPS, 2, *ffn_w.shape[1:3], 2 * width), low),
            shape((2 * down_w.shape[0], D), low),
        ],
        scratch_shapes=[
            pltpu.VMEM((tok, D), full),
            pltpu.VMEM((5, ROW, D), low),
            pltpu.VMEM((2, ROW // 2, D), low),
            pltpu.VMEM((*ffn_w.shape[1:3], 2 * width), low),
            pltpu.VMEM(down_w.shape, low),
            pltpu.SemaphoreType.DMA((6,)),
            pltpu.SemaphoreType.DMA((48,)),
            *net_scratch(40),
        ],
        compiler_params=pltpu.CompilerParams(
            collective_id=4, has_side_effects=True, vmem_limit_bytes=56 * 1024 * 1024
        ),
        cost_estimate=pl.CostEstimate(
            flops=5_000_000_000, bytes_accessed=200_000_000, transcendentals=0
        ),
    )(*args)


def quarters(w):
    n, rows, columns = w.shape
    return w.reshape(n, 4, rows // 4, columns)


def per_device(
    tokens,
    cond,
    text,
    segments,
    positions,
    counts,
    ada_weight,
    ada_bias,
    gains,
    attn_weight,
    out_weight,
    text_weight,
    ffn_weight,
    down_weight,
    cotangent,
):
    low = jnp.bfloat16
    full = jnp.float32
    plane = lax.axis_index("bucket")
    slot = lax.axis_index("fsdp")
    core = slot % 2
    chip = slot // 2
    ff = ffn_weight.shape[2] // CHIPS

    gain_pad = lax.dynamic_update_slice_in_dim(
        jnp.zeros((8, D), full), jnp.pad(gains.astype(full), ((0, 2), (0, 0))), slot * 192, axis=1
    )
    bias = lax.dynamic_update_slice_in_dim(
        jnp.zeros((ada_weight.shape[1],), full), ada_bias.astype(full), slot * ada_bias.shape[0], 0
    )
    bias_pad = jnp.repeat(bias.reshape(2, 3072), 4, axis=0)
    seg = segments[0]
    idx = jnp.concatenate([seg[None, :], positions[0], jnp.zeros((5, ROW), jnp.int32)], axis=0)
    quarter = HDIM // 4
    freq = np.tile(10000.0 ** (-np.arange(quarter) / quarter), (8, 128 // quarter))
    freq_row = jnp.asarray(freq.astype(np.float32))
    (
        mod, gain_f, h_rows, idx_all, attn_w, text_rows, query, keyed, valued, text_keys, text_vals,
        inv_q, inv_k, inv_t, cosine, sine, seg_col, gain_s, seg_own, weight_row,
    ) = open_layer(
        cond[0], gain_pad, bias_pad, ada_weight, tokens[0],
        counts[None, :], idx, freq_row, quarters(attn_weight), quarters(text_weight), text[0],
    )
    attn_w = attn_w.reshape(D, 3 * HW)
    h_all = h_rows.reshape(CHIPS * ROW, D)
    text_all = text_rows.reshape(CHIPS * IMGS * TXT, -1)
    (
        comb, cross_out, q_rot, k_rot, text_rot, branch, x_one, h_two_rows, d_ffn_rows, out_w, ffn_w,
        down_w,
    ) = forward_layer(
        query, keyed, valued, inv_q, inv_k, cosine, sine, text_keys, inv_t, text_vals,
        seg_col, idx_all, gain_s, mod, seg_own, gain_f, tokens[0], cotangent[0], weight_row,
        out_weight, quarters(ffn_weight), down_weight,
    )
    ffn_w = ffn_w.reshape(D, 2 * ff)
    h_two_all = h_two_rows.reshape(CHIPS * ROW, D)
    d_ffn_all = d_ffn_rows.reshape(CHIPS * ROW, D)
    both = mult(h_two_all, ffn_w)
    gate_pre = both[:, :ff]
    upper = both[:, ff:]
    d_hidden = dot_t(d_ffn_all, down_w)
    sigm = jax.nn.sigmoid(gate_pre)
    silu_pre = gate_pre * sigm
    hidden = (silu_pre * upper).astype(low)
    d_pre = (d_hidden * upper * sigm * (1.0 + gate_pre * (1.0 - sigm))).astype(low)
    d_up = (d_hidden * silu_pre).astype(low)
    d_both = jnp.concatenate([d_pre, d_up], axis=1)
    d_h_two = dot_t(d_both, ffn_w).astype(low)
    ffn_out = mult(hidden, down_w).astype(low)
    g_down = t_dot(hidden, d_ffn_all).astype(low)
    g_ffn = t_dot(h_two_all, d_both).astype(low)

    (
        block_out, token_grad, d_branch_rows, d_qkv, d_text, d_mod, gg_full, gg_slice, ffn_sum, down_sum,
    ) = back_layer(
        [
            d_h_two, ffn_out, x_one, branch, cotangent[0], weight_row, mod,
            seg_own, gain_f, tokens[0], idx_all, gain_s,
        ],
        [
            out_w, attn_w, q_rot, k_rot, valued, text_rot, text_vals, cross_out, query, keyed,
            text_keys, inv_q, inv_k, inv_t, cosine, sine, seg_col,
        ],
        g_ffn.reshape(1, 4, 4, 2, 48, 2 * ff),
        g_down.reshape(4, 2, 128, D),
    )
    d_branch_all = d_branch_rows.reshape(CHIPS * ROW, D)
    g_attn = t_dot(h_all, d_qkv).astype(low)
    g_out = t_dot(comb, d_branch_all).astype(low)
    s_down = to_row_owner(down_sum)
    s_text, s_attn, s_out, s_ffn, s_ada_w, small = close_layer(
        text_all,
        d_text,
        g_attn.reshape(1, 4, 4, 2, 48, 3 * HW),
        g_out.reshape(4, 2, 48, D),
        ffn_sum,
        d_mod,
        gg_full,
        gg_slice,
        cond[0],
    )
    rank = plane * 8 + slot
    s_gains = lax.dynamic_slice_in_dim(small[:6], rank * 48, 48, axis=1)
    s_ada_b = lax.dynamic_slice_in_dim(small[8:12].reshape(-1), rank * 192, 192, axis=0)
    return (
        block_out[None],
        token_grad[None],
        s_ada_w,
        s_ada_b,
        s_gains,
        s_attn.astype(full),
        s_out.astype(full),
        s_text.astype(full),
        s_ffn.astype(full),
        s_down,
    )


def solution(mesh):
    in_specs = (
        P(("bucket", "fsdp"), None, None),
        P(("bucket", "fsdp"), None, None),
        P(("bucket", "fsdp"), None, None),
        P(("bucket", "fsdp"), None),
        P(("bucket", "fsdp"), None, None),
        P(),
        P("fsdp", None),
        P("fsdp"),
        P(None, "fsdp"),
        P(None, "fsdp", None),
        P("fsdp", None),
        P(None, "fsdp", None),
        P(None, "fsdp", None),
        P("fsdp", None),
        P(("bucket", "fsdp"), None, None),
    )
    out_specs = (
        P(("bucket", "fsdp"), None, None),
        P(("bucket", "fsdp"), None, None),
        P(("bucket", "fsdp"), None),
        P(("bucket", "fsdp")),
        P(None, ("bucket", "fsdp")),
        P(None, ("bucket", "fsdp"), None),
        P(("bucket", "fsdp"), None),
        P(None, ("bucket", "fsdp"), None),
        P(None, ("bucket", "fsdp"), None),
        P(("bucket", "fsdp"), None),
    )
    fast = mesh.shape["fsdp"] == 8 and mesh.shape["bucket"] == 4
    return jax.shard_map(
        per_device if fast else per_device_general, mesh=mesh, in_specs=in_specs, out_specs=out_specs, check_vma=False
    )
```

```python
import jax
import jax.numpy as jnp
import numpy as np
from jax import lax
from jax.experimental import pallas as pl
from jax.experimental.pallas import tpu as pltpu
from jax.sharding import PartitionSpec as P

D = 1536
HEADS = 24
HDIM = 64
IMGS = 4
TXT = 64


EPS = 1e-06
NEGATIVE = -1e30
HIGH = lax.Precision.HIGHEST


def silu(v):
    return v * jax.nn.sigmoid(v)


def norm_rows(v):
    inverse = lax.rsqrt(jnp.mean(v * v, axis=-1, keepdims=True) + EPS)
    return (v * inverse, inverse)


def norm_back(grad, normed, inverse):
    return inverse * (grad - normed * jnp.mean(grad * normed, axis=-1, keepdims=True))


def rotary_tables(pos):
    quarter = HDIM // 4
    freq = 10000.0 ** (-jnp.arange(quarter, dtype=jnp.float32) / quarter)
    angle = jnp.transpose(pos.astype(jnp.float32), (1, 0))[:, :, None] * freq[None, None, :]
    return (jnp.cos(angle), jnp.sin(angle))


def rotate(v, cosine, sine):
    rows = v.shape[0]
    parts = v.reshape(rows, HEADS, 2, 2, HDIM // 4)
    first = parts[:, :, :, 0]
    second = parts[:, :, :, 1]
    cosine = cosine[:, None]
    sine = sine[:, None]
    turned = jnp.stack([first * cosine - second * sine, first * sine + second * cosine], axis=3)
    return turned.reshape(rows, HEADS * HDIM)


def to_pairs(v):
    return jnp.transpose(v.reshape(v.shape[0], HEADS // 2, 2 * HDIM), (1, 0, 2))


def from_pairs(v):
    return jnp.transpose(v, (1, 0, 2)).reshape(v.shape[1], HEADS * HDIM)


def pair_scores(query, keys):
    q_heads = query.reshape(query.shape[0], 2, HDIM)
    k_heads = keys.reshape(keys.shape[0], 2, HDIM)
    return jnp.einsum(
        "rhd,khd->hrk", q_heads, k_heads, preferred_element_type=jnp.float32
    ) * HDIM ** (-0.5)


def attend_forward(q_b, k_b, v_b, allowed):

    def one_pair(item):
        query, keys, values = item
        scores = jnp.where(allowed[None], pair_scores(query, keys), NEGATIVE)
        top = jnp.max(scores, axis=-1, keepdims=True)
        expo = jnp.exp(scores - top)
        total = jnp.sum(expo, axis=-1, keepdims=True)
        probs = (expo / total).astype(jnp.bfloat16)
        result = jnp.einsum(
            "hrk,khd->rhd",
            probs,
            values.reshape(values.shape[0], 2, HDIM),
            preferred_element_type=jnp.float32,
        )
        return (result.reshape(query.shape[0], 2 * HDIM), (top + jnp.log(total))[..., 0])

    outputs, saved = lax.map(one_pair, (to_pairs(q_b), to_pairs(k_b), to_pairs(v_b)))
    return (from_pairs(outputs), saved)


def attend_back(q_b, k_b, v_b, saved, grad_b, allowed):

    def one_pair(item):
        query, keys, values, lse_pair, grad = item
        rows = query.shape[0]
        count = keys.shape[0]
        scores = jnp.where(allowed[None], pair_scores(query, keys), NEGATIVE)
        probs = jnp.exp(scores - lse_pair[..., None])
        probs_b = probs.astype(jnp.bfloat16)
        grad_heads = grad.reshape(rows, 2, HDIM)
        dprob = jnp.einsum(
            "rhd,khd->hrk",
            grad_heads,
            values.reshape(count, 2, HDIM),
            preferred_element_type=jnp.float32,
        )
        dscore = (probs * (dprob - jnp.sum(probs * dprob, axis=-1, keepdims=True))).astype(
            jnp.bfloat16
        )
        factor = HDIM ** (-0.5)
        dquery = (
            jnp.einsum(
                "hrk,khd->rhd",
                dscore,
                keys.reshape(count, 2, HDIM),
                preferred_element_type=jnp.float32,
            )
            * factor
        )
        dkeys = (
            jnp.einsum(
                "hrk,rhd->khd",
                dscore,
                query.reshape(rows, 2, HDIM),
                preferred_element_type=jnp.float32,
            )
            * factor
        )
        dvalues = jnp.einsum(
            "hrk,rhd->khd", probs_b, grad_heads, preferred_element_type=jnp.float32
        )
        return (
            dquery.reshape(rows, 2 * HDIM),
            dkeys.reshape(count, 2 * HDIM),
            dvalues.reshape(count, 2 * HDIM),
        )

    d_query, d_keys, d_values = lax.map(
        one_pair, (to_pairs(q_b), to_pairs(k_b), to_pairs(v_b), saved, to_pairs(grad_b))
    )
    return (from_pairs(d_query), from_pairs(d_keys), from_pairs(d_values))


def mult(left, right):
    return jnp.dot(left, right, preferred_element_type=jnp.float32)


def per_device_general(
    tokens,
    cond,
    text,
    segments,
    positions,
    counts,
    ada_weight,
    ada_bias,
    gains,
    attn_weight,
    out_weight,
    text_weight,
    ffn_weight,
    down_weight,
    cotangent,
):
    ada_w, ada_b, gain_rows, attn_w, out_w, text_w = (
        lax.all_gather(ada_weight, "fsdp", axis=0, tiled=True),
        lax.all_gather(ada_bias, "fsdp", axis=0, tiled=True),
        lax.all_gather(gains, "fsdp", axis=1, tiled=True),
        lax.all_gather(attn_weight, "fsdp", axis=1, tiled=True),
        lax.all_gather(out_weight, "fsdp", axis=0, tiled=True),
        lax.all_gather(text_weight, "fsdp", axis=1, tiled=True),
    )
    gain_f = gain_rows.astype(jnp.float32)
    x = tokens[0].astype(jnp.float32)
    seg = segments[0]
    cosine, sine = rotary_tables(positions[0])
    text_b = text[0]
    cond_act = silu(cond[0].astype(jnp.float32)).astype(jnp.bfloat16)
    mod = mult(cond_act, ada_w) + ada_b.astype(jnp.float32)[None, :]
    pick = (seg[:, None] == jnp.arange(IMGS, dtype=jnp.int32)[None, :]).astype(jnp.float32)
    per_token = jnp.dot(pick, mod, precision=HIGH)
    scale1 = per_token[:, :D]
    gate1 = per_token[:, D : 2 * D]
    scale2 = per_token[:, 2 * D : 3 * D]
    gate2 = per_token[:, 3 * D :]
    normed1, inverse1 = norm_rows(x)
    h_one = (normed1 * gain_f[0] * (1.0 + scale1)).astype(jnp.bfloat16)
    query = mult(h_one, attn_w[0])
    keyed = mult(h_one, attn_w[1])
    valued = mult(h_one, attn_w[2]).astype(jnp.bfloat16)
    q_norm, q_inv = norm_rows(query)
    k_norm, k_inv = norm_rows(keyed)
    q_rot = rotate(q_norm * gain_f[2], cosine, sine).astype(jnp.bfloat16)
    k_rot = rotate(k_norm * gain_f[3], cosine, sine).astype(jnp.bfloat16)
    text_keys = mult(text_b, text_w[0])
    text_vals = mult(text_b, text_w[1]).astype(jnp.bfloat16)
    t_norm, t_inv = norm_rows(text_keys)
    text_rot = (t_norm * gain_f[4]).astype(jnp.bfloat16)
    same = seg[:, None] == seg[None, :]
    owner = jnp.arange(IMGS * TXT, dtype=jnp.int32) // TXT
    mine = seg[:, None] == owner[None, :]
    self_out, self_lse = attend_forward(q_rot, k_rot, valued, same)
    cross_out, cross_lse = attend_forward(q_rot, text_rot, text_vals, mine)
    cross_gate = jnp.tanh(gain_f[5])
    comb = (self_out + cross_gate * cross_out).astype(jnp.bfloat16)
    branch = mult(comb, out_w)
    tanh_one = jnp.tanh(gate1)
    x_one = x + tanh_one * branch
    normed2, inverse2 = norm_rows(x_one)
    h_two = (normed2 * gain_f[1] * (1.0 + scale2)).astype(jnp.bfloat16)
    ffn_w, down_w = (
        lax.all_gather(ffn_weight, "fsdp", axis=1, tiled=True),
        lax.all_gather(down_weight, "fsdp", axis=0, tiled=True),
    )
    gate_pre = mult(h_two, ffn_w[0])
    upper = mult(h_two, ffn_w[1])
    sigm = jax.nn.sigmoid(gate_pre)
    silu_pre = gate_pre * sigm
    hidden = (silu_pre * upper).astype(jnp.bfloat16)
    ffn_out = mult(hidden, down_w)
    tanh_two = jnp.tanh(gate2)
    block_out = (x_one + tanh_two * ffn_out).astype(jnp.bfloat16)
    totals = counts.astype(jnp.float32)
    here = jnp.sum(
        jnp.where(
            jnp.arange(totals.shape[0], dtype=jnp.int32) == lax.axis_index("bucket"), totals, 0.0
        )
    )
    weight = lax.axis_size("bucket") * here / jnp.sum(totals)
    grad = cotangent[0].astype(jnp.float32) * weight
    back_ffn, back_down = (
        lax.all_gather(ffn_weight, "fsdp", axis=1, tiled=True),
        lax.all_gather(down_weight, "fsdp", axis=0, tiled=True),
    )
    d_gate2 = grad * ffn_out * (1.0 - tanh_two * tanh_two)
    d_ffn = (grad * tanh_two).astype(jnp.bfloat16)
    d_hidden = mult(d_ffn, back_down.T)
    g_down = mult(hidden.T, d_ffn)
    d_pre = (d_hidden * upper * sigm * (1.0 + gate_pre * (1.0 - sigm))).astype(jnp.bfloat16)
    d_up = (d_hidden * silu_pre).astype(jnp.bfloat16)
    d_h_two = mult(d_pre, back_ffn[0].T) + mult(d_up, back_ffn[1].T)
    g_ffn = jnp.stack([mult(h_two.T, d_pre), mult(h_two.T, d_up)])
    s_ffn, s_down = (
        lax.psum_scatter(g_ffn, ("bucket", "fsdp"), scatter_dimension=1, tiled=True),
        lax.psum_scatter(g_down, ("bucket", "fsdp"), scatter_dimension=0, tiled=True),
    )
    back_attn, back_out = (
        lax.all_gather(attn_weight, "fsdp", axis=1, tiled=True),
        lax.all_gather(out_weight, "fsdp", axis=0, tiled=True),
    )
    g_gain_one = jnp.sum(d_h_two * normed2 * (1.0 + scale2), axis=0)
    d_scale2 = d_h_two * normed2 * gain_f[1]
    d_x_one = grad + norm_back(d_h_two * gain_f[1] * (1.0 + scale2), normed2, inverse2)
    d_gate1 = d_x_one * branch * (1.0 - tanh_one * tanh_one)
    d_branch = (d_x_one * tanh_one).astype(jnp.bfloat16)
    d_comb = mult(d_branch, back_out.T)
    g_out = mult(comb.T, d_branch)
    g_gain_five = jnp.sum(d_comb * cross_out, axis=0) * (1.0 - cross_gate * cross_gate)
    d_self = d_comb.astype(jnp.bfloat16)
    d_cross = (d_comb * cross_gate).astype(jnp.bfloat16)
    dq_self, dk_self, dv_self = attend_back(q_rot, k_rot, valued, self_lse, d_self, same)
    dq_cross, dk_text, dv_text = attend_back(q_rot, text_rot, text_vals, cross_lse, d_cross, mine)
    d_q_norm = rotate(dq_self + dq_cross, cosine, -sine)
    g_gain_two = jnp.sum(d_q_norm * q_norm, axis=0)
    d_query = norm_back(d_q_norm * gain_f[2], q_norm, q_inv).astype(jnp.bfloat16)
    d_k_norm = rotate(dk_self, cosine, -sine)
    g_gain_three = jnp.sum(d_k_norm * k_norm, axis=0)
    d_keyed = norm_back(d_k_norm * gain_f[3], k_norm, k_inv).astype(jnp.bfloat16)
    d_valued = dv_self.astype(jnp.bfloat16)
    g_gain_four = jnp.sum(dk_text * t_norm, axis=0)
    d_text_keys = norm_back(dk_text * gain_f[4], t_norm, t_inv).astype(jnp.bfloat16)
    d_text_vals = dv_text.astype(jnp.bfloat16)
    g_text = jnp.stack([mult(text_b.T, d_text_keys), mult(text_b.T, d_text_vals)])
    d_h_one = (
        mult(d_query, back_attn[0].T)
        + mult(d_keyed, back_attn[1].T)
        + mult(d_valued, back_attn[2].T)
    )
    g_attn = jnp.stack([mult(h_one.T, d_query), mult(h_one.T, d_keyed), mult(h_one.T, d_valued)])
    g_gain_zero = jnp.sum(d_h_one * normed1 * (1.0 + scale1), axis=0)
    d_scale1 = d_h_one * normed1 * gain_f[0]
    token_grad = d_x_one + norm_back(d_h_one * gain_f[0] * (1.0 + scale1), normed1, inverse1)
    d_token_mod = jnp.concatenate([d_scale1, d_gate1, d_scale2, d_gate2], axis=1)
    d_mod = jnp.dot(pick.T, d_token_mod, precision=HIGH)
    g_ada_b = jnp.sum(d_mod, axis=0)
    g_ada_w = mult(cond_act.T, d_mod.astype(jnp.bfloat16))
    g_gains = jnp.stack(
        [g_gain_zero, g_gain_one, g_gain_two, g_gain_three, g_gain_four, g_gain_five]
    )
    s_ada_w, s_ada_b, s_gains, s_attn, s_out, s_text = (
        lax.psum_scatter(g_ada_w, ("bucket", "fsdp"), scatter_dimension=0, tiled=True),
        lax.psum_scatter(g_ada_b, ("bucket", "fsdp"), scatter_dimension=0, tiled=True),
        lax.psum_scatter(g_gains, ("bucket", "fsdp"), scatter_dimension=1, tiled=True),
        lax.psum_scatter(g_attn, ("bucket", "fsdp"), scatter_dimension=1, tiled=True),
        lax.psum_scatter(g_out, ("bucket", "fsdp"), scatter_dimension=0, tiled=True),
        lax.psum_scatter(g_text, ("bucket", "fsdp"), scatter_dimension=1, tiled=True),
    )
    return (
        block_out[None],
        token_grad[None],
        s_ada_w,
        s_ada_b,
        s_gains,
        s_attn,
        s_out,
        s_text,
        s_ffn,
        s_down,
    )


ROW = 128
CHIPS = 4
HW = D // CHIPS
PAIRS = HW // 128


def partner(u):
    lane = lax.broadcasted_iota(jnp.int32, u.shape, 1)
    ahead = pltpu.roll(u, u.shape[1] - 16, 1)
    behind = pltpu.roll(u, 16, 1)
    return jnp.where((lane // 16) % 2 == 0, ahead, behind)


def dot_t(a, b):
    return lax.dot_general(a, b, (((1,), (1,)), ((), ())), preferred_element_type=jnp.float32)


def dot_n(a, b):
    return lax.dot_general(a, b, (((1,), (0,)), ((), ())), preferred_element_type=jnp.float32)


def t_dot(a, b):
    return lax.dot_general(a, b, (((0,), (0,)), ((), ())), preferred_element_type=jnp.float32)


def softmax_of(scores, allowed):
    scores = jnp.where(allowed, scores * HDIM ** (-0.5), NEGATIVE)
    top = jnp.max(scores, axis=-1, keepdims=True)
    expo = jnp.exp(scores - top)
    return expo / jnp.sum(expo, axis=-1, keepdims=True)


def head_mask(v, head):
    lane = lax.broadcasted_iota(jnp.int32, v.shape, 1)
    return jnp.where((lane // HDIM) == head, v, jnp.zeros_like(v))


def masks_of(seg_col, seg_row, captions):
    same = seg_col == seg_row
    owner = lax.broadcasted_iota(jnp.int32, (seg_col.shape[0], captions), 1) // TXT
    return same, seg_col == owner


def attend_kernel(
    q_ref, k_ref, v_ref, iq_ref, ik_ref, cos_ref, sin_ref, tk_ref, it_ref, tv_ref, sc_ref, sr_ref,
    g_ref, comb_ref, cross_ref, qr_ref, kr_ref, tr_ref,
):
    same, mine = masks_of(sc_ref[...], sr_ref[...], tk_ref.shape[0])
    cosine = cos_ref[...]
    sine = sin_ref[...]
    low = jnp.bfloat16
    for pair in range(PAIRS):
        at = pl.ds(pair * 128, 128)
        qn = q_ref[:, at] * iq_ref[...] * g_ref[2:3, at]
        kn = k_ref[:, at] * ik_ref[...] * g_ref[3:4, at]
        qr = (qn * cosine + partner(qn) * sine).astype(low)
        kr = (kn * cosine + partner(kn) * sine).astype(low)
        tr = (tk_ref[:, at] * it_ref[...] * g_ref[4:5, at]).astype(low)
        qr_ref[:, at] = qr
        kr_ref[:, at] = kr
        tr_ref[:, at] = tr
        vv = v_ref[:, at]
        tv = tv_ref[:, at]
        self_out = jnp.zeros(qn.shape, jnp.float32)
        cross_out = jnp.zeros(qn.shape, jnp.float32)
        for head in range(2):
            qh = head_mask(qr, head)
            probs = softmax_of(dot_t(qh, kr), same).astype(low)
            self_out = self_out + head_mask(dot_n(probs, vv), head)
            probs = softmax_of(dot_t(qh, tr), mine).astype(low)
            cross_out = cross_out + head_mask(dot_n(probs, tv), head)
        cross_ref[:, at] = cross_out
        comb_ref[:, at] = (self_out + jnp.tanh(g_ref[5:6, at]) * cross_out).astype(low)


def attend_back_kernel(
    qr_ref, kr_ref, v_ref, tr_ref, tv_ref, dc_ref, cross_ref, q_ref, k_ref, tk_ref, iq_ref, ik_ref,
    it_ref, cos_ref, sin_ref, sc_ref, sr_ref, g_ref,
    dq_ref, dk_ref, dv_ref, dt_ref, dtv_ref, gg_ref,
):
    same, mine = masks_of(sc_ref[...], sr_ref[...], tk_ref.shape[0])
    cosine = cos_ref[...]
    sine = sin_ref[...]
    low = jnp.bfloat16
    factor = HDIM ** (-0.5)
    for pair in range(PAIRS):
        at = pl.ds(pair * 128, 128)
        qr = qr_ref[:, at]
        kr = kr_ref[:, at]
        vv = v_ref[:, at]
        tr = tr_ref[:, at]
        tv = tv_ref[:, at]
        dcomb = dc_ref[:, at]
        d_self = dcomb.astype(low)
        d_cross = (dcomb * jnp.tanh(g_ref[5:6, at])).astype(low)
        dq = jnp.zeros(dcomb.shape, jnp.float32)
        dk = jnp.zeros(dcomb.shape, jnp.float32)
        dv = jnp.zeros(dcomb.shape, jnp.float32)
        dt = jnp.zeros((tr.shape[0], 128), jnp.float32)
        dtv = jnp.zeros((tr.shape[0], 128), jnp.float32)
        for head in range(2):
            qh = head_mask(qr, head)
            probs = softmax_of(dot_t(qh, kr), same)
            grad = head_mask(d_self, head)
            dprob = dot_t(grad, vv)
            dscore = probs * (dprob - jnp.sum(probs * dprob, axis=-1, keepdims=True))
            dscore = dscore.astype(low)
            dq = dq + dot_n(dscore, head_mask(kr, head))
            dk = dk + t_dot(dscore, qh)
            dv = dv + t_dot(probs.astype(low), grad)
            probs = softmax_of(dot_t(qh, tr), mine)
            grad = head_mask(d_cross, head)
            dprob = dot_t(grad, tv)
            dscore = probs * (dprob - jnp.sum(probs * dprob, axis=-1, keepdims=True))
            dscore = dscore.astype(low)
            dq = dq + dot_n(dscore, head_mask(tr, head))
            dt = dt + t_dot(dscore, qh)
            dtv = dtv + t_dot(probs.astype(low), grad)
        dq = dq * factor
        dk = dk * factor
        dt = dt * factor
        dq = dq * cosine - partner(dq) * sine
        dk = dk * cosine - partner(dk) * sine
        q_norm = q_ref[:, at] * iq_ref[...]
        k_norm = k_ref[:, at] * ik_ref[...]
        t_norm = tk_ref[:, at] * it_ref[...]
        gg_ref[0:1, at] += jnp.sum(dq * q_norm, axis=0, keepdims=True)
        gg_ref[1:2, at] += jnp.sum(dk * k_norm, axis=0, keepdims=True)
        gg_ref[2:3, at] += jnp.sum(dt * t_norm, axis=0, keepdims=True)
        gg_ref[3:4, at] += jnp.sum(dcomb * cross_ref[:, at], axis=0, keepdims=True)
        dq = dq * g_ref[2:3, at]
        dk = dk * g_ref[3:4, at]
        dt = dt * g_ref[4:5, at]
        dq_ref[:, at] = dq
        dk_ref[:, at] = dk
        dv_ref[:, at] = dv.astype(low)
        dt_ref[:, at] = dt
        dtv_ref[:, at] = dtv.astype(low)


MESH_IDS = pl.DeviceIdType.MESH
VMEM_SPEC = pl.BlockSpec(memory_space=pltpu.VMEM)
ANY_SPEC = pl.BlockSpec(memory_space=pl.ANY)


def to_row_owner(block):
    pairs = [
        (a * 8 + b * 2 + k, b * 8 + a * 2 + k) for a in range(4) for b in range(4) for k in range(2)
    ]
    return lax.ppermute(block, ("bucket", "fsdp"), pairs).astype(jnp.float32)


class Net:
    def __init__(self, send_sems, recv_sems):
        self.me = lax.axis_index("fsdp")
        self.send_sems = send_sems
        self.recv_sems = recv_sems
        self.count = 0
        self.all = []

    def peer(self, mask):
        out = self.me
        for bit in (1, 2, 4):
            if mask & bit:
                out = out + bit * (1 - 2 * ((self.me // bit) % 2))
        return out

    def meet(self, masks):
        sem = pltpu.get_barrier_semaphore()
        for mask in masks:
            pl.semaphore_signal(
                sem, inc=1, device_id={"fsdp": self.peer(mask)}, device_id_type=MESH_IDS
            )
        pl.semaphore_wait(sem, len(masks))

    def send(self, src, dst, mask):
        assert self.count < self.send_sems.shape[0]
        copy = pltpu.make_async_remote_copy(
            src_ref=src,
            dst_ref=dst,
            send_sem=self.send_sems.at[self.count],
            recv_sem=self.recv_sems.at[self.count],
            device_id={"fsdp": self.peer(mask)},
            device_id_type=MESH_IDS,
        )
        self.count += 1
        copy.start()
        self.all.append(copy)
        return copy

    def close(self):
        for copy in self.all:
            copy.wait_send()


def net_scratch(count):
    return [pltpu.SemaphoreType.DMA((count,)), pltpu.SemaphoreType.DMA((count,))]


def share4_start(net, out):
    return net.send(out.at[0], out.at[1], 2), net.send(out.at[0], out.at[2], 4)


def share4_relay(net, out, by_x, by_y):
    half = out.shape[1] // 2
    top, bottom = pl.ds(0, half), pl.ds(half, half)
    by_x.wait_recv()
    first = net.send(out.at[1, top], out.at[3, top], 4)
    by_y.wait_recv()
    second = net.send(out.at[2, bottom], out.at[3, bottom], 2)
    return first, second


def collect4(net, part, buf, far):
    half = far.shape[1]
    rows = (pl.ds(0, half), pl.ds(half, half))
    low = jnp.bfloat16
    full = jnp.float32
    for i in (0, 1):
        buf[2, rows[i]] = part(3, i).astype(low)
    far_x = net.send(buf.at[2, rows[0]], far.at[0], 2)
    far_y = net.send(buf.at[2, rows[1]], far.at[1], 4)
    buf[0, rows[0]] = part(1, 0).astype(low)
    one_a = net.send(buf.at[0, rows[0]], buf.at[3, rows[0]], 2)
    buf[1, rows[1]] = part(2, 1).astype(low)
    two_b = net.send(buf.at[1, rows[1]], buf.at[4, rows[1]], 4)
    later = []

    def middle():
        far_x.wait_recv()
        buf[1, rows[0]] = (part(2, 0) + far[0].astype(full)).astype(low)
        later.append(net.send(buf.at[1, rows[0]], buf.at[4, rows[0]], 4))
        far_y.wait_recv()
        buf[0, rows[1]] = (part(1, 1) + far[1].astype(full)).astype(low)
        later.append(net.send(buf.at[0, rows[1]], buf.at[3, rows[1]], 2))

    def finish(i):
        (one_a, two_b)[i].wait_recv()
        later[i].wait_recv()
        return part(0, i) + buf[3, rows[i]].astype(full) + buf[4, rows[i]].astype(full)

    return middle, finish


def pick_rows(table, seg, first):
    out = table[first + IMGS - 1 : first + IMGS]
    for i in range(IMGS - 2, -1, -1):
        out = jnp.where(seg == i, table[first + i : first + i + 1], out)
    return out


def row_sums(a, b):
    ones = jnp.ones((8, a.shape[1]), jnp.float32)

    def one(v):
        return lax.dot_general(
            ones, v, (((1,), (1,)), ((), ())), precision=HIGH, preferred_element_type=jnp.float32
        )

    if b is None:
        return one(a)
    got = one(a)
    return jnp.where(lax.broadcasted_iota(jnp.int32, got.shape, 0) < 4, got, one(b))


class Lines:
    MASKS = (2, 4, 6)

    def __init__(self, net, src, dst, width, sems, local):
        self.net, self.src, self.dst, self.width, self.sems = net, src, dst, width, sems
        self.plane = lax.axis_index("bucket")
        self.chip = net.me // 2
        self.core = net.me % 2
        self.local = local
        self.ids = range(src.shape[0])

    def columns(self, c):
        return pl.ds(pl.multiple_of(c * self.width, 128), self.width)

    def lanes(self, i):
        return pl.ds(i * self.width, self.width)

    def away_start(self):
        own = self.dst.at[self.chip, self.core, self.plane]
        self.away = [
            self.net.send(
                self.src.at[i, self.plane, :, self.columns(self.net.peer(m) // 2)],
                own.at[:, self.lanes(i)],
                m,
            )
            for m in self.MASKS
            for i in self.ids
        ]

    def own_start(self):
        own = self.dst.at[self.chip, self.core]
        cuts = [self.src.at[i, :, :, self.columns(self.chip)] for i in self.ids]
        puts = [own.at[:, :, self.lanes(i)] for i in self.ids]
        self.ready = [self.net.send(a, b, 1) for a, b in zip(cuts, puts)]
        self.here = [self.local(i, a, b) for i, (a, b) in enumerate(zip(cuts, puts))]

    def copy(self, up, k, slab):
        at = self.dst.at[self.net.peer(self.MASKS[k]) // 2, self.core, slab]
        first = ((k * 2 + (0 if up else 1)) * 4 + slab) * 2
        return pltpu.make_async_remote_copy(
            src_ref=at,
            dst_ref=at,
            send_sem=self.sems.at[first],
            recv_sem=self.sems.at[first + 1],
            device_id={"bucket": self.plane + (1 if up else -1)},
            device_id_type=MESH_IDS,
        )

    def moves(self, h):
        for up in (True, False):
            slab = self.plane - h if up else self.plane + h
            there = (slab >= 0) if up else (slab <= 3)
            sends = (self.plane <= 2) if up else (self.plane >= 1)
            yield up, slab, there, sends

    def hop(self, h):
        if h == 0:
            for c in self.away:
                c.wait_recv()
        for up, slab, there, sends in self.moves(h):

            @pl.when(there)
            def _(up=up, slab=slab, sends=sends):
                for k in range(3):
                    if h > 0:
                        self.copy(up, k, slab).wait_recv()
                    if h < 3:

                        @pl.when(sends)
                        def _(k=k):
                            self.copy(up, k, slab).start()

    def finish(self):
        self.hop(3)
        for m in self.MASKS:
            at = self.dst.at[self.net.peer(m) // 2, self.core]
            self.ready.append(self.net.send(at, at, 1))

    def wait(self):
        for c in self.ready:
            c.wait_recv()

    def close(self):
        for h in range(3):
            for up, slab, there, sends in self.moves(h):

                @pl.when(there & sends)
                def _(up=up, slab=slab):
                    for k in range(3):
                        self.copy(up, k, slab).wait_send()


def meet_line(net, masks):
    plane = lax.axis_index("bucket")
    sem = pltpu.get_barrier_semaphore()
    for mask in masks:
        pl.semaphore_signal(
            sem, inc=1, device_id={"fsdp": net.peer(mask)}, device_id_type=MESH_IDS
        )
    for inner, step in ((plane >= 1, -1), (plane <= 2, 1)):

        @pl.when(inner)
        def _(step=step):
            pl.semaphore_signal(
                sem, inc=1, device_id={"bucket": plane + step}, device_id_type=MESH_IDS
            )

    one = jnp.int32(1)
    zero = jnp.int32(0)
    pl.semaphore_wait(
        sem, len(masks) + jnp.where(plane >= 1, one, zero) + jnp.where(plane <= 2, one, zero)
    )


ALL_PEERS = (1, 2, 3, 4, 5, 6, 7)


def open_kernel(
    cond_ref, gain_ref, bias_ref, ada_ref, tok_ref, counts_ref, idx_ref, freq_ref, attn_ref, textw_ref,
    text_ref,
    mod_ref, gains_ref, h_out, idxs_ref, aw_out, ta_out, q_out, k_out, v_out, tk_ref, tv_ref,
    iq_ref, ik_ref, it_ref, cos_ref, sin_ref, sc_ref, gs_ref,
    seg_ref, w_ref, h_ref, aw_ref, q_ref, k_ref, v_ref, conds, parts, mods, gbuf, tw_ref, ta_ref, sums, tsums, local_sems, out_sems, attn_sems, text_sems,
    send_sems, recv_sems,
):
    low = jnp.bfloat16
    full = jnp.float32
    net = Net(send_sems, recv_sems)
    me = net.me
    chip = me // 2
    meet_line(net, ALL_PEERS)

    act = cond_ref[...].astype(full)
    act = (act * jax.nn.sigmoid(act)).astype(low).astype(full)
    act = jnp.concatenate([act, act], axis=0)
    for j in range(8):
        gbuf[8, :, 128 * j : 128 * j + 128] = act[:, 128 * j : 128 * j + 128]
    waits = []
    for m in ALL_PEERS:
        at = pl.ds(pl.multiple_of(net.peer(m) * 128, 128), 128)
        waits.append(net.send(gbuf.at[8, :, at], conds.at[m], m))
    conds[0] = gbuf[8, :, pl.ds(pl.multiple_of(me * 128, 128), 128)]
    gwaits = [net.send(gain_ref, gbuf.at[m], m) for m in ALL_PEERS]
    iwaits = [net.send(idx_ref, idxs_ref.at[i], m) for i, m in ((1, 2), (2, 4), (3, 6))]
    idxs_ref[0] = idx_ref[...]

    def local(first):
        def go(i, src, dst):
            copy = pltpu.make_async_copy(src, dst, local_sems.at[first + i])
            copy.start()
            return copy

        return go

    attn_io = Lines(net, attn_ref, aw_ref, HW, attn_sems, local(3))
    text_io = Lines(net, textw_ref, tw_ref, HW, text_sems, local(6))
    attn_io.away_start()
    text_io.away_start()
    own_text = local(2)(0, text_ref, ta_ref.at[0])

    for w in waits:
        w.wait_recv()
    lhs = jnp.concatenate([conds[m] for m in range(8)], axis=0).astype(low)
    half_cols = 3072
    step = 512

    def mod_cols(i, _):
        lo = pl.ds(pl.multiple_of(i * step, step), step)
        hi = pl.ds(pl.multiple_of(half_cols + i * step, step), step)
        a = jnp.dot(lhs, ada_ref[:, lo], preferred_element_type=full)
        b = jnp.dot(lhs, ada_ref[:, hi], preferred_element_type=full)
        row = lax.broadcasted_iota(jnp.int32, (8, step), 0)
        for m in range(8):
            parts[m, :, lo] = (
                jnp.where(row < 4, a[8 * m : 8 * m + 8], b[8 * m : 8 * m + 8]) + bias_ref[:, lo]
            )
        return 0

    lax.fori_loop(0, half_cols // step, mod_cols, 0)
    waits = [net.send(parts.at[m], mods.at[m], m) for m in ALL_PEERS]

    attn_io.own_start()
    text_io.own_start()
    own_text.wait()

    def keep(j):
        copy = pltpu.make_async_copy(ta_ref.at[j], ta_out.at[j], out_sems.at[j])
        copy.start()
        return copy

    kept = [keep(0)]
    chunks = 4
    size = ta_ref.shape[1] // chunks
    tx, ty = [None] * chunks, [None] * chunks

    def text_send(s):
        i, j = s, (s + chunks // 2) % chunks
        at = pl.ds(i * size, size)
        tx[i] = net.send(ta_ref.at[0, at], ta_ref.at[1, at], 2)
        at = pl.ds(j * size, size)
        ty[j] = net.send(ta_ref.at[0, at], ta_ref.at[2, at], 4)

    text_send(0)
    attn_io.hop(0)
    text_io.hop(0)
    seg_ref[...] = jnp.transpose(idx_ref[...].astype(full))[:, 0:1].astype(jnp.int32)
    totals = counts_ref[...].astype(full)
    bucket = lax.broadcasted_iota(jnp.int32, totals.shape, 1) == lax.axis_index("bucket")
    here = jnp.sum(jnp.where(bucket, totals, 0.0), axis=-1, keepdims=True)
    weight = CHIPS * here / jnp.sum(totals, axis=-1, keepdims=True)
    w_ref[...] = jnp.broadcast_to(weight, w_ref.shape)
    for w in gwaits:
        w.wait_recv()
    gains = gain_ref[...]
    for m in ALL_PEERS:
        gains = gains + gbuf[m]
    gains_ref[...] = gains
    for w in waits:
        w.wait_recv()

    def mod_sum(i, _):
        at = pl.ds(pl.multiple_of(i * step, step), step)
        total = parts[0, :, at]
        for m in ALL_PEERS:
            total = total + mods[m, :, at]
        mod_ref[:, at] = total
        return 0

    lax.fori_loop(0, half_cols // step, mod_sum, 0)

    block = 32

    def first_norm(i, _):
        at = pl.ds(pl.multiple_of(i * block, block), block)
        x = tok_ref[at, :].astype(full)
        normed = x * lax.rsqrt(jnp.mean(x * x, axis=-1, keepdims=True) + EPS)
        scale = pick_rows(mod_ref[:, :D], seg_ref[at, :], 0)
        h_ref[0, at, :] = (normed * gains_ref[0:1, :] * (1.0 + scale)).astype(low)
        return 0

    lax.fori_loop(0, ROW // block, first_norm, 0)
    hx, hy = share4_start(net, h_ref)

    text_send(1)
    attn_io.hop(1)
    h_far = share4_relay(net, h_ref, hx, hy)
    for i in range(2, chunks):
        text_send(i)
    text_io.hop(1)
    attn_io.hop(2)
    attn_io.finish()
    text_io.hop(2)
    relays = []
    for s in range(chunks // 2):
        i, j = s, s + chunks // 2
        tx[i].wait_recv()
        at = pl.ds(i * size, size)
        relays.append(net.send(ta_ref.at[1, at], ta_ref.at[3, at], 4))
        ty[j].wait_recv()
        at = pl.ds(j * size, size)
        relays.append(net.send(ta_ref.at[2, at], ta_ref.at[3, at], 2))

    for c in iwaits:
        c.wait_recv()
    gs_ref[...] = gains_ref[:, pl.ds(pl.multiple_of(chip * HW, 128), HW)]
    lane = lax.broadcasted_iota(jnp.int32, (ROW, 128), 1)
    sign = jnp.where((lane // 16) % 2 == 0, -1.0, 1.0)
    for j in range(CHIPS):
        at = pl.ds(j * ROW, ROW)
        cols = jnp.transpose(idxs_ref[j].astype(full))
        sc_ref[at, :] = cols[:, 0:1].astype(jnp.int32)
        place = jnp.where((lane // 32) % 2 == 0, cols[:, 1:2], cols[:, 2:3])
        angle = place * freq_ref[0:1, :]
        cos_ref[at, :] = jnp.cos(angle)
        sin_ref[at, :] = sign * jnp.sin(angle)

    attn_io.wait()
    for c in attn_io.here:
        c.wait()
    for c in h_far:
        c.wait_recv()

    def columns(lo, hi):
        return aw_ref[:, :, :, :, lo:hi].reshape(D, hi - lo)

    for j in range(CHIPS):
        h = h_ref[j]
        at = pl.ds(j * ROW, ROW)
        qv = jnp.dot(h, columns(0, HW), preferred_element_type=full)
        q_ref[at, :] = qv
        kv = jnp.dot(h, columns(HW, 2 * HW), preferred_element_type=full)
        k_ref[at, :] = kv
        v_ref[at, :] = jnp.dot(h, columns(2 * HW, 3 * HW), preferred_element_type=full).astype(low)
        sums[0, :, at] = row_sums(qv * qv, kv * kv)
    sum_io = [net.send(sums.at[0], sums.at[i], m) for i, m in ((1, 2), (2, 4), (3, 6))]
    early = ((h_ref, h_out), (aw_ref, aw_out), (q_ref, q_out), (k_ref, k_out), (v_ref, v_out))
    for i, (src, dst) in enumerate(early):
        kept.append(pltpu.make_async_copy(src, dst, out_sems.at[CHIPS + i]))
        kept[-1].start()

    text_io.finish()
    text_io.wait()
    for c in text_io.here:
        c.wait()

    def text_rows(j, lo, count):
        kt = 1024

        def body(i, acc):
            at = pl.ds(pl.multiple_of(i * kt, kt), kt)
            rows = ta_ref[j, pl.ds(lo, count), at]
            return acc + jnp.dot(rows, tw_ref[i].reshape(kt, 2 * HW), preferred_element_type=full)

        both = lax.fori_loop(0, ta_ref.shape[2] // kt, body, jnp.zeros((count, 2 * HW), full))
        keys, vals = both[:, :HW], both[:, HW:]
        at = pl.ds(j * ta_ref.shape[1] + lo, count)
        tk_ref[at, :] = keys
        tv_ref[at, :] = vals.astype(low)
        tsums[0, :, at] = row_sums(keys * keys, None)

    cap = ta_ref.shape[1]
    half = cap // 2
    text_rows(0, 0, cap)
    for i, c in enumerate(sum_io):
        c.wait_recv()
    for j in range(CHIPS):
        total = sums[0, :, pl.ds(j * ROW, ROW)]
        for i in (1, 2, 3):
            total = total + sums[i, :, pl.ds((j ^ i) * ROW, ROW)]
        both = jnp.transpose(lax.rsqrt(total / D + EPS))
        iq_ref[pl.ds(j * ROW, ROW), :] = both[:, 0:1]
        ik_ref[pl.ds(j * ROW, ROW), :] = both[:, 4:5]
    text_rows(1, 0, half)
    text_rows(2, half, half)
    for s in range(chunks // 2):
        tx[s + chunks // 2].wait_recv()
        ty[s].wait_recv()
    kept += [keep(1), keep(2)]
    text_rows(1, half, half)
    text_rows(2, 0, half)
    for c in relays:
        c.wait_recv()
    kept.append(keep(3))
    text_rows(3, 0, cap)
    sum_io = [net.send(tsums.at[0], tsums.at[i], m) for i, m in ((1, 2), (2, 4), (3, 6))]
    for c in sum_io:
        c.wait_recv()
    for j in range(CHIPS):
        total = tsums[0, :, pl.ds(j * cap, cap)]
        for i in (1, 2, 3):
            total = total + tsums[i, :, pl.ds((j ^ i) * cap, cap)]
        it_ref[pl.ds(j * cap, cap), :] = jnp.transpose(lax.rsqrt(total / D + EPS))[:, 0:1]
    for c in kept:
        c.wait()
    attn_io.close()
    text_io.close()
    net.close()


def open_layer(cond, gain_pad, bias_pad, ada, tok, counts, idx, freq, attn, textw, text):
    low = jnp.bfloat16
    full = jnp.float32
    shape = jax.ShapeDtypeStruct
    cap, txtd = text.shape
    V = VMEM_SPEC
    return pl.pallas_call(
        open_kernel,
        in_specs=[V] * 8 + [ANY_SPEC] * 3,
        out_specs=[V, V, ANY_SPEC, V] + [ANY_SPEC] * 5 + [V] * 11,
        out_shape=[
            shape((8, 3072), full),
            shape((8, D), full),
            shape((CHIPS, ROW, D), low),
            shape((CHIPS, 8, ROW), jnp.int32),
            shape((CHIPS, 2, *attn.shape[1:3], 3 * HW), low),
            shape((CHIPS, cap, txtd), low),
            shape((CHIPS * ROW, HW), full),
            shape((CHIPS * ROW, HW), full),
            shape((CHIPS * ROW, HW), low),
            shape((CHIPS * cap, HW), full),
            shape((CHIPS * cap, HW), low),
            shape((CHIPS * ROW, 1), full),
            shape((CHIPS * ROW, 1), full),
            shape((CHIPS * cap, 1), full),
            shape((CHIPS * ROW, 128), full),
            shape((CHIPS * ROW, 128), full),
            shape((CHIPS * ROW, 1), jnp.int32),
            shape((8, HW), full),
            shape((ROW, 1), jnp.int32),
            shape((8, 128), full),
        ],
        scratch_shapes=[
            pltpu.VMEM((CHIPS, ROW, D), low),
            pltpu.VMEM((CHIPS, 2, *attn.shape[1:3], 3 * HW), low),
            pltpu.VMEM((CHIPS * ROW, HW), full),
            pltpu.VMEM((CHIPS * ROW, HW), full),
            pltpu.VMEM((CHIPS * ROW, HW), low),
            pltpu.VMEM((8, 8, 128), full),
            pltpu.VMEM((8, 8, 3072), full),
            pltpu.VMEM((8, 8, 3072), full),
            pltpu.VMEM((9, 8, D), full),
            pltpu.VMEM((CHIPS, 2, *textw.shape[1:3], 2 * HW), low),
            pltpu.VMEM((CHIPS, cap, txtd), low),
            pltpu.VMEM((CHIPS, 8, CHIPS * ROW), full),
            pltpu.VMEM((CHIPS, 8, CHIPS * cap), full),
            pltpu.SemaphoreType.DMA((8,)),
            pltpu.SemaphoreType.DMA((CHIPS + 5,)),
            pltpu.SemaphoreType.DMA((48,)),
            pltpu.SemaphoreType.DMA((48,)),
            *net_scratch(80),
        ],
        compiler_params=pltpu.CompilerParams(
            collective_id=1, has_side_effects=True, vmem_limit_bytes=56 * 1024 * 1024
        ),
        cost_estimate=pl.CostEstimate(
            flops=10_000_000_000, bytes_accessed=400_000_000, transcendentals=0
        ),
    )(cond, gain_pad, bias_pad, ada, tok, counts, idx, freq, attn, textw, text)


class Chain:
    def __init__(self, net, grad, mine, arrive, total, sems, columns):
        self.net = net
        self.grad = grad
        self.mine = mine
        self.arrive = arrive
        self.total = total
        self.sems = sems
        self.columns = columns
        self.plane = lax.axis_index("bucket")
        self.core = net.me % 2

    def piece(self, ref, p):
        return ref.at[:, p] if self.columns else ref.at[p]

    def half(self, core):
        return self.grad.at[:, :, :, core] if self.columns else self.grad.at[:, core]

    def each(self, ref, body):
        lead = ref.shape[:-2]
        if not lead:
            body(())
            return
        total = 1
        for n in lead:
            total *= n

        def step(i, _):
            index = []
            for n in reversed(lead):
                index.insert(0, i % n)
                i = i // n
            body(tuple(index))
            return 0

        lax.fori_loop(0, total, step, 0)

    def core_start(self, keep=None, sem=None):
        self.exchange = self.net.send(self.half(1 - self.core), self.mine, 1)
        self.keep = self.half(self.core)
        self.load = None
        if keep is not None:
            self.load = pltpu.make_async_copy(self.keep, keep, sem)
            self.load.start()
            self.keep = keep

    def add(self, into, other):
        def body(index):
            value = into[index].astype(jnp.float32) + other[index].astype(jnp.float32)
            into[index] = value.astype(into.dtype)

        self.each(into, body)

    def core_finish(self):
        self.exchange.wait_recv()
        if self.load is not None:
            self.load.wait()
        self.add(self.mine, self.keep)

    def copy(self, up, p, slot):
        first = 0 if up else 8
        return pltpu.make_async_remote_copy(
            src_ref=self.piece(self.mine, p),
            dst_ref=self.arrive.at[slot],
            send_sem=self.sems.at[first + p],
            recv_sem=self.sems.at[first + 4 + p],
            device_id={"bucket": self.plane + (1 if up else -1)},
            device_id_type=MESH_IDS,
        )

    def moves(self, t):
        up = self.plane + 3 - t
        down = self.plane - 3 + t
        return (
            (True, up, up, self.plane <= t, self.plane >= 1),
            (False, down, 4 if t == 2 else down, self.plane >= 3 - t, self.plane <= 2),
        )

    def step(self, t):
        for up, p, slot, sends, inner in self.moves(t):

            @pl.when(sends)
            def _(up=up, p=p, slot=slot, inner=inner):
                @pl.when(inner)
                def _():
                    self.copy(up, p, p).wait_recv()
                    self.add(self.piece(self.mine, p), self.arrive.at[p])

                self.copy(up, p, slot).start()

    def finish(self):
        own = self.piece(self.mine, self.plane)

        def first(index):
            self.total[index] = own[index].astype(jnp.float32)

        self.each(self.total, first)
        for up, slot, inner in ((True, self.plane, self.plane >= 1), (False, 4, self.plane <= 2)):

            @pl.when(inner)
            def _(up=up, slot=slot):
                self.copy(up, self.plane, slot).wait_recv()
                self.add(self.total, self.arrive.at[slot])

    def close(self):
        for t in range(3):
            for up, p, slot, sends, inner in self.moves(t):

                @pl.when(sends)
                def _(up=up, p=p, slot=slot):
                    self.copy(up, p, slot).wait_send()


def chain_scratch(columns, shape, width):
    low = jnp.bfloat16
    if columns:
        n, rows = shape
        return [
            pltpu.VMEM((n, 4, 4, rows, width), low),
            pltpu.VMEM((5, n, 4, rows, width), low),
            pltpu.VMEM((n, 4, rows, width), jnp.float32),
            pltpu.SemaphoreType.DMA((16,)),
        ]
    return [
        pltpu.VMEM((4, shape, width), low),
        pltpu.VMEM((5, shape, width), low),
        pltpu.VMEM((shape, width), jnp.float32),
        pltpu.SemaphoreType.DMA((16,)),
    ]


class Columns:
    def __init__(self, net, total, stage, wide):
        self.net, self.total, self.stage, self.wide = net, total, stage, wide

    def start(self):
        net = self.net
        chip = net.me // 2
        n, _, rows, width = self.stage.shape
        parts = self.wide.shape[0]
        width = width // parts
        at = pl.ds(pl.multiple_of(chip * width, width), width)

        def cast(i, _):
            self.stage[i // 4, i % 4] = self.total[i // 4, i % 4].astype(jnp.bfloat16)
            return 0

        if self.total is not None:
            lax.fori_loop(0, n * 4, cast, 0)
        self.copies = [
            net.send(
                self.stage.at[0, net.peer(m) // 2, :, pl.ds(i * width, width)],
                self.wide.at[i, :, at],
                m,
            )
            for m in (2, 4, 6)
            for i in range(parts)
        ]
        for i in range(parts):
            self.wide[i, :, at] = self.stage[0, chip, :, i * width : i * width + width]

    def finish(self):
        for c in self.copies:
            c.wait_recv()


def meet_all(net, far=False):
    plane = lax.axis_index("bucket")
    chip = net.me // 2
    sem = pltpu.get_barrier_semaphore()
    for mask in ALL_PEERS:
        pl.semaphore_signal(
            sem, inc=1, device_id={"fsdp": net.peer(mask)}, device_id_type=MESH_IDS
        )
    for inner, step in ((plane >= 1, -1), (plane <= 2, 1)):

        @pl.when(inner)
        def _(step=step):
            pl.semaphore_signal(
                sem, inc=1, device_id={"bucket": plane + step}, device_id_type=MESH_IDS
            )

    @pl.when(chip != plane)
    def _():
        pl.semaphore_signal(
            sem,
            inc=1,
            device_id={"bucket": chip, "fsdp": plane * 2 + net.me % 2},
            device_id_type=MESH_IDS,
        )

    if far:
        pl.semaphore_signal(
            sem,
            inc=1,
            device_id={"bucket": plane + 2 - 4 * (plane // 2)},
            device_id_type=MESH_IDS,
        )
    one = jnp.int32(1)
    zero = jnp.int32(0)
    count = (
        (8 if far else 7)
        + jnp.where(plane >= 1, one, zero)
        + jnp.where(plane <= 2, one, zero)
        + jnp.where(chip != plane, one, zero)
    )
    pl.semaphore_wait(sem, count)


def transposed(net, src, dst, sems):
    plane = lax.axis_index("bucket")
    return pltpu.make_async_remote_copy(
        src_ref=src,
        dst_ref=dst,
        send_sem=sems.at[0],
        recv_sem=sems.at[1],
        device_id={"bucket": net.me // 2, "fsdp": plane * 2 + net.me % 2},
        device_id_type=MESH_IDS,
    )


class Spread:
    def __init__(self, buf, sems):
        self.buf, self.sems = buf, sems
        self.plane = lax.axis_index("bucket")

    def copy(self, up, slab):
        first = 0 if up else 8
        return pltpu.make_async_remote_copy(
            src_ref=self.buf.at[slab],
            dst_ref=self.buf.at[slab],
            send_sem=self.sems.at[first + slab],
            recv_sem=self.sems.at[first + 4 + slab],
            device_id={"bucket": self.plane + (1 if up else -1)},
            device_id_type=MESH_IDS,
        )

    def hop(self, h):
        for up in (True, False):
            slab = self.plane - h if up else self.plane + h
            there = (slab >= 0) if up else (slab <= 3)
            sends = (self.plane <= 2) if up else (self.plane >= 1)

            @pl.when(there)
            def _(up=up, slab=slab, sends=sends):
                if h > 0:
                    self.copy(up, slab).wait_recv()

                @pl.when(sends)
                def _():
                    self.copy(up, slab).start()

    def close(self):
        for h in range(4):
            for up in (True, False):
                slab = self.plane - h if up else self.plane + h
                there = (slab >= 0) if up else (slab <= 3)
                sends = (self.plane <= 2) if up else (self.plane >= 1)

                @pl.when(there & sends)
                def _(up=up, slab=slab):
                    self.copy(up, slab).wait_send()


def close_kernel(
    ta_ref, dt_ref, attn_g, out_g, ffn_t, dmod_ref, gg_ref, gs_ref, cond_ref,
    t_wide, a_wide, out_o, f_wide, ada_o, small_o,
    tm, ta, tt, ts, am, aa, at_, as_, om, oa, ot, os_,
    t_stage, a_stage, o_stage, o_got, o_sem,
    mods, mods_other, mod_sems, smalls, got, z_sems, ada_s, ta_s, text_g, ta_sem, send_sems, recv_sems,
):
    low = jnp.bfloat16
    full = jnp.float32
    net = Net(send_sems, recv_sems)
    load = pltpu.make_async_copy(ta_ref, ta_s, ta_sem.at[0])
    load.start()
    meet_all(net, True)
    plane = lax.axis_index("bucket")
    me = net.me
    chip = me // 2
    out = Chain(net, out_g, om, oa, ot, os_, False)
    attn = Chain(net, attn_g, am, aa, at_, as_, True)
    text = Chain(net, text_g, tm, ta, tt, ts, True)
    chains = [out, attn, text]
    first = [out, attn]
    for c in first:
        c.core_start()

    def caption_grad(core):
        def block(i, _):
            at = (i // 4) * 1024 + (i % 4) * 256 + core * 128
            part = t_dot(ta_s[:, pl.ds(pl.multiple_of(at, 128), 128)], dt_ref[...])
            text_g[0, i // 4, i % 4, core] = part.astype(low)
            return 0

        lax.fori_loop(0, 16, block, 0)

    act = cond_ref[...].astype(full)
    act = act * jax.nn.sigmoid(act)
    mods[plane, 0, :, 2 * D :] = jnp.concatenate([act, act], axis=0).astype(low)
    mods[plane, 0, :, : 2 * D] = dmod_ref[...].astype(low)
    mine = mods.at[plane, 0]
    mod_io = [net.send(mine, mods.at[plane, i], m) for i, m in ((1, 2), (2, 4), (3, 6))]

    smalls[...] = jnp.zeros(smalls.shape, full)
    smalls[0:2, :] = gg_ref[0:2, :]
    smalls[2:6, pl.ds(pl.multiple_of(chip * HW, 128), HW)] = gs_ref[0:4, :]
    for p in range(4):
        rows = dmod_ref[4 * (p // 2) : 4 * (p // 2) + 4, (p % 2) * D : (p % 2 + 1) * D]
        smalls[8 + p : 9 + p, :] = jnp.sum(rows, axis=0, keepdims=True)
    order = [None]

    def small_send(i):
        if i < 3:
            order[0] = net.send(smalls, got.at[i], (1, 2, 4)[i])
            return
        there = plane + 1 - 2 * (plane % 2) if i == 3 else plane + 2 - 4 * (plane // 2)
        copy = pltpu.make_async_remote_copy(
            src_ref=smalls,
            dst_ref=got.at[i],
            send_sem=z_sems.at[2 * (i - 3)],
            recv_sem=z_sems.at[2 * (i - 3) + 1],
            device_id={"bucket": there},
            device_id_type=MESH_IDS,
        )
        copy.start()
        order[0] = copy

    def small_add(i):
        order[0].wait()
        net.all = [c for c in net.all if c is not order[0]]
        smalls[...] = smalls[...] + got[i]

    small_send(0)
    f_cols = Columns(net, None, ffn_t, f_wide)
    f_cols.start()
    for c in first:
        c.core_finish()
        c.step(0)
    load.wait()
    caption_grad(1 - me % 2)
    text.core_start()
    small_add(0)
    small_send(1)
    for c in first:
        c.step(1)
    for c in mod_io:
        c.wait_recv()
    lines = Spread(mods, mod_sems)
    lines.hop(0)
    caption_grad(me % 2)
    text.core_finish()
    text.step(0)
    small_add(1)
    small_send(2)
    for c in first:
        c.step(2)
    lines.hop(1)
    small_add(2)
    small_send(3)
    f_cols.finish()
    text.step(1)
    lines.hop(2)
    small_add(3)
    small_send(4)
    text.step(2)
    lines.hop(3)
    other = net.send(mods, mods_other, 1)
    small_add(4)
    small_o[...] = smalls[...]
    out.finish()
    o_stage[...] = ot[...].astype(low)

    @pl.when(chip != plane)
    def _():
        transposed(net, o_stage, o_got, o_sem).start()

    other.wait_recv()
    rank = plane * 8 + me
    lanes = pl.ds(pl.multiple_of(2 * D + (rank // 4) * 128, 128), 128)
    total = 128
    both = []
    for ref in (mods, mods_other):
        acts = ref[:, :, :, lanes].astype(full).reshape(total, 128)
        both.append(acts)
    acts = jnp.concatenate(both, axis=0)
    upper = (lax.broadcasted_iota(jnp.int32, acts.shape, 0) % 8) < 4
    parts = (jnp.where(upper, acts, 0.0).astype(low), jnp.where(upper, 0.0, acts).astype(low))
    wide = 512

    def ada_cols(i, _):
        at = pl.ds(pl.multiple_of(i * wide, wide), wide)
        rows = jnp.concatenate(
            [r[:, :, :, at].astype(full).reshape(total, wide) for r in (mods, mods_other)], axis=0
        ).astype(low)
        for p in range(2):
            ada_s[...] = t_dot(parts[p], rows)
            to = pl.ds(pl.multiple_of(p * 2 * D + i * wide, wide), wide)
            ada_o[:, to] = ada_s[pl.ds(pl.multiple_of((rank % 4) * 32, 32), 32), :]
        return 0

    lax.fori_loop(0, 2 * D // wide, ada_cols, 0)
    attn.finish()
    attn_cols = Columns(net, at_, a_stage, a_wide)
    attn_cols.start()

    @pl.when(chip != plane)
    def _():
        transposed(net, o_stage, o_got, o_sem).wait()
        out_o[...] = o_got[...]

    @pl.when(chip == plane)
    def _():
        out_o[...] = o_stage[...]

    text.finish()
    text_cols = Columns(net, tt, t_stage, t_wide)
    text_cols.start()
    attn_cols.finish()
    text_cols.finish()
    for c in chains:
        c.close()
    lines.close()
    net.close()


def close_layer(text_all, d_text, attn_g, out_g, ffn_t, dmod, gg, gs, cond):
    low = jnp.bfloat16
    full = jnp.float32
    shape = jax.ShapeDtypeStruct
    V = VMEM_SPEC
    tr, tw = text_all.shape[1] // 32, d_text.shape[1] // 2
    ar, aw = attn_g.shape[-2], attn_g.shape[-1] // 3
    orow, ow = out_g.shape[-2:]
    fr, fw = ffn_t.shape[-2], ffn_t.shape[-1] // 2
    return pl.pallas_call(
        close_kernel,
        in_specs=[ANY_SPEC] + [V] * 8,
        out_specs=[V] * 6,
        out_shape=[
            shape((2, tr, 4 * tw), low),
            shape((3, ar, 4 * aw), low),
            shape((orow, ow), low),
            shape((2, fr, 4 * fw), low),
            shape((32, 4 * D), full),
            shape((16, D), full),
        ],
        scratch_shapes=[
            *chain_scratch(True, (1, tr), 2 * tw),
            *chain_scratch(True, (1, ar), 3 * aw),
            *chain_scratch(False, orow, ow),
            pltpu.VMEM((1, 4, tr, 2 * tw), low),
            pltpu.VMEM((1, 4, ar, 3 * aw), low),
            pltpu.VMEM((orow, ow), low),
            pltpu.VMEM((orow, ow), low),
            pltpu.SemaphoreType.DMA((2,)),
            pltpu.VMEM((4, CHIPS, 8, 2 * D + cond.shape[1]), low),
            pltpu.VMEM((4, CHIPS, 8, 2 * D + cond.shape[1]), low),
            pltpu.SemaphoreType.DMA((16,)),
            pltpu.VMEM((16, D), full),
            pltpu.VMEM((5, 16, D), full),
            pltpu.SemaphoreType.DMA((4,)),
            pltpu.VMEM((128, 512), full),
            pltpu.VMEM(text_all.shape, low),
            pltpu.VMEM((1, 4, 4, 2, tr, 2 * tw), low),
            pltpu.SemaphoreType.DMA((1,)),
            *net_scratch(40),
        ],
        compiler_params=pltpu.CompilerParams(
            collective_id=2, has_side_effects=True, vmem_limit_bytes=60 * 1024 * 1024
        ),
        cost_estimate=pl.CostEstimate(
            flops=1_000_000, bytes_accessed=400_000_000, transcendentals=0
        ),
    )(text_all, d_text, attn_g, out_g, ffn_t, dmod, gg, gs, cond)


def back_kernel(
    dh2_ref, fo_ref, x1_ref, branch_ref, cot_ref, w_ref, mod_ref, seg_ref, gain_ref, tok_ref,
    sr_ref, gs_ref, *rest,
):
    late, rest = rest[:LATE], rest[LATE:]
    places, rest = rest[-LATE - 1 : -1], rest[: -LATE - 1] + rest[-1:]
    loads = [
        pltpu.make_async_copy(src, dst, rest[-1].at[i])
        for i, (src, dst) in enumerate(zip(late, places))
    ]
    back_body(
        dh2_ref, fo_ref, x1_ref, branch_ref, cot_ref, w_ref, mod_ref, seg_ref, gain_ref, tok_ref,
        *places, sr_ref, gs_ref, *rest[:-1], loads,
    )


LATE = 17


def back_body(
    dh2_ref, fo_ref, x1_ref, branch_ref, cot_ref, w_ref, mod_ref, seg_ref, gain_ref, tok_ref,
    ow_ref, aw_ref, qr_ref, kr_ref, v_ref, tr_ref, tv_ref, cross_ref, q_ref, k_ref, tk_ref,
    iq_ref, ik_ref, it_ref, cos_ref, sin_ref, sc_ref, sr_ref, gs_ref, ffn_g, down_g,
    block_o, token_o, db_ref, dqkv_o, dtkv_o, dmod_o, gg_o, gs_o, ffn_o, down_o,
    dx_s, dc_s, dqf, dkf, dtf, part_s, sums, tsums, buf_a, far_a, buf_b, far_b, buf_c, far_c,
    fm, fa, ft, fs, dm, da, dt_c, ds_, f_keep, d_keep, keep_sem, send_sems, recv_sems, loads,
):
    low = jnp.bfloat16
    full = jnp.float32
    net = Net(send_sems, recv_sems)
    meet_all(net)
    plane = lax.axis_index("bucket")
    chip = net.me // 2
    ffn = Chain(net, ffn_g, fm, fa, ft, fs, True)
    down = Chain(net, down_g, dm, da, dt_c, ds_, False)
    ffn.core_start(f_keep, keep_sem.at[0])
    down.core_start(d_keep, keep_sem.at[1])
    for c in loads:
        c.start()

    def rows_of(ref):
        half = ROW // 2
        return lambda j, i: ref[pl.ds(j * ROW + i * half, half), :].astype(full)

    middle, finish = collect4(net, rows_of(dh2_ref), buf_a, far_a)
    middle()
    ffn.core_finish()
    ffn.step(0)
    down.core_finish()
    down.step(0)
    half = ROW // 2
    for i in (0, 1):
        dx_s[pl.ds(i * half, half), :] = finish(i)
    part_s[pl.ds(0, ROW), :] = dx_s[...]
    block = 32
    weight = w_ref[0:1, 0:1]

    def second_norm(at):
        x1 = x1_ref[at, :]
        inverse = lax.rsqrt(jnp.mean(x1 * x1, axis=-1, keepdims=True) + EPS)
        scale = pick_rows(mod_ref[:, :D], seg_ref[at, :], 4)
        return x1 * inverse, inverse, scale

    def to_branch(b, _):
        at = pl.ds(pl.multiple_of(b * block, block), block)
        normed, inverse, scale = second_norm(at)
        dn = dx_s[at, :] * gain_ref[1:2, :] * (1.0 + scale)
        back = inverse * (dn - normed * jnp.mean(dn * normed, axis=-1, keepdims=True))
        dx = cot_ref[at, :].astype(full) * weight + back
        dx_s[at, :] = dx
        gate = jnp.tanh(pick_rows(mod_ref[:, D:], seg_ref[at, :], 0))
        db_ref[0, at, :] = (dx * gate).astype(low)
        return 0

    lax.fori_loop(0, ROW // block, to_branch, 0)
    bx, by = share4_start(net, db_ref)

    def by_image(value, seg, row, lo):
        for i in range(IMGS):
            dmod_o[row + i : row + i + 1, lo : lo + D] += jnp.sum(
                jnp.where(seg == i, value, 0.0), axis=0, keepdims=True
            )

    dmod_o[...] = jnp.zeros(dmod_o.shape, full)
    gg_o[...] = jnp.zeros(gg_o.shape, full)

    def second_sums(b, _):
        at = pl.ds(pl.multiple_of(b * block, block), block)
        normed, inverse, scale = second_norm(at)
        seg = seg_ref[at, :]
        dh = part_s[at, :] * normed
        gg_o[1:2, :] += jnp.sum(dh * (1.0 + scale), axis=0, keepdims=True)
        by_image(dh * gain_ref[1:2, :], seg, 4, 0)
        gate = jnp.tanh(pick_rows(mod_ref[:, D:], seg, 0))
        by_image(dx_s[at, :] * branch_ref[at, :] * (1.0 - gate * gate), seg, 0, D)
        return 0

    lax.fori_loop(0, ROW // block, second_sums, 0)
    far = share4_relay(net, db_ref, bx, by)
    middle_b, finish_b = collect4(net, rows_of(fo_ref), buf_b, far_b)
    gs_o[...] = jnp.zeros(gs_o.shape, full)
    for c in loads:
        c.wait()
    cap = IMGS * TXT

    def attention_row(j, _):
        @pl.when(j == 3)
        def _():
            for c in far:
                c.wait_recv()

        @pl.when(j == 1)
        def _():
            ffn.step(1)
            down.step(1)

        @pl.when(j == 3)
        def _():
            ffn.step(2)
            down.step(2)

        rows = pl.ds(pl.multiple_of(j * ROW, ROW), ROW)
        text = pl.ds(pl.multiple_of(j * cap, cap), cap)
        dc_s[...] = dot_t(db_ref[j], ow_ref[...])
        dqv, dkv, dtv = dqf.at[rows], dkf.at[rows], dtf.at[text]
        attend_back_kernel(
            qr_ref.at[rows], kr_ref.at[rows], v_ref.at[rows], tr_ref.at[text], tv_ref.at[text],
            dc_s, cross_ref.at[rows], q_ref.at[rows], k_ref.at[rows], tk_ref.at[text],
            iq_ref.at[rows], ik_ref.at[rows], it_ref.at[text], cos_ref.at[rows], sin_ref.at[rows],
            sc_ref.at[rows], sr_ref.at[j, pl.ds(0, 1)], gs_ref,
            dqv, dkv, dqkv_o.at[rows, pl.ds(2 * HW, HW)], dtv, dtkv_o.at[text, pl.ds(HW, HW)], gs_o,
        )
        sums[0, :, rows] = row_sums(
            dqv[...] * (q_ref[rows, :] * iq_ref[rows, :]),
            dkv[...] * (k_ref[rows, :] * ik_ref[rows, :]),
        )
        tsums[0, :, text] = row_sums(dtv[...] * (tk_ref[text, :] * it_ref[text, :]), None)
        return 0

    lax.fori_loop(0, CHIPS, attention_row, 0)
    sum_io = []
    for i, m in ((1, 2), (2, 4), (3, 6)):
        sum_io.append(net.send(sums.at[0], sums.at[i], m))
        sum_io.append(net.send(tsums.at[0], tsums.at[i], m))
    middle_b()
    for i in (0, 1):
        part_s[pl.ds(i * half, half), :] = finish_b(i)

    def block_rows(b, _):
        at = pl.ds(pl.multiple_of(b * block, block), block)
        seg = seg_ref[at, :]
        gate = jnp.tanh(pick_rows(mod_ref[:, D:], seg, 4))
        out = part_s[at, :]
        block_o[at, :] = (x1_ref[at, :] + gate * out).astype(low)
        grad = cot_ref[at, :].astype(full) * weight
        by_image(grad * out * (1.0 - gate * gate), seg, 4, D)
        return 0

    for c in sum_io:
        c.wait_recv()
    for j in range(CHIPS):
        rows = pl.ds(j * ROW, ROW)
        text = pl.ds(j * cap, cap)
        total = sums[0, :, rows]
        words = tsums[0, :, text]
        for i in (1, 2, 3):
            total = total + sums[i, :, pl.ds((j ^ i) * ROW, ROW)]
            words = words + tsums[i, :, pl.ds((j ^ i) * cap, cap)]
        mean = jnp.transpose(total / D)
        iq, ik, it = iq_ref[rows, :], ik_ref[rows, :], it_ref[text, :]
        dqkv_o[rows, :HW] = (iq * (dqf[rows, :] - q_ref[rows, :] * iq * mean[:, 0:1])).astype(low)
        dqkv_o[rows, HW : 2 * HW] = (ik * (dkf[rows, :] - k_ref[rows, :] * ik * mean[:, 4:5])).astype(low)
        mean = jnp.transpose(words / D)
        dtkv_o[text, :HW] = (it * (dtf[text, :] - tk_ref[text, :] * it * mean[:, 0:1])).astype(low)

    lax.fori_loop(0, ROW // block, block_rows, 0)
    wide = 256

    def first_grad(n, _):
        at = pl.ds(pl.multiple_of(n * wide, wide), wide)
        part_s[:, at] = dot_t(dqkv_o[...], aw_ref[at, :])
        return 0

    lax.fori_loop(0, D // wide, first_grad, 0)
    middle_c, finish_c = collect4(net, rows_of(part_s), buf_c, far_c)
    ffn.finish()
    middle_c()

    def ffn_cast(i, _):
        ffn_o[0, i] = ft[0, i].astype(low)
        return 0

    lax.fori_loop(0, 4, ffn_cast, 0)
    down.finish()
    down_o[...] = dt_c[...].astype(low)
    gate = jnp.tanh(gs_ref[5:6, :])
    gs_o[3:4, :] = gs_o[3:4, :] * (1.0 - gate * gate)
    for i in (0, 1):
        part_s[pl.ds(i * half, half), :] = finish_c(i)

    def first_rows(b, _):
        at = pl.ds(pl.multiple_of(b * block, block), block)
        x = tok_ref[at, :].astype(full)
        inverse = lax.rsqrt(jnp.mean(x * x, axis=-1, keepdims=True) + EPS)
        normed = x * inverse
        seg = seg_ref[at, :]
        scale = pick_rows(mod_ref[:, :D], seg, 0)
        dh = part_s[at, :]
        gg_o[0:1, :] += jnp.sum(dh * normed * (1.0 + scale), axis=0, keepdims=True)
        by_image(dh * normed * gain_ref[0:1, :], seg, 0, 0)
        dn = dh * gain_ref[0:1, :] * (1.0 + scale)
        token_o[at, :] = dx_s[at, :] + inverse * (
            dn - normed * jnp.mean(dn * normed, axis=-1, keepdims=True)
        )
        return 0

    lax.fori_loop(0, ROW // block, first_rows, 0)
    ffn.close()
    down.close()
    net.close()


def back_layer(early, late, ffn_g, down_g):
    low = jnp.bfloat16
    full = jnp.float32
    shape = jax.ShapeDtypeStruct
    V = VMEM_SPEC
    cap = IMGS * TXT
    fr, fw = ffn_g.shape[-2], ffn_g.shape[-1] // 2
    dr, dw = down_g.shape[-2:]
    tok = CHIPS * ROW
    reduce_scratch = [pltpu.VMEM((5, ROW, D), low), pltpu.VMEM((2, ROW // 2, D), low)]
    return pl.pallas_call(
        back_kernel,
        in_specs=[V] * len(early) + [ANY_SPEC] * (LATE + 2),
        out_specs=[V] * 10,
        out_shape=[
            shape((ROW, D), low),
            shape((ROW, D), full),
            shape((CHIPS, ROW, D), low),
            shape((tok, 3 * HW), low),
            shape((CHIPS * cap, 2 * HW), low),
            shape((8, 2 * D), full),
            shape((8, D), full),
            shape((8, HW), full),
            shape((1, 4, fr, 2 * fw), low),
            shape((dr, dw), low),
        ],
        scratch_shapes=[
            pltpu.VMEM((ROW, D), full),
            pltpu.VMEM((ROW, HW), full),
            pltpu.VMEM((tok, HW), full),
            pltpu.VMEM((tok, HW), full),
            pltpu.VMEM((CHIPS * cap, HW), full),
            pltpu.VMEM((tok, D), full),
            pltpu.VMEM((CHIPS, 8, tok), full),
            pltpu.VMEM((CHIPS, 8, CHIPS * cap), full),
            *reduce_scratch, *reduce_scratch, *reduce_scratch,
            *chain_scratch(True, (1, fr), 2 * fw),
            *chain_scratch(False, dr, dw),
            pltpu.VMEM((1, 4, 4, fr, 2 * fw), low),
            pltpu.VMEM((4, dr, dw), low),
            pltpu.SemaphoreType.DMA((2,)),
            *net_scratch(48),
            *[pltpu.VMEM(v.shape, v.dtype) for v in late],
            pltpu.SemaphoreType.DMA((LATE,)),
        ],
        compiler_params=pltpu.CompilerParams(
            collective_id=3, has_side_effects=True, vmem_limit_bytes=63 * 1024 * 1024
        ),
        cost_estimate=pl.CostEstimate(
            flops=10_000_000_000, bytes_accessed=400_000_000, transcendentals=0
        ),
    )(*early, *late, ffn_g, down_g)


def row_spec(rows, width):
    return pl.BlockSpec((rows, width), lambda i: (i, 0))


def forward_kernel(
    q_ref, k_ref, v_ref, iq_ref, ik_ref, cos_ref, sin_ref, tk_ref, it_ref, tv_ref, sc_ref, sr_ref,
    gs_ref, mod_ref, seg_ref, gain_ref, tok_ref, cot_ref, w_ref, outw_ref, ffnw_ref, downw_ref,
    comb_e, cross_e, qr_e, kr_e, tr_e, branch_o, x1_o, h_o, df_e, ow_o, fw_o, dw_o,
    comb_o, cross_o, qr_o, kr_o, tr_o, df_o, early_sems, part_s, buf, far, f_own, d_own, local_sems, line_sems, send_sems, recv_sems,
):
    low = jnp.bfloat16
    full = jnp.float32
    net = Net(send_sems, recv_sems)
    meet_line(net, (1, 2, 4, 6))
    me = net.me
    chip = me // 2
    width = fw_o.shape[4] // 2
    rows = outw_ref.shape[0]

    def local(src, dst, i):
        copy = pltpu.make_async_copy(src, dst, local_sems.at[i])
        copy.start()
        return copy

    def own(ref, count):
        return ref.at[pl.ds(pl.multiple_of((me % 2) * count, count), count), :]

    out_here = local(outw_ref, own(ow_o, rows), 0)
    out_core = net.send(outw_ref, own(ow_o, rows), 1)
    down_rows = downw_ref.shape[0]
    down_here = local(downw_ref, d_own, 1)
    down_core = net.send(downw_ref, own(dw_o, down_rows), 1)

    def stage(i, src, dst):
        return local(src, f_own.at[:, :, pl.ds(i * width, width)], 2 + i)

    ffn_io = Lines(net, ffnw_ref, fw_o, width, line_sems, stage)
    ffn_io.away_start()
    ffn_io.own_start()
    block = 32
    weight = w_ref[0:1, 0:1]

    def ffn_grad(b, _):
        at = pl.ds(pl.multiple_of(b * block, block), block)
        gate = jnp.tanh(pick_rows(mod_ref[:, D:], seg_ref[at, :], 4))
        df_o[0, at, :] = (cot_ref[at, :].astype(full) * weight * gate).astype(low)
        return 0

    lax.fori_loop(0, ROW // block, ffn_grad, 0)
    dx, dy = share4_start(net, df_o)
    out_here.wait()
    out_core.wait_recv()
    cap = IMGS * TXT

    def attention_row(i, _):
        @pl.when(i == 1)
        def _():
            ffn_io.hop(0)

        @pl.when(i == 3)
        def _():
            ffn_io.hop(1)

        j = 3 - i
        at = pl.ds(pl.multiple_of(j * ROW, ROW), ROW)
        text = pl.ds(pl.multiple_of(j * cap, cap), cap)
        attend_kernel(
            q_ref.at[at], k_ref.at[at], v_ref.at[at], iq_ref.at[at], ik_ref.at[at],
            cos_ref.at[at], sin_ref.at[at], tk_ref.at[text], it_ref.at[text], tv_ref.at[text],
            sc_ref.at[at], sr_ref.at[j, pl.ds(0, 1)], gs_ref,
            comb_o.at[at], cross_o.at[at], qr_o.at[at], kr_o.at[at], tr_o.at[text],
        )
        part_s[at, :] = jnp.dot(comb_o[at, :], ow_o[...], preferred_element_type=full)
        return 0

    lax.fori_loop(0, CHIPS, attention_row, 0)
    half = ROW // 2
    middle, finish = collect4(
        net, lambda j, i: part_s[pl.ds(j * ROW + i * half, half), :], buf, far
    )
    df_far = share4_relay(net, df_o, dx, dy)
    kept = []

    def keep(src, dst):
        kept.append(pltpu.make_async_copy(src, dst, early_sems.at[len(kept)]))
        kept[-1].start()

    for src, dst in (
        (comb_o, comb_e), (cross_o, cross_e), (qr_o, qr_e), (kr_o, kr_e), (tr_o, tr_e)
    ):
        keep(src, dst)

    down_here.wait()
    down_out = local(d_own, own(dw_o, down_rows), 4)
    for c in ffn_io.here:
        c.wait()
    f_out = local(f_own, fw_o.at[chip, me % 2], 5)
    middle()
    ffn_io.hop(2)
    for i in (0, 1):
        branch_o[pl.ds(i * half, half), :] = finish(i)

    def second(b, _):
        at = pl.ds(pl.multiple_of(b * block, block), block)
        seg = seg_ref[at, :]
        gate = jnp.tanh(pick_rows(mod_ref[:, D:], seg, 0))
        x1 = tok_ref[at, :].astype(full) + gate * branch_o[at, :]
        x1_o[at, :] = x1
        normed = x1 * lax.rsqrt(jnp.mean(x1 * x1, axis=-1, keepdims=True) + EPS)
        scale = pick_rows(mod_ref[:, :D], seg, 4)
        h_o[0, at, :] = (normed * gain_ref[1:2, :] * (1.0 + scale)).astype(low)
        return 0

    lax.fori_loop(0, ROW // block, second, 0)
    hx, hy = share4_start(net, h_o)
    for c in df_far:
        c.wait_recv()
    keep(df_o, df_e)
    ffn_io.finish()
    last = share4_relay(net, h_o, hx, hy)
    for c in (*last, down_core):
        c.wait_recv()
    ffn_io.wait()
    for c in (*kept, down_out, f_out):
        c.wait()
    ffn_io.close()
    net.close()


def forward_layer(*args):
    low = jnp.bfloat16
    full = jnp.float32
    shape = jax.ShapeDtypeStruct
    V = VMEM_SPEC
    cap = IMGS * TXT
    tok = CHIPS * ROW
    out_w, ffn_w, down_w = args[-3:]
    width = ffn_w.shape[3] // CHIPS
    return pl.pallas_call(
        forward_kernel,
        in_specs=[V] * (len(args) - 3) + [ANY_SPEC] * 3,
        out_specs=[ANY_SPEC] * 5 + [V] * 3 + [ANY_SPEC, V, ANY_SPEC, ANY_SPEC],
        out_shape=[
            shape((tok, HW), low),
            shape((tok, HW), full),
            shape((tok, HW), low),
            shape((tok, HW), low),
            shape((CHIPS * cap, HW), low),
            shape((ROW, D), full),
            shape((ROW, D), full),
            shape((CHIPS, ROW, D), low),
            shape((CHIPS, ROW, D), low),
            shape((2 * out_w.shape[0], D), low),
            shape((CHIPS, 2, *ffn_w.shape[1:3], 2 * width), low),
            shape((2 * down_w.shape[0], D), low),
        ],
        scratch_shapes=[
            pltpu.VMEM((tok, HW), low),
            pltpu.VMEM((tok, HW), full),
            pltpu.VMEM((tok, HW), low),
            pltpu.VMEM((tok, HW), low),
            pltpu.VMEM((CHIPS * cap, HW), low),
            pltpu.VMEM((CHIPS, ROW, D), low),
            pltpu.SemaphoreType.DMA((6,)),
            pltpu.VMEM((tok, D), full),
            pltpu.VMEM((5, ROW, D), low),
            pltpu.VMEM((2, ROW // 2, D), low),
            pltpu.VMEM((*ffn_w.shape[1:3], 2 * width), low),
            pltpu.VMEM(down_w.shape, low),
            pltpu.SemaphoreType.DMA((6,)),
            pltpu.SemaphoreType.DMA((48,)),
            *net_scratch(40),
        ],
        compiler_params=pltpu.CompilerParams(
            collective_id=4, has_side_effects=True, vmem_limit_bytes=56 * 1024 * 1024
        ),
        cost_estimate=pl.CostEstimate(
            flops=5_000_000_000, bytes_accessed=200_000_000, transcendentals=0
        ),
    )(*args)


def quarters(w):
    n, rows, columns = w.shape
    return w.reshape(n, 4, rows // 4, columns)


def per_device(
    tokens,
    cond,
    text,
    segments,
    positions,
    counts,
    ada_weight,
    ada_bias,
    gains,
    attn_weight,
    out_weight,
    text_weight,
    ffn_weight,
    down_weight,
    cotangent,
):
    low = jnp.bfloat16
    full = jnp.float32
    plane = lax.axis_index("bucket")
    slot = lax.axis_index("fsdp")
    core = slot % 2
    chip = slot // 2
    ff = ffn_weight.shape[2] // CHIPS

    gain_pad = lax.dynamic_update_slice_in_dim(
        jnp.zeros((8, D), full), jnp.pad(gains.astype(full), ((0, 2), (0, 0))), slot * 192, axis=1
    )
    bias = lax.dynamic_update_slice_in_dim(
        jnp.zeros((ada_weight.shape[1],), full), ada_bias.astype(full), slot * ada_bias.shape[0], 0
    )
    bias_pad = jnp.repeat(bias.reshape(2, 3072), 4, axis=0)
    seg = segments[0]
    idx = jnp.concatenate([seg[None, :], positions[0], jnp.zeros((5, ROW), jnp.int32)], axis=0)
    quarter = HDIM // 4
    freq = np.tile(10000.0 ** (-np.arange(quarter) / quarter), (8, 128 // quarter))
    freq_row = jnp.asarray(freq.astype(np.float32))
    (
        mod, gain_f, h_rows, idx_all, attn_w, text_rows, query, keyed, valued, text_keys, text_vals,
        inv_q, inv_k, inv_t, cosine, sine, seg_col, gain_s, seg_own, weight_row,
    ) = open_layer(
        cond[0], gain_pad, bias_pad, ada_weight, tokens[0],
        counts[None, :], idx, freq_row, quarters(attn_weight), quarters(text_weight), text[0],
    )
    attn_w = attn_w.reshape(D, 3 * HW)
    h_all = h_rows.reshape(CHIPS * ROW, D)
    text_all = text_rows.reshape(CHIPS * IMGS * TXT, -1)
    (
        comb, cross_out, q_rot, k_rot, text_rot, branch, x_one, h_two_rows, d_ffn_rows, out_w, ffn_w,
        down_w,
    ) = forward_layer(
        query, keyed, valued, inv_q, inv_k, cosine, sine, text_keys, inv_t, text_vals,
        seg_col, idx_all, gain_s, mod, seg_own, gain_f, tokens[0], cotangent[0], weight_row,
        out_weight, quarters(ffn_weight), down_weight,
    )
    ffn_w = ffn_w.reshape(D, 2 * ff)
    h_two_all = h_two_rows.reshape(CHIPS * ROW, D)
    d_ffn_all = d_ffn_rows.reshape(CHIPS * ROW, D)
    both = mult(h_two_all, ffn_w)
    gate_pre = both[:, :ff]
    upper = both[:, ff:]
    d_hidden = dot_t(d_ffn_all, down_w)
    sigm = jax.nn.sigmoid(gate_pre)
    silu_pre = gate_pre * sigm
    hidden = (silu_pre * upper).astype(low)
    d_pre = (d_hidden * upper * sigm * (1.0 + gate_pre * (1.0 - sigm))).astype(low)
    d_up = (d_hidden * silu_pre).astype(low)
    d_both = jnp.concatenate([d_pre, d_up], axis=1)
    d_h_two = dot_t(d_both, ffn_w).astype(low)
    ffn_out = mult(hidden, down_w).astype(low)
    g_down = t_dot(hidden, d_ffn_all).astype(low)
    g_ffn = t_dot(h_two_all, d_both).astype(low)

    (
        block_out, token_grad, d_branch_rows, d_qkv, d_text, d_mod, gg_full, gg_slice, ffn_sum, down_sum,
    ) = back_layer(
        [
            d_h_two, ffn_out, x_one, branch, cotangent[0], weight_row, mod,
            seg_own, gain_f, tokens[0], idx_all, gain_s,
        ],
        [
            out_w, attn_w, q_rot, k_rot, valued, text_rot, text_vals, cross_out, query, keyed,
            text_keys, inv_q, inv_k, inv_t, cosine, sine, seg_col,
        ],
        g_ffn.reshape(1, 4, 4, 2, 48, 2 * ff),
        g_down.reshape(4, 2, 128, D),
    )
    d_branch_all = d_branch_rows.reshape(CHIPS * ROW, D)
    g_attn = t_dot(h_all, d_qkv).astype(low)
    g_out = t_dot(comb, d_branch_all).astype(low)
    s_down = to_row_owner(down_sum)
    s_text, s_attn, s_out, s_ffn, s_ada_w, small = close_layer(
        text_all,
        d_text,
        g_attn.reshape(1, 4, 4, 2, 48, 3 * HW),
        g_out.reshape(4, 2, 48, D),
        ffn_sum,
        d_mod,
        gg_full,
        gg_slice,
        cond[0],
    )
    rank = plane * 8 + slot
    s_gains = lax.dynamic_slice_in_dim(small[:6], rank * 48, 48, axis=1)
    s_ada_b = lax.dynamic_slice_in_dim(small[8:12].reshape(-1), rank * 192, 192, axis=0)
    return (
        block_out[None],
        token_grad[None],
        s_ada_w,
        s_ada_b,
        s_gains,
        s_attn.astype(full),
        s_out.astype(full),
        s_text.astype(full),
        s_ffn.astype(full),
        s_down,
    )


def solution(mesh):
    in_specs = (
        P(("bucket", "fsdp"), None, None),
        P(("bucket", "fsdp"), None, None),
        P(("bucket", "fsdp"), None, None),
        P(("bucket", "fsdp"), None),
        P(("bucket", "fsdp"), None, None),
        P(),
        P("fsdp", None),
        P("fsdp"),
        P(None, "fsdp"),
        P(None, "fsdp", None),
        P("fsdp", None),
        P(None, "fsdp", None),
        P(None, "fsdp", None),
        P("fsdp", None),
        P(("bucket", "fsdp"), None, None),
    )
    out_specs = (
        P(("bucket", "fsdp"), None, None),
        P(("bucket", "fsdp"), None, None),
        P(("bucket", "fsdp"), None),
        P(("bucket", "fsdp")),
        P(None, ("bucket", "fsdp")),
        P(None, ("bucket", "fsdp"), None),
        P(("bucket", "fsdp"), None),
        P(None, ("bucket", "fsdp"), None),
        P(None, ("bucket", "fsdp"), None),
        P(("bucket", "fsdp"), None),
    )
    fast = mesh.shape["fsdp"] == 8 and mesh.shape["bucket"] == 4
    return jax.shard_map(
        per_device if fast else per_device_general, mesh=mesh, in_specs=in_specs, out_specs=out_specs, check_vma=False
    )
```
